128 devices in a mesh: dp: 16 (over z, y), row: 2 (over x_hi), col: 4 (over x_lo, core).
Axes of the slice: x: 4 (x_hi: 2, x_lo: 2; x = x_hi * 2 + x_lo), y: 4, z: 4, core: 2. Of those that a mesh axis runs over, the one named last changes fastest.
Arguments:
- inputs: bfloat16 [16384, 2048], P(('dp', 'col'), 'row'), may hold values from -6 to 6
- cotangent: bfloat16 [16384, 2048], P(('dp', 'col'), 'row'), may hold values from -16 to 16
- lengths: int32 [16], P('dp'), may hold values from 512 to 1024, as said below
- attention_norm_gain: float32 [2048], P('row'), may hold values from 0.5 to 1.5
- attention_norm_bias: float32 [2048], P('row'), may hold values from -1.75 to 1.75
- qkv_weight: bfloat16 [2048, 6144], P(('row', 'dp'), 'col'), may hold values from -0.125 to 0.125
- query_bias: bfloat16 [2048], P(('col', 'dp')), may hold values from -3 to 3
- value_bias: bfloat16 [2048], P(('col', 'dp')), may hold values from -3 to 3
- dense_weight: bfloat16 [2048, 2048], P(('col', 'dp'), 'row'), may hold values from -0.375 to 0.375
- dense_bias: bfloat16 [2048], P(('row', 'dp')), may hold values from -1.75 to 1.75
- feedforward_norm_gain: float32 [2048], P('row'), may hold values from 0.5 to 1.5
- feedforward_norm_bias: float32 [2048], P('row'), may hold values from -1.75 to 1.75
- fc1_weight: bfloat16 [2048, 8192], P(('row', 'dp'), 'col'), may hold values from -0.125 to 0.125
- fc1_bias: bfloat16 [8192], P(('col', 'dp')), may hold values from -1.75 to 1.75
- fc2_weight: bfloat16 [8192, 2048], P(('col', 'dp'), 'row'), may hold values from -0.09375 to 0.09375
- fc2_bias: bfloat16 [2048], P(('row', 'dp')), may hold values from -1.75 to 1.75
Outputs:
- outputs: bfloat16 [16384, 2048], P(('dp', 'col'), 'row')
- input_gradient: float32 [16384, 2048], P(('dp', 'col'), 'row')
- grad_qkv_weight: float32 [2048, 6144], P(('row', 'dp'), 'col')
- grad_query_bias: float32 [2048], P(('col', 'dp'))
- grad_value_bias: float32 [2048], P(('col', 'dp'))
- grad_dense_weight: float32 [2048, 2048], P(('col', 'dp'), 'row')
- grad_dense_bias: float32 [2048], P(('row', 'dp'))
- grad_fc1_weight: float32 [2048, 8192], P(('row', 'dp'), 'col')
- grad_fc1_bias: float32 [8192], P(('col', 'dp'))
- grad_fc2_weight: float32 [8192, 2048], P(('col', 'dp'), 'row')
- grad_fc2_bias: float32 [2048], P(('row', 'dp'))
- grad_norm1_gain: float32 [2048], P('row')
- grad_norm1_bias: float32 [2048], P('row')
- grad_norm2_gain: float32 [2048], P('row')
- grad_norm2_bias: float32 [2048], P('row')
The draws below stay inside these ranges and needn't reach their ends.
Inputs may be any that keep to these rules, and one draw needn't show every extreme that they name: `lengths`: some sequence has all 1024 tokens valid.
All inputs are finite; a program needn't handle non-finite values.
Results may differ from the reference program's by a relative error of at most 0.023.
Values may be sent and summed in bfloat16 or wider, within the bound.
A program may use at most 192 MiB of HBM per device.

```python
import jax
import jax.numpy as jnp
from jax import lax

D = 2048
HEADS = 32
HEAD_DIM = 64
FF = 8192
SEQ_LEN = 1024
BLOCK = 256
QBLOCK = 512
SEQS = 16
TOKENS = 16384


def draw_lengths(key, part):
    pick_key, fill_key = jax.random.split(key)
    drawn = jax.random.randint(fill_key, (SEQS,), SEQ_LEN // 2, SEQ_LEN + 1)
    chosen = jax.random.randint(pick_key, (), 0, SEQS)
    return jnp.where(jnp.arange(SEQS) == chosen, SEQ_LEN, drawn).astype(jnp.int32)


def strengthened(entries, own_key, source, target, parts, factor):
    def block_of(position):
        return (jnp.arange(entries.shape[position]) // (entries.shape[position] // parts)).reshape((-1,) + (1,) * (entries.ndim - 1 - position))

    near = jax.random.permutation(own_key, parts)[block_of(target)]
    other_side = (block_of(target) + parts // 2) % parts
    return jnp.where((block_of(source) == near) | (block_of(source) == other_side), factor * entries, entries)


def steps_of(own_key, shape, pieces, low, high):
    def one(position, shards_of):
        draws = jax.random.uniform(jax.random.fold_in(jax.random.fold_in(own_key, 6), position), (shards_of,), jnp.float32, low / len(pieces), high / len(pieces))
        return jnp.repeat(jnp.exp(draws), shape[position] // shards_of).reshape((-1,) + (1,) * (len(shape) - position - 1))

    level = one(*pieces[0])
    for cut in pieces[1:]:
        level = level * one(*cut)
    return level


def gaussian(own_key, dims, scale, most, cuts=(), kind=jnp.bfloat16):
    result = scale * jax.random.normal(own_key, dims, jnp.float32)
    if cuts:
        result = result * steps_of(own_key, dims, cuts, -0.22, 0.18)
    return jnp.clip(result, -most, most).astype(kind)


def bell_draw_with(stream_key, shape, scale, bound, pieces, heavy, kind=jnp.bfloat16):
    values = scale * jax.random.normal(stream_key, shape, jnp.float32)
    if pieces:
        values = values * steps_of(stream_key, shape, pieces, -0.22, 0.18)
    return jnp.clip(strengthened(values, jax.random.fold_in(stream_key, 3), *heavy), -bound, bound).astype(kind)


def setup_inputs(seed: int = 0) -> dict:
    key_list = jax.random.split(jax.random.key(seed), 17)
    inputs = gaussian(key_list[0], (TOKENS, D), 1.0, 6.0, ((0, 64), (1, 2)))
    cotangent = bell_draw_with(key_list[1], (TOKENS, D), 1.0, 16.0, ((0, 64), (1, 2)), (0, 1, 64, 4.0))
    lengths = draw_lengths(jax.random.fold_in(key_list[16], 71), 0)
    attention_norm_gain = jnp.clip(1.0 + 0.1 * jax.random.normal(key_list[3], (D,), jnp.float32), 0.5, 1.5)
    attention_norm_bias = gaussian(key_list[4], (D,), 0.3, 1.75, ((0, 2),), jnp.float32)
    qkv_weight = gaussian(key_list[5], (D, 3 * D), D ** -0.5, 0.125, ((0, 32), (1, 4)))
    query_bias = gaussian(key_list[6], (D,), 0.5, 3.0, ((0, 64),))
    value_bias = gaussian(key_list[7], (D,), 0.5, 3.0, ((0, 64),))
    dense_weight = gaussian(key_list[8], (D, D), (D // 8) ** -0.5, 0.375, ((0, 64), (1, 2)))
    dense_bias = gaussian(key_list[9], (D,), 0.3, 1.75, ((0, 32),))
    feedforward_norm_gain = jnp.clip(1.0 + 0.1 * jax.random.normal(key_list[10], (D,), jnp.float32), 0.5, 1.5)
    feedforward_norm_bias = gaussian(key_list[11], (D,), 0.3, 1.75, ((0, 2),), jnp.float32)
    fc1_weight = gaussian(key_list[12], (D, FF), D ** -0.5, 0.125, ((0, 32), (1, 4)))
    fc1_bias = gaussian(key_list[13], (FF,), 0.3, 1.75, ((0, 64),))
    fc2_weight = gaussian(key_list[14], (FF, D), (FF // 2) ** -0.5, 0.09375, ((0, 64), (1, 2)))
    fc2_bias = gaussian(key_list[15], (D,), 0.3, 1.75, ((0, 32),))
    return {"inputs": inputs, "cotangent": cotangent, "lengths": lengths, "attention_norm_gain": attention_norm_gain, "attention_norm_bias": attention_norm_bias, "qkv_weight": qkv_weight, "query_bias": query_bias, "value_bias": value_bias, "dense_weight": dense_weight, "dense_bias": dense_bias, "feedforward_norm_gain": feedforward_norm_gain, "feedforward_norm_bias": feedforward_norm_bias, "fc1_weight": fc1_weight, "fc1_bias": fc1_bias, "fc2_weight": fc2_weight, "fc2_bias": fc2_bias}


EPSILON = 1e-05
MASKED = -1e+30
PRECISE = lax.Precision.HIGHEST

@jax.custom_vjp
def low(v):
    return lax.optimization_barrier(v.astype(jnp.bfloat16)).astype(jnp.float32)

@jax.custom_vjp
def low_back(v):
    return v

def low_keep(v):
    return (low(v), None)

def low_pass(kept, grad):
    return (grad,)

def back_keep(v):
    return (v, None)

def back_low(kept, grad):
    return (low(grad),)
low.defvjp(low_keep, low_pass)
low_back.defvjp(back_keep, back_low)

def layer_norm(values, layer_norm_gain, offset):
    average = lax.optimization_barrier(jnp.mean(values, -1, keepdims=True))
    spread = lax.optimization_barrier(jnp.mean((values - average) ** 2, -1, keepdims=True))
    return (values - average) * lax.rsqrt(spread + EPSILON) * layer_norm_gain + offset

def matmul(left_side, right_side):
    return jnp.dot(left_side, right_side, precision=PRECISE, preferred_element_type=jnp.float32)

def attend(queries, key_heads, values, length):
    seq_len = queries.shape[0]
    key_pos = jnp.arange(seq_len, dtype=jnp.int32)
    slopes = jnp.exp2(-8.0 * (jnp.arange(HEADS, dtype=jnp.float32) + 1.0) / HEADS)

    def one_block(block_start):
        query_block = lax.dynamic_slice_in_dim(queries, block_start, QBLOCK, 0)
        query_pos = block_start + jnp.arange(QBLOCK, dtype=jnp.int32)
        scores = jnp.einsum('qhe,khe->hqk', query_block, key_heads, precision=PRECISE) * HEAD_DIM ** (-0.5)
        distance = jnp.abs(query_pos[:, None] - key_pos[None, :]).astype(jnp.float32)
        scores = low_back(scores - slopes[:, None, None] * distance[None])
        allowed = (key_pos[None, :] // BLOCK <= query_pos[:, None] // BLOCK) & (key_pos[None, :] < length)
        scores = jnp.where(allowed[None], scores, MASKED)
        row_peak = lax.optimization_barrier(jnp.max(scores, -1, keepdims=True))
        exponent = jnp.exp(scores - row_peak)
        probability = exponent / lax.optimization_barrier(jnp.sum(exponent, -1, keepdims=True))
        return jnp.einsum('hqk,khe->qhe', low(probability), values, precision=PRECISE)
    starts = jnp.arange(seq_len // QBLOCK, dtype=jnp.int32) * QBLOCK
    blocks = lax.map(jax.checkpoint(one_block), starts)
    return blocks.reshape(seq_len, HEADS, HEAD_DIM)

def residual_block(inputs, params, length):
    attention_norm_gain, attention_norm_bias, qkv_weight, query_bias, value_bias, dense_weight, dense_bias, feedforward_norm_gain, feedforward_norm_bias, fc1_weight, fc1_bias, fc2_weight, fc2_bias = params
    seq_len = inputs.shape[0]
    first_normalized_rows = low(layer_norm(inputs, attention_norm_gain, attention_norm_bias))
    projected = matmul(first_normalized_rows, qkv_weight).reshape(seq_len, HEADS, 3, HEAD_DIM)
    queries = low(low_back(projected[:, :, 0] + query_bias.reshape(HEADS, HEAD_DIM)))
    key_heads = low(low_back(projected[:, :, 1]))
    values = low(low_back(projected[:, :, 2] + value_bias.reshape(HEADS, HEAD_DIM)))
    attended = low(low_back(attend(queries, key_heads, values, length).reshape(seq_len, D)))
    residual_stream = inputs + low_back(matmul(attended, dense_weight) + dense_bias)
    second_normalized_rows = low(layer_norm(residual_stream, feedforward_norm_gain, feedforward_norm_bias))
    hidden = low_back(matmul(second_normalized_rows, fc1_weight) + fc1_bias)
    activated = low(jax.nn.gelu(hidden, approximate=False))
    return residual_stream + low_back(matmul(activated, fc2_weight) + fc2_bias)

def reference(inputs, cotangent, lengths, attention_norm_gain, attention_norm_bias, qkv_weight, query_bias, value_bias, dense_weight, dense_bias, feedforward_norm_gain, feedforward_norm_bias, fc1_weight, fc1_bias, fc2_weight, fc2_bias):
    params = tuple((item_array.astype(jnp.float32) for item_array in (attention_norm_gain, attention_norm_bias, qkv_weight, query_bias, value_bias, dense_weight, dense_bias, feedforward_norm_gain, feedforward_norm_bias, fc1_weight, fc1_bias, fc2_weight, fc2_bias)))
    sources = inputs.astype(jnp.float32).reshape(SEQS, SEQ_LEN, D)
    cotangents = cotangent.astype(jnp.float32).reshape(SEQS, SEQ_LEN, D)

    def one_sequence(running_totals, sequence_item):
        source_rows, cotangent_seq, length = sequence_item
        outputs, pullback = jax.vjp(lambda value_seq, weights: residual_block(value_seq, weights, length), source_rows, params)
        grad_source, grad_params = pullback(cotangent_seq)
        running_totals = jax.tree.map(lambda running, extra: running + extra, running_totals, grad_params)
        return (running_totals, (outputs, grad_source))
    initial = jax.tree.map(jnp.zeros_like, params)
    running_totals, (outputs, input_grads) = lax.scan(one_sequence, initial, (sources, cotangents, lengths))
    g_norm1_gain, g_norm1_bias, g_qkv, g_query, g_value, g_dense, g_dense_bias, g_norm2_gain, g_norm2_bias, g_fc1, g_fc1_bias, g_fc2, g_fc2_bias = running_totals
    return (outputs.reshape(TOKENS, D).astype(jnp.bfloat16), input_grads.reshape(TOKENS, D), g_qkv, g_query, g_value, g_dense, g_dense_bias, g_fc1, g_fc1_bias, g_fc2, g_fc2_bias, g_norm1_gain, g_norm1_bias, g_norm2_gain, g_norm2_bias)
```

```python
from functools import partial

import jax
import jax.numpy as jnp
from jax import lax
from jax.experimental import pallas as pl
from jax.experimental.pallas import tpu as pltpu
from jax.sharding import PartitionSpec as P

HEADS = 32
HEAD_DIM = 64
BLOCK = 256
SEQ = 1024
WIDTH = 2048
HALF = WIDTH // 2
LOCAL = 256
EPSILON = 1e-05
FAR = 1e30
MESH = pl.DeviceIdType.MESH
F32 = jnp.float32
BF16 = jnp.bfloat16


def wrap(position):
    return lax.rem(position + 4, 4)


class Place:
    def __init__(self):
        self.row = lax.axis_index("row")
        self.col = lax.axis_index("col")
        self.dp = lax.axis_index("dp")
        self.chip = self.row * 2 + lax.div(self.col, 2)
        self.core = lax.rem(self.col, 2)
        self.z = lax.div(self.dp, 4)
        self.y = lax.rem(self.dp, 4)

    def on_x(self, step):
        return self.x_at(wrap(self.chip + step), self.core)

    def x_at(self, chip, core):
        return {"row": lax.div(chip, 2), "col": lax.rem(chip, 2) * 2 + core}

    def on_y(self, step):
        return {"dp": self.z * 4 + wrap(self.y + step)}

    def on_z(self, step):
        return {"dp": wrap(self.z + step) * 4 + self.y}

    def partner(self):
        return {"row": 1 - self.row}

    def mate(self):
        return {"col": lax.div(self.col, 2) * 2 + 1 - self.core}


class Net:
    def __init__(self, send, recv):
        self.send, self.recv, self.used = send, recv, 0

    def copy(self, source, target, device):
        slot = self.used
        self.used += 1
        return pltpu.make_async_remote_copy(
            src_ref=source,
            dst_ref=target,
            send_sem=self.send.at[slot],
            recv_sem=self.recv.at[slot],
            device_id=device,
            device_id_type=MESH,
        )


class Near:
    def __init__(self, sems):
        self.sems, self.used = sems, 0

    def copy(self, source, target):
        slot = self.used
        self.used += 1
        return pltpu.make_async_copy(source, target, self.sems.at[slot])


def greet(devices):
    barrier = pltpu.get_barrier_semaphore()
    for device in devices:
        pl.semaphore_signal(barrier, inc=1, device_id=device, device_id_type=MESH)
    pl.semaphore_wait(barrier, len(devices))


class RingGather:
    def __init__(self, net, block, me, right, left, own=None):
        before, after = wrap(me - 1), wrap(me + 1)
        own = own or (lambda half: block(me, half))
        self.first = [
            net.copy(own(0), block(me, 0), right),
            net.copy(own(1), block(me, 1), left),
        ]
        self.second = [
            net.copy(own(1), block(me, 1), right),
            net.copy(own(0), block(me, 0), left),
        ]
        self.passed = [
            net.copy(block(before, 0), block(before, 0), right),
            net.copy(block(after, 1), block(after, 1), left),
        ]

    def start(self):
        for copy in self.first + self.second:
            copy.start()

    def forward(self):
        for came, on in zip(self.first, self.passed):
            came.wait_recv()
            on.start()

    def near_done(self):
        for copy in self.second:
            copy.wait_recv()

    def far_done(self):
        for copy in self.passed:
            copy.wait_recv()

    def drain(self):
        for copy in self.first + self.second + self.passed:
            copy.wait_send()


class GroupGather:
    def __init__(self, net, place, block, own):
        core, chip = place.core, place.chip
        self.ring = RingGather(
            net,
            lambda position, half: block(position, core, half),
            chip,
            place.on_x(1),
            place.on_x(-1),
            own,
        )
        whole = [
            own(None),
            block(wrap(chip - 1), core, None),
            block(wrap(chip + 1), core, None),
            block(wrap(chip + 2), core, None),
        ]
        target = [block(chip, core, None)] + whole[1:]
        self.mates = [
            net.copy(source, there, place.mate()) for source, there in zip(whole, target)
        ]

    def start(self):
        self.ring.start()
        self.mates[0].start()

    def forward(self):
        self.ring.forward()

    def share(self):
        self.ring.near_done()
        self.mates[1].start()
        self.mates[2].start()

    def finish(self):
        self.ring.far_done()
        self.mates[3].start()
        for copy in self.mates:
            copy.wait_recv()
        self.ring.drain()
        for copy in self.mates:
            copy.wait_send()


def sweep(rows, step, body):
    def one(index, carry):
        body(pl.multiple_of(index * step, step))
        return carry

    lax.fori_loop(0, rows // step, one, 0)


class GroupScatter:
    SEMS = 10

    def __init__(self, net, place, part, slices, shape, mate_in, total, ring_in, comb):
        self.part, self.slices, self.place = part, slices, place
        self.rows, self.cols = shape
        self.mate_in, self.total = mate_in, total
        self.ring_in, self.comb = ring_in, comb
        chip = place.chip
        half = self.rows // 2
        self.half = half
        self.order = [wrap(chip + 2), wrap(chip + 1), wrap(chip - 1), chip]
        mate = place.mate()
        self.mates = []
        for index, there in enumerate(self.order):
            rows, cols = slices(there, 1 - place.core)
            self.mates.append(
                net.copy(
                    part.at[pl.ds(rows, self.rows), pl.ds(cols, self.cols)],
                    mate_in.at[index],
                    mate,
                )
            )
        right, left = place.on_x(1), place.on_x(-1)
        top, low = pl.ds(0, half), pl.ds(half, half)
        self.sends = [
            net.copy(total.at[0, top], ring_in.at[0], right),
            net.copy(total.at[0, low], ring_in.at[1], left),
            net.copy(total.at[1, low], ring_in.at[2], right),
            net.copy(total.at[2, top], ring_in.at[3], left),
            net.copy(comb.at[0], ring_in.at[4], right),
            net.copy(comb.at[1], ring_in.at[5], left),
        ]

    def start(self):
        for copy in self.mates:
            copy.start()

    def mine(self, index, row, step):
        rows, cols = self.slices(self.order[index], self.place.core)
        return self.part[
            pl.ds(pl.multiple_of(rows + row, 16), step), pl.ds(cols, self.cols)
        ].astype(F32)

    def first(self):
        for index in range(3):
            self.mates[index].wait_recv()

            def add(row, index=index):
                here = pl.ds(row, 16)
                self.total[index, here, :] = (
                    self.mine(index, row, 16) + self.mate_in[index, here, :].astype(F32)
                ).astype(BF16)

            sweep(self.rows, 16, add)
            if index == 0:
                self.sends[0].start()
                self.sends[1].start()
            else:
                self.sends[index + 1].start()

    def second(self):
        for side in range(2):
            self.sends[side].wait_recv()

            def add(row, side=side):
                here = pl.ds(row, 16)
                there = pl.ds(pl.multiple_of(row + side * self.half, 16), 16)
                self.comb[side, here, :] = (
                    self.total[1 + side, there, :].astype(F32)
                    + self.ring_in[side, here, :].astype(F32)
                ).astype(BF16)

            sweep(self.half, 16, add)
            self.sends[4 + side].start()

    def arrive(self):
        self.mates[3].wait_recv()
        for index in range(2, 6):
            self.sends[index].wait_recv()

    def result(self, side, row):
        here = pl.ds(row, 16)
        there = pl.multiple_of(row + side * self.half, 16)
        one, two = ((4, 3), (2, 5))[side]
        return (
            self.mine(3, there, 16)
            + self.mate_in[3, pl.ds(there, 16), :].astype(F32)
            + self.ring_in[one, here, :].astype(F32)
            + self.ring_in[two, here, :].astype(F32)
        )

    def drain(self):
        for copy in self.mates + self.sends:
            copy.wait_send()


def scatter_scratch(rows, cols):
    return [
        pltpu.VMEM((4, rows, cols), BF16),
        pltpu.VMEM((3, rows, cols), BF16),
        pltpu.VMEM((6, rows // 2, cols), BF16),
        pltpu.VMEM((2, rows // 2, cols), BF16),
    ]


class RingScatter:
    def __init__(self, net, part, me, right, left, ring_in, comb, target):
        before, after, across = wrap(me - 1), wrap(me + 1), wrap(me + 2)
        self.part, self.me, self.near = part, me, (after, before)
        self.ring_in, self.comb, self.target = ring_in, comb, target
        self.sends = [
            net.copy(part(across, 0), ring_in.at[0], right),
            net.copy(part(across, 1), ring_in.at[1], left),
            net.copy(part(after, 1), ring_in.at[2], right),
            net.copy(part(before, 0), ring_in.at[3], left),
            net.copy(comb.at[0], ring_in.at[4], right),
            net.copy(comb.at[1], ring_in.at[5], left),
        ]

    def start(self):
        for copy in self.sends[:4]:
            copy.start()

    def add(self, target, sources):
        shape = target.shape
        if len(shape) == 3:
            for index in range(shape[0]):
                self.add(target.at[index], [source.at[index] for source in sources])
            return

        def one(row):
            here = pl.ds(row, 16)
            total = sources[0][here, :].astype(F32)
            for source in sources[1:]:
                total = total + source[here, :].astype(F32)
            target[here, :] = total.astype(BF16)

        sweep(shape[0], 16, one)

    def middle(self):
        for side in range(2):
            self.sends[side].wait_recv()
            self.add(
                self.comb.at[side],
                [self.part(self.near[side], side), self.ring_in.at[side]],
            )
            self.sends[4 + side].start()

    def finish(self):
        for index in range(2, 6):
            self.sends[index].wait_recv()
        for side, (one, two) in enumerate(((4, 3), (2, 5))):
            self.add(
                self.target(side),
                [self.part(self.me, side), self.ring_in.at[one], self.ring_in.at[two]],
            )

    def drain(self):
        for copy in self.sends:
            copy.wait_send()


def any_specs(count):
    return [pl.BlockSpec(memory_space=pl.ANY)] * count


def vmem_specs(count):
    return [pl.BlockSpec(memory_space=pltpu.VMEM)] * count


def sem_arrays(remote, near=0):
    arrays = [pltpu.SemaphoreType.DMA((remote,)), pltpu.SemaphoreType.DMA((remote,))]
    if near:
        arrays.append(pltpu.SemaphoreType.DMA((near,)))
    return arrays


def comm_params(identity, megabytes=60):
    return pltpu.CompilerParams(
        collective_id=identity, has_side_effects=True, vmem_limit_bytes=megabytes << 20
    )


def quarter_block(ref):
    def block(chip, core, half):
        rows = (lax.rem(chip, 2) * 2 + core) * 256
        cols = lax.div(chip, 2) * HALF
        if half is None:
            return ref.at[pl.ds(rows, 256), pl.ds(cols, HALF)]
        return ref.at[pl.ds(rows + 128 * half, 128), pl.ds(cols, HALF)]

    return block


def rows_of(chip, core):
    return (lax.rem(chip, 2) * 2 + core) * 256 + lax.div(chip, 2) * 128


def row_block(ref):
    def block(chip, core, half):
        rows = rows_of(chip, core)
        if half is None:
            return ref.at[pl.ds(rows, 128), :]
        return ref.at[pl.ds(rows + 64 * half, 64), :]

    return block


def row_slices(chip, core):
    return rows_of(chip, core), 0


def quarter_slices(chip, core):
    return (lax.rem(chip, 2) * 2 + core) * 256, lax.div(chip, 2) * HALF


def stacked(ref, size):
    def at(part, z, y, rows):
        return ref.at[part, z, y, rows, :]

    return at, size


def beside(ref, size):
    def at(part, z, y, rows):
        return ref.at[z, y, rows, pl.ds(part * HALF, HALF)]

    return at, size


def gather_kernel(
    x, cot, qkv, dense, fc1, fc2, small, norms,
    gx, gcot, gqkv, gdense, gfc1, gfc2, gsmall, gnorm,
    send, recv, near_sems,
):
    place = Place()
    net, near = Net(send, recv), Near(near_sems)
    row, z, y = place.row, place.z, place.y
    partner = place.partner()
    greet(
        [partner, place.on_x(1), place.on_x(-1), place.mate()]
        + [place.on_y(1), place.on_y(-1), place.on_z(1), place.on_z(-1)]
    )
    weights = [
        (stacked(gqkv, 64), qkv.at[row], qkv.at[1 - row]),
        (stacked(gsmall, 16), small, small),
        (beside(gdense, 32), dense, dense),
        (stacked(gfc1, 64), fc1.at[row], fc1.at[1 - row]),
        (beside(gfc2, 64), fc2.at[row], fc2.at[1 - row]),
    ]
    swaps, copies = [], []
    swap_norms = net.copy(norms, gnorm.at[row], partner)
    swap_norms.start()
    for (at, size), own, other in weights:
        there = at(row, z, y, pl.ds(0, size))
        swap = net.copy(other, there, partner)
        swap.start()
        swaps.append(swap)
        copies.append(near.copy(own, there))
    groups = []
    for source, target in ((x, gx), (cot, gcot)):
        block = quarter_block(target)

        def own(half, source=source):
            if half is None:
                return source
            return source.at[pl.ds(128 * half, 128), :]

        groups.append(GroupGather(net, place, block, own))
        copies.append(near.copy(source, block(place.chip, place.core, None)))
    copies.append(near.copy(norms, gnorm.at[row]))
    groups[0].start()
    for copy in copies:
        copy.start()
    ones = []
    for (at, size), own, other in weights:
        half_rows = size // 2

        def along_y(position, half, at=at, half_rows=half_rows):
            return at(row, z, position, pl.ds(half * half_rows, half_rows))

        def along_z(position, half, at=at, half_rows=half_rows):
            return at(1 - row, position, y, pl.ds(half * half_rows, half_rows))

        def mine(half, own=own, half_rows=half_rows):
            return own.at[pl.ds(half * half_rows, half_rows), :]

        ones.append(
            (
                RingGather(net, along_y, y, place.on_y(1), place.on_y(-1), mine),
                RingGather(net, along_z, z, place.on_z(1), place.on_z(-1)),
            )
        )
    twos = []
    for (at, size), own, other in weights:
        rows = pl.ds(0, size)

        def along_z(position, half, at=at, rows=rows):
            return at(row, position, pl.ds(2 * half, 2), rows)

        def along_y(position, half, at=at, rows=rows):
            return at(1 - row, pl.ds(2 * half, 2), position, rows)

        twos.append(
            (
                RingGather(net, along_z, z, place.on_z(1), place.on_z(-1)),
                RingGather(net, along_y, y, place.on_y(1), place.on_y(-1)),
            )
        )
    for first, second in ones:
        first.start()
    for swap, (first, second) in zip(swaps, ones):
        swap.wait_recv()
        second.start()
    groups[1].start()
    for copy in copies:
        copy.wait()
    groups[0].forward()
    for (one, other), (two, also) in zip(ones, twos):
        one.forward()
        other.forward()
        one.near_done()
        one.far_done()
        two.start()
        other.near_done()
        other.far_done()
        also.start()
    groups[0].share()
    groups[1].forward()
    groups[0].finish()
    for two, also in twos:
        two.forward()
        also.forward()
    groups[1].share()
    groups[1].finish()
    for two, also in twos:
        two.near_done()
        two.far_done()
        also.near_done()
        also.far_done()
    swap_norms.wait_recv()
    swap_norms.wait_send()
    for swap in swaps:
        swap.wait_send()
    for pair in ones + twos:
        for ring in pair:
            ring.drain()


def gather_all(x, cot, qkv, dense, fc1, fc2, small, norms):
    remote = 6 + 2 * 10 + 5 * 4 * 6
    return pl.pallas_call(
        gather_kernel,
        out_shape=(
            jax.ShapeDtypeStruct((SEQ, WIDTH), BF16),
            jax.ShapeDtypeStruct((SEQ, WIDTH), BF16),
            jax.ShapeDtypeStruct((2, 4, 4, 64, 768), BF16),
            jax.ShapeDtypeStruct((4, 4, 32, 2048), BF16),
            jax.ShapeDtypeStruct((2, 4, 4, 64, 1024), BF16),
            jax.ShapeDtypeStruct((4, 4, 64, 2048), BF16),
            jax.ShapeDtypeStruct((2, 4, 4, 16, 128), BF16),
            jax.ShapeDtypeStruct((2, 8, HALF), F32),
        ),
        in_specs=any_specs(8),
        out_specs=tuple(any_specs(8)),
        scratch_shapes=sem_arrays(remote, 8),
        compiler_params=comm_params(0),
        name="gather_all",
    )(x, cot, qkv, dense, fc1, fc2, small, norms)


def head_mask(values, head):
    lane = lax.broadcasted_iota(jnp.int32, values.shape, 1)
    return jnp.where(lax.div(lane, HEAD_DIM) == head, values, jnp.zeros_like(values))


def distances(length, start, keys):
    key = lax.broadcasted_iota(jnp.int32, (keys, BLOCK), 0)
    query = lax.broadcasted_iota(jnp.int32, (keys, BLOCK), 1) + start
    return jnp.where(key < length, jnp.abs(query - key).astype(F32), FAR)


def slope_of(head):
    base = lax.axis_index("col") * 8 + lax.axis_index("row") * 4
    number = (base + head + 1).astype(F32)
    return jnp.exp2(jnp.full((1, BLOCK), -8.0 / HEADS, F32) * number)


def nt(left, right):
    return lax.dot_general(left, right, (((1,), (1,)), ((), ())), preferred_element_type=F32)


def nn(left, right):
    return jnp.dot(left, right, preferred_element_type=F32)


def attend_kernel(length, q, k, v, attended, logs, vt, out_t):
    vt[...] = v[...].T
    for block in range(4):
        start, keys = block * BLOCK, (block + 1) * BLOCK
        here = pl.ds(start, BLOCK)
        apart = distances(length[0], start, keys)

        def one(head, carry):
            scores = nt(head_mask(k[0:keys, :], head), q[here, :])
            scores = scores - slope_of(head) * apart
            peak = jnp.max(scores, 0, keepdims=True)
            exponent = jnp.exp(scores - peak)
            total = jnp.sum(exponent, 0, keepdims=True)
            lines = pl.ds(pl.multiple_of(head * HEAD_DIM, HEAD_DIM), HEAD_DIM)
            out_t[lines, here] = nn(vt[lines, 0:keys], exponent.astype(BF16)) / total
            logs[head, :, here] = peak + jnp.log(total)
            return carry

        lax.fori_loop(0, 4, one, 0)
    attended[...] = out_t[...].T.astype(BF16)


def attend(length, q, k, v):
    return pl.pallas_call(
        attend_kernel,
        out_shape=(
            jax.ShapeDtypeStruct((SEQ, LOCAL), BF16),
            jax.ShapeDtypeStruct((4, 1, SEQ), F32),
        ),
        in_specs=[pl.BlockSpec(memory_space=pltpu.SMEM)] + vmem_specs(3),
        out_specs=tuple(vmem_specs(2)),
        scratch_shapes=[pltpu.VMEM((LOCAL, SEQ), BF16), pltpu.VMEM((LOCAL, SEQ), F32)],
        compiler_params=pltpu.CompilerParams(vmem_limit_bytes=48 << 20),
        name="attend",
    )(length, q, k, v)


def attend_back_kernel(length, q, k, v, grad, logs, out, kt, dk, dv, dqt):
    kt[...] = k[...].T
    dk[...] = jnp.zeros_like(dk)
    dv[...] = jnp.zeros_like(dv)
    for block in range(4):
        start, keys = block * BLOCK, (block + 1) * BLOCK
        here = pl.ds(start, BLOCK)
        apart = distances(length[0], start, keys)

        def one(head, carry):
            scores = nt(head_mask(k[0:keys, :], head), q[here, :])
            prob = jnp.exp(scores - slope_of(head) * apart - logs[head, :, here])
            dprob = nt(head_mask(v[0:keys, :], head), grad[here, :])
            delta = jnp.sum(prob * dprob, 0, keepdims=True)
            dscore = (prob * (dprob - delta)).astype(BF16)
            dv[0:keys, :] += nn(prob.astype(BF16), head_mask(grad[here, :], head))
            dk[0:keys, :] += nn(dscore, head_mask(q[here, :], head))
            lines = pl.ds(pl.multiple_of(head * HEAD_DIM, HEAD_DIM), HEAD_DIM)
            dqt[lines, here] = nn(kt[lines, 0:keys], dscore)
            return carry

        lax.fori_loop(0, 4, one, 0)
    out[:, 0:256] = (dqt[...].T * HEAD_DIM**-0.5).astype(BF16)
    out[:, 256:512] = dk[...].astype(BF16)
    out[:, 512:768] = dv[...].astype(BF16)


def attend_back(length, q, k, v, grad, logs):
    return pl.pallas_call(
        attend_back_kernel,
        out_shape=jax.ShapeDtypeStruct((SEQ, 3 * LOCAL), BF16),
        in_specs=[pl.BlockSpec(memory_space=pltpu.SMEM)] + vmem_specs(5),
        out_specs=vmem_specs(1)[0],
        scratch_shapes=[
            pltpu.VMEM((LOCAL, SEQ), BF16),
            pltpu.VMEM((SEQ, LOCAL), F32),
            pltpu.VMEM((SEQ, LOCAL), F32),
            pltpu.VMEM((LOCAL, SEQ), F32),
        ],
        compiler_params=pltpu.CompilerParams(vmem_limit_bytes=48 << 20),
        name="attend_back",
    )(length, q, k, v, grad, logs)


def normalize(values):
    mean = jnp.mean(values, 1, keepdims=True)
    centered = values - mean
    scale = lax.rsqrt(jnp.mean(centered * centered, 1, keepdims=True) + EPSILON)
    return centered * scale, scale


def x_devices(place):
    return [place.on_x(1), place.on_x(-1), place.mate()]


def middle_kernel(
    part, x, add, gain, offset, gathered, residual,
    mate_in, total, ring_in, comb, own, send, recv, near_sems,
):
    place = Place()
    net = Net(send, recv)
    greet(x_devices(place))
    scatter = GroupScatter(
        net, place, part, row_slices, (128, WIDTH), mate_in, total, ring_in, comb
    )
    block = row_block(gathered)
    group = GroupGather(
        net,
        place,
        block,
        lambda half: own if half is None else own.at[pl.ds(64 * half, 64), :],
    )
    scatter.start()
    scatter.first()
    scatter.second()
    scatter.arrive()
    for side in range(2):

        def one(row, side=side):
            here = pl.ds(pl.multiple_of(row + 64 * side, 16), 16)
            values = x[here, :].astype(F32) + scatter.result(side, row) + add[...]
            residual[here, :] = values
            own[here, :] = (normalize(values)[0] * gain[...] + offset[...]).astype(BF16)

        sweep(64, 16, one)
    group.start()
    keep = Near(near_sems).copy(own, block(place.chip, place.core, None))
    keep.start()
    group.forward()
    group.share()
    group.finish()
    keep.wait()
    scatter.drain()


def middle(part, x, add, gain, offset):
    return pl.pallas_call(
        middle_kernel,
        out_shape=(
            jax.ShapeDtypeStruct((SEQ, WIDTH), BF16),
            jax.ShapeDtypeStruct((128, WIDTH), F32),
        ),
        in_specs=vmem_specs(5),
        out_specs=(any_specs(1)[0], vmem_specs(1)[0]),
        scratch_shapes=scatter_scratch(128, WIDTH)
        + [pltpu.VMEM((128, WIDTH), BF16)]
        + sem_arrays(20, 1),
        compiler_params=comm_params(1),
        name="middle",
    )(part, x, add, gain, offset)


def turn_kernel(
    part, residual, cot, gain, gathered, sums,
    mate_in, total, ring_in, comb, own, send, recv, near_sems,
):
    place = Place()
    net = Net(send, recv)
    greet(x_devices(place))
    scatter = GroupScatter(
        net, place, part, row_slices, (128, WIDTH), mate_in, total, ring_in, comb
    )
    block = row_block(gathered)
    group = GroupGather(
        net,
        place,
        block,
        lambda half: own if half is None else own.at[pl.ds(64 * half, 64), :],
    )
    scatter.start()
    scatter.first()
    scatter.second()
    sums[...] = jnp.zeros_like(sums)
    scatter.arrive()
    for side in range(2):

        def one(row, side=side):
            here = pl.ds(pl.multiple_of(row + 64 * side, 16), 16)
            arrived = scatter.result(side, row)
            xhat, scale = normalize(residual[here, :])
            scaled = arrived * gain[...]
            flat = jnp.mean(scaled, 1, keepdims=True)
            cross = jnp.mean(scaled * xhat, 1, keepdims=True)
            own[here, :] = (
                cot[here, :].astype(F32) + scale * (scaled - flat - xhat * cross)
            ).astype(BF16)
            sums[0:1, :] += jnp.sum(arrived * xhat, 0, keepdims=True)
            sums[1:2, :] += jnp.sum(arrived, 0, keepdims=True)

        sweep(64, 16, one)
    group.start()
    keep = Near(near_sems).copy(own, block(place.chip, place.core, None))
    keep.start()
    group.forward()
    group.share()
    group.finish()
    keep.wait()
    scatter.drain()


def turn(part, residual, cot, gain):
    return pl.pallas_call(
        turn_kernel,
        out_shape=(
            jax.ShapeDtypeStruct((SEQ, WIDTH), BF16),
            jax.ShapeDtypeStruct((8, WIDTH), F32),
        ),
        in_specs=vmem_specs(4),
        out_specs=(any_specs(1)[0], vmem_specs(1)[0]),
        scratch_shapes=scatter_scratch(128, WIDTH)
        + [pltpu.VMEM((128, WIDTH), BF16)]
        + sem_arrays(20, 1),
        compiler_params=comm_params(2),
        name="turn",
    )(part, residual, cot, gain)


def last_kernel(
    part, part_out, x, mean, scale, branch, gain, residual, add, small,
    gqkv, gdense, gfc1, gfc2,
    ingrad, out, rqkv, rdense, rfc1, rfc2, vector,
    *scratch,
):
    scratch = list(scratch)

    def take(count):
        taken = scratch[:count]
        del scratch[:count]
        return taken

    place = Place()
    row, z, y = place.row, place.z, place.y
    send, recv, near_sems = take(3)
    net, near = Net(send, recv), Near(near_sems)
    x_group = [
        place.x_at(wrap(place.chip + step), core)
        for step in range(4)
        for core in (place.core, 1 - place.core)
    ][1:]
    y_ring = [place.on_y(step) for step in (1, 2, 3)]
    z_ring = [place.on_z(step) for step in (1, 2, 3)]
    greet(x_group + y_ring + z_ring)
    scatter = GroupScatter(net, place, part, quarter_slices, (256, HALF), *take(4))
    scatter_out = GroupScatter(net, place, part_out, row_slices, (128, WIDTH), *take(4))
    result, stats_out, stats_in, group_in, y_in, z_in, vec_a, vec_b = take(8)
    weights = []
    for at, size, cols, final in (
        (stacked(gfc1, 64)[0], 64, 1024, rfc1),
        (beside(gfc2, 64)[0], 64, 1024, rfc2),
        (beside(gdense, 32)[0], 32, 1024, rdense),
        (stacked(gqkv, 64)[0], 64, 768, rqkv),
    ):
        done = take(1)[0]
        pairs = []
        for part_index in range(2):
            ring_in1, comb1, mid, ring_in2, comb2 = take(5)
            half_rows = size // 2

            def along_z(pos, half, at=at, size=size, h=part_index):
                return at(h, pos, pl.ds(2 * half, 2), pl.ds(0, size))

            def along_y(pos, half, at=at, size=size, h=part_index):
                return at(h, pl.ds(2 * half, 2), pos, pl.ds(0, size))

            def inner(pos, half, mid=mid, half_rows=half_rows):
                return mid.at[pos, pl.ds(half * half_rows, half_rows), :]

            def mid_half(half, mid=mid):
                return mid.at[pl.ds(2 * half, 2)]

            def done_half(half, done=done, half_rows=half_rows, h=part_index):
                return done.at[h, pl.ds(half * half_rows, half_rows), :]

            over_z = (z, place.on_z(1), place.on_z(-1))
            over_y = (y, place.on_y(1), place.on_y(-1))
            if part_index == 0:
                one = RingScatter(net, along_z, *over_z, ring_in1, comb1, mid_half)
                two = RingScatter(net, inner, *over_y, ring_in2, comb2, done_half)
            else:
                one = RingScatter(net, along_y, *over_y, ring_in1, comb1, mid_half)
                two = RingScatter(net, inner, *over_z, ring_in2, comb2, done_half)
            pairs.append((one, two))
        swap = net.copy(done.at[1 - row], final.at[row], place.partner())
        keep = near.copy(done.at[row], final.at[row])
        weights.append((pairs, swap, keep))

    scatter.start()
    for pairs, swap, keep in weights:
        for one, two in pairs:
            one.start()
    scatter.first()
    scatter_out.start()
    scatter.second()
    scatter_out.first()
    for pairs, swap, keep in weights[:2]:
        for one, two in pairs:
            one.middle()
    scatter.arrive()

    vec_a[...] = small[...]
    lane = lax.broadcasted_iota(jnp.int32, (16, 128), 1)
    cols = pl.ds(pl.multiple_of(row * HALF, HALF), HALF)
    for side in range(2):

        def sums(pos, side=side):
            here = pl.ds(pl.multiple_of(pos + 128 * side, 16), 16)
            arrived = scatter.result(side, pos)
            scaled = arrived * gain[...]
            xhat = (x[here, :].astype(F32) - mean[here, :]) * scale[here, :]
            flat = jnp.sum(scaled, 1, keepdims=True)
            cross = jnp.sum(scaled * xhat, 1, keepdims=True)
            stats_out[here, :] = jnp.where(lane == 0, flat, cross)
            ingrad[here, :] = arrived
            vec_a[0:1, cols] += jnp.sum(arrived * xhat, 0, keepdims=True)
            vec_a[1:2, cols] += jnp.sum(arrived, 0, keepdims=True)

        sweep(128, 16, sums)
    stats = net.copy(stats_out, stats_in, place.partner())
    stats.start()
    group_sends = [
        net.copy(vec_a, group_in.at[index], device)
        for index, device in enumerate(x_group)
    ]
    for copy in group_sends:
        copy.start()
    scatter_out.second()
    for pairs, swap, keep in weights[2:]:
        for one, two in pairs:
            one.middle()
    stats.wait_recv()

    def apply(pos):
        here = pl.ds(pos, 16)
        both = (stats_out[here, :] + stats_in[here, :]) / WIDTH
        xhat = (x[here, :].astype(F32) - mean[here, :]) * scale[here, :]
        ingrad[here, :] = branch[here, :].astype(F32) + scale[here, :] * (
            ingrad[here, :] * gain[...] - both[:, 0:1] - xhat * both[:, 1:2]
        )

    sweep(256, 16, apply)
    for copy in group_sends:
        copy.wait_recv()
    vec_b[...] = vec_a[...]
    for index in range(7):
        vec_b[0:4, :] += group_in[index, 0:4, :]
    vec_b[7:8, :] = group_in[3, 6:7, :]
    y_sends = [net.copy(vec_b, y_in.at[i], device) for i, device in enumerate(y_ring)]
    for copy in y_sends:
        copy.start()
    for pairs, swap, keep in weights:
        for one, two in pairs:
            one.finish()
            two.start()
    scatter_out.arrive()
    for side in range(2):

        def finish(pos, side=side):
            here = pl.ds(pl.multiple_of(pos + 64 * side, 16), 16)
            result[here, :] = (
                residual[here, :] + scatter_out.result(side, pos) + add[...]
            ).astype(BF16)

        sweep(64, 16, finish)
    there = pl.ds(row * 128, 128)
    out_swap = net.copy(
        result.at[:, pl.ds((1 - row) * HALF, HALF)], out.at[there, :], place.partner()
    )
    out_keep = near.copy(result.at[:, pl.ds(row * HALF, HALF)], out.at[there, :])
    out_swap.start()
    out_keep.start()
    for copy in y_sends:
        copy.wait_recv()
    for copy in group_sends:
        copy.wait_send()
    vec_a[...] = vec_b[...]
    for index in range(3):
        vec_a[...] += y_in[index]
    z_sends = [net.copy(vec_a, z_in.at[i], device) for i, device in enumerate(z_ring)]
    for copy in z_sends:
        copy.start()
    for pairs, swap, keep in weights:
        for one, two in pairs:
            two.middle()
    for pairs, swap, keep in weights:
        for one, two in pairs:
            two.finish()
        swap.start()
        keep.start()
    for copy in z_sends:
        copy.wait_recv()
    vector[...] = vec_a[...]
    for index in range(3):
        vector[...] += z_in[index]
    out_swap.wait_recv()
    for pairs, swap, keep in weights:
        swap.wait_recv()
        keep.wait()
        swap.wait_send()
        for one, two in pairs:
            one.drain()
            two.drain()
    out_keep.wait()
    out_swap.wait_send()
    stats.wait_send()
    for copy in y_sends + z_sends:
        copy.wait_send()
    scatter.drain()
    scatter_out.drain()


def last(part, part_out, x, mean, scale, branch, gain, residual, add, small, *grads):
    scratch = sem_arrays(2 * 10 + 4 * (2 * 12 + 1) + 1 + 7 + 1 + 6, 5)
    scratch += scatter_scratch(256, HALF) + scatter_scratch(128, WIDTH)
    scratch += [
        pltpu.VMEM((128, WIDTH), BF16),
        pltpu.VMEM((256, 128), F32),
        pltpu.VMEM((256, 128), F32),
        pltpu.VMEM((7, 8, WIDTH), F32),
        pltpu.VMEM((3, 8, WIDTH), F32),
        pltpu.VMEM((3, 8, WIDTH), F32),
        pltpu.VMEM((8, WIDTH), F32),
        pltpu.VMEM((8, WIDTH), F32),
    ]
    for size, cols in ((64, 1024), (64, 1024), (32, 1024), (64, 768)):
        scratch.append(pltpu.VMEM((2, size, cols), BF16))
        for _ in range(2):
            scratch += [
                pltpu.VMEM((6, 2, size, cols), BF16),
                pltpu.VMEM((2, 2, size, cols), BF16),
                pltpu.VMEM((4, size, cols), BF16),
                pltpu.VMEM((6, size // 2, cols), BF16),
                pltpu.VMEM((2, size // 2, cols), BF16),
            ]
    return pl.pallas_call(
        last_kernel,
        out_shape=(
            jax.ShapeDtypeStruct((256, HALF), F32),
            jax.ShapeDtypeStruct((256, HALF), BF16),
            jax.ShapeDtypeStruct((2, 64, 768), BF16),
            jax.ShapeDtypeStruct((2, 32, 1024), BF16),
            jax.ShapeDtypeStruct((2, 64, 1024), BF16),
            jax.ShapeDtypeStruct((2, 64, 1024), BF16),
            jax.ShapeDtypeStruct((8, WIDTH), F32),
        ),
        in_specs=vmem_specs(14),
        out_specs=tuple(vmem_specs(7)),
        scratch_shapes=scratch,
        compiler_params=comm_params(3),
        name="last",
    )(part, part_out, x, mean, scale, branch, gain, residual, add, small, *grads)


def inner_rows(left_side, right_side):
    return lax.dot_general(
        left_side, right_side, (((0,), (0,)), ((), ())), preferred_element_type=F32
    )


def local(
    inputs,
    cotangent,
    lengths,
    attention_norm_gain,
    attention_norm_bias,
    qkv_weight,
    query_bias,
    value_bias,
    dense_weight,
    dense_bias,
    feedforward_norm_gain,
    feedforward_norm_bias,
    fc1_weight,
    fc1_bias,
    fc2_weight,
    fc2_bias,
):
    row = lax.axis_index("row")
    col = lax.axis_index("col")
    dp = lax.axis_index("dp")

    qkv_cut = qkv_weight.reshape(64, 2, 4, 3, 64).transpose(1, 0, 3, 2, 4)
    qkv_cut = qkv_cut.reshape(2, 64, 768)
    fc1_cut = fc1_weight.reshape(64, 16, 2, 64).transpose(2, 0, 1, 3)
    fc1_cut = fc1_cut.reshape(2, 64, 1024)
    fc2_cut = fc2_weight.reshape(2, 64, 1024)
    small = jnp.zeros((16, 128), BF16)
    small = small.at[0, :].set(fc1_bias)
    small = small.at[1, :].set(jnp.concatenate([query_bias, value_bias, dense_bias]))
    small = small.at[2, 0:64].set(fc2_bias)
    norms = jnp.concatenate(
        [
            jnp.stack(
                [
                    attention_norm_gain,
                    attention_norm_bias,
                    feedforward_norm_gain,
                    feedforward_norm_bias,
                ]
            ),
            jnp.zeros((4, HALF), F32),
        ]
    )
    rows_x, rows_cot, qkv_full, dense_full, fc1_full, fc2_full, smalls, norm_parts = (
        gather_all(
            inputs, cotangent, qkv_cut, dense_weight, fc1_cut, fc2_cut, small, norms
        )
    )
    qkv_full = qkv_full.reshape(WIDTH, 768)
    dense_full = lax.dynamic_slice_in_dim(
        dense_full.reshape(512, WIDTH), row * LOCAL, LOCAL, 0
    )
    fc1_full = fc1_full.reshape(WIDTH, 1024)
    fc2_full = fc2_full.reshape(1024, WIDTH)
    smalls = smalls.reshape(2, 16, 16, 128).astype(F32)
    hidden_add = lax.dynamic_index_in_dim(
        smalls[0, :, 0, :].reshape(16, 2, 64), row, 1, False
    ).reshape(1, 1024)
    query_add = lax.dynamic_slice_in_dim(
        smalls[0, :, 1, 0:32].reshape(512), row * LOCAL, LOCAL
    )
    value_add = lax.dynamic_slice_in_dim(
        smalls[0, :, 1, 32:64].reshape(512), row * LOCAL, LOCAL
    )
    dense_add = smalls[:, :, 1, 64:128].reshape(1, WIDTH)
    output_add = smalls[:, :, 2, 0:64].reshape(1, WIDTH)
    gain_one, offset_one, gain_two, offset_two = (
        norm_parts[:, index].reshape(1, WIDTH) for index in range(4)
    )

    row_start = col * 256 + row * 128
    source = rows_x.astype(F32)
    mean_one = jnp.mean(source, 1, keepdims=True)
    centered = source - mean_one
    scale_one = lax.rsqrt(jnp.mean(centered * centered, 1, keepdims=True) + EPSILON)
    rows_one = (centered * scale_one * gain_one + offset_one).astype(BF16)
    projected = jnp.dot(rows_one, qkv_full, preferred_element_type=F32)
    queries = (projected[:, 0:256] + query_add).astype(BF16) * BF16(HEAD_DIM**-0.5)
    keys = projected[:, 256:512].astype(BF16)
    values = (projected[:, 512:768] + value_add).astype(BF16)
    attended, logs = attend(lengths, queries, keys, values)
    partial_residual = jnp.dot(attended, dense_full, preferred_element_type=F32).astype(
        BF16
    )
    x_rows = lax.dynamic_slice_in_dim(rows_x, row_start, 128, 0)
    rows_two, residual = middle(partial_residual, x_rows, dense_add, gain_two, offset_two)
    hidden = jnp.dot(rows_two, fc1_full, preferred_element_type=F32) + hidden_add
    gelu_value, gelu_pullback = jax.vjp(partial(jax.nn.gelu, approximate=False), hidden)
    activated = gelu_value.astype(BF16)
    grad_act = lax.dot_general(
        rows_cot, fc2_full, (((1,), (1,)), ((), ())), preferred_element_type=F32
    )
    grad_hidden = gelu_pullback(grad_act)[0].astype(BF16)
    part_two = lax.dot_general(
        grad_hidden, fc1_full, (((1,), (1,)), ((), ())), preferred_element_type=F32
    ).astype(BF16)
    cot_rows = lax.dynamic_slice_in_dim(rows_cot, row_start, 128, 0)
    rows_branch, sums_two = turn(part_two, residual, cot_rows, gain_two)
    grad_attended = lax.dot_general(
        rows_branch, dense_full, (((1,), (1,)), ((), ())), preferred_element_type=F32
    ).astype(BF16)
    grad_projected = attend_back(lengths, queries, keys, values, grad_attended, logs)
    part_one = lax.dot_general(
        grad_projected, qkv_full, (((1,), (1,)), ((), ())), preferred_element_type=F32
    ).astype(BF16)
    part_out = jnp.dot(activated, fc2_full, preferred_element_type=F32).astype(BF16)
    grad_fc2 = inner_rows(activated, rows_cot).astype(BF16).reshape(4, 4, 64, WIDTH)
    grad_fc1 = inner_rows(rows_two, grad_hidden).astype(BF16)
    grad_fc1 = grad_fc1.reshape(2, 4, 4, 64, 1024)
    grad_dense = inner_rows(attended, rows_branch).astype(BF16)
    empty = jnp.zeros_like(grad_dense)
    grad_dense = jnp.where(
        row == 0,
        jnp.concatenate([grad_dense, empty]),
        jnp.concatenate([empty, grad_dense]),
    ).reshape(4, 4, 32, WIDTH)
    grad_qkv = inner_rows(rows_one, grad_projected).astype(BF16)
    grad_qkv = grad_qkv.reshape(2, 4, 4, 64, 768)
    bias_sums = jnp.sum(grad_projected.astype(F32), 0)
    own_sums = jnp.concatenate(
        [
            jnp.sum(grad_hidden.astype(F32), 0),
            bias_sums[0:256],
            bias_sums[512:768],
            jnp.zeros((512,), F32),
        ]
    )
    zero = jnp.zeros((WIDTH,), F32)
    vector = jnp.stack(
        [
            zero,
            zero,
            sums_two[0],
            sums_two[1],
            jnp.sum(rows_branch.astype(F32), 0),
            jnp.sum(rows_cot.astype(F32), 0),
            own_sums,
            zero,
        ]
    )
    own_rows = col * 256
    own_cols = row * HALF
    input_gradient, outputs, red_qkv, red_dense, red_fc1, red_fc2, total = last(
        part_one,
        part_out,
        inputs,
        lax.dynamic_slice_in_dim(mean_one, own_rows, 256, 0),
        lax.dynamic_slice_in_dim(scale_one, own_rows, 256, 0),
        lax.dynamic_slice(rows_branch, (own_rows, own_cols), (256, HALF)),
        attention_norm_gain.reshape(1, HALF),
        residual,
        output_add,
        vector,
        grad_qkv,
        grad_dense,
        grad_fc1,
        grad_fc2,
    )
    red_qkv = (
        red_qkv.reshape(2, 64, 3, 4, 64).transpose(1, 0, 3, 2, 4).reshape(64, 1536)
    ).astype(F32)
    red_fc1 = (
        red_fc1.reshape(2, 64, 16, 64).transpose(1, 2, 0, 3).reshape(64, 2048)
    ).astype(F32)
    red_fc2 = red_fc2.reshape(128, HALF).astype(F32)
    red_dense = red_dense[0].astype(F32) + red_dense[1].astype(F32)

    halves = total[0:6].reshape(6, 2, HALF)
    mine = lax.dynamic_index_in_dim(halves, row, 1, False)
    red_dense_add = lax.dynamic_slice_in_dim(mine[4], dp * 64, 64)
    red_output_add = lax.dynamic_slice_in_dim(mine[5], dp * 64, 64)
    pair = jnp.where(row == 0, total[6:8], total[6:8][::-1])
    hidden_sums = pair[:, 0:1024].reshape(2, 16, 64)
    red_hidden_add = lax.dynamic_index_in_dim(hidden_sums, dp, 1, False).reshape(128)
    red_query = lax.dynamic_slice_in_dim(pair[:, 1024:1280].reshape(512), dp * 32, 32)
    red_value = lax.dynamic_slice_in_dim(pair[:, 1280:1536].reshape(512), dp * 32, 32)
    return (
        outputs,
        input_gradient,
        red_qkv,
        red_query,
        red_value,
        red_dense,
        red_dense_add,
        red_fc1,
        red_hidden_add,
        red_fc2,
        red_output_add,
        mine[0],
        mine[1],
        mine[2],
        mine[3],
    )


def solution(mesh):
    return jax.shard_map(
        local,
        mesh=mesh,
        in_specs=(
            P(("dp", "col"), "row"),
            P(("dp", "col"), "row"),
            P("dp"),
            P("row"),
            P("row"),
            P(("row", "dp"), "col"),
            P(("col", "dp")),
            P(("col", "dp")),
            P(("col", "dp"), "row"),
            P(("row", "dp")),
            P("row"),
            P("row"),
            P(("row", "dp"), "col"),
            P(("col", "dp")),
            P(("col", "dp"), "row"),
            P(("row", "dp")),
        ),
        out_specs=(
            P(("dp", "col"), "row"),
            P(("dp", "col"), "row"),
            P(("row", "dp"), "col"),
            P(("col", "dp")),
            P(("col", "dp")),
            P(("col", "dp"), "row"),
            P(("row", "dp")),
            P(("row", "dp"), "col"),
            P(("col", "dp")),
            P(("col", "dp"), "row"),
            P(("row", "dp")),
            P("row"),
            P("row"),
            P("row"),
            P("row"),
        ),
        check_vma=False,
    )
```

```python
from functools import partial

import jax
import jax.numpy as jnp
from jax import lax
from jax.experimental import pallas as pl
from jax.experimental.pallas import tpu as pltpu
from jax.sharding import PartitionSpec as P

HEADS = 32
HEAD_DIM = 64
BLOCK = 256
SEQ = 1024
WIDTH = 2048
HALF = WIDTH // 2
LOCAL = 256
EPSILON = 1e-05
FAR = 1e30
MESH = pl.DeviceIdType.MESH
F32 = jnp.float32
BF16 = jnp.bfloat16


def wrap(position):
    return lax.rem(position + 4, 4)


class Place:
    def __init__(self):
        self.row = lax.axis_index("row")
        self.col = lax.axis_index("col")
        self.dp = lax.axis_index("dp")
        self.chip = self.row * 2 + lax.div(self.col, 2)
        self.core = lax.rem(self.col, 2)
        self.z = lax.div(self.dp, 4)
        self.y = lax.rem(self.dp, 4)

    def on_x(self, step):
        return self.x_at(wrap(self.chip + step), self.core)

    def x_at(self, chip, core):
        return {"row": lax.div(chip, 2), "col": lax.rem(chip, 2) * 2 + core}

    def on_y(self, step):
        return {"dp": self.z * 4 + wrap(self.y + step)}

    def on_z(self, step):
        return {"dp": wrap(self.z + step) * 4 + self.y}

    def partner(self):
        return {"row": 1 - self.row}

    def mate(self):
        return {"col": lax.div(self.col, 2) * 2 + 1 - self.core}


class Net:
    def __init__(self, send, recv):
        self.send, self.recv, self.used = send, recv, 0

    def copy(self, source, target, device):
        slot = self.used
        self.used += 1
        return pltpu.make_async_remote_copy(
            src_ref=source,
            dst_ref=target,
            send_sem=self.send.at[slot],
            recv_sem=self.recv.at[slot],
            device_id=device,
            device_id_type=MESH,
        )


class Near:
    def __init__(self, sems):
        self.sems, self.used = sems, 0

    def copy(self, source, target):
        slot = self.used
        self.used += 1
        return pltpu.make_async_copy(source, target, self.sems.at[slot])


def greet(devices):
    barrier = pltpu.get_barrier_semaphore()
    for device in devices:
        pl.semaphore_signal(barrier, inc=1, device_id=device, device_id_type=MESH)
    pl.semaphore_wait(barrier, len(devices))


class RingGather:
    def __init__(self, net, block, me, right, left, own=None):
        before, after = wrap(me - 1), wrap(me + 1)
        own = own or (lambda half: block(me, half))
        self.first = [
            net.copy(own(0), block(me, 0), right),
            net.copy(own(1), block(me, 1), left),
        ]
        self.second = [
            net.copy(own(1), block(me, 1), right),
            net.copy(own(0), block(me, 0), left),
        ]
        self.passed = [
            net.copy(block(before, 0), block(before, 0), right),
            net.copy(block(after, 1), block(after, 1), left),
        ]

    def start(self):
        for copy in self.first + self.second:
            copy.start()

    def forward(self):
        for came, on in zip(self.first, self.passed):
            came.wait_recv()
            on.start()

    def near_done(self):
        for copy in self.second:
            copy.wait_recv()

    def far_done(self):
        for copy in self.passed:
            copy.wait_recv()

    def drain(self):
        for copy in self.first + self.second + self.passed:
            copy.wait_send()


class GroupGather:
    def __init__(self, net, place, block, own):
        core, chip = place.core, place.chip
        self.ring = RingGather(
            net,
            lambda position, half: block(position, core, half),
            chip,
            place.on_x(1),
            place.on_x(-1),
            own,
        )
        whole = [
            own(None),
            block(wrap(chip - 1), core, None),
            block(wrap(chip + 1), core, None),
            block(wrap(chip + 2), core, None),
        ]
        target = [block(chip, core, None)] + whole[1:]
        self.mates = [
            net.copy(source, there, place.mate()) for source, there in zip(whole, target)
        ]

    def start(self):
        self.ring.start()
        self.mates[0].start()

    def forward(self):
        self.ring.forward()

    def share(self):
        self.ring.near_done()
        self.mates[1].start()
        self.mates[2].start()

    def finish(self):
        self.ring.far_done()
        self.mates[3].start()
        for copy in self.mates:
            copy.wait_recv()
        self.ring.drain()
        for copy in self.mates:
            copy.wait_send()


def sweep(rows, step, body):
    def one(index, carry):
        body(pl.multiple_of(index * step, step))
        return carry

    lax.fori_loop(0, rows // step, one, 0)


class GroupScatter:
    SEMS = 10

    def __init__(self, net, place, part, slices, shape, mate_in, total, ring_in, comb):
        self.part, self.slices, self.place = part, slices, place
        self.rows, self.cols = shape
        self.mate_in, self.total = mate_in, total
        self.ring_in, self.comb = ring_in, comb
        chip = place.chip
        half = self.rows // 2
        self.half = half
        self.order = [wrap(chip + 2), wrap(chip + 1), wrap(chip - 1), chip]
        mate = place.mate()
        self.mates = []
        for index, there in enumerate(self.order):
            rows, cols = slices(there, 1 - place.core)
            self.mates.append(
                net.copy(
                    part.at[pl.ds(rows, self.rows), pl.ds(cols, self.cols)],
                    mate_in.at[index],
                    mate,
                )
            )
        right, left = place.on_x(1), place.on_x(-1)
        top, low = pl.ds(0, half), pl.ds(half, half)
        self.sends = [
            net.copy(total.at[0, top], ring_in.at[0], right),
            net.copy(total.at[0, low], ring_in.at[1], left),
            net.copy(total.at[1, low], ring_in.at[2], right),
            net.copy(total.at[2, top], ring_in.at[3], left),
            net.copy(comb.at[0], ring_in.at[4], right),
            net.copy(comb.at[1], ring_in.at[5], left),
        ]

    def start(self):
        for copy in self.mates:
            copy.start()

    def mine(self, index, row, step):
        rows, cols = self.slices(self.order[index], self.place.core)
        return self.part[
            pl.ds(pl.multiple_of(rows + row, 16), step), pl.ds(cols, self.cols)
        ].astype(F32)

    def first(self):
        for index in range(3):
            self.mates[index].wait_recv()

            def add(row, index=index):
                here = pl.ds(row, 16)
                self.total[index, here, :] = (
                    self.mine(index, row, 16) + self.mate_in[index, here, :].astype(F32)
                ).astype(BF16)

            sweep(self.rows, 16, add)
            if index == 0:
                self.sends[0].start()
                self.sends[1].start()
            else:
                self.sends[index + 1].start()

    def second(self):
        for side in range(2):
            self.sends[side].wait_recv()

            def add(row, side=side):
                here = pl.ds(row, 16)
                there = pl.ds(pl.multiple_of(row + side * self.half, 16), 16)
                self.comb[side, here, :] = (
                    self.total[1 + side, there, :].astype(F32)
                    + self.ring_in[side, here, :].astype(F32)
                ).astype(BF16)

            sweep(self.half, 16, add)
            self.sends[4 + side].start()

    def arrive(self):
        self.mates[3].wait_recv()
        for index in range(2, 6):
            self.sends[index].wait_recv()

    def result(self, side, row):
        here = pl.ds(row, 16)
        there = pl.multiple_of(row + side * self.half, 16)
        one, two = ((4, 3), (2, 5))[side]
        return (
            self.mine(3, there, 16)
            + self.mate_in[3, pl.ds(there, 16), :].astype(F32)
            + self.ring_in[one, here, :].astype(F32)
            + self.ring_in[two, here, :].astype(F32)
        )

    def drain(self):
        for copy in self.mates + self.sends:
            copy.wait_send()


def scatter_scratch(rows, cols):
    return [
        pltpu.VMEM((4, rows, cols), BF16),
        pltpu.VMEM((3, rows, cols), BF16),
        pltpu.VMEM((6, rows // 2, cols), BF16),
        pltpu.VMEM((2, rows // 2, cols), BF16),
    ]


class RingScatter:
    def __init__(self, net, part, me, right, left, ring_in, comb, target):
        before, after, across = wrap(me - 1), wrap(me + 1), wrap(me + 2)
        self.part, self.me, self.near = part, me, (after, before)
        self.ring_in, self.comb, self.target = ring_in, comb, target
        self.sends = [
            net.copy(part(across, 0), ring_in.at[0], right),
            net.copy(part(across, 1), ring_in.at[1], left),
            net.copy(part(after, 1), ring_in.at[2], right),
            net.copy(part(before, 0), ring_in.at[3], left),
            net.copy(comb.at[0], ring_in.at[4], right),
            net.copy(comb.at[1], ring_in.at[5], left),
        ]

    def start(self):
        for copy in self.sends[:4]:
            copy.start()

    def add(self, target, sources):
        shape = target.shape
        if len(shape) == 3:
            for index in range(shape[0]):
                self.add(target.at[index], [source.at[index] for source in sources])
            return

        def one(row):
            here = pl.ds(row, 16)
            total = sources[0][here, :].astype(F32)
            for source in sources[1:]:
                total = total + source[here, :].astype(F32)
            target[here, :] = total.astype(BF16)

        sweep(shape[0], 16, one)

    def middle(self):
        for side in range(2):
            self.sends[side].wait_recv()
            self.add(
                self.comb.at[side],
                [self.part(self.near[side], side), self.ring_in.at[side]],
            )
            self.sends[4 + side].start()

    def finish(self):
        for index in range(2, 6):
            self.sends[index].wait_recv()
        for side, (one, two) in enumerate(((4, 3), (2, 5))):
            self.add(
                self.target(side),
                [self.part(self.me, side), self.ring_in.at[one], self.ring_in.at[two]],
            )

    def drain(self):
        for copy in self.sends:
            copy.wait_send()


def any_specs(count):
    return [pl.BlockSpec(memory_space=pl.ANY)] * count


def vmem_specs(count):
    return [pl.BlockSpec(memory_space=pltpu.VMEM)] * count


def sem_arrays(remote, near=0):
    arrays = [pltpu.SemaphoreType.DMA((remote,)), pltpu.SemaphoreType.DMA((remote,))]
    if near:
        arrays.append(pltpu.SemaphoreType.DMA((near,)))
    return arrays


def comm_params(identity, megabytes=60):
    return pltpu.CompilerParams(
        collective_id=identity, has_side_effects=True, vmem_limit_bytes=megabytes << 20
    )


def quarter_block(ref):
    def block(chip, core, half):
        rows = (lax.rem(chip, 2) * 2 + core) * 256
        cols = lax.div(chip, 2) * HALF
        if half is None:
            return ref.at[pl.ds(rows, 256), pl.ds(cols, HALF)]
        return ref.at[pl.ds(rows + 128 * half, 128), pl.ds(cols, HALF)]

    return block


def rows_of(chip, core):
    return (lax.rem(chip, 2) * 2 + core) * 256 + lax.div(chip, 2) * 128


def row_block(ref):
    def block(chip, core, half):
        rows = rows_of(chip, core)
        if half is None:
            return ref.at[pl.ds(rows, 128), :]
        return ref.at[pl.ds(rows + 64 * half, 64), :]

    return block


def row_slices(chip, core):
    return rows_of(chip, core), 0


def quarter_slices(chip, core):
    return (lax.rem(chip, 2) * 2 + core) * 256, lax.div(chip, 2) * HALF


def stacked(ref, size):
    def at(part, z, y, rows):
        return ref.at[part, z, y, rows, :]

    return at, size


def beside(ref, size):
    def at(part, z, y, rows):
        return ref.at[z, y, rows, pl.ds(part * HALF, HALF)]

    return at, size


def head_mask(values, head):
    lane = lax.broadcasted_iota(jnp.int32, values.shape, 1)
    return jnp.where(lax.div(lane, HEAD_DIM) == head, values, jnp.zeros_like(values))


def distances(length, start, keys):
    key = lax.broadcasted_iota(jnp.int32, (keys, BLOCK), 0)
    query = lax.broadcasted_iota(jnp.int32, (keys, BLOCK), 1) + start
    return jnp.where(key < length, jnp.abs(query - key).astype(F32), FAR)


def slope_of(head):
    base = lax.axis_index("col") * 8 + lax.axis_index("row") * 4
    number = (base + head + 1).astype(F32)
    return jnp.exp2(jnp.full((1, BLOCK), -8.0 / HEADS, F32) * number)


def nt(left, right):
    return lax.dot_general(left, right, (((1,), (1,)), ((), ())), preferred_element_type=F32)


def nn(left, right):
    return jnp.dot(left, right, preferred_element_type=F32)


def attend_back_kernel(length, q, k, v, grad, logs, out, kt, dk, dv, dqt):
    kt[...] = k[...].T
    dk[...] = jnp.zeros_like(dk)
    dv[...] = jnp.zeros_like(dv)
    for block in range(4):
        start, keys = block * BLOCK, (block + 1) * BLOCK
        here = pl.ds(start, BLOCK)
        apart = distances(length[0], start, keys)

        def one(head, carry):
            scores = nt(head_mask(k[0:keys, :], head), q[here, :])
            prob = jnp.exp(scores - slope_of(head) * apart - logs[head, :, here])
            dprob = nt(head_mask(v[0:keys, :], head), grad[here, :])
            delta = jnp.sum(prob * dprob, 0, keepdims=True)
            dscore = (prob * (dprob - delta)).astype(BF16)
            dv[0:keys, :] += nn(prob.astype(BF16), head_mask(grad[here, :], head))
            dk[0:keys, :] += nn(dscore, head_mask(q[here, :], head))
            lines = pl.ds(pl.multiple_of(head * HEAD_DIM, HEAD_DIM), HEAD_DIM)
            dqt[lines, here] = nn(kt[lines, 0:keys], dscore)
            return carry

        lax.fori_loop(0, 4, one, 0)
    out[:, 0:256] = (dqt[...].T * HEAD_DIM**-0.5).astype(BF16)
    out[:, 256:512] = dk[...].astype(BF16)
    out[:, 512:768] = dv[...].astype(BF16)


def attend_back(length, q, k, v, grad, logs):
    return pl.pallas_call(
        attend_back_kernel,
        out_shape=jax.ShapeDtypeStruct((SEQ, 3 * LOCAL), BF16),
        in_specs=[pl.BlockSpec(memory_space=pltpu.SMEM)] + vmem_specs(5),
        out_specs=vmem_specs(1)[0],
        scratch_shapes=[
            pltpu.VMEM((LOCAL, SEQ), BF16),
            pltpu.VMEM((SEQ, LOCAL), F32),
            pltpu.VMEM((SEQ, LOCAL), F32),
            pltpu.VMEM((LOCAL, SEQ), F32),
        ],
        compiler_params=pltpu.CompilerParams(vmem_limit_bytes=48 << 20),
        name="attend_back",
    )(length, q, k, v, grad, logs)


def normalize(values):
    mean = jnp.mean(values, 1, keepdims=True)
    centered = values - mean
    scale = lax.rsqrt(jnp.mean(centered * centered, 1, keepdims=True) + EPSILON)
    return centered * scale, scale


def x_devices(place):
    return [place.on_x(1), place.on_x(-1), place.mate()]


def spread(small, line, base, per, first, width):
    entry = lax.broadcasted_iota(jnp.int32, (256, width), 1)
    piece = lax.broadcasted_iota(jnp.int32, (256, width), 0)
    wanted = (lax.div(entry, per) + first) * 16 + line
    chosen = jnp.where(piece == wanted, 1.0, 0.0).astype(BF16)
    spread_out = lax.dot_general(
        small, chosen, (((0,), (0,)), ((), ())), preferred_element_type=F32
    )
    lane = lax.broadcasted_iota(jnp.int32, (128, width), 0)
    entry = lax.broadcasted_iota(jnp.int32, (128, width), 1)
    return jnp.sum(
        jnp.where(lane == base + lax.rem(entry, per), spread_out, 0.0), 0, keepdims=True
    )


def attend_block(block, length, q, k, vt, out_t, logs):
    start, keys = block * BLOCK, (block + 1) * BLOCK
    here = pl.ds(start, BLOCK)
    apart = distances(length, start, keys)

    def one(head, carry):
        scores = nt(head_mask(k[0:keys, :], head), q[here, :])
        scores = scores - slope_of(head) * apart
        peak = jnp.max(scores, 0, keepdims=True)
        exponent = jnp.exp(scores - peak)
        total = jnp.sum(exponent, 0, keepdims=True)
        lines = pl.ds(pl.multiple_of(head * HEAD_DIM, HEAD_DIM), HEAD_DIM)
        out_t[lines, here] = nn(vt[lines, 0:keys], exponent.astype(BF16)) / total
        logs[head, :, here] = peak + jnp.log(total)
        return carry

    lax.fori_loop(0, 4, one, 0)


def forward_kernel(
    length, x, cot, qkv, dense, fc1, fc2, small, norms,
    gcot, gqkv, gdense, gfc1, gfc2, rows_one, rows_two, heads, logs, residual, stats,
    vectors, grad_act,
    vx, vcot, vqkv, vdense, vfc2, vsmall, vnorm, n1, vheads, vt, out_t, part, own, tile,
    vlogs, mate_in, total, ring_in, comb, send, recv, near_sems,
):
    place = Place()
    net, near = Net(send, recv), Near(near_sems)
    row, z, y = place.row, place.z, place.y
    partner = place.partner()
    greet(
        [partner, place.on_x(1), place.on_x(-1), place.mate()]
        + [place.on_y(1), place.on_y(-1), place.on_z(1), place.on_z(-1)]
    )
    weights = [
        (stacked(vqkv, 64), qkv.at[row], qkv.at[1 - row]),
        (stacked(vsmall, 16), small, small),
        (beside(vdense, 32), dense, dense),
        (stacked(gfc1, 64), fc1.at[row], fc1.at[1 - row]),
        (beside(vfc2, 64), fc2.at[row], fc2.at[1 - row]),
    ]
    swaps, copies = [], []
    for (at, size), own_cut, other in weights:
        there = at(row, z, y, pl.ds(0, size))
        swaps.append(net.copy(other, there, partner))
        copies.append(near.copy(own_cut, there))
    swap_norms = net.copy(norms, vnorm.at[row], partner)
    groups = []
    for source, target in ((x, vx), (cot, vcot)):
        block = quarter_block(target)

        def own_part(half, source=source):
            if half is None:
                return source
            return source.at[pl.ds(128 * half, 128), :]

        groups.append(GroupGather(net, place, block, own_part))
        copies.append(near.copy(source, block(place.chip, place.core, None)))
    copies.append(near.copy(norms, vnorm.at[row]))
    ones, twos = [], []
    for (at, size), own_cut, other in weights:
        half_rows = size // 2
        rows = pl.ds(0, size)

        def along_y(position, half, at=at, half_rows=half_rows):
            return at(row, z, position, pl.ds(half * half_rows, half_rows))

        def along_z(position, half, at=at, half_rows=half_rows):
            return at(1 - row, position, y, pl.ds(half * half_rows, half_rows))

        def mine(half, own_cut=own_cut, half_rows=half_rows):
            return own_cut.at[pl.ds(half * half_rows, half_rows), :]

        def planes_z(position, half, at=at, rows=rows):
            return at(row, position, pl.ds(2 * half, 2), rows)

        def planes_y(position, half, at=at, rows=rows):
            return at(1 - row, pl.ds(2 * half, 2), position, rows)

        over_y = (y, place.on_y(1), place.on_y(-1))
        over_z = (z, place.on_z(1), place.on_z(-1))
        ones.append(
            (RingGather(net, along_y, *over_y, mine), RingGather(net, along_z, *over_z))
        )
        twos.append((RingGather(net, planes_z, *over_z), RingGather(net, planes_y, *over_y)))

    def begin(index):
        ones[index][0].start()
        swaps[index].wait_recv()
        ones[index][1].start()

    def pass_one(index):
        for ring in ones[index]:
            ring.forward()

    def turn_over(index):
        for ring, then in zip(ones[index], twos[index]):
            ring.near_done()
            ring.far_done()
            then.start()

    def pass_two(index):
        for ring in twos[index]:
            ring.forward()

    def complete(index):
        for ring in twos[index]:
            ring.near_done()
            ring.far_done()

    group_x, group_cot = groups
    swaps[0].start()
    ones[0][0].start()
    swap_norms.start()
    swaps[1].start()
    group_x.start()
    for copy in copies:
        copy.start()
    for swap in swaps[2:]:
        swap.start()
    swaps[0].wait_recv()
    ones[0][1].start()
    begin(1)
    for copy in copies:
        copy.wait()
    pass_one(0)
    group_x.forward()
    turn_over(0)
    pass_one(1)
    begin(2)
    begin(3)
    begin(4)
    turn_over(1)
    group_x.share()
    pass_two(0)
    pass_two(1)
    for index in (2, 3, 4):
        pass_one(index)
    group_x.finish()
    group_cot.start()
    turn_over(2)
    turn_over(3)
    swap_norms.wait_recv()

    def first_norm(pos):
        here = pl.ds(pos, 16)
        left, right = vx[here, 0:HALF].astype(F32), vx[here, HALF:WIDTH].astype(F32)
        mean = (
            jnp.sum(left, 1, keepdims=True) + jnp.sum(right, 1, keepdims=True)
        ) / WIDTH
        left, right = left - mean, right - mean
        scale = lax.rsqrt(
            (
                jnp.sum(left * left, 1, keepdims=True)
                + jnp.sum(right * right, 1, keepdims=True)
            )
            / WIDTH
            + EPSILON
        )
        lane = lax.broadcasted_iota(jnp.int32, (16, 128), 1)
        vlogs[here, :] = jnp.where(lane == 0, mean, scale)
        n1[here, 0:HALF] = (left * scale * vnorm[0, 0:1, :] + vnorm[0, 1:2, :]).astype(BF16)
        n1[here, HALF:WIDTH] = (
            right * scale * vnorm[1, 0:1, :] + vnorm[1, 1:2, :]
        ).astype(BF16)

    sweep(SEQ, 16, first_norm)
    turn_over(4)
    keep_n1 = near.copy(n1, rows_one)
    keep_n1.start()
    complete(1)
    smalls = [vsmall[index].reshape(256, 128) for index in range(2)]
    query_add = spread(smalls[0], 1, 0, 32, 8 * row, LOCAL)
    value_add = spread(smalls[0], 1, 32, 32, 8 * row, LOCAL)
    for side in range(2):
        half = pl.ds(side * HALF, HALF)
        vectors[0:1, half] = spread(smalls[side], 1, 64, 64, 0, HALF)
        vectors[1:2, half] = spread(smalls[side], 2, 0, 64, 0, HALF)
        vectors[3:4, half] = vnorm[side, 2:3, :]
        vectors[4:5, half] = vnorm[side, 3:4, :]
    complete(0)
    keep_qkv = near.copy(vqkv, gqkv)
    keep_qkv.start()

    def project(index, carry):
        here = pl.ds(pl.multiple_of(index * 256, 256), 256)
        for third, add in enumerate((query_add, None, value_add)):
            cols = slice(third * 256, (third + 1) * 256)
            made = nn(n1[here, :], vqkv[:, :, :, :, cols].reshape(WIDTH, 256))
            if add is not None:
                made = made + add
            made = made.astype(BF16)
            if third == 0:
                made = made * BF16(HEAD_DIM**-0.5)
            vheads[third, here, :] = made
        return carry

    lax.fori_loop(0, 4, project, 0)
    group_cot.forward()
    vt[...] = vheads[2].T
    args = (length[0], vheads.at[0], vheads.at[1], vt, out_t, logs)
    attend_block(0, *args)
    attend_block(1, *args)
    pass_two(2)
    group_cot.share()
    attend_block(2, *args)
    pass_two(3)
    attend_block(3, *args)
    vheads[3] = out_t[...].T.astype(BF16)
    complete(2)
    keep_heads = near.copy(vheads, heads)
    keep_heads.start()
    keep_dense = near.copy(vdense, gdense)
    keep_dense.start()

    scatter = GroupScatter(
        net, place, part, row_slices, (128, WIDTH), mate_in, total, ring_in, comb
    )
    weight = vdense[pl.ds(2 * row, 2)].reshape(LOCAL, WIDTH)
    for index, chip in enumerate(scatter.order):
        starts = [pl.multiple_of(rows_of(chip, core), 128) for core in range(2)]
        both = jnp.concatenate([vheads[3, pl.ds(start, 128), :] for start in starts], 0)
        made = nn(both, weight).astype(BF16)
        part[pl.ds(starts[0], 128), :] = made[0:128]
        part[pl.ds(starts[1], 128), :] = made[128:256]
        scatter.mates[index].start()
    scatter.first()
    group_cot.finish()
    keep_cot = near.copy(vcot, gcot)
    keep_cot.start()
    pass_two(4)
    complete(3)
    vectors[2:3, 0:HALF] = jnp.where(
        row == 0,
        spread(smalls[0], 0, 0, 64, 0, HALF),
        spread(smalls[0], 0, 64, 64, 0, HALF),
    )
    scatter.second()
    scatter.arrive()
    group_two = GroupGather(
        net,
        place,
        row_block(rows_two),
        lambda half: own if half is None else own.at[pl.ds(64 * half, 64), :],
    )
    keep_own = near.copy(own, row_block(rows_two)(place.chip, place.core, None))
    first_row = rows_of(place.chip, place.core)
    for side in range(2):

        def one(pos, side=side):
            here = pl.ds(pl.multiple_of(pos + 64 * side, 16), 16)
            there = pl.ds(pl.multiple_of(first_row + pos + 64 * side, 16), 16)
            values = (
                vx[there, :].astype(F32) + scatter.result(side, pos) + vectors[0:1, :]
            )
            residual[here, :] = values
            own[here, :] = (
                normalize(values)[0] * vectors[3:4, :] + vectors[4:5, :]
            ).astype(BF16)

        sweep(64, 16, one)
    group_two.start()
    keep_own.start()
    stats[...] = vlogs[pl.ds(pl.multiple_of(place.col * 256, 256), 256), :]
    complete(4)
    keep_fc2 = near.copy(vfc2, gfc2)
    keep_fc2.start()
    keeps = []
    for index in range(4):
        here = pl.ds(index * 256, 256)
        for piece in range(4):
            lines = vfc2[piece].reshape(256, WIDTH)
            tile[index, :, pl.ds(piece * 256, 256)] = nt(vcot[here, :], lines)
        keep = near.copy(tile.at[index], grad_act.at[here, :])
        keep.start()
        keeps.append(keep)
        if index == 1:
            group_two.forward()
        if index == 3:
            group_two.share()
    group_two.finish()
    keeps += [keep_n1, keep_qkv, keep_heads, keep_dense, keep_cot, keep_own, keep_fc2]
    for keep in keeps:
        keep.wait()
    swap_norms.wait_send()
    for swap in swaps:
        swap.wait_send()
    for pair in ones + twos:
        for ring in pair:
            ring.drain()
    scatter.drain()


def forward(length, x, cot, qkv, dense, fc1, fc2, small, norms):
    remote = 6 + 3 * 10 + 10 + 5 * 4 * 6
    bf, full = (lambda *shape: jax.ShapeDtypeStruct(shape, BF16)), (
        lambda *shape: jax.ShapeDtypeStruct(shape, F32)
    )
    return pl.pallas_call(
        forward_kernel,
        out_shape=(
            bf(SEQ, WIDTH),
            bf(2, 4, 4, 64, 768),
            bf(4, 4, 32, 2048),
            bf(2, 4, 4, 64, 1024),
            bf(4, 4, 64, 2048),
            bf(SEQ, WIDTH),
            bf(SEQ, WIDTH),
            bf(4, SEQ, LOCAL),
            full(4, 1, SEQ),
            full(128, WIDTH),
            full(256, 128),
            full(8, WIDTH),
            full(SEQ, 1024),
        ),
        in_specs=[pl.BlockSpec(memory_space=pltpu.SMEM)] + any_specs(8),
        out_specs=tuple(any_specs(8) + vmem_specs(4) + any_specs(1)),
        scratch_shapes=[
            pltpu.VMEM((SEQ, WIDTH), BF16),
            pltpu.VMEM((SEQ, WIDTH), BF16),
            pltpu.VMEM((2, 4, 4, 64, 768), BF16),
            pltpu.VMEM((4, 4, 32, 2048), BF16),
            pltpu.VMEM((4, 4, 64, 2048), BF16),
            pltpu.VMEM((2, 4, 4, 16, 128), BF16),
            pltpu.VMEM((2, 8, HALF), F32),
            pltpu.VMEM((SEQ, WIDTH), BF16),
            pltpu.VMEM((4, SEQ, LOCAL), BF16),
            pltpu.VMEM((LOCAL, SEQ), BF16),
            pltpu.VMEM((LOCAL, SEQ), F32),
            pltpu.VMEM((SEQ, WIDTH), BF16),
            pltpu.VMEM((128, WIDTH), BF16),
            pltpu.VMEM((4, 256, 1024), F32),
            pltpu.VMEM((SEQ, 128), F32),
        ]
        + scatter_scratch(128, WIDTH)
        + sem_arrays(remote, 20),
        compiler_params=comm_params(0),
        name="forward",
    )(length, x, cot, qkv, dense, fc1, fc2, small, norms)


def turn_kernel(
    part, residual, cot, gain, gathered, sums,
    mate_in, total, ring_in, comb, own, send, recv, near_sems,
):
    place = Place()
    net = Net(send, recv)
    greet(x_devices(place))
    scatter = GroupScatter(
        net, place, part, row_slices, (128, WIDTH), mate_in, total, ring_in, comb
    )
    block = row_block(gathered)
    group = GroupGather(
        net,
        place,
        block,
        lambda half: own if half is None else own.at[pl.ds(64 * half, 64), :],
    )
    scatter.start()
    scatter.first()
    scatter.second()
    sums[...] = jnp.zeros_like(sums)
    scatter.arrive()
    for side in range(2):

        def one(row, side=side):
            here = pl.ds(pl.multiple_of(row + 64 * side, 16), 16)
            arrived = scatter.result(side, row)
            xhat, scale = normalize(residual[here, :])
            scaled = arrived * gain[...]
            flat = jnp.mean(scaled, 1, keepdims=True)
            cross = jnp.mean(scaled * xhat, 1, keepdims=True)
            own[here, :] = (
                cot[here, :].astype(F32) + scale * (scaled - flat - xhat * cross)
            ).astype(BF16)
            sums[0:1, :] += jnp.sum(arrived * xhat, 0, keepdims=True)
            sums[1:2, :] += jnp.sum(arrived, 0, keepdims=True)

        sweep(64, 16, one)
    group.start()
    keep = Near(near_sems).copy(own, block(place.chip, place.core, None))
    keep.start()
    group.forward()
    group.share()
    group.finish()
    keep.wait()
    scatter.drain()


def turn(part, residual, cot, gain):
    return pl.pallas_call(
        turn_kernel,
        out_shape=(
            jax.ShapeDtypeStruct((SEQ, WIDTH), BF16),
            jax.ShapeDtypeStruct((8, WIDTH), F32),
        ),
        in_specs=vmem_specs(4),
        out_specs=(any_specs(1)[0], vmem_specs(1)[0]),
        scratch_shapes=scatter_scratch(128, WIDTH)
        + [pltpu.VMEM((128, WIDTH), BF16)]
        + sem_arrays(20, 1),
        compiler_params=comm_params(2),
        name="turn",
    )(part, residual, cot, gain)


def last_kernel(
    part, part_out, x, mean, scale, branch, gain, residual, add, small,
    gqkv, gdense, gfc1, gfc2,
    ingrad, out, rqkv, rdense, rfc1, rfc2, vector,
    *scratch,
):
    scratch = list(scratch)

    def take(count):
        taken = scratch[:count]
        del scratch[:count]
        return taken

    place = Place()
    row, z, y = place.row, place.z, place.y
    send, recv, near_sems = take(3)
    net, near = Net(send, recv), Near(near_sems)
    x_group = [
        place.x_at(wrap(place.chip + step), core)
        for step in range(4)
        for core in (place.core, 1 - place.core)
    ][1:]
    y_ring = [place.on_y(step) for step in (1, 2, 3)]
    z_ring = [place.on_z(step) for step in (1, 2, 3)]
    greet(x_group + y_ring + z_ring)
    scatter = GroupScatter(net, place, part, quarter_slices, (256, HALF), *take(4))
    scatter_out = GroupScatter(net, place, part_out, row_slices, (128, WIDTH), *take(4))
    result, stats_out, stats_in, group_in, y_in, z_in, vec_a, vec_b = take(8)
    weights = []
    for at, size, cols, final in (
        (stacked(gfc1, 64)[0], 64, 1024, rfc1),
        (beside(gfc2, 64)[0], 64, 1024, rfc2),
        (beside(gdense, 32)[0], 32, 1024, rdense),
        (stacked(gqkv, 64)[0], 64, 768, rqkv),
    ):
        done = take(1)[0]
        pairs = []
        for part_index in range(2):
            ring_in1, comb1, mid, ring_in2, comb2 = take(5)
            half_rows = size // 2

            def along_z(pos, half, at=at, size=size, h=part_index):
                return at(h, pos, pl.ds(2 * half, 2), pl.ds(0, size))

            def along_y(pos, half, at=at, size=size, h=part_index):
                return at(h, pl.ds(2 * half, 2), pos, pl.ds(0, size))

            def inner(pos, half, mid=mid, half_rows=half_rows):
                return mid.at[pos, pl.ds(half * half_rows, half_rows), :]

            def mid_half(half, mid=mid):
                return mid.at[pl.ds(2 * half, 2)]

            def done_half(half, done=done, half_rows=half_rows, h=part_index):
                return done.at[h, pl.ds(half * half_rows, half_rows), :]

            over_z = (z, place.on_z(1), place.on_z(-1))
            over_y = (y, place.on_y(1), place.on_y(-1))
            if part_index == 0:
                one = RingScatter(net, along_z, *over_z, ring_in1, comb1, mid_half)
                two = RingScatter(net, inner, *over_y, ring_in2, comb2, done_half)
            else:
                one = RingScatter(net, along_y, *over_y, ring_in1, comb1, mid_half)
                two = RingScatter(net, inner, *over_z, ring_in2, comb2, done_half)
            pairs.append((one, two))
        swap = net.copy(done.at[1 - row], final.at[row], place.partner())
        keep = near.copy(done.at[row], final.at[row])
        weights.append((pairs, swap, keep))

    scatter.start()
    for pairs, swap, keep in weights:
        for one, two in pairs:
            one.start()
    scatter.first()
    scatter_out.start()
    scatter.second()
    scatter_out.first()
    for pairs, swap, keep in weights[:2]:
        for one, two in pairs:
            one.middle()
    scatter.arrive()

    vec_a[...] = small[...]
    lane = lax.broadcasted_iota(jnp.int32, (16, 128), 1)
    cols = pl.ds(pl.multiple_of(row * HALF, HALF), HALF)
    for side in range(2):

        def sums(pos, side=side):
            here = pl.ds(pl.multiple_of(pos + 128 * side, 16), 16)
            arrived = scatter.result(side, pos)
            scaled = arrived * gain[...]
            xhat = (x[here, :].astype(F32) - mean[here, :]) * scale[here, :]
            flat = jnp.sum(scaled, 1, keepdims=True)
            cross = jnp.sum(scaled * xhat, 1, keepdims=True)
            stats_out[here, :] = jnp.where(lane == 0, flat, cross)
            ingrad[here, :] = arrived
            vec_a[0:1, cols] += jnp.sum(arrived * xhat, 0, keepdims=True)
            vec_a[1:2, cols] += jnp.sum(arrived, 0, keepdims=True)

        sweep(128, 16, sums)
    stats = net.copy(stats_out, stats_in, place.partner())
    stats.start()
    group_sends = [
        net.copy(vec_a, group_in.at[index], device)
        for index, device in enumerate(x_group)
    ]
    for copy in group_sends:
        copy.start()
    scatter_out.second()
    for pairs, swap, keep in weights[2:]:
        for one, two in pairs:
            one.middle()
    stats.wait_recv()

    def apply(pos):
        here = pl.ds(pos, 16)
        both = (stats_out[here, :] + stats_in[here, :]) / WIDTH
        xhat = (x[here, :].astype(F32) - mean[here, :]) * scale[here, :]
        ingrad[here, :] = branch[here, :].astype(F32) + scale[here, :] * (
            ingrad[here, :] * gain[...] - both[:, 0:1] - xhat * both[:, 1:2]
        )

    sweep(256, 16, apply)
    for copy in group_sends:
        copy.wait_recv()
    vec_b[...] = vec_a[...]
    for index in range(7):
        vec_b[0:4, :] += group_in[index, 0:4, :]
    vec_b[7:8, :] = group_in[3, 6:7, :]
    y_sends = [net.copy(vec_b, y_in.at[i], device) for i, device in enumerate(y_ring)]
    for copy in y_sends:
        copy.start()
    for pairs, swap, keep in weights:
        for one, two in pairs:
            one.finish()
            two.start()
    scatter_out.arrive()
    for side in range(2):

        def finish(pos, side=side):
            here = pl.ds(pl.multiple_of(pos + 64 * side, 16), 16)
            result[here, :] = (
                residual[here, :] + scatter_out.result(side, pos) + add[...]
            ).astype(BF16)

        sweep(64, 16, finish)
    there = pl.ds(row * 128, 128)
    out_swap = net.copy(
        result.at[:, pl.ds((1 - row) * HALF, HALF)], out.at[there, :], place.partner()
    )
    out_keep = near.copy(result.at[:, pl.ds(row * HALF, HALF)], out.at[there, :])
    out_swap.start()
    out_keep.start()
    for copy in y_sends:
        copy.wait_recv()
    for copy in group_sends:
        copy.wait_send()
    vec_a[...] = vec_b[...]
    for index in range(3):
        vec_a[...] += y_in[index]
    z_sends = [net.copy(vec_a, z_in.at[i], device) for i, device in enumerate(z_ring)]
    for copy in z_sends:
        copy.start()
    for pairs, swap, keep in weights:
        for one, two in pairs:
            two.middle()
    for pairs, swap, keep in weights:
        for one, two in pairs:
            two.finish()
        swap.start()
        keep.start()
    for copy in z_sends:
        copy.wait_recv()
    vector[...] = vec_a[...]
    for index in range(3):
        vector[...] += z_in[index]
    out_swap.wait_recv()
    for pairs, swap, keep in weights:
        swap.wait_recv()
        keep.wait()
        swap.wait_send()
        for one, two in pairs:
            one.drain()
            two.drain()
    out_keep.wait()
    out_swap.wait_send()
    stats.wait_send()
    for copy in y_sends + z_sends:
        copy.wait_send()
    scatter.drain()
    scatter_out.drain()


def last(part, part_out, x, mean, scale, branch, gain, residual, add, small, *grads):
    scratch = sem_arrays(2 * 10 + 4 * (2 * 12 + 1) + 1 + 7 + 1 + 6, 5)
    scratch += scatter_scratch(256, HALF) + scatter_scratch(128, WIDTH)
    scratch += [
        pltpu.VMEM((128, WIDTH), BF16),
        pltpu.VMEM((256, 128), F32),
        pltpu.VMEM((256, 128), F32),
        pltpu.VMEM((7, 8, WIDTH), F32),
        pltpu.VMEM((3, 8, WIDTH), F32),
        pltpu.VMEM((3, 8, WIDTH), F32),
        pltpu.VMEM((8, WIDTH), F32),
        pltpu.VMEM((8, WIDTH), F32),
    ]
    for size, cols in ((64, 1024), (64, 1024), (32, 1024), (64, 768)):
        scratch.append(pltpu.VMEM((2, size, cols), BF16))
        for _ in range(2):
            scratch += [
                pltpu.VMEM((6, 2, size, cols), BF16),
                pltpu.VMEM((2, 2, size, cols), BF16),
                pltpu.VMEM((4, size, cols), BF16),
                pltpu.VMEM((6, size // 2, cols), BF16),
                pltpu.VMEM((2, size // 2, cols), BF16),
            ]
    return pl.pallas_call(
        last_kernel,
        out_shape=(
            jax.ShapeDtypeStruct((256, HALF), F32),
            jax.ShapeDtypeStruct((256, HALF), BF16),
            jax.ShapeDtypeStruct((2, 64, 768), BF16),
            jax.ShapeDtypeStruct((2, 32, 1024), BF16),
            jax.ShapeDtypeStruct((2, 64, 1024), BF16),
            jax.ShapeDtypeStruct((2, 64, 1024), BF16),
            jax.ShapeDtypeStruct((8, WIDTH), F32),
        ),
        in_specs=vmem_specs(14),
        out_specs=tuple(vmem_specs(7)),
        scratch_shapes=scratch,
        compiler_params=comm_params(3),
        name="last",
    )(part, part_out, x, mean, scale, branch, gain, residual, add, small, *grads)


def inner_rows(left_side, right_side):
    return lax.dot_general(
        left_side, right_side, (((0,), (0,)), ((), ())), preferred_element_type=F32
    )


def local(
    inputs,
    cotangent,
    lengths,
    attention_norm_gain,
    attention_norm_bias,
    qkv_weight,
    query_bias,
    value_bias,
    dense_weight,
    dense_bias,
    feedforward_norm_gain,
    feedforward_norm_bias,
    fc1_weight,
    fc1_bias,
    fc2_weight,
    fc2_bias,
):
    row = lax.axis_index("row")
    col = lax.axis_index("col")
    dp = lax.axis_index("dp")

    qkv_cut = qkv_weight.reshape(64, 2, 4, 3, 64).transpose(1, 0, 3, 2, 4)
    qkv_cut = qkv_cut.reshape(2, 64, 768)
    fc1_cut = fc1_weight.reshape(64, 16, 2, 64).transpose(2, 0, 1, 3)
    fc1_cut = fc1_cut.reshape(2, 64, 1024)
    fc2_cut = fc2_weight.reshape(2, 64, 1024)
    small = jnp.zeros((16, 128), BF16)
    small = small.at[0, :].set(fc1_bias)
    small = small.at[1, :].set(jnp.concatenate([query_bias, value_bias, dense_bias]))
    small = small.at[2, 0:64].set(fc2_bias)
    norms = jnp.concatenate(
        [
            jnp.stack(
                [
                    attention_norm_gain,
                    attention_norm_bias,
                    feedforward_norm_gain,
                    feedforward_norm_bias,
                ]
            ),
            jnp.zeros((4, HALF), F32),
        ]
    )
    (
        rows_cot, qkv_full, dense_full, fc1_full, fc2_full, rows_one, rows_two, heads,
        logs, residual, stats, vectors, grad_act,
    ) = forward(
        lengths, inputs, cotangent, qkv_cut, dense_weight, fc1_cut, fc2_cut, small, norms
    )
    qkv_full = qkv_full.reshape(WIDTH, 768)
    dense_full = lax.dynamic_slice_in_dim(
        dense_full.reshape(512, WIDTH), row * LOCAL, LOCAL, 0
    )
    fc1_full = fc1_full.reshape(WIDTH, 1024)
    fc2_full = fc2_full.reshape(1024, WIDTH)
    queries, keys, values, attended = (heads[index] for index in range(4))
    output_add, hidden_add, gain_two = (
        vectors[1:2], vectors[2:3, 0:HALF], vectors[3:4]
    )
    row_start = col * 256 + row * 128
    hidden = jnp.dot(rows_two, fc1_full, preferred_element_type=F32) + hidden_add
    gelu_value, gelu_pullback = jax.vjp(partial(jax.nn.gelu, approximate=False), hidden)
    activated = gelu_value.astype(BF16)
    grad_hidden = gelu_pullback(grad_act)[0].astype(BF16)
    part_two = lax.dot_general(
        grad_hidden, fc1_full, (((1,), (1,)), ((), ())), preferred_element_type=F32
    ).astype(BF16)
    cot_rows = lax.dynamic_slice_in_dim(rows_cot, row_start, 128, 0)
    rows_branch, sums_two = turn(part_two, residual, cot_rows, gain_two)
    grad_attended = lax.dot_general(
        rows_branch, dense_full, (((1,), (1,)), ((), ())), preferred_element_type=F32
    ).astype(BF16)
    grad_projected = attend_back(lengths, queries, keys, values, grad_attended, logs)
    part_one = lax.dot_general(
        grad_projected, qkv_full, (((1,), (1,)), ((), ())), preferred_element_type=F32
    ).astype(BF16)
    part_out = jnp.dot(activated, fc2_full, preferred_element_type=F32).astype(BF16)
    grad_fc2 = inner_rows(activated, rows_cot).astype(BF16).reshape(4, 4, 64, WIDTH)
    grad_fc1 = inner_rows(rows_two, grad_hidden).astype(BF16)
    grad_fc1 = grad_fc1.reshape(2, 4, 4, 64, 1024)
    grad_dense = inner_rows(attended, rows_branch).astype(BF16)
    empty = jnp.zeros_like(grad_dense)
    grad_dense = jnp.where(
        row == 0,
        jnp.concatenate([grad_dense, empty]),
        jnp.concatenate([empty, grad_dense]),
    ).reshape(4, 4, 32, WIDTH)
    grad_qkv = inner_rows(rows_one, grad_projected).astype(BF16)
    grad_qkv = grad_qkv.reshape(2, 4, 4, 64, 768)
    bias_sums = jnp.sum(grad_projected.astype(F32), 0)
    own_sums = jnp.concatenate(
        [
            jnp.sum(grad_hidden.astype(F32), 0),
            bias_sums[0:256],
            bias_sums[512:768],
            jnp.zeros((512,), F32),
        ]
    )
    zero = jnp.zeros((WIDTH,), F32)
    vector = jnp.stack(
        [
            zero,
            zero,
            sums_two[0],
            sums_two[1],
            jnp.sum(rows_branch.astype(F32), 0),
            jnp.sum(rows_cot.astype(F32), 0),
            own_sums,
            zero,
        ]
    )
    own_rows = col * 256
    own_cols = row * HALF
    input_gradient, outputs, red_qkv, red_dense, red_fc1, red_fc2, total = last(
        part_one,
        part_out,
        inputs,
        stats[:, 0:1],
        stats[:, 1:2],
        lax.dynamic_slice(rows_branch, (own_rows, own_cols), (256, HALF)),
        attention_norm_gain.reshape(1, HALF),
        residual,
        output_add,
        vector,
        grad_qkv,
        grad_dense,
        grad_fc1,
        grad_fc2,
    )
    red_qkv = (
        red_qkv.reshape(2, 64, 3, 4, 64).transpose(1, 0, 3, 2, 4).reshape(64, 1536)
    ).astype(F32)
    red_fc1 = (
        red_fc1.reshape(2, 64, 16, 64).transpose(1, 2, 0, 3).reshape(64, 2048)
    ).astype(F32)
    red_fc2 = red_fc2.reshape(128, HALF).astype(F32)
    red_dense = red_dense[0].astype(F32) + red_dense[1].astype(F32)

    halves = total[0:6].reshape(6, 2, HALF)
    mine = lax.dynamic_index_in_dim(halves, row, 1, False)
    red_dense_add = lax.dynamic_slice_in_dim(mine[4], dp * 64, 64)
    red_output_add = lax.dynamic_slice_in_dim(mine[5], dp * 64, 64)
    pair = jnp.where(row == 0, total[6:8], total[6:8][::-1])
    hidden_sums = pair[:, 0:1024].reshape(2, 16, 64)
    red_hidden_add = lax.dynamic_index_in_dim(hidden_sums, dp, 1, False).reshape(128)
    red_query = lax.dynamic_slice_in_dim(pair[:, 1024:1280].reshape(512), dp * 32, 32)
    red_value = lax.dynamic_slice_in_dim(pair[:, 1280:1536].reshape(512), dp * 32, 32)
    return (
        outputs,
        input_gradient,
        red_qkv,
        red_query,
        red_value,
        red_dense,
        red_dense_add,
        red_fc1,
        red_hidden_add,
        red_fc2,
        red_output_add,
        mine[0],
        mine[1],
        mine[2],
        mine[3],
    )


def solution(mesh):
    return jax.shard_map(
        local,
        mesh=mesh,
        in_specs=(
            P(("dp", "col"), "row"),
            P(("dp", "col"), "row"),
            P("dp"),
            P("row"),
            P("row"),
            P(("row", "dp"), "col"),
            P(("col", "dp")),
            P(("col", "dp")),
            P(("col", "dp"), "row"),
            P(("row", "dp")),
            P("row"),
            P("row"),
            P(("row", "dp"), "col"),
            P(("col", "dp")),
            P(("col", "dp"), "row"),
            P(("row", "dp")),
        ),
        out_specs=(
            P(("dp", "col"), "row"),
            P(("dp", "col"), "row"),
            P(("row", "dp"), "col"),
            P(("col", "dp")),
            P(("col", "dp")),
            P(("col", "dp"), "row"),
            P(("row", "dp")),
            P(("row", "dp"), "col"),
            P(("col", "dp")),
            P(("col", "dp"), "row"),
            P(("row", "dp")),
            P("row"),
            P("row"),
            P("row"),
            P("row"),
        ),
        check_vma=False,
    )
```

```python
import jax
import jax.numpy as jnp
from jax import lax
from jax.experimental import pallas as pl
from jax.experimental.pallas import tpu as pltpu
from jax.sharding import PartitionSpec as P

HEADS = 32
HEAD_DIM = 64
BLOCK = 256
SEQ = 1024
WIDTH = 2048
HALF = WIDTH // 2
LOCAL = 256
EPSILON = 1e-05
FAR = 1e30
MESH = pl.DeviceIdType.MESH
F32 = jnp.float32
BF16 = jnp.bfloat16


def wrap(position):
    return lax.rem(position + 4, 4)


class Place:
    def __init__(self):
        self.row = lax.axis_index("row")
        self.col = lax.axis_index("col")
        self.dp = lax.axis_index("dp")
        self.chip = self.row * 2 + lax.div(self.col, 2)
        self.core = lax.rem(self.col, 2)
        self.z = lax.div(self.dp, 4)
        self.y = lax.rem(self.dp, 4)

    def on_x(self, step):
        return self.x_at(wrap(self.chip + step), self.core)

    def x_at(self, chip, core):
        return {"row": lax.div(chip, 2), "col": lax.rem(chip, 2) * 2 + core}

    def on_y(self, step):
        return {"dp": self.z * 4 + wrap(self.y + step)}

    def on_z(self, step):
        return {"dp": wrap(self.z + step) * 4 + self.y}

    def partner(self):
        return {"row": 1 - self.row}

    def mate(self):
        return {"col": lax.div(self.col, 2) * 2 + 1 - self.core}


class Net:
    def __init__(self, send, recv):
        self.send, self.recv, self.used = send, recv, 0

    def copy(self, source, target, device):
        slot = self.used
        self.used += 1
        return pltpu.make_async_remote_copy(
            src_ref=source,
            dst_ref=target,
            send_sem=self.send.at[slot],
            recv_sem=self.recv.at[slot],
            device_id=device,
            device_id_type=MESH,
        )


class Near:
    def __init__(self, sems):
        self.sems, self.used = sems, 0

    def copy(self, source, target):
        slot = self.used
        self.used += 1
        return pltpu.make_async_copy(source, target, self.sems.at[slot])


def greet(devices):
    barrier = pltpu.get_barrier_semaphore()
    for device in devices:
        pl.semaphore_signal(barrier, inc=1, device_id=device, device_id_type=MESH)
    pl.semaphore_wait(barrier, len(devices))


class RingGather:
    def __init__(self, net, block, me, right, left, own=None):
        before, after = wrap(me - 1), wrap(me + 1)
        own = own or (lambda half: block(me, half))
        self.first = [
            net.copy(own(0), block(me, 0), right),
            net.copy(own(1), block(me, 1), left),
        ]
        self.second = [
            net.copy(own(1), block(me, 1), right),
            net.copy(own(0), block(me, 0), left),
        ]
        self.passed = [
            net.copy(block(before, 0), block(before, 0), right),
            net.copy(block(after, 1), block(after, 1), left),
        ]

    def start(self):
        for copy in self.first + self.second:
            copy.start()

    def forward(self):
        for came, on in zip(self.first, self.passed):
            came.wait_recv()
            on.start()

    def near_done(self):
        for copy in self.second:
            copy.wait_recv()

    def far_done(self):
        for copy in self.passed:
            copy.wait_recv()

    def drain(self):
        for copy in self.first + self.second + self.passed:
            copy.wait_send()


class GroupGather:
    def __init__(self, net, place, block, own):
        core, chip = place.core, place.chip
        self.ring = RingGather(
            net,
            lambda position, half: block(position, core, half),
            chip,
            place.on_x(1),
            place.on_x(-1),
            own,
        )
        whole = [
            own(None),
            block(wrap(chip - 1), core, None),
            block(wrap(chip + 1), core, None),
            block(wrap(chip + 2), core, None),
        ]
        target = [block(chip, core, None)] + whole[1:]
        self.mates = [
            net.copy(source, there, place.mate()) for source, there in zip(whole, target)
        ]

    def start(self):
        self.ring.start()
        self.mates[0].start()

    def forward(self):
        self.ring.forward()

    def share(self):
        self.ring.near_done()
        self.mates[1].start()
        self.mates[2].start()

    def finish(self):
        self.ring.far_done()
        self.mates[3].start()
        for copy in self.mates:
            copy.wait_recv()
        self.ring.drain()
        for copy in self.mates:
            copy.wait_send()


def sweep(rows, step, body):
    def one(index, carry):
        body(pl.multiple_of(index * step, step))
        return carry

    lax.fori_loop(0, rows // step, one, 0)


class GroupScatter:
    def __init__(self, net, place, part, slices, shape, total, ring_in):
        self.part, self.slices, self.place = part, slices, place
        self.rows, self.cols = shape
        self.total, self.ring_in = total, ring_in
        chip = place.chip
        half = self.rows // 2
        self.half = half
        self.order = [wrap(chip + 2), wrap(chip + 1), wrap(chip - 1), chip]
        mate = place.mate()
        self.mates = []
        for index, there in enumerate(self.order):
            rows, cols = slices(there, 1 - place.core)
            self.mates.append(
                net.copy(
                    part.at[pl.ds(rows, self.rows), pl.ds(cols, self.cols)],
                    total.at[index],
                    mate,
                )
            )
        right, left = place.on_x(1), place.on_x(-1)
        top, low = pl.ds(0, half), pl.ds(half, half)
        self.sends = [
            net.copy(total.at[0, top], ring_in.at[0], right),
            net.copy(total.at[0, low], ring_in.at[1], left),
            net.copy(total.at[1, low], ring_in.at[2], right),
            net.copy(total.at[2, top], ring_in.at[3], left),
            net.copy(ring_in.at[0], ring_in.at[4], right),
            net.copy(ring_in.at[1], ring_in.at[5], left),
        ]

    def start(self):
        for copy in self.mates:
            copy.start()

    def mine(self, index, row, step):
        rows, cols = self.slices(self.order[index], self.place.core)
        return self.part[
            pl.ds(pl.multiple_of(rows + row, 16), step), pl.ds(cols, self.cols)
        ].astype(F32)

    def first(self, *indices):
        for index in indices:
            self.mates[index].wait_recv()

            def add(row, index=index):
                here = pl.ds(row, 16)
                self.total[index, here, :] = (
                    self.mine(index, row, 16) + self.total[index, here, :].astype(F32)
                ).astype(BF16)

            sweep(self.rows, 16, add)
            if index == 0:
                self.sends[0].start()
                self.sends[1].start()
            else:
                self.sends[index + 1].start()

    def second(self):
        for side in range(2):
            self.sends[side].wait_recv()

            def add(row, side=side):
                here = pl.ds(row, 16)
                there = pl.ds(pl.multiple_of(row + side * self.half, 16), 16)
                self.ring_in[side, here, :] = (
                    self.total[1 + side, there, :].astype(F32)
                    + self.ring_in[side, here, :].astype(F32)
                ).astype(BF16)

            sweep(self.half, 16, add)
            self.sends[4 + side].start()

    def arrive(self):
        self.mates[3].wait_recv()
        for index in range(2, 6):
            self.sends[index].wait_recv()

    def result(self, side, row):
        here = pl.ds(row, 16)
        there = pl.multiple_of(row + side * self.half, 16)
        one, two = ((4, 3), (2, 5))[side]
        return (
            self.mine(3, there, 16)
            + self.total[3, pl.ds(there, 16), :].astype(F32)
            + self.ring_in[one, here, :].astype(F32)
            + self.ring_in[two, here, :].astype(F32)
        )

    def drain(self):
        for copy in self.mates + self.sends:
            copy.wait_send()


def scatter_scratch(rows, cols):
    return [
        pltpu.VMEM((4, rows, cols), BF16),
        pltpu.VMEM((6, rows // 2, cols), BF16),
    ]


class RingScatter:
    def __init__(self, net, part, me, right, left, ring_in, target):
        before, after, across = wrap(me - 1), wrap(me + 1), wrap(me + 2)
        self.part, self.me, self.near = part, me, (after, before)
        self.ring_in, self.target = ring_in, target
        self.sends = [
            net.copy(part(across, 0), ring_in.at[0], right),
            net.copy(part(across, 1), ring_in.at[1], left),
            net.copy(part(after, 1), ring_in.at[2], right),
            net.copy(part(before, 0), ring_in.at[3], left),
            net.copy(ring_in.at[0], ring_in.at[4], right),
            net.copy(ring_in.at[1], ring_in.at[5], left),
        ]

    def start(self):
        for copy in self.sends[:4]:
            copy.start()

    def add(self, target, sources):
        shape = target.shape
        if len(shape) == 3:
            for index in range(shape[0]):
                self.add(target.at[index], [source.at[index] for source in sources])
            return

        def one(row):
            here = pl.ds(row, 16)
            total = sources[0][here, :].astype(F32)
            for source in sources[1:]:
                total = total + source[here, :].astype(F32)
            target[here, :] = total.astype(BF16)

        sweep(shape[0], 16, one)

    def middle(self):
        for side in range(2):
            self.sends[side].wait_recv()
            self.add(
                self.ring_in.at[side],
                [self.part(self.near[side], side), self.ring_in.at[side]],
            )
            self.sends[4 + side].start()

    def finish(self):
        for index in range(2, 6):
            self.sends[index].wait_recv()
        for side, (one, two) in enumerate(((4, 3), (2, 5))):
            self.add(
                self.target(side),
                [self.part(self.me, side), self.ring_in.at[one], self.ring_in.at[two]],
            )

    def drain(self):
        for copy in self.sends:
            copy.wait_send()


class WeightScatter:
    def __init__(self, net, near, place, at, size, final, buffers):
        row, z, y = place.row, place.z, place.y
        done, *rest = buffers
        half_rows = size // 2
        self.ones, self.twos = [], []
        for h in range(2):
            ring_one, mid, ring_two = rest[3 * h : 3 * h + 3]

            def along_z(pos, half, h=h):
                return at(h, pos, pl.ds(2 * half, 2), pl.ds(0, size))

            def along_y(pos, half, h=h):
                return at(h, pl.ds(2 * half, 2), pos, pl.ds(0, size))

            def inner(pos, half, mid=mid):
                return mid.at[pos, pl.ds(half * half_rows, half_rows), :]

            def mid_half(half, mid=mid):
                return mid.at[pl.ds(2 * half, 2)]

            def done_half(half, h=h):
                return done.at[h, pl.ds(half * half_rows, half_rows), :]

            over_z = (z, place.on_z(1), place.on_z(-1))
            over_y = (y, place.on_y(1), place.on_y(-1))
            outer, inside = ((along_z, over_z), over_y) if h == 0 else (
                (along_y, over_y), over_z
            )
            self.ones.append(RingScatter(net, outer[0], *outer[1], ring_one, mid_half))
            self.twos.append(RingScatter(net, inner, *inside, ring_two, done_half))
        self.swap = net.copy(done.at[1 - row], final.at[row], place.partner())
        self.keep = near.copy(done.at[row], final.at[row])

    def start(self):
        for ring in self.ones:
            ring.start()

    def middle(self):
        for ring in self.ones:
            ring.middle()

    def turn_over(self):
        for ring, then in zip(self.ones, self.twos):
            ring.finish()
            then.start()

    def middle_two(self):
        for ring in self.twos:
            ring.middle()

    def finish(self):
        for ring in self.twos:
            ring.finish()
        self.swap.start()
        self.keep.start()

    def close(self):
        self.swap.wait_recv()
        self.keep.wait()
        self.swap.wait_send()
        for ring in self.ones + self.twos:
            ring.drain()


def weight_scratch(size, cols):
    arrays = [pltpu.VMEM((2, size, cols), BF16)]
    for _ in range(2):
        arrays += [
            pltpu.VMEM((6, 2, size, cols), BF16),
            pltpu.VMEM((4, size, cols), BF16),
            pltpu.VMEM((6, size // 2, cols), BF16),
        ]
    return arrays


WEIGHT_SEMS = 2 * 12 + 1


def any_specs(count):
    return [pl.BlockSpec(memory_space=pl.ANY)] * count


def vmem_specs(count):
    return [pl.BlockSpec(memory_space=pltpu.VMEM)] * count


def sem_arrays(remote, near=0):
    arrays = [pltpu.SemaphoreType.DMA((remote,)), pltpu.SemaphoreType.DMA((remote,))]
    if near:
        arrays.append(pltpu.SemaphoreType.DMA((near,)))
    return arrays


def comm_params(identity, megabytes=60):
    return pltpu.CompilerParams(
        collective_id=identity, has_side_effects=True, vmem_limit_bytes=megabytes << 20
    )


def quarter_block(ref):
    def block(chip, core, half):
        rows = (lax.rem(chip, 2) * 2 + core) * 256
        cols = lax.div(chip, 2) * HALF
        if half is None:
            return ref.at[pl.ds(rows, 256), pl.ds(cols, HALF)]
        return ref.at[pl.ds(rows + 128 * half, 128), pl.ds(cols, HALF)]

    return block


def rows_of(chip, core):
    return (lax.rem(chip, 2) * 2 + core) * 256 + lax.div(chip, 2) * 128


def row_block(ref):
    def block(chip, core, half):
        rows = rows_of(chip, core)
        if half is None:
            return ref.at[pl.ds(rows, 128), :]
        return ref.at[pl.ds(rows + 64 * half, 64), :]

    return block


def row_slices(chip, core):
    return rows_of(chip, core), 0


def quarter_slices(chip, core):
    return (lax.rem(chip, 2) * 2 + core) * 256, lax.div(chip, 2) * HALF


def stacked(ref, size):
    def at(part, z, y, rows):
        return ref.at[part, z, y, rows, :]

    return at, size


def beside(ref, size):
    def at(part, z, y, rows):
        return ref.at[z, y, rows, pl.ds(part * HALF, HALF)]

    return at, size


def head_mask(values, head):
    lane = lax.broadcasted_iota(jnp.int32, values.shape, 1)
    return jnp.where(lax.div(lane, HEAD_DIM) == head, values, jnp.zeros_like(values))


def distances(length, start, keys):
    key = lax.broadcasted_iota(jnp.int32, (keys, BLOCK), 0)
    query = lax.broadcasted_iota(jnp.int32, (keys, BLOCK), 1) + start
    return jnp.where(key < length, jnp.abs(query - key).astype(F32), FAR)


def slope_of(head):
    base = lax.axis_index("col") * 8 + lax.axis_index("row") * 4
    number = (base + head + 1).astype(F32)
    return jnp.exp2(jnp.full((1, BLOCK), -8.0 / HEADS, F32) * number)


def nt(left, right):
    return lax.dot_general(left, right, (((1,), (1,)), ((), ())), preferred_element_type=F32)


def nn(left, right):
    return jnp.dot(left, right, preferred_element_type=F32)


def attend_back_block(block, length, q, k, v, grad, logs, kt, dk, dv, dqt):
    start, keys = block * BLOCK, (block + 1) * BLOCK
    here = pl.ds(start, BLOCK)
    apart = distances(length, start, keys)

    def one(head, carry):
        scores = nt(head_mask(k[0:keys, :], head), q[here, :])
        prob = jnp.exp(scores - slope_of(head) * apart - logs[head, :, here])
        dprob = nt(head_mask(v[0:keys, :], head), grad[here, :])
        delta = jnp.sum(prob * dprob, 0, keepdims=True)
        dscore = (prob * (dprob - delta)).astype(BF16)
        dv[0:keys, :] += nn(prob.astype(BF16), head_mask(grad[here, :], head))
        dk[0:keys, :] += nn(dscore, head_mask(q[here, :], head))
        lines = pl.ds(pl.multiple_of(head * HEAD_DIM, HEAD_DIM), HEAD_DIM)
        dqt[lines, here] = nn(kt[lines, 0:keys], dscore).astype(BF16)
        return carry

    lax.fori_loop(0, 4, one, 0)


def normalize(values):
    mean = jnp.mean(values, 1, keepdims=True)
    centered = values - mean
    scale = lax.rsqrt(jnp.mean(centered * centered, 1, keepdims=True) + EPSILON)
    return centered * scale, scale


def x_devices(place):
    return [place.on_x(1), place.on_x(-1), place.mate()]


def spread(small, line, base, per, first, width):
    entry = lax.broadcasted_iota(jnp.int32, (256, width), 1)
    piece = lax.broadcasted_iota(jnp.int32, (256, width), 0)
    wanted = (lax.div(entry, per) + first) * 16 + line
    chosen = jnp.where(piece == wanted, 1.0, 0.0).astype(BF16)
    spread_out = lax.dot_general(
        small, chosen, (((0,), (0,)), ((), ())), preferred_element_type=F32
    )
    lane = lax.broadcasted_iota(jnp.int32, (128, width), 0)
    entry = lax.broadcasted_iota(jnp.int32, (128, width), 1)
    return jnp.sum(
        jnp.where(lane == base + lax.rem(entry, per), spread_out, 0.0), 0, keepdims=True
    )


def attend_block(block, length, q, k, vt, out_t, logs):
    start, keys = block * BLOCK, (block + 1) * BLOCK
    here = pl.ds(start, BLOCK)
    apart = distances(length, start, keys)

    def one(head, carry):
        scores = nt(head_mask(k[0:keys, :], head), q[here, :])
        scores = scores - slope_of(head) * apart
        peak = jnp.max(scores, 0, keepdims=True)
        exponent = jnp.exp(scores - peak)
        total = jnp.sum(exponent, 0, keepdims=True)
        lines = pl.ds(pl.multiple_of(head * HEAD_DIM, HEAD_DIM), HEAD_DIM)
        out_t[lines, here] = nn(vt[lines, 0:keys], exponent.astype(BF16)) / total
        logs[head, :, here] = peak + jnp.log(total)
        return carry

    lax.fori_loop(0, 4, one, 0)


def forward_kernel(
    length, x, cot, qkv, dense, fc1, fc2, small, norms,
    gcot, gqkv, gdense, gfc1, gfc2, rows_one, rows_two, heads, logs, residual, stats,
    vectors, grad_act,
    vx, vcot, vqkv, vdense, vfc2, vsmall, vnorm, n1, vheads, vt, out_t, part, own, tile,
    vlogs, total, ring_in, send, recv, near_sems,
):
    place = Place()
    net, near = Net(send, recv), Near(near_sems)
    row, z, y = place.row, place.z, place.y
    partner = place.partner()
    greet(
        [partner, place.on_x(1), place.on_x(-1), place.mate()]
        + [place.on_y(1), place.on_y(-1), place.on_z(1), place.on_z(-1)]
    )
    weights = [
        (stacked(vqkv, 64), qkv.at[row], qkv.at[1 - row]),
        (stacked(vsmall, 16), small, small),
        (beside(vdense, 32), dense, dense),
        (stacked(gfc1, 64), fc1.at[row], fc1.at[1 - row]),
        (beside(vfc2, 64), fc2.at[row], fc2.at[1 - row]),
    ]
    swaps, copies = [], []
    for (at, size), own_cut, other in weights:
        there = at(row, z, y, pl.ds(0, size))
        swaps.append(net.copy(other, there, partner))
        copies.append(near.copy(own_cut, there))
    swap_norms = net.copy(norms, vnorm.at[row], partner)
    groups = []
    for source, target in ((x, vx), (cot, vcot)):
        block = quarter_block(target)

        def own_part(half, source=source):
            if half is None:
                return source
            return source.at[pl.ds(128 * half, 128), :]

        groups.append(GroupGather(net, place, block, own_part))
        copies.append(near.copy(source, block(place.chip, place.core, None)))
    copies.append(near.copy(norms, vnorm.at[row]))
    ones, twos = [], []
    for (at, size), own_cut, other in weights:
        half_rows = size // 2
        rows = pl.ds(0, size)

        def along_y(position, half, at=at, half_rows=half_rows):
            return at(row, z, position, pl.ds(half * half_rows, half_rows))

        def along_z(position, half, at=at, half_rows=half_rows):
            return at(1 - row, position, y, pl.ds(half * half_rows, half_rows))

        def mine(half, own_cut=own_cut, half_rows=half_rows):
            return own_cut.at[pl.ds(half * half_rows, half_rows), :]

        def planes_z(position, half, at=at, rows=rows):
            return at(row, position, pl.ds(2 * half, 2), rows)

        def planes_y(position, half, at=at, rows=rows):
            return at(1 - row, pl.ds(2 * half, 2), position, rows)

        over_y = (y, place.on_y(1), place.on_y(-1))
        over_z = (z, place.on_z(1), place.on_z(-1))
        ones.append(
            (RingGather(net, along_y, *over_y, mine), RingGather(net, along_z, *over_z))
        )
        twos.append((RingGather(net, planes_z, *over_z), RingGather(net, planes_y, *over_y)))

    def begin(index):
        ones[index][0].start()
        swaps[index].wait_recv()
        ones[index][1].start()

    def pass_one(index):
        for ring in ones[index]:
            ring.forward()

    def turn_over(index):
        for ring, then in zip(ones[index], twos[index]):
            ring.near_done()
            ring.far_done()
            then.start()

    def pass_two(index):
        for ring in twos[index]:
            ring.forward()

    def complete(index):
        for ring in twos[index]:
            ring.near_done()
            ring.far_done()

    group_x, group_cot = groups
    swaps[0].start()
    ones[0][0].start()
    swap_norms.start()
    swaps[1].start()
    group_x.start()
    for copy in copies:
        copy.start()
    for swap in swaps[2:]:
        swap.start()
    swaps[0].wait_recv()
    ones[0][1].start()
    begin(1)
    for copy in copies:
        copy.wait()
    pass_one(0)
    group_x.forward()
    turn_over(0)
    pass_one(1)
    begin(2)
    begin(3)
    begin(4)
    turn_over(1)
    group_x.share()
    pass_two(0)
    pass_two(1)
    for index in (2, 3, 4):
        pass_one(index)
    group_x.finish()
    group_cot.start()
    turn_over(2)
    turn_over(3)
    swap_norms.wait_recv()

    def first_norm(pos):
        here = pl.ds(pos, 16)
        left, right = vx[here, 0:HALF].astype(F32), vx[here, HALF:WIDTH].astype(F32)
        mean = (
            jnp.sum(left, 1, keepdims=True) + jnp.sum(right, 1, keepdims=True)
        ) / WIDTH
        left, right = left - mean, right - mean
        scale = lax.rsqrt(
            (
                jnp.sum(left * left, 1, keepdims=True)
                + jnp.sum(right * right, 1, keepdims=True)
            )
            / WIDTH
            + EPSILON
        )
        lane = lax.broadcasted_iota(jnp.int32, (16, 128), 1)
        vlogs[here, :] = jnp.where(lane == 0, mean, scale)
        n1[here, 0:HALF] = (left * scale * vnorm[0, 0:1, :] + vnorm[0, 1:2, :]).astype(BF16)
        n1[here, HALF:WIDTH] = (
            right * scale * vnorm[1, 0:1, :] + vnorm[1, 1:2, :]
        ).astype(BF16)

    sweep(SEQ, 16, first_norm)
    turn_over(4)
    keep_n1 = near.copy(n1, rows_one)
    keep_n1.start()
    complete(1)
    smalls = [vsmall[index].reshape(256, 128) for index in range(2)]
    query_add = spread(smalls[0], 1, 0, 32, 8 * row, LOCAL)
    value_add = spread(smalls[0], 1, 32, 32, 8 * row, LOCAL)
    for side in range(2):
        half = pl.ds(side * HALF, HALF)
        vectors[0:1, half] = spread(smalls[side], 1, 64, 64, 0, HALF)
        vectors[1:2, half] = spread(smalls[side], 2, 0, 64, 0, HALF)
        vectors[3:4, half] = vnorm[side, 2:3, :]
        vectors[4:5, half] = vnorm[side, 3:4, :]
    complete(0)
    keep_qkv = near.copy(vqkv, gqkv)
    keep_qkv.start()

    def project(index, carry):
        here = pl.ds(pl.multiple_of(index * 256, 256), 256)
        for third, add in enumerate((query_add, None, value_add)):
            cols = slice(third * 256, (third + 1) * 256)
            made = nn(n1[here, :], vqkv[:, :, :, :, cols].reshape(WIDTH, 256))
            if add is not None:
                made = made + add
            made = made.astype(BF16)
            if third == 0:
                made = made * BF16(HEAD_DIM**-0.5)
            vheads[third, here, :] = made
        return carry

    lax.fori_loop(0, 4, project, 0)
    group_cot.forward()
    vt[...] = vheads[2].T
    args = (length[0], vheads.at[0], vheads.at[1], vt, out_t, logs)
    attend_block(0, *args)
    attend_block(1, *args)
    pass_two(2)
    group_cot.share()
    attend_block(2, *args)
    pass_two(3)
    attend_block(3, *args)
    vheads[3] = out_t[...].T.astype(BF16)
    complete(2)
    keep_heads = near.copy(vheads, heads)
    keep_heads.start()
    keep_dense = near.copy(vdense, gdense)
    keep_dense.start()

    scatter = GroupScatter(
        net, place, part, row_slices, (128, WIDTH), total, ring_in
    )
    weight = vdense[pl.ds(2 * row, 2)].reshape(LOCAL, WIDTH)
    for index, chip in enumerate(scatter.order):
        starts = [pl.multiple_of(rows_of(chip, core), 128) for core in range(2)]
        both = jnp.concatenate([vheads[3, pl.ds(start, 128), :] for start in starts], 0)
        made = nn(both, weight).astype(BF16)
        part[pl.ds(starts[0], 128), :] = made[0:128]
        part[pl.ds(starts[1], 128), :] = made[128:256]
        scatter.mates[index].start()
    scatter.first(0, 1, 2)
    group_cot.finish()
    keep_cot = near.copy(vcot, gcot)
    keep_cot.start()
    pass_two(4)
    complete(3)
    vectors[2:3, 0:HALF] = jnp.where(
        row == 0,
        spread(smalls[0], 0, 0, 64, 0, HALF),
        spread(smalls[0], 0, 64, 64, 0, HALF),
    )
    scatter.second()
    scatter.arrive()
    group_two = GroupGather(
        net,
        place,
        row_block(rows_two),
        lambda half: own if half is None else own.at[pl.ds(64 * half, 64), :],
    )
    keep_own = near.copy(own, row_block(rows_two)(place.chip, place.core, None))
    first_row = rows_of(place.chip, place.core)
    for side in range(2):

        def one(pos, side=side):
            here = pl.ds(pl.multiple_of(pos + 64 * side, 16), 16)
            there = pl.ds(pl.multiple_of(first_row + pos + 64 * side, 16), 16)
            values = (
                vx[there, :].astype(F32) + scatter.result(side, pos) + vectors[0:1, :]
            )
            residual[here, :] = values
            own[here, :] = (
                normalize(values)[0] * vectors[3:4, :] + vectors[4:5, :]
            ).astype(BF16)

        sweep(64, 16, one)
    group_two.start()
    keep_own.start()
    stats[...] = vlogs[pl.ds(pl.multiple_of(place.col * 256, 256), 256), :]
    complete(4)
    keep_fc2 = near.copy(vfc2, gfc2)
    keep_fc2.start()
    keeps = []
    for index in range(4):
        here = pl.ds(index * 256, 256)
        for piece in range(4):
            lines = vfc2[piece].reshape(256, WIDTH)
            tile[index, :, pl.ds(piece * 256, 256)] = nt(vcot[here, :], lines)
        keep = near.copy(tile.at[index], grad_act.at[here, :])
        keep.start()
        keeps.append(keep)
        if index == 1:
            group_two.forward()
        if index == 3:
            group_two.share()
    group_two.finish()
    keeps += [keep_n1, keep_qkv, keep_heads, keep_dense, keep_cot, keep_own, keep_fc2]
    for keep in keeps:
        keep.wait()
    swap_norms.wait_send()
    for swap in swaps:
        swap.wait_send()
    for pair in ones + twos:
        for ring in pair:
            ring.drain()
    scatter.drain()


def forward(length, x, cot, qkv, dense, fc1, fc2, small, norms):
    remote = 6 + 3 * 10 + 10 + 5 * 4 * 6
    bf, full = (lambda *shape: jax.ShapeDtypeStruct(shape, BF16)), (
        lambda *shape: jax.ShapeDtypeStruct(shape, F32)
    )
    return pl.pallas_call(
        forward_kernel,
        out_shape=(
            bf(SEQ, WIDTH),
            bf(2, 4, 4, 64, 768),
            bf(4, 4, 32, 2048),
            bf(2, 4, 4, 64, 1024),
            bf(4, 4, 64, 2048),
            bf(SEQ, WIDTH),
            bf(SEQ, WIDTH),
            bf(4, SEQ, LOCAL),
            full(4, 1, SEQ),
            full(128, WIDTH),
            full(256, 128),
            full(8, WIDTH),
            full(SEQ, 1024),
        ),
        in_specs=[pl.BlockSpec(memory_space=pltpu.SMEM)] + any_specs(8),
        out_specs=tuple(any_specs(8) + vmem_specs(4) + any_specs(1)),
        scratch_shapes=[
            pltpu.VMEM((SEQ, WIDTH), BF16),
            pltpu.VMEM((SEQ, WIDTH), BF16),
            pltpu.VMEM((2, 4, 4, 64, 768), BF16),
            pltpu.VMEM((4, 4, 32, 2048), BF16),
            pltpu.VMEM((4, 4, 64, 2048), BF16),
            pltpu.VMEM((2, 4, 4, 16, 128), BF16),
            pltpu.VMEM((2, 8, HALF), F32),
            pltpu.VMEM((SEQ, WIDTH), BF16),
            pltpu.VMEM((4, SEQ, LOCAL), BF16),
            pltpu.VMEM((LOCAL, SEQ), BF16),
            pltpu.VMEM((LOCAL, SEQ), F32),
            pltpu.VMEM((SEQ, WIDTH), BF16),
            pltpu.VMEM((128, WIDTH), BF16),
            pltpu.VMEM((4, 256, 1024), F32),
            pltpu.VMEM((SEQ, 128), F32),
        ]
        + scatter_scratch(128, WIDTH)
        + sem_arrays(remote, 20),
        compiler_params=comm_params(0),
        name="forward",
    )(length, x, cot, qkv, dense, fc1, fc2, small, norms)


def tn(left, right):
    return lax.dot_general(left, right, (((0,), (0,)), ((), ())), preferred_element_type=F32)


def turn_kernel(
    rows_two, fc1, fc2, cot, grad_act, residual, vectors,
    gathered, part_out, grad_fc1, red_fc2, sums,
    n2, w1, w2, vcot, gact, act, gh, part, own, pout, g1, g2, total, ring_in, *rest,
):
    *buffers, send, recv, near_sems = rest
    place = Place()
    net, near = Net(send, recv), Near(near_sems)
    load_n2, load_w1 = near.copy(rows_two, n2), near.copy(fc1, w1)
    load_n2.start()
    load_w1.start()
    scatter = GroupScatter(
        net, place, part, row_slices, (128, WIDTH), total, ring_in
    )
    tiles = [
        [pl.multiple_of(rows_of(chip, core), 128) for core in range(2)]
        for chip in scatter.order
    ]
    load_act = []
    for index, starts in enumerate(tiles):
        load_act.append(
            [
                near.copy(
                    grad_act.at[pl.ds(start, 128), :],
                    gact.at[index % 2, pl.ds(128 * core, 128), :],
                )
                for core, start in enumerate(starts)
            ]
        )
    for index in range(2):
        for copy in load_act[index]:
            copy.start()
    load_w2, load_cot = near.copy(fc2, w2), near.copy(cot, vcot)
    load_w2.start()
    load_cot.start()
    greet(
        x_devices(place)
        + [place.partner()]
        + [place.on_y(1), place.on_y(-1), place.on_z(1), place.on_z(-1)]
    )
    sums[...] = jnp.zeros_like(sums)
    load_n2.wait()
    load_w1.wait()
    for index, starts in enumerate(tiles):
        for copy in load_act[index]:
            copy.wait()
        rows = [pl.ds(start, 128) for start in starts]
        both = jnp.concatenate([n2[here, :] for here in rows], 0)
        for piece in range(4):
            cols = slice(piece * 256, (piece + 1) * 256)
            hidden = (
                nn(both, w1[:, :, :, :, cols].reshape(WIDTH, 256)) + vectors[2:3, cols]
            )
            below = 0.5 + 0.5 * lax.erf(hidden * 0.5**0.5)
            density = jnp.exp(-0.5 * hidden * hidden) * 0.3989422804014327
            made = (hidden * below).astype(BF16)
            back = (
                gact[index % 2, :, cols] * (below + hidden * density)
            ).astype(BF16)
            for core, here in enumerate(rows):
                act[here, cols] = made[128 * core : 128 * core + 128]
                gh[here, cols] = back[128 * core : 128 * core + 128]
            sums[3:4, cols] += jnp.sum(back.astype(F32), 0, keepdims=True)
        if index < 2:
            for copy in load_act[index + 2]:
                copy.start()
        back = jnp.concatenate([gh[here, :] for here in rows], 0)
        for side in range(2):
            for piece in range(4):
                cols = slice(side * HALF + piece * 256, side * HALF + piece * 256 + 256)
                made = nt(back, w1[side, piece].reshape(256, 1024)).astype(BF16)
                for core, here in enumerate(rows):
                    part[here, cols] = made[128 * core : 128 * core + 128]
        scatter.mates[index].start()
        if index > 0:
            scatter.first(index - 1)
    load_w2.wait()
    load_cot.wait()

    def one_g2(index, carry):
        cols = pl.ds(pl.multiple_of(index * 256, 256), 256)
        for side in range(2):
            half = slice(side * HALF, (side + 1) * HALF)
            made = tn(act[:, cols], vcot[:, half]).astype(BF16)
            g2[index, :, :, half] = made.reshape(4, 64, HALF)
        return carry

    lax.fori_loop(0, 2, one_g2, 0)
    scatter.second()
    lax.fori_loop(2, 4, one_g2, 0)
    over = WeightScatter(net, near, place, beside(g2, 64)[0], 64, red_fc2, buffers)
    over.start()

    def one_out(index, carry):
        here = pl.ds(pl.multiple_of(index * 256, 256), 256)
        for side in range(2):
            half = slice(side * HALF, (side + 1) * HALF)
            made = nn(act[here, :], w2[:, :, :, half].reshape(1024, HALF))
            pout[here, half] = made.astype(BF16)
        return carry

    lax.fori_loop(0, 3, one_out, 0)
    over.middle()
    scatter.arrive()
    group = GroupGather(
        net,
        place,
        row_block(gathered),
        lambda half: own if half is None else own.at[pl.ds(64 * half, 64), :],
    )
    first_row = rows_of(place.chip, place.core)
    for side in range(2):

        def one(pos, side=side):
            here = pl.ds(pl.multiple_of(pos + 64 * side, 16), 16)
            there = pl.ds(pl.multiple_of(first_row + pos + 64 * side, 16), 16)
            arrived = scatter.result(side, pos)
            xhat, scale = normalize(residual[here, :])
            scaled = arrived * vectors[3:4, :]
            flat = jnp.mean(scaled, 1, keepdims=True)
            cross = jnp.mean(scaled * xhat, 1, keepdims=True)
            own[here, :] = (
                vcot[there, :].astype(F32) + scale * (scaled - flat - xhat * cross)
            ).astype(BF16)
            sums[0:1, :] += jnp.sum(arrived * xhat, 0, keepdims=True)
            sums[1:2, :] += jnp.sum(arrived, 0, keepdims=True)

        sweep(64, 16, one)
    group.start()
    keep_own = near.copy(own, row_block(gathered)(place.chip, place.core, None))
    keep_own.start()
    over.turn_over()
    lax.fori_loop(3, 4, one_out, 0)
    keep_out = near.copy(pout, part_out)
    keep_out.start()

    def one_g1(index, carry):
        side, piece = lax.div(index, 4), lax.rem(index, 4)
        cols = pl.ds(pl.multiple_of(index * 256, 256), 256)
        g1[side, piece] = tn(n2[:, cols], gh[...]).astype(BF16).reshape(4, 64, 1024)
        return carry

    lax.fori_loop(0, 4, one_g1, 0)
    group.forward()
    lax.fori_loop(4, 8, one_g1, 0)
    keep_g1 = near.copy(g1, grad_fc1)
    keep_g1.start()
    over.middle_two()
    group.share()

    def add_cot(pos):
        here = pl.ds(pos, 16)
        sums[2:3, :] += jnp.sum(vcot[here, :].astype(F32), 0, keepdims=True)

    sweep(SEQ, 16, add_cot)
    group.finish()
    over.finish()
    for keep in (keep_own, keep_out, keep_g1):
        keep.wait()
    over.close()
    scatter.drain()


def turn(rows_two, fc1, fc2, cot, grad_act, residual, vectors):
    bf = lambda *shape: jax.ShapeDtypeStruct(shape, BF16)
    return pl.pallas_call(
        turn_kernel,
        out_shape=(
            bf(SEQ, WIDTH),
            bf(SEQ, WIDTH),
            bf(2, 4, 4, 64, 1024),
            bf(2, 64, 1024),
            jax.ShapeDtypeStruct((8, WIDTH), F32),
        ),
        in_specs=any_specs(5) + vmem_specs(2),
        out_specs=tuple(any_specs(3) + vmem_specs(2)),
        scratch_shapes=[
            pltpu.VMEM((SEQ, WIDTH), BF16),
            pltpu.VMEM((2, 4, 4, 64, 1024), BF16),
            pltpu.VMEM((4, 4, 64, 2048), BF16),
            pltpu.VMEM((SEQ, WIDTH), BF16),
            pltpu.VMEM((2, 256, 1024), F32),
            pltpu.VMEM((SEQ, 1024), BF16),
            pltpu.VMEM((SEQ, 1024), BF16),
            pltpu.VMEM((SEQ, WIDTH), BF16),
            pltpu.VMEM((128, WIDTH), BF16),
            pltpu.VMEM((SEQ, WIDTH), BF16),
            pltpu.VMEM((2, 4, 4, 64, 1024), BF16),
            pltpu.VMEM((4, 4, 64, 2048), BF16),
        ]
        + scatter_scratch(128, WIDTH)
        + weight_scratch(64, 1024)
        + sem_arrays(20 + WEIGHT_SEMS, 20),
        compiler_params=comm_params(2),
        name="turn",
    )(rows_two, fc1, fc2, cot, grad_act, residual, vectors)


def last_kernel(
    length, x, stats, branch, dense, qkv, heads, logs, rows_one, part_out, grad_fc1,
    gain, residual, vectors, sums_two,
    ingrad, out, rqkv, rdense, rfc1, vector,
    rows, wd, wq, vheads, datt, kt, dk, dv, dqt, gproj, part, pout, g1, gd, gq,
    own_branch, result, stats_out, stats_in, group_in, y_in, z_in, vec_a, vec_b,
    total, ring_in, total_out, ring_out, *rest,
):
    *buffers, send, recv, near_sems = rest
    place = Place()
    row, z, y = place.row, place.z, place.y
    net, near = Net(send, recv), Near(near_sems)
    load_rows = near.copy(branch, rows)
    load_wd = near.copy(dense.at[pl.ds(2 * row, 2)], wd)
    load_heads = near.copy(heads, vheads)
    load_g1 = near.copy(grad_fc1, g1)
    load_out = near.copy(part_out, pout)
    load_wq = near.copy(qkv, wq)
    quarter = quarter_slices(place.chip, place.core)
    load_own = near.copy(branch.at[pl.ds(quarter[0], 256), pl.ds(quarter[1], HALF)], own_branch)
    for load in (load_rows, load_wd, load_heads, load_g1, load_out, load_wq, load_own):
        load.start()
    x_group = [
        place.x_at(wrap(place.chip + step), core)
        for step in range(4)
        for core in (place.core, 1 - place.core)
    ][1:]
    y_ring = [place.on_y(step) for step in (1, 2, 3)]
    z_ring = [place.on_z(step) for step in (1, 2, 3)]
    greet(x_group + y_ring + z_ring)
    scatter = GroupScatter(net, place, part, quarter_slices, (256, HALF), total, ring_in)
    scatter_out = GroupScatter(
        net, place, pout, row_slices, (128, WIDTH), total_out, ring_out
    )
    over_fc1 = WeightScatter(
        net, near, place, stacked(g1, 64)[0], 64, rfc1, buffers[0:7]
    )
    over_dense = WeightScatter(
        net, near, place, beside(gd, 32)[0], 32, rdense, buffers[7:14]
    )
    over_qkv = WeightScatter(
        net, near, place, stacked(gq, 64)[0], 64, rqkv, buffers[14:21]
    )
    load_rows.wait()
    load_wd.wait()
    load_g1.wait()
    over_fc1.start()

    def back_attended(index, carry):
        here = pl.ds(pl.multiple_of(index * 256, 256), 256)
        datt[here, :] = nt(rows[here, :], wd[...].reshape(LOCAL, WIDTH)).astype(BF16)
        return carry

    lax.fori_loop(0, 4, back_attended, 0)
    load_out.wait()
    scatter_out.start()
    load_heads.wait()
    for side in range(2):
        half = slice(side * HALF, (side + 1) * HALF)
        made = tn(vheads[3], rows[:, half]).astype(BF16).reshape(2, 4, 32, HALF)
        gd[pl.ds(2 * row, 2), :, :, half] = made
        gd[pl.ds(2 - 2 * row, 2), :, :, half] = jnp.zeros_like(made)
    over_dense.start()
    vec_a[...] = jnp.zeros_like(vec_a)
    vec_a[2:4, :] = sums_two[0:2, :]
    vec_a[5:6, :] = sums_two[2:3, :]
    vec_a[6:7, 0:HALF] = sums_two[3:4, 0:HALF]

    def add_branch(pos):
        here = pl.ds(pos, 16)
        vec_a[4:5, :] += jnp.sum(rows[here, :].astype(F32), 0, keepdims=True)

    sweep(SEQ, 16, add_branch)
    load_own.wait()
    load_one = near.copy(rows_one, rows)
    load_one.start()
    kt[...] = vheads[1].T
    dk[...] = jnp.zeros_like(dk)
    dv[...] = jnp.zeros_like(dv)
    args = (length[0], vheads.at[0], vheads.at[1], vheads.at[2], datt, logs, kt, dk, dv, dqt)
    attend_back_block(0, *args)
    scatter_out.first(0, 1, 2)
    attend_back_block(1, *args)
    over_fc1.middle()
    attend_back_block(2, *args)
    scatter_out.second()
    over_dense.middle()
    attend_back_block(3, *args)
    gproj[:, 0:256] = dqt[...].T * BF16(HEAD_DIM**-0.5)
    gproj[:, 256:512] = dk[...].astype(BF16)
    gproj[:, 512:768] = dv[...].astype(BF16)
    load_wq.wait()
    for index, chip in enumerate(scatter.order):
        here = pl.ds(pl.multiple_of(lax.rem(chip, 2) * 512, 512), 512)
        cols = pl.ds(pl.multiple_of(lax.div(chip, 2) * HALF, HALF), HALF)
        weight = wq[lax.div(chip, 2)].reshape(HALF, 768)
        part[here, cols] = nt(gproj[here, :], weight).astype(BF16)
        scatter.mates[index].start()
        if index > 0:
            scatter.first(index - 1)
    load_one.wait()

    def one_gq(index, carry):
        side, piece = lax.div(index, 4), lax.rem(index, 4)
        cols = pl.ds(pl.multiple_of(index * 256, 256), 256)
        gq[side, piece] = tn(rows[:, cols], gproj[...]).astype(BF16).reshape(4, 64, 768)
        return carry

    lax.fori_loop(0, 4, one_gq, 0)
    scatter.second()
    lax.fori_loop(4, 8, one_gq, 0)
    over_qkv.start()
    over_fc1.turn_over()
    over_dense.turn_over()
    for third, lane in ((0, 1024), (2, 1280)):
        cols = slice(third * 256, third * 256 + 256)
        vec_a[6:7, lane : lane + 256] = jnp.sum(
            gproj[:, cols].astype(F32), 0, keepdims=True
        )
    scatter.arrive()
    over_qkv.middle()

    lane = lax.broadcasted_iota(jnp.int32, (16, 128), 1)
    cols = pl.ds(pl.multiple_of(row * HALF, HALF), HALF)
    for side in range(2):

        def sums(pos, side=side):
            here = pl.ds(pl.multiple_of(pos + 128 * side, 16), 16)
            arrived = scatter.result(side, pos)
            scaled = arrived * gain[...]
            xhat = (x[here, :].astype(F32) - stats[here, 0:1]) * stats[here, 1:2]
            flat = jnp.sum(scaled, 1, keepdims=True)
            cross = jnp.sum(scaled * xhat, 1, keepdims=True)
            stats_out[here, :] = jnp.where(lane == 0, flat, cross)
            ingrad[here, :] = arrived
            vec_a[0:1, cols] += jnp.sum(arrived * xhat, 0, keepdims=True)
            vec_a[1:2, cols] += jnp.sum(arrived, 0, keepdims=True)

        sweep(128, 16, sums)
    swap_stats = net.copy(stats_out, stats_in, place.partner())
    swap_stats.start()
    group_sends = [
        net.copy(vec_a, group_in.at[index], device)
        for index, device in enumerate(x_group)
    ]
    for copy in group_sends:
        copy.start()
    over_fc1.middle_two()
    over_dense.middle_two()
    over_qkv.turn_over()
    scatter_out.arrive()
    for side in range(2):

        def finish(pos, side=side):
            here = pl.ds(pl.multiple_of(pos + 64 * side, 16), 16)
            result[here, :] = (
                residual[here, :] + scatter_out.result(side, pos) + vectors[1:2, :]
            ).astype(BF16)

        sweep(64, 16, finish)
    there = pl.ds(row * 128, 128)
    out_swap = net.copy(
        result.at[:, pl.ds((1 - row) * HALF, HALF)], out.at[there, :], place.partner()
    )
    out_keep = near.copy(result.at[:, pl.ds(row * HALF, HALF)], out.at[there, :])
    out_swap.start()
    out_keep.start()
    swap_stats.wait_recv()

    def apply(pos):
        here = pl.ds(pos, 16)
        both = (stats_out[here, :] + stats_in[here, :]) / WIDTH
        xhat = (x[here, :].astype(F32) - stats[here, 0:1]) * stats[here, 1:2]
        ingrad[here, :] = own_branch[here, :].astype(F32) + stats[here, 1:2] * (
            ingrad[here, :] * gain[...] - both[:, 0:1] - xhat * both[:, 1:2]
        )

    sweep(256, 16, apply)
    for copy in group_sends:
        copy.wait_recv()
    vec_b[...] = vec_a[...]
    for index in range(7):
        vec_b[0:4, :] += group_in[index, 0:4, :]
    vec_b[7:8, :] = group_in[3, 6:7, :]
    y_sends = [net.copy(vec_b, y_in.at[i], device) for i, device in enumerate(y_ring)]
    for copy in y_sends:
        copy.start()
    over_fc1.finish()
    over_dense.finish()
    over_qkv.middle_two()
    for copy in y_sends:
        copy.wait_recv()
    for copy in group_sends:
        copy.wait_send()
    vec_a[...] = vec_b[...]
    for index in range(3):
        vec_a[...] += y_in[index]
    z_sends = [net.copy(vec_a, z_in.at[i], device) for i, device in enumerate(z_ring)]
    for copy in z_sends:
        copy.start()
    over_qkv.finish()
    for copy in z_sends:
        copy.wait_recv()
    vector[...] = vec_a[...]
    for index in range(3):
        vector[...] += z_in[index]
    out_swap.wait_recv()
    for over in (over_fc1, over_dense, over_qkv):
        over.close()
    out_keep.wait()
    out_swap.wait_send()
    swap_stats.wait_send()
    for copy in y_sends + z_sends:
        copy.wait_send()
    scatter.drain()
    scatter_out.drain()


def last(*args):
    bf = lambda *shape: jax.ShapeDtypeStruct(shape, BF16)
    full = lambda *shape: jax.ShapeDtypeStruct(shape, F32)
    anywhere, inside = any_specs(1)[0], vmem_specs(1)[0]
    where = (
        [pl.BlockSpec(memory_space=pltpu.SMEM), inside, inside]
        + [anywhere] * 4
        + [inside]
        + [anywhere] * 3
        + [inside] * 4
    )
    return pl.pallas_call(
        last_kernel,
        out_shape=(
            full(256, HALF),
            bf(256, HALF),
            bf(2, 64, 768),
            bf(2, 32, 1024),
            bf(2, 64, 1024),
            full(8, WIDTH),
        ),
        in_specs=where,
        out_specs=tuple(vmem_specs(6)),
        scratch_shapes=[
            pltpu.VMEM((SEQ, WIDTH), BF16),
            pltpu.VMEM((2, 4, 32, WIDTH), BF16),
            pltpu.VMEM((2, 4, 4, 64, 768), BF16),
            pltpu.VMEM((4, SEQ, LOCAL), BF16),
            pltpu.VMEM((SEQ, LOCAL), BF16),
            pltpu.VMEM((LOCAL, SEQ), BF16),
            pltpu.VMEM((SEQ, LOCAL), F32),
            pltpu.VMEM((SEQ, LOCAL), F32),
            pltpu.VMEM((LOCAL, SEQ), BF16),
            pltpu.VMEM((SEQ, 768), BF16),
            pltpu.VMEM((SEQ, WIDTH), BF16),
            pltpu.VMEM((SEQ, WIDTH), BF16),
            pltpu.VMEM((2, 4, 4, 64, 1024), BF16),
            pltpu.VMEM((4, 4, 32, 2048), BF16),
            pltpu.VMEM((2, 4, 4, 64, 768), BF16),
            pltpu.VMEM((256, HALF), BF16),
            pltpu.VMEM((128, WIDTH), BF16),
            pltpu.VMEM((256, 128), F32),
            pltpu.VMEM((256, 128), F32),
            pltpu.VMEM((7, 8, WIDTH), F32),
            pltpu.VMEM((3, 8, WIDTH), F32),
            pltpu.VMEM((3, 8, WIDTH), F32),
            pltpu.VMEM((8, WIDTH), F32),
            pltpu.VMEM((8, WIDTH), F32),
        ]
        + scatter_scratch(256, HALF)
        + scatter_scratch(128, WIDTH)
        + weight_scratch(64, 1024)
        + weight_scratch(32, 1024)
        + weight_scratch(64, 768)
        + sem_arrays(20 + 3 * WEIGHT_SEMS + 15, 20),
        compiler_params=comm_params(3, 62),
        name="last",
    )(*args)


def local(
    inputs,
    cotangent,
    lengths,
    attention_norm_gain,
    attention_norm_bias,
    qkv_weight,
    query_bias,
    value_bias,
    dense_weight,
    dense_bias,
    feedforward_norm_gain,
    feedforward_norm_bias,
    fc1_weight,
    fc1_bias,
    fc2_weight,
    fc2_bias,
):
    row = lax.axis_index("row")
    col = lax.axis_index("col")
    dp = lax.axis_index("dp")

    qkv_cut = qkv_weight.reshape(64, 2, 4, 3, 64).transpose(1, 0, 3, 2, 4)
    qkv_cut = qkv_cut.reshape(2, 64, 768)
    fc1_cut = fc1_weight.reshape(64, 16, 2, 64).transpose(2, 0, 1, 3)
    fc1_cut = fc1_cut.reshape(2, 64, 1024)
    fc2_cut = fc2_weight.reshape(2, 64, 1024)
    small = jnp.zeros((16, 128), BF16)
    small = small.at[0, :].set(fc1_bias)
    small = small.at[1, :].set(jnp.concatenate([query_bias, value_bias, dense_bias]))
    small = small.at[2, 0:64].set(fc2_bias)
    norms = jnp.concatenate(
        [
            jnp.stack(
                [
                    attention_norm_gain,
                    attention_norm_bias,
                    feedforward_norm_gain,
                    feedforward_norm_bias,
                ]
            ),
            jnp.zeros((4, HALF), F32),
        ]
    )
    (
        rows_cot, qkv_full, dense_full, fc1_full, fc2_full, rows_one, rows_two, heads,
        logs, residual, stats, vectors, grad_act,
    ) = forward(
        lengths, inputs, cotangent, qkv_cut, dense_weight, fc1_cut, fc2_cut, small, norms
    )
    rows_branch, part_out, grad_fc1, red_fc2, sums_two = turn(
        rows_two, fc1_full, fc2_full, rows_cot, grad_act, residual, vectors
    )
    input_gradient, outputs, red_qkv, red_dense, red_fc1, total = last(
        lengths, inputs, stats, rows_branch, dense_full, qkv_full, heads, logs, rows_one,
        part_out, grad_fc1, attention_norm_gain.reshape(1, HALF), residual, vectors,
        sums_two,
    )
    red_qkv = (
        red_qkv.reshape(2, 64, 3, 4, 64).transpose(1, 0, 3, 2, 4).reshape(64, 1536)
    ).astype(F32)
    red_fc1 = (
        red_fc1.reshape(2, 64, 16, 64).transpose(1, 2, 0, 3).reshape(64, 2048)
    ).astype(F32)
    red_fc2 = red_fc2.reshape(128, HALF).astype(F32)
    red_dense = red_dense[0].astype(F32) + red_dense[1].astype(F32)

    halves = total[0:6].reshape(6, 2, HALF)
    mine = lax.dynamic_index_in_dim(halves, row, 1, False)
    red_dense_add = lax.dynamic_slice_in_dim(mine[4], dp * 64, 64)
    red_output_add = lax.dynamic_slice_in_dim(mine[5], dp * 64, 64)
    pair = jnp.where(row == 0, total[6:8], total[6:8][::-1])
    hidden_sums = pair[:, 0:1024].reshape(2, 16, 64)
    red_hidden_add = lax.dynamic_index_in_dim(hidden_sums, dp, 1, False).reshape(128)
    red_query = lax.dynamic_slice_in_dim(pair[:, 1024:1280].reshape(512), dp * 32, 32)
    red_value = lax.dynamic_slice_in_dim(pair[:, 1280:1536].reshape(512), dp * 32, 32)
    return (
        outputs,
        input_gradient,
        red_qkv,
        red_query,
        red_value,
        red_dense,
        red_dense_add,
        red_fc1,
        red_hidden_add,
        red_fc2,
        red_output_add,
        mine[0],
        mine[1],
        mine[2],
        mine[3],
    )


def solution(mesh):
    return jax.shard_map(
        local,
        mesh=mesh,
        in_specs=(
            P(("dp", "col"), "row"),
            P(("dp", "col"), "row"),
            P("dp"),
            P("row"),
            P("row"),
            P(("row", "dp"), "col"),
            P(("col", "dp")),
            P(("col", "dp")),
            P(("col", "dp"), "row"),
            P(("row", "dp")),
            P("row"),
            P("row"),
            P(("row", "dp"), "col"),
            P(("col", "dp")),
            P(("col", "dp"), "row"),
            P(("row", "dp")),
        ),
        out_specs=(
            P(("dp", "col"), "row"),
            P(("dp", "col"), "row"),
            P(("row", "dp"), "col"),
            P(("col", "dp")),
            P(("col", "dp")),
            P(("col", "dp"), "row"),
            P(("row", "dp")),
            P(("row", "dp"), "col"),
            P(("col", "dp")),
            P(("col", "dp"), "row"),
            P(("row", "dp")),
            P("row"),
            P("row"),
            P("row"),
            P("row"),
        ),
        check_vma=False,
    )
```

```python
import jax
import jax.numpy as jnp
from jax import lax
from jax.experimental import pallas as pl
from jax.experimental.pallas import tpu as pltpu
from jax.sharding import PartitionSpec as P

HEADS = 32
HEAD_DIM = 64
BLOCK = 256
SEQ = 1024
WIDTH = 2048
HALF = WIDTH // 2
LOCAL = 256
EPSILON = 1e-05
FAR = 1e30
MESH = pl.DeviceIdType.MESH
F32 = jnp.float32
BF16 = jnp.bfloat16


def wrap(position):
    return lax.rem(position + 4, 4)


class Place:
    def __init__(self):
        self.row = lax.axis_index("row")
        self.col = lax.axis_index("col")
        self.dp = lax.axis_index("dp")
        self.chip = self.row * 2 + lax.div(self.col, 2)
        self.core = lax.rem(self.col, 2)
        self.z = lax.div(self.dp, 4)
        self.y = lax.rem(self.dp, 4)

    def on_x(self, step):
        return self.x_at(wrap(self.chip + step), self.core)

    def x_at(self, chip, core):
        return {"row": lax.div(chip, 2), "col": lax.rem(chip, 2) * 2 + core}

    def on_y(self, step):
        return {"dp": self.z * 4 + wrap(self.y + step)}

    def on_z(self, step):
        return {"dp": wrap(self.z + step) * 4 + self.y}

    def partner(self):
        return {"row": 1 - self.row}

    def mate(self):
        return {"col": lax.div(self.col, 2) * 2 + 1 - self.core}


class Net:
    def __init__(self, send, recv):
        self.send, self.recv, self.used = send, recv, 0

    def copy(self, source, target, device):
        slot = self.used
        self.used += 1
        return pltpu.make_async_remote_copy(
            src_ref=source,
            dst_ref=target,
            send_sem=self.send.at[slot],
            recv_sem=self.recv.at[slot],
            device_id=device,
            device_id_type=MESH,
        )


class Near:
    def __init__(self, sems):
        self.sems, self.used = sems, 0

    def copy(self, source, target):
        slot = self.used
        self.used += 1
        return pltpu.make_async_copy(source, target, self.sems.at[slot])


def announce(devices):
    barrier = pltpu.get_barrier_semaphore()
    for device in devices:
        pl.semaphore_signal(barrier, inc=1, device_id=device, device_id_type=MESH)


def meet(devices):
    pl.semaphore_wait(pltpu.get_barrier_semaphore(), len(devices))


class RingGather:
    def __init__(self, net, block, me, right, left, own=None):
        before, after = wrap(me - 1), wrap(me + 1)
        own = own or (lambda half: block(me, half))
        self.first = [
            net.copy(own(0), block(me, 0), right),
            net.copy(own(1), block(me, 1), left),
        ]
        self.second = [
            net.copy(own(1), block(me, 1), right),
            net.copy(own(0), block(me, 0), left),
        ]
        self.passed = [
            net.copy(block(before, 0), block(before, 0), right),
            net.copy(block(after, 1), block(after, 1), left),
        ]

    def start(self):
        for copy in self.first + self.second:
            copy.start()

    def forward(self):
        for came, on in zip(self.first, self.passed):
            came.wait_recv()
            on.start()

    def near_done(self):
        for copy in self.second:
            copy.wait_recv()

    def far_done(self):
        for copy in self.passed:
            copy.wait_recv()

    def drain(self):
        for copy in self.first + self.second + self.passed:
            copy.wait_send()


class DirectGather:
    def __init__(self, net, own, target, devices):
        self.sends = [net.copy(own, target, device) for device in devices]

    def start(self):
        for copy in self.sends:
            copy.start()

    def forward(self):
        pass

    def near_done(self):
        for copy in self.sends:
            copy.wait_recv()

    def far_done(self):
        pass

    def drain(self):
        for copy in self.sends:
            copy.wait_send()


class GroupGather:
    def __init__(self, net, place, block, own):
        core, chip = place.core, place.chip
        self.ring = RingGather(
            net,
            lambda position, half: block(position, core, half),
            chip,
            place.on_x(1),
            place.on_x(-1),
            own,
        )
        whole = [
            own(None),
            block(wrap(chip - 1), core, None),
            block(wrap(chip + 1), core, None),
            block(wrap(chip + 2), core, None),
        ]
        target = [block(chip, core, None)] + whole[1:]
        self.mates = [
            net.copy(source, there, place.mate()) for source, there in zip(whole, target)
        ]

    def start(self):
        self.ring.start()
        self.mates[0].start()

    def forward(self):
        self.ring.forward()

    def share(self):
        self.ring.near_done()
        self.mates[1].start()
        self.mates[2].start()

    def near_finish(self):
        for copy in self.mates[1:3]:
            copy.wait_recv()

    def finish(self):
        self.ring.far_done()
        self.mates[3].start()
        for copy in (self.mates[0], self.mates[3]):
            copy.wait_recv()
        self.ring.drain()
        for copy in self.mates:
            copy.wait_send()


def sweep(rows, step, body, unroll=2):
    def one(index, carry):
        body(pl.multiple_of(index * step, step))
        return carry

    lax.fori_loop(0, rows // step, one, 0, unroll=unroll)


class GroupScatter:
    def __init__(self, net, place, part, slices, shape, total, ring_in):
        self.part, self.slices, self.place = part, slices, place
        self.rows, self.cols = shape
        self.total, self.ring_in = total, ring_in
        chip = place.chip
        half = self.rows // 2
        self.half = half
        self.order = [wrap(chip + 2), wrap(chip + 1), wrap(chip - 1), chip]
        mate = place.mate()
        self.mates = []
        for index, there in enumerate(self.order):
            rows, cols = slices(there, 1 - place.core)
            self.mates.append(
                net.copy(
                    part.at[pl.ds(rows, self.rows), pl.ds(cols, self.cols)],
                    total.at[index],
                    mate,
                )
            )
        right, left = place.on_x(1), place.on_x(-1)
        top, low = pl.ds(0, half), pl.ds(half, half)
        self.sends = [
            net.copy(total.at[0, top], ring_in.at[0], right),
            net.copy(total.at[0, low], ring_in.at[1], left),
            net.copy(total.at[1, low], ring_in.at[2], right),
            net.copy(total.at[2, top], ring_in.at[3], left),
            net.copy(ring_in.at[0], ring_in.at[4], right),
            net.copy(ring_in.at[1], ring_in.at[5], left),
        ]

    def start(self):
        for copy in self.mates:
            copy.start()

    def mine(self, index, row, step):
        rows, cols = self.slices(self.order[index], self.place.core)
        return self.part[
            pl.ds(pl.multiple_of(rows + row, 16), step), pl.ds(cols, self.cols)
        ].astype(F32)

    def first(self, *indices):
        for index in indices:
            self.mates[index].wait_recv()

            def add(row, index=index):
                here = pl.ds(row, 16)
                self.total[index, here, :] = (
                    self.mine(index, row, 16) + self.total[index, here, :].astype(F32)
                ).astype(BF16)

            sweep(self.rows, 16, add)
            if index == 0:
                self.sends[0].start()
                self.sends[1].start()
            else:
                self.sends[index + 1].start()

    def second(self):
        for side in range(2):
            self.sends[side].wait_recv()

            def add(row, side=side):
                here = pl.ds(row, 16)
                there = pl.ds(pl.multiple_of(row + side * self.half, 16), 16)
                self.ring_in[side, here, :] = (
                    self.total[1 + side, there, :].astype(F32)
                    + self.ring_in[side, here, :].astype(F32)
                ).astype(BF16)

            sweep(self.half, 16, add)
            self.sends[4 + side].start()

    def arrive(self):
        self.mates[3].wait_recv()
        for index in range(2, 6):
            self.sends[index].wait_recv()

    def result(self, side, row):
        here = pl.ds(row, 16)
        there = pl.multiple_of(row + side * self.half, 16)
        one, two = ((4, 3), (2, 5))[side]
        return (
            self.mine(3, there, 16)
            + self.total[3, pl.ds(there, 16), :].astype(F32)
            + self.ring_in[one, here, :].astype(F32)
            + self.ring_in[two, here, :].astype(F32)
        )

    def drain(self):
        for copy in self.mates + self.sends:
            copy.wait_send()


def scatter_scratch(rows, cols):
    return [
        pltpu.VMEM((4, rows, cols), BF16),
        pltpu.VMEM((6, rows // 2, cols), BF16),
    ]


def add_rows(target, sources):
    shape = target.shape
    if len(shape) == 3:
        for index in range(shape[0]):
            add_rows(target.at[index], [source.at[index] for source in sources])
        return

    def one(row):
        here = pl.ds(row, 16)
        total = sources[0][here, :].astype(F32)
        for source in sources[1:]:
            total = total + source[here, :].astype(F32)
        target[here, :] = total.astype(BF16)

    sweep(shape[0], 16, one)


class RingScatter:
    def __init__(self, net, part, me, right, left, ring_in, target, read=None):
        before, after, across = wrap(me - 1), wrap(me + 1), wrap(me + 2)
        self.read = read or [part(after, 0), part(before, 1), part(me, 0), part(me, 1)]
        self.ring_in, self.target = ring_in, target
        self.sends = [
            net.copy(part(across, 0), ring_in.at[0], right),
            net.copy(part(across, 1), ring_in.at[1], left),
            net.copy(part(after, 1), ring_in.at[2], right),
            net.copy(part(before, 0), ring_in.at[3], left),
            net.copy(ring_in.at[0], ring_in.at[4], right),
            net.copy(ring_in.at[1], ring_in.at[5], left),
        ]

    def start(self):
        for copy in self.sends[:4]:
            copy.start()

    def middle(self):
        for side in range(2):
            self.sends[side].wait_recv()
            add_rows(
                self.ring_in.at[side], [self.read[side], self.ring_in.at[side]]
            )
            self.sends[4 + side].start()

    def finish(self):
        for index in range(2, 6):
            self.sends[index].wait_recv()
        for side, (one, two) in enumerate(((4, 3), (2, 5))):
            add_rows(
                self.target(side),
                [self.read[2 + side], self.ring_in.at[one], self.ring_in.at[two]],
            )

    def drain(self):
        for copy in self.sends:
            copy.wait_send()


class DirectScatter:
    def __init__(self, net, part, me, devices, arrived, target, mine=None):
        self.arrived, self.target = arrived, target
        self.mine = part(me) if mine is None else mine
        self.sends = [
            net.copy(part(wrap(me + step)), arrived.at[index], device)
            for index, (step, device) in enumerate(zip((1, 3, 2), devices))
        ]

    def start(self):
        for copy in self.sends:
            copy.start()

    def finish(self):
        for copy in self.sends:
            copy.wait_recv()
        add_rows(
            self.target, [self.mine] + [self.arrived.at[index] for index in range(3)]
        )

    def drain(self):
        for copy in self.sends:
            copy.wait_send()


class OuterScatter:
    def __init__(self, net, place, at, size, rings, mids, reads=None):
        z, y = place.z, place.y
        self.rings = []
        for h in range(2):

            def along_z(pos, half, h=h):
                return at(h, pos, pl.ds(2 * half, 2), pl.ds(0, size))

            def along_y(pos, half, h=h):
                return at(h, pl.ds(2 * half, 2), pos, pl.ds(0, size))

            def mid_half(half, h=h):
                return mids[h].at[pl.ds(2 * half, 2)]

            outer = (
                (along_z, z, place.on_z(1), place.on_z(-1))
                if h == 0
                else (along_y, y, place.on_y(1), place.on_y(-1))
            )
            read = reads[h] if reads else None
            self.rings.append(RingScatter(net, *outer, rings[h], mid_half, read))

    def start(self):
        for ring in self.rings:
            ring.start()

    def middle(self):
        for ring in self.rings:
            ring.middle()

    def finish(self):
        for ring in self.rings:
            ring.finish()

    def drain(self):
        for ring in self.rings:
            ring.drain()


class InnerScatter:
    def __init__(self, net, near, place, mids, mine, arrived, done, final):
        row, z, y = place.row, place.z, place.y
        over_y = [place.on_y(step) for step in (1, 3, 2)]
        over_z = [place.on_z(step) for step in (1, 3, 2)]
        self.stages = []
        for h in range(2):
            me, devices = (y, over_y) if h == 0 else (z, over_z)
            self.stages.append(
                DirectScatter(
                    net,
                    lambda pos, mid=mids[h]: mid.at[pos],
                    me,
                    devices,
                    arrived[h],
                    done.at[h],
                    mine[h] if mine else None,
                )
            )
        self.swap = net.copy(done.at[1 - row], final.at[row], place.partner())
        self.keep = near.copy(done.at[row], final.at[row])

    def start(self):
        for stage in self.stages:
            stage.start()

    def finish(self):
        for stage in self.stages:
            stage.finish()
        self.swap.start()
        self.keep.start()

    def close(self):
        self.swap.wait_recv()
        self.keep.wait()
        self.swap.wait_send()
        for stage in self.stages:
            stage.drain()


def outer_scratch(size, cols):
    return [pltpu.VMEM((6, 2, size, cols), BF16)] * 2


def mid_scratch(size, cols):
    return [pltpu.VMEM((4, size, cols), BF16)] * 2


def inner_scratch(size, cols):
    return [pltpu.VMEM((3, size, cols), BF16)] * 2 + [pltpu.VMEM((2, size, cols), BF16)]


def any_specs(count):
    return [pl.BlockSpec(memory_space=pl.ANY)] * count


def vmem_specs(count):
    return [pl.BlockSpec(memory_space=pltpu.VMEM)] * count


def sem_arrays(remote, near=0):
    arrays = [pltpu.SemaphoreType.DMA((remote,)), pltpu.SemaphoreType.DMA((remote,))]
    if near:
        arrays.append(pltpu.SemaphoreType.DMA((near,)))
    return arrays


def comm_params(identity, megabytes=60):
    return pltpu.CompilerParams(
        collective_id=identity, has_side_effects=True, vmem_limit_bytes=megabytes << 20
    )


def quarter_block(ref):
    def block(chip, core, half):
        rows = (lax.rem(chip, 2) * 2 + core) * 256
        cols = lax.div(chip, 2) * HALF
        if half is None:
            return ref.at[pl.ds(rows, 256), pl.ds(cols, HALF)]
        return ref.at[pl.ds(rows + 128 * half, 128), pl.ds(cols, HALF)]

    return block


def rows_of(chip, core):
    return (lax.rem(chip, 2) * 2 + core) * 256 + lax.div(chip, 2) * 128


def row_block(ref):
    def block(chip, core, half):
        rows = rows_of(chip, core)
        if half is None:
            return ref.at[pl.ds(rows, 128), :]
        return ref.at[pl.ds(rows + 64 * half, 64), :]

    return block


def row_slices(chip, core):
    return rows_of(chip, core), 0


def quarter_slices(chip, core):
    return (lax.rem(chip, 2) * 2 + core) * 256, lax.div(chip, 2) * HALF


def stacked(ref, size):
    def at(part, z, y, rows):
        return ref.at[part, z, y, rows, :]

    return at, size


def beside(ref, size):
    def at(part, z, y, rows):
        return ref.at[z, y, rows, pl.ds(part * HALF, HALF)]

    return at, size


def head_mask(values, head):
    lane = lax.broadcasted_iota(jnp.int32, values.shape, 1)
    return jnp.where(lax.div(lane, HEAD_DIM) == head, values, jnp.zeros_like(values))


def distances(length, start, keys):
    key = lax.broadcasted_iota(jnp.int32, (keys, BLOCK), 0)
    query = lax.broadcasted_iota(jnp.int32, (keys, BLOCK), 1) + start
    return jnp.where(key < length, jnp.abs(query - key).astype(F32), FAR)


def slope_of(head):
    base = lax.axis_index("col") * 8 + lax.axis_index("row") * 4
    number = (base + head + 1).astype(F32)
    return jnp.exp2(jnp.full((1, BLOCK), -8.0 / HEADS, F32) * number)


def nt(left, right):
    return lax.dot_general(left, right, (((1,), (1,)), ((), ())), preferred_element_type=F32)


def nn(left, right):
    return jnp.dot(left, right, preferred_element_type=F32)


def attend_back_block(block, length, q, k, v, grad, logs, kt, dk, dv, dqt):
    start, keys = block * BLOCK, (block + 1) * BLOCK
    here = pl.ds(start, BLOCK)
    apart = distances(length, start, keys)

    def pair(index, carry):
        probs, dscores = [], []
        heads = (2 * index, 2 * index + 1)
        for head in heads:
            scores = nt(head_mask(k[0:keys, :], head), q[here, :])
            prob = jnp.exp(scores - slope_of(head) * apart - logs[head, :, here])
            dprob = nt(head_mask(v[0:keys, :], head), grad[here, :])
            delta = jnp.sum(prob * dprob, 0, keepdims=True)
            dscore = (prob * (dprob - delta)).astype(BF16)
            lines = pl.ds(pl.multiple_of(head * HEAD_DIM, HEAD_DIM), HEAD_DIM)
            dqt[lines, here] = nn(kt[lines, 0:keys], dscore).astype(BF16)
            probs.append(prob.astype(BF16))
            dscores.append(dscore)
        both = [
            jnp.concatenate([head_mask(ref[here, :], head) for head in heads], 0)
            for ref in (grad, q)
        ]
        dv[0:keys, :] += nn(jnp.concatenate(probs, 1), both[0])
        dk[0:keys, :] += nn(jnp.concatenate(dscores, 1), both[1])
        return carry

    lax.fori_loop(0, 2, pair, 0)


def normalize(values):
    mean = jnp.mean(values, 1, keepdims=True)
    centered = values - mean
    scale = lax.rsqrt(jnp.mean(centered * centered, 1, keepdims=True) + EPSILON)
    return centered * scale, scale


def x_devices(place):
    return [place.on_x(1), place.on_x(-1), place.mate()]


def merge(left, right, swap_left, swap_right):
    left, right = left.astype(F32), right.astype(F32)
    left = pltpu.roll(left, 64, 1) if swap_left else left
    right = pltpu.roll(right, 64, 1) if swap_right else right
    lane = lax.broadcasted_iota(jnp.int32, left.shape, 1)
    return jnp.where(lane < 64, left, right)


def group_of(ref, index):
    return ref[:, index * 128 : (index + 1) * 128]


def spread(small, line, base, per, first, width):
    entry = lax.broadcasted_iota(jnp.int32, (128, width), 1)
    piece = lax.broadcasted_iota(jnp.int32, (128, width), 0)
    wanted = (lax.div(entry, per) + first) * 8 + line
    chosen = jnp.where(piece == wanted, 1.0, 0.0).astype(BF16)
    spread_out = lax.dot_general(
        small, chosen, (((0,), (0,)), ((), ())), preferred_element_type=F32
    )
    lane = lax.broadcasted_iota(jnp.int32, (128, width), 0)
    entry = lax.broadcasted_iota(jnp.int32, (128, width), 1)
    return jnp.sum(
        jnp.where(lane == base + lax.rem(entry, per), spread_out, 0.0), 0, keepdims=True
    )


def attend_block(block, length, q, k, vt, out_t, logs):
    start, keys = block * BLOCK, (block + 1) * BLOCK
    here = pl.ds(start, BLOCK)
    apart = distances(length, start, keys)

    def one(head, carry):
        scores = nt(head_mask(k[0:keys, :], head), q[here, :])
        scores = scores - slope_of(head) * apart
        peak = jnp.max(scores, 0, keepdims=True)
        exponent = jnp.exp(scores - peak)
        total = jnp.sum(exponent, 0, keepdims=True)
        lines = pl.ds(pl.multiple_of(head * HEAD_DIM, HEAD_DIM), HEAD_DIM)
        out_t[lines, here] = nn(vt[lines, 0:keys], exponent.astype(BF16)) / total
        logs[head, :, here] = peak + jnp.log(total)
        return carry

    lax.fori_loop(0, 4, one, 0, unroll=2)


def forward_kernel(
    length, x, cot, qkv_own, dense, fc1_own, fc2, small_own, norm_a, norm_b, norm_c, norm_d,
    gcot, gqkv, gdense, gfc1, gfc2, rows_one, rows_two, heads, logs, residual, stats,
    vectors, grad_act,
    vx, vcot, vqkv, vdense, vfc2, vsmall, vnorm, n1, vheads, vt, out_t, part, own, tile,
    vlogs, qkv, fc1, small, norms, total, ring_in, send, recv, near_sems,
):
    place = Place()
    net, near = Net(send, recv), Near(near_sems)
    row, z, y = place.row, place.z, place.y
    partner = place.partner()
    y_ring = [place.on_y(step) for step in (1, 3, 2)]
    z_ring = [place.on_z(step) for step in (1, 3, 2)]
    peers = [partner, place.on_x(1), place.on_x(-1), place.mate()] + y_ring + z_ring
    announce(peers)
    for part_of in range(2):
        for third in range(3):
            for pair in range(2):
                left = (4 * part_of + 2 * pair) * 3 + third
                right = left + 3
                made = merge(
                    group_of(qkv_own, left // 2),
                    group_of(qkv_own, right // 2),
                    left % 2 == 1,
                    right % 2 == 0,
                )
                start = (third * 2 + pair) * 128
                qkv[part_of, :, start : start + 128] = made.astype(BF16)
    for pair in range(8):
        left, right = group_of(fc1_own, 2 * pair), group_of(fc1_own, 2 * pair + 1)
        for part_of in range(2):
            made = merge(left, right, part_of == 1, part_of == 0)
            fc1[part_of, :, pair * 128 : pair * 128 + 128] = made.astype(BF16)
    small[...] = jnp.zeros_like(small)
    for line in range(3):
        small[line : line + 1, :] = group_of(small_own, line)
    for line, source in enumerate((norm_a, norm_b, norm_c, norm_d)):
        norms[line : line + 1, :] = source[...]
        norms[line + 4 : line + 5, :] = source[...]
    weights = [
        (stacked(vqkv, 64), qkv.at[row], qkv.at[1 - row]),
        (stacked(vsmall, 8), small, small),
        (beside(vdense, 32), dense, dense),
        (stacked(gfc1, 64), fc1.at[row], fc1.at[1 - row]),
        (beside(vfc2, 64), fc2.at[row], fc2.at[1 - row]),
    ]
    swaps, copies = [], []
    for (at, size), own_cut, other in weights:
        there = at(row, z, y, pl.ds(0, size))
        swaps.append(net.copy(other, there, partner))
        copies.append(near.copy(own_cut, there))
    swap_norms = net.copy(norms, vnorm.at[row], partner)
    groups = []
    for source, target in ((x, vx), (cot, vcot)):
        block = quarter_block(target)

        def own_part(half, source=source):
            if half is None:
                return source
            return source.at[pl.ds(128 * half, 128), :]

        groups.append(GroupGather(net, place, block, own_part))
        copies.append(near.copy(source, block(place.chip, place.core, None)))
    copies.append(near.copy(norms, vnorm.at[row]))
    for copy in copies:
        copy.start()
    meet(peers)
    ones, twos = [], []
    for (at, size), own_cut, other in weights:
        half_rows = size // 2
        rows = pl.ds(0, size)

        def along_y(position, half, at=at, half_rows=half_rows):
            return at(row, z, position, pl.ds(half * half_rows, half_rows))

        def along_z(position, half, at=at, half_rows=half_rows):
            return at(1 - row, position, y, pl.ds(half * half_rows, half_rows))

        def mine(half, own_cut=own_cut, half_rows=half_rows):
            return own_cut.at[pl.ds(half * half_rows, half_rows), :]

        def planes_z(position, half, at=at, rows=rows):
            return at(row, position, pl.ds(2 * half, 2), rows)

        def planes_y(position, half, at=at, rows=rows):
            return at(1 - row, pl.ds(2 * half, 2), position, rows)

        over_y = (y, place.on_y(1), place.on_y(-1))
        over_z = (z, place.on_z(1), place.on_z(-1))
        if len(ones) < 2:
            there = at(1 - row, z, y, rows)
            ones.append(
                (
                    DirectGather(net, own_cut, at(row, z, y, rows), y_ring),
                    DirectGather(net, there, there, z_ring),
                )
            )
        else:
            ones.append(
                (
                    RingGather(net, along_y, *over_y, mine),
                    RingGather(net, along_z, *over_z),
                )
            )
        twos.append((RingGather(net, planes_z, *over_z), RingGather(net, planes_y, *over_y)))

    def begin(index):
        ones[index][0].start()
        swaps[index].wait_recv()
        ones[index][1].start()

    def pass_one(index):
        for ring in ones[index]:
            ring.forward()

    def turn_over(index):
        for ring, then in zip(ones[index], twos[index]):
            ring.near_done()
            ring.far_done()
            then.start()

    def pass_two(index):
        for ring in twos[index]:
            ring.forward()

    def complete(index):
        for ring in twos[index]:
            ring.near_done()
            ring.far_done()

    group_x, group_cot = groups
    swaps[0].start()
    ones[0][0].start()
    swap_norms.start()
    swaps[1].start()
    ones[1][0].start()
    group_x.start()
    for swap in swaps[2:]:
        swap.start()
    swaps[0].wait_recv()
    ones[0][1].start()
    swaps[1].wait_recv()
    ones[1][1].start()
    for copy in copies:
        copy.wait()
    turn_over(0)
    group_x.forward()
    turn_over(1)
    pass_two(0)
    pass_two(1)
    begin(2)
    begin(3)
    begin(4)
    group_x.share()
    swap_norms.wait_recv()

    def first_norm(pos):
        here = pl.ds(pos, 16)
        left, right = vx[here, 0:HALF].astype(F32), vx[here, HALF:WIDTH].astype(F32)
        mean = (
            jnp.sum(left, 1, keepdims=True) + jnp.sum(right, 1, keepdims=True)
        ) / WIDTH
        left, right = left - mean, right - mean
        scale = lax.rsqrt(
            (
                jnp.sum(left * left, 1, keepdims=True)
                + jnp.sum(right * right, 1, keepdims=True)
            )
            / WIDTH
            + EPSILON
        )
        lane = lax.broadcasted_iota(jnp.int32, (16, 128), 1)
        vlogs[here, :] = jnp.where(lane == 0, mean, scale)
        n1[here, 0:HALF] = (left * scale * vnorm[0, 0:1, :] + vnorm[0, 1:2, :]).astype(BF16)
        n1[here, HALF:WIDTH] = (
            right * scale * vnorm[1, 0:1, :] + vnorm[1, 1:2, :]
        ).astype(BF16)

    def norm_rows(start):
        sweep(512, 16, lambda pos: first_norm(pl.multiple_of(start + pos, 16)), 4)

    group_x.near_finish()
    norm_rows(512 - 512 * lax.rem(place.chip, 2))
    group_x.finish()
    group_cot.start()
    norm_rows(512 * lax.rem(place.chip, 2))
    for index in (2, 3, 4):
        pass_one(index)
    keep_n1 = near.copy(n1, rows_one)
    keep_n1.start()
    complete(1)
    smalls = [vsmall[index].reshape(128, 128).astype(BF16) for index in range(2)]
    query_add = spread(smalls[0], 1, 0, 32, 8 * row, LOCAL)
    value_add = spread(smalls[0], 1, 32, 32, 8 * row, LOCAL)
    complete(0)
    keep_qkv = near.copy(vqkv, gqkv)
    keep_qkv.start()

    def project(index, carry):
        here = pl.ds(pl.multiple_of(index * 256, 256), 256)
        for third, add in enumerate((query_add, None, value_add)):
            cols = slice(third * 256, (third + 1) * 256)
            made = nn(n1[here, :], vqkv[:, :, :, :, cols].reshape(WIDTH, 256))
            if add is not None:
                made = made + add
            made = made.astype(BF16)
            if third == 0:
                made = made * BF16(HEAD_DIM**-0.5)
            vheads[third, here, :] = made
        return carry

    turn_over(2)
    lax.fori_loop(0, 4, project, 0)
    group_cot.forward()
    vt[...] = vheads[2].T
    args = (length[0], vheads.at[0], vheads.at[1], vt, out_t, logs)
    attend_block(0, *args)
    pass_two(2)
    turn_over(3)
    turn_over(4)
    attend_block(1, *args)
    attend_block(2, *args)
    group_cot.share()
    group_cot.near_finish()
    attend_block(3, *args)
    vheads[3] = out_t[...].T.astype(BF16)
    complete(2)
    keep_heads = near.copy(vheads, heads)
    keep_heads.start()
    keep_dense = near.copy(vdense, gdense)
    keep_dense.start()

    scatter = GroupScatter(
        net, place, part, row_slices, (128, WIDTH), total, ring_in
    )
    weight = vdense[pl.ds(2 * row, 2)].reshape(LOCAL, WIDTH)
    for index, chip in enumerate(scatter.order):
        starts = [pl.multiple_of(rows_of(chip, core), 128) for core in range(2)]
        both = jnp.concatenate([vheads[3, pl.ds(start, 128), :] for start in starts], 0)
        made = nn(both, weight).astype(BF16)
        part[pl.ds(starts[0], 128), :] = made[0:128]
        part[pl.ds(starts[1], 128), :] = made[128:256]
        scatter.mates[index].start()
    scatter.first(0, 1, 2)
    group_cot.finish()
    keep_cot = near.copy(vcot, gcot)
    keep_cot.start()
    for side in range(2):
        half = pl.ds(side * HALF, HALF)
        vectors[0:1, half] = spread(smalls[side], 1, 64, 64, 0, HALF)
        vectors[1:2, half] = spread(smalls[side], 2, 0, 64, 0, HALF)
        vectors[3:4, half] = vnorm[side, 2:3, :]
        vectors[4:5, half] = vnorm[side, 3:4, :]
    vectors[2:3, 0:HALF] = jnp.where(
        row == 0,
        spread(smalls[0], 0, 0, 64, 0, HALF),
        spread(smalls[0], 0, 64, 64, 0, HALF),
    )
    scatter.second()
    pass_two(3)
    pass_two(4)
    scatter.arrive()
    group_two = GroupGather(
        net,
        place,
        row_block(rows_two),
        lambda half: own if half is None else own.at[pl.ds(64 * half, 64), :],
    )
    keep_own = near.copy(own, row_block(rows_two)(place.chip, place.core, None))
    first_row = rows_of(place.chip, place.core)
    for side in range(2):

        def one(pos, side=side):
            here = pl.ds(pl.multiple_of(pos + 64 * side, 16), 16)
            there = pl.ds(pl.multiple_of(first_row + pos + 64 * side, 16), 16)
            values = (
                vx[there, :].astype(F32) + scatter.result(side, pos) + vectors[0:1, :]
            )
            residual[here, :] = values
            own[here, :] = (
                normalize(values)[0] * vectors[3:4, :] + vectors[4:5, :]
            ).astype(BF16)

        sweep(64, 16, one)
    group_two.start()
    keep_own.start()
    complete(3)
    stats[...] = vlogs[pl.ds(pl.multiple_of(place.col * 256, 256), 256), :]
    complete(4)
    keep_fc2 = near.copy(vfc2, gfc2)
    keep_fc2.start()
    keeps = []
    for index in range(4):
        here = pl.ds(index * 256, 256)
        for piece in range(4):
            lines = vfc2[piece].reshape(256, WIDTH)
            tile[index, :, pl.ds(piece * 256, 256)] = nt(vcot[here, :], lines)
        keep = near.copy(tile.at[index], grad_act.at[here, :])
        keep.start()
        keeps.append(keep)
        if index == 1:
            group_two.forward()
        if index == 3:
            group_two.share()
    group_two.near_finish()
    group_two.finish()
    keeps += [keep_n1, keep_qkv, keep_heads, keep_dense, keep_cot, keep_own, keep_fc2]
    for keep in keeps:
        keep.wait()
    swap_norms.wait_send()
    for swap in swaps:
        swap.wait_send()
    for pair in ones + twos:
        for ring in pair:
            ring.drain()
    scatter.drain()


def forward(*args):
    remote = 6 + 3 * 10 + 10 + 5 * 4 * 6
    bf, full = (lambda *shape: jax.ShapeDtypeStruct(shape, BF16)), (
        lambda *shape: jax.ShapeDtypeStruct(shape, F32)
    )
    return pl.pallas_call(
        forward_kernel,
        out_shape=(
            bf(SEQ, WIDTH),
            bf(2, 4, 4, 64, 768),
            bf(4, 4, 32, 2048),
            bf(2, 4, 4, 64, 1024),
            bf(4, 4, 64, 2048),
            bf(SEQ, WIDTH),
            bf(SEQ, WIDTH),
            bf(4, SEQ, LOCAL),
            full(4, 1, SEQ),
            full(128, WIDTH),
            full(256, 128),
            full(8, WIDTH),
            full(SEQ, 1024),
        ),
        in_specs=[pl.BlockSpec(memory_space=pltpu.SMEM)]
        + any_specs(2)
        + vmem_specs(1)
        + any_specs(1)
        + vmem_specs(1)
        + any_specs(1)
        + vmem_specs(5),
        out_specs=tuple(any_specs(8) + vmem_specs(4) + any_specs(1)),
        scratch_shapes=[
            pltpu.VMEM((SEQ, WIDTH), BF16),
            pltpu.VMEM((SEQ, WIDTH), BF16),
            pltpu.VMEM((2, 4, 4, 64, 768), BF16),
            pltpu.VMEM((4, 4, 32, 2048), BF16),
            pltpu.VMEM((4, 4, 64, 2048), BF16),
            pltpu.VMEM((2, 4, 4, 8, 128), F32),
            pltpu.VMEM((2, 8, HALF), F32),
            pltpu.VMEM((SEQ, WIDTH), BF16),
            pltpu.VMEM((4, SEQ, LOCAL), BF16),
            pltpu.VMEM((LOCAL, SEQ), BF16),
            pltpu.VMEM((LOCAL, SEQ), F32),
            pltpu.VMEM((SEQ, WIDTH), BF16),
            pltpu.VMEM((128, WIDTH), BF16),
            pltpu.VMEM((4, 256, 1024), F32),
            pltpu.VMEM((SEQ, 128), F32),
            pltpu.VMEM((2, 64, 768), BF16),
            pltpu.VMEM((2, 64, 1024), BF16),
            pltpu.VMEM((8, 128), F32),
            pltpu.VMEM((8, HALF), F32),
        ]
        + scatter_scratch(128, WIDTH)
        + sem_arrays(remote, 20),
        compiler_params=comm_params(0),
        name="forward",
    )(*args)


def tn(left, right):
    return lax.dot_general(left, right, (((0,), (0,)), ((), ())), preferred_element_type=F32)


def turn_kernel(
    rows_two, fc1, fc2, cot, grad_act, residual, vectors,
    gathered, part_out, grad_fc1, mid_fc2, sums,
    n2, w1, w2, vcot, gact, act, gh, part, own, pout, g1, g2, many, total, ring_in, *rest,
):
    *rings, send, recv, near_sems = rest
    place = Place()
    net, near = Net(send, recv), Near(near_sems)
    peers = (
        x_devices(place)
        + [place.on_y(1), place.on_y(-1), place.on_z(1), place.on_z(-1)]
    )
    announce(peers)
    load_n2, load_w1 = near.copy(rows_two, n2), near.copy(fc1, w1)
    load_n2.start()
    load_w1.start()
    scatter = GroupScatter(
        net, place, part, row_slices, (128, WIDTH), total, ring_in
    )
    tiles = [
        [pl.multiple_of(rows_of(chip, core), 128) for core in range(2)]
        for chip in scatter.order
    ]
    load_act = []
    for index, starts in enumerate(tiles):
        load_act.append(
            [
                near.copy(
                    grad_act.at[pl.ds(start, 128), :],
                    gact.at[index % 2, pl.ds(128 * core, 128), :],
                )
                for core, start in enumerate(starts)
            ]
        )
    for index in range(2):
        for copy in load_act[index]:
            copy.start()
    load_w2, load_cot = near.copy(fc2, w2), near.copy(cot, vcot)
    sums[...] = jnp.zeros_like(sums)
    load_n2.wait()
    load_w1.wait()
    for index, starts in enumerate(tiles):
        for copy in load_act[index]:
            copy.wait()
        rows = [pl.ds(start, 128) for start in starts]
        both = jnp.concatenate([n2[here, :] for here in rows], 0)
        for piece in range(4):
            cols = slice(piece * 256, (piece + 1) * 256)
            hidden = (
                nn(both, w1[:, :, :, :, cols].reshape(WIDTH, 256)) + vectors[2:3, cols]
            )
            below = 0.5 + 0.5 * lax.erf(hidden * 0.5**0.5)
            density = jnp.exp(-0.5 * hidden * hidden) * 0.3989422804014327
            made = (hidden * below).astype(BF16)
            back = (
                gact[index % 2, :, cols] * (below + hidden * density)
            ).astype(BF16)
            for core, here in enumerate(rows):
                act[here, cols] = made[128 * core : 128 * core + 128]
                gh[here, cols] = back[128 * core : 128 * core + 128]
            sums[3:4, cols] += jnp.sum(back.astype(F32), 0, keepdims=True)
        if index < 2:
            for copy in load_act[index + 2]:
                copy.start()
        back = jnp.concatenate([gh[here, :] for here in rows], 0)
        if index > 0:
            scatter.first(index - 1)
        for side in range(2):
            for piece in range(4):
                cols = slice(side * HALF + piece * 256, side * HALF + piece * 256 + 256)
                made = nt(back, w1[side, piece].reshape(256, 1024)).astype(BF16)
                for core, here in enumerate(rows):
                    part[here, cols] = made[128 * core : 128 * core + 128]
        if index == 0:
            load_w2.start()
            load_cot.start()
            meet(peers)
        scatter.mates[index].start()
    load_w2.wait()
    load_cot.wait()

    def one_g2(index, carry):
        cols = pl.ds(pl.multiple_of(index * 256, 256), 256)
        for side in range(2):
            half = slice(side * HALF, (side + 1) * HALF)
            made = tn(act[:, cols], vcot[:, half]).astype(BF16)
            g2[index, :, :, half] = made.reshape(4, 64, HALF)
        return carry

    lax.fori_loop(0, 2, one_g2, 0)
    scatter.second()
    lax.fori_loop(2, 4, one_g2, 0)
    mids = [mid_fc2.at[index] for index in range(2)]
    over = OuterScatter(net, place, beside(g2, 64)[0], 64, rings, mids)
    over.start()

    def one_out(index, carry):
        here = pl.ds(pl.multiple_of(index * 256, 256), 256)
        for side in range(2):
            half = slice(side * HALF, (side + 1) * HALF)
            made = nn(act[here, :], w2[:, :, :, half].reshape(1024, HALF))
            pout[here, half] = made.astype(BF16)
        return carry

    lax.fori_loop(0, 3, one_out, 0)
    over.middle()
    many[...] = jnp.zeros_like(many)
    scatter.arrive()
    group = GroupGather(
        net,
        place,
        row_block(gathered),
        lambda half: own if half is None else own.at[pl.ds(64 * half, 64), :],
    )
    first_row = rows_of(place.chip, place.core)
    for side in range(2):

        def one(pos, side=side):
            here = pl.ds(pl.multiple_of(pos + 64 * side, 16), 16)
            there = pl.ds(pl.multiple_of(first_row + pos + 64 * side, 16), 16)
            arrived = scatter.result(side, pos)
            xhat, scale = normalize(residual[here, :])
            scaled = arrived * vectors[3:4, :]
            flat = jnp.mean(scaled, 1, keepdims=True)
            cross = jnp.mean(scaled * xhat, 1, keepdims=True)
            given = vcot[there, :].astype(F32)
            branch = (given + scale * (scaled - flat - xhat * cross)).astype(BF16)
            own[here, :] = branch
            many[0] += arrived * xhat
            many[1] += arrived
            many[2] += given
            many[3] += branch.astype(F32)

        sweep(64, 16, one)
    group.start()
    keep_own = near.copy(own, row_block(gathered)(place.chip, place.core, None))
    keep_own.start()
    for index, line in enumerate((0, 1, 2, 4)):
        sums[line : line + 1, :] = jnp.sum(many[index], 0, keepdims=True)
    lax.fori_loop(3, 4, one_out, 0)
    keep_out = near.copy(pout, part_out)
    keep_out.start()

    def one_g1(index, carry):
        side, piece = lax.div(index, 4), lax.rem(index, 4)
        cols = pl.ds(pl.multiple_of(index * 256, 256), 256)
        g1[side, piece] = tn(n2[:, cols], gh[...]).astype(BF16).reshape(4, 64, 1024)
        return carry

    lax.fori_loop(0, 4, one_g1, 0)
    group.forward()
    lax.fori_loop(4, 8, one_g1, 0)
    keep_g1 = near.copy(g1, grad_fc1)
    keep_g1.start()
    group.share()
    over.finish()

    group.near_finish()
    group.finish()
    for keep in (keep_own, keep_out, keep_g1):
        keep.wait()
    over.drain()
    scatter.drain()


def turn(rows_two, fc1, fc2, cot, grad_act, residual, vectors):
    bf = lambda *shape: jax.ShapeDtypeStruct(shape, BF16)
    return pl.pallas_call(
        turn_kernel,
        out_shape=(
            bf(SEQ, WIDTH),
            bf(SEQ, WIDTH),
            bf(2, 4, 4, 64, 1024),
            bf(2, 4, 64, 1024),
            jax.ShapeDtypeStruct((8, WIDTH), F32),
        ),
        in_specs=any_specs(5) + vmem_specs(2),
        out_specs=tuple(any_specs(3) + vmem_specs(2)),
        scratch_shapes=[
            pltpu.VMEM((SEQ, WIDTH), BF16),
            pltpu.VMEM((2, 4, 4, 64, 1024), BF16),
            pltpu.VMEM((4, 4, 64, 2048), BF16),
            pltpu.VMEM((SEQ, WIDTH), BF16),
            pltpu.VMEM((2, 256, 1024), F32),
            pltpu.VMEM((SEQ, 1024), BF16),
            pltpu.VMEM((SEQ, 1024), BF16),
            pltpu.VMEM((SEQ, WIDTH), BF16),
            pltpu.VMEM((128, WIDTH), BF16),
            pltpu.VMEM((SEQ, WIDTH), BF16),
            pltpu.VMEM((2, 4, 4, 64, 1024), BF16),
            pltpu.VMEM((4, 4, 64, 2048), BF16),
            pltpu.VMEM((4, 16, WIDTH), F32),
        ]
        + scatter_scratch(128, WIDTH)
        + outer_scratch(64, 1024)
        + sem_arrays(20 + 12, 20),
        compiler_params=comm_params(2),
        name="turn",
    )(rows_two, fc1, fc2, cot, grad_act, residual, vectors)


def last_kernel(
    length, x, stats, branch, dense, qkv, heads, logs, rows_one, part_out, grad_fc1,
    mid_fc2, gain, residual, vectors, sums_two,
    raw, out, rqkv, rdense, rfc1, rfc2, vector, first_sums, swapped, own_branch,
    rows, wd, wq, vheads, datt, kt, dk, dv, dqt, gproj, part, pout, g1, mine_fc2, gd, gq,
    result, stats_out, stats_in, group_in, y_in, z_in, vec_a, vec_b,
    stacks, late, late_two, late_group, late_y, late_z,
    total, ring_in, total_out, ring_out, *rest,
):
    *rest, send, recv, near_sems = rest
    rest = list(rest)

    def take(count):
        taken = rest[:count]
        del rest[:count]
        return taken

    place = Place()
    row, z, y = place.row, place.z, place.y
    net, near = Net(send, recv), Near(near_sems)
    load_rows = near.copy(branch, rows)
    load_wd = near.copy(dense.at[pl.ds(2 * row, 2)], wd)
    load_heads = near.copy(heads, vheads)
    load_g1 = []
    reads = []
    for h, me in enumerate((z, y)):
        views = []
        for index, (pos, half) in enumerate(
            ((wrap(me + 1), 0), (wrap(me - 1), 1), (me, 0), (me, 1))
        ):
            pair = pl.ds(2 * half, 2)
            source = grad_fc1.at[0, pos, pair] if h == 0 else grad_fc1.at[1, pair, pos]
            load_g1.append(near.copy(source, g1.at[h, index]))
            views.append(g1.at[h, index])
        reads.append(views)
    load_mid = [
        near.copy(mid_fc2.at[h, me], mine_fc2.at[h]) for h, me in enumerate((y, z))
    ]
    load_out = near.copy(part_out, pout)
    load_wq = near.copy(qkv, wq)
    quarter = quarter_slices(place.chip, place.core)
    load_own = near.copy(
        branch.at[pl.ds(quarter[0], 256), pl.ds(quarter[1], HALF)], own_branch
    )
    load_own.start()
    load_rows.start()
    load_wd.start()
    load_heads.start()
    x_group = [
        place.x_at(wrap(place.chip + step), core)
        for step in range(4)
        for core in (place.core, 1 - place.core)
    ][1:]
    y_ring = [place.on_y(step) for step in (1, 2, 3)]
    z_ring = [place.on_z(step) for step in (1, 2, 3)]
    peers = x_group + y_ring + z_ring
    announce(peers)
    scatter = GroupScatter(net, place, part, quarter_slices, (256, HALF), total, ring_in)
    scatter_out = GroupScatter(
        net, place, pout, row_slices, (128, WIDTH), total_out, ring_out
    )
    rings_fc1, rings_dense, rings_qkv = take(2), take(2), take(2)
    mids_fc1, mids_dense, mids_qkv = take(2), take(2), take(2)
    out_fc1 = OuterScatter(
        net, place, stacked(grad_fc1, 64)[0], 64, rings_fc1, mids_fc1, reads
    )
    out_dense = OuterScatter(net, place, beside(gd, 32)[0], 32, rings_dense, mids_dense)
    out_qkv = OuterScatter(net, place, stacked(gq, 64)[0], 64, rings_qkv, mids_qkv)
    inner = []
    for mids, mine, final in (
        ([mid_fc2.at[h] for h in range(2)], [mine_fc2.at[h] for h in range(2)], rfc2),
        (mids_fc1, None, rfc1),
        (mids_dense, None, rdense),
        (mids_qkv, None, rqkv),
    ):
        arrived, done = take(2), take(1)[0]
        inner.append(InnerScatter(net, near, place, mids, mine, arrived, done, final))
    in_fc2, in_fc1, in_dense, in_qkv = inner
    vec_a[...] = jnp.zeros_like(vec_a)
    vec_a[2:4, :] = sums_two[0:2, :]
    vec_a[4:5, :] = sums_two[4:5, :]
    vec_a[5:6, :] = sums_two[2:3, :]
    vec_a[6:7, 0:HALF] = sums_two[3:4, 0:HALF]
    load_rows.wait()
    load_wd.wait()
    load_heads.wait()
    for load in load_g1 + load_mid:
        load.start()
    load_out.start()
    load_wq.start()

    def back_attended(index, carry):
        here = pl.ds(pl.multiple_of(index * 256, 256), 256)
        datt[here, :] = nt(rows[here, :], wd[...].reshape(LOCAL, WIDTH)).astype(BF16)
        return carry

    lax.fori_loop(0, 4, back_attended, 0)
    meet(peers)
    load_out.wait()
    scatter_out.start()
    in_fc2.start()
    out_fc1.start()
    group_sends = [
        net.copy(vec_a, group_in.at[index], device)
        for index, device in enumerate(x_group)
    ]
    for copy in group_sends:
        copy.start()
    for side in range(2):
        half = slice(side * HALF, (side + 1) * HALF)
        made = tn(vheads[3], rows[:, half]).astype(BF16).reshape(2, 4, 32, HALF)
        gd[pl.ds(2 * row, 2), :, :, half] = made
        gd[pl.ds(2 - 2 * row, 2), :, :, half] = jnp.zeros_like(made)
    out_dense.start()
    for load in load_g1 + load_mid:
        load.wait()
    load_one = near.copy(rows_one, rows)
    load_one.start()
    kt[...] = vheads[1].T
    dk[...] = jnp.zeros_like(dk)
    dv[...] = jnp.zeros_like(dv)
    args = (length[0], vheads.at[0], vheads.at[1], vheads.at[2], datt, logs, kt, dk, dv, dqt)
    attend_back_block(0, *args)
    scatter_out.first(0, 1, 2)
    attend_back_block(1, *args)
    attend_back_block(2, *args)
    scatter_out.second()
    for copy in group_sends:
        copy.wait_recv()
    vec_b[...] = vec_a[...]
    for index in range(7):
        vec_b[2:6, :] += group_in[index, 2:6, :]
    vec_b[7:8, :] = group_in[3, 6:7, :]
    y_sends = [net.copy(vec_b, y_in.at[i], device) for i, device in enumerate(y_ring)]
    for copy in y_sends:
        copy.start()
    attend_back_block(3, *args)
    gproj[:, 0:256] = dqt[...].T * BF16(HEAD_DIM**-0.5)
    gproj[:, 256:512] = dk[...].astype(BF16)
    gproj[:, 512:768] = dv[...].astype(BF16)
    load_wq.wait()
    load_one.wait()
    columns = jnp.concatenate(
        [
            jnp.sum(gproj[:, third * 256 : third * 256 + 256].astype(F32), 0, keepdims=True)
            for third in range(3)
        ],
        1,
    )
    lane = lax.broadcasted_iota(jnp.int32, (256, 128), 1)
    stacks[...] = jnp.zeros_like(stacks)

    def one_gq(index, carry):
        side, piece = lax.div(index, 4), lax.rem(index, 4)
        cols = pl.ds(pl.multiple_of(index * 256, 256), 256)
        made = tn(rows[:, cols], gproj[...])
        weight = wq[side, piece].reshape(256, 768).astype(F32)
        gq[side, piece] = made.astype(BF16).reshape(4, 64, 768)
        stacks[...] += jnp.where(
            lane == index, jnp.sum(weight * made, 1, keepdims=True), 0.0
        ) + jnp.where(lane == index + 8, jnp.sum(weight * columns, 1, keepdims=True), 0.0)
        return carry

    lax.fori_loop(0, 4, one_gq, 0)
    out_qkv.rings[0].start()
    lax.fori_loop(4, 8, one_gq, 0)
    out_qkv.rings[1].start()
    for index, chip in enumerate(scatter.order):
        here = pl.ds(pl.multiple_of(lax.rem(chip, 2) * 512, 512), 512)
        cols = pl.ds(pl.multiple_of(lax.div(chip, 2) * HALF, HALF), HALF)
        weight = wq[lax.div(chip, 2)].reshape(HALF, 768)
        part[here, cols] = nt(gproj[here, :], weight).astype(BF16)
        scatter.mates[index].start()
        if index > 0:
            scatter.first(index - 1)
    late[...] = jnp.zeros_like(late)
    late[0:16, :] = stacks[...].T[0:16, :]
    late[16:17, :] = columns[:, 0:256]
    late[17:18, :] = columns[:, 512:768]
    late_x_sends = [
        net.copy(late, late_group.at[index], device) for index, device in enumerate(x_group)
    ]
    for copy in late_x_sends:
        copy.start()
    out_fc1.middle()
    scatter.second()
    out_dense.middle()
    out_fc1.finish()
    in_fc1.start()
    out_qkv.middle()
    for copy in y_sends:
        copy.wait_recv()
    for copy in group_sends:
        copy.wait_send()
    vec_a[...] = vec_b[...]
    for index in range(3):
        vec_a[...] += y_in[index]
    z_sends = [net.copy(vec_a, z_in.at[i], device) for i, device in enumerate(z_ring)]
    for copy in z_sends:
        copy.start()
    out_dense.finish()
    in_dense.start()
    for copy in late_x_sends:
        copy.wait_recv()
    late_two[...] = late[...]
    for index in range(7):
        late_two[0:16, :] += late_group[index, 0:16, :]
    late_two[18:20, :] = late_group[3, 16:18, :]
    late_y_sends = [
        net.copy(late_two, late_y.at[i], device) for i, device in enumerate(y_ring)
    ]
    for copy in late_y_sends:
        copy.start()
    in_fc2.finish()
    scatter.arrive()

    lane = lax.broadcasted_iota(jnp.int32, (16, 128), 1)
    for side in range(2):

        def sums(pos, side=side):
            here = pl.ds(pl.multiple_of(pos + 128 * side, 16), 16)
            arrived = scatter.result(side, pos)
            scaled = arrived * gain[...]
            xhat = (x[here, :].astype(F32) - stats[here, 0:1]) * stats[here, 1:2]
            flat = jnp.sum(scaled, 1, keepdims=True)
            cross = jnp.sum(scaled * xhat, 1, keepdims=True)
            stats_out[here, :] = jnp.where(lane == 0, flat, cross)
            raw[here, :] = arrived

        sweep(128, 16, sums, 4)
    swap_stats = net.copy(stats_out, stats_in, place.partner())
    swap_stats.start()
    out_qkv.finish()
    in_qkv.start()
    in_fc1.finish()
    in_dense.finish()
    scatter_out.arrive()
    for side in range(2):

        def finish_rows(pos, side=side):
            here = pl.ds(pl.multiple_of(pos + 64 * side, 16), 16)
            result[here, :] = (
                residual[here, :] + scatter_out.result(side, pos) + vectors[1:2, :]
            ).astype(BF16)

        sweep(64, 16, finish_rows)
    there = pl.ds(row * 128, 128)
    out_swap = net.copy(
        result.at[:, pl.ds((1 - row) * HALF, HALF)], out.at[there, :], place.partner()
    )
    out_keep = near.copy(result.at[:, pl.ds(row * HALF, HALF)], out.at[there, :])
    out_swap.start()
    out_keep.start()
    for copy in late_y_sends:
        copy.wait_recv()
    for copy in late_x_sends:
        copy.wait_send()
    late[...] = late_two[...]
    for index in range(3):
        late[...] += late_y[index]
    late_z_sends = [net.copy(late, late_z.at[i], device) for i, device in enumerate(z_ring)]
    for copy in late_z_sends:
        copy.start()
    in_qkv.finish()
    swap_stats.wait_recv()
    swapped[...] = stats_out[...] + stats_in[...]
    for copy in z_sends + late_z_sends:
        copy.wait_recv()
    vector[...] = vec_a[...]
    first_sums[...] = late[...]
    for index in range(3):
        vector[...] += z_in[index]
        first_sums[...] += late_z[index]
    load_own.wait()
    out_swap.wait_recv()
    for stage in (out_fc1, out_dense, out_qkv):
        stage.drain()
    for stage in inner:
        stage.close()
    out_keep.wait()
    out_swap.wait_send()
    swap_stats.wait_send()
    for copy in y_sends + late_y_sends + z_sends + late_z_sends:
        copy.wait_send()
    scatter.drain()
    scatter_out.drain()


def last(*args):
    bf = lambda *shape: jax.ShapeDtypeStruct(shape, BF16)
    full = lambda *shape: jax.ShapeDtypeStruct(shape, F32)
    anywhere, inside = any_specs(1)[0], vmem_specs(1)[0]
    where = (
        [pl.BlockSpec(memory_space=pltpu.SMEM), inside, inside]
        + [anywhere] * 4
        + [inside]
        + [anywhere] * 4
        + [inside] * 4
    )
    return pl.pallas_call(
        last_kernel,
        out_shape=(
            full(256, HALF),
            bf(256, HALF),
            bf(2, 64, 768),
            bf(2, 32, 1024),
            bf(2, 64, 1024),
            bf(2, 64, 1024),
            full(8, WIDTH),
            full(24, 256),
            full(256, 128),
            bf(256, HALF),
        ),
        in_specs=where,
        out_specs=tuple(vmem_specs(9) + any_specs(1)),
        scratch_shapes=[
            pltpu.VMEM((SEQ, WIDTH), BF16),
            pltpu.VMEM((2, 4, 32, WIDTH), BF16),
            pltpu.VMEM((2, 4, 4, 64, 768), BF16),
            pltpu.VMEM((4, SEQ, LOCAL), BF16),
            pltpu.VMEM((SEQ, LOCAL), BF16),
            pltpu.VMEM((LOCAL, SEQ), BF16),
            pltpu.VMEM((SEQ, LOCAL), F32),
            pltpu.VMEM((SEQ, LOCAL), F32),
            pltpu.VMEM((LOCAL, SEQ), BF16),
            pltpu.VMEM((SEQ, 768), BF16),
            pltpu.VMEM((SEQ, WIDTH), BF16),
            pltpu.VMEM((SEQ, WIDTH), BF16),
            pltpu.VMEM((2, 4, 2, 64, 1024), BF16),
            pltpu.VMEM((2, 64, 1024), BF16),
            pltpu.VMEM((4, 4, 32, 2048), BF16),
            pltpu.VMEM((2, 4, 4, 64, 768), BF16),
            pltpu.VMEM((128, WIDTH), BF16),
            pltpu.VMEM((256, 128), F32),
            pltpu.VMEM((256, 128), F32),
            pltpu.VMEM((7, 8, WIDTH), F32),
            pltpu.VMEM((3, 8, WIDTH), F32),
            pltpu.VMEM((3, 8, WIDTH), F32),
            pltpu.VMEM((8, WIDTH), F32),
            pltpu.VMEM((8, WIDTH), F32),
            pltpu.VMEM((256, 128), F32),
            pltpu.VMEM((24, 256), F32),
            pltpu.VMEM((24, 256), F32),
            pltpu.VMEM((7, 24, 256), F32),
            pltpu.VMEM((3, 24, 256), F32),
            pltpu.VMEM((3, 24, 256), F32),
        ]
        + scatter_scratch(256, HALF)
        + scatter_scratch(128, WIDTH)
        + outer_scratch(64, 1024)
        + outer_scratch(32, 1024)
        + outer_scratch(64, 768)
        + mid_scratch(64, 1024)
        + mid_scratch(32, 1024)
        + mid_scratch(64, 768)
        + inner_scratch(64, 1024)
        + inner_scratch(64, 1024)
        + inner_scratch(32, 1024)
        + inner_scratch(64, 768)
        + sem_arrays(20 + 3 * 12 + 4 * 7 + 30, 28),
        compiler_params=comm_params(3, 62),
        name="last",
    )(*args)


def finish_kernel(
    raw, rows_out, rqkv, rdense, rfc1, rfc2, vector, first_sums, swapped, own_branch,
    x, stats, gain, offset,
    outputs, ingrad, qkv, query, value, dense, dense_add, fc1, hidden_add, fc2, output_add,
    gain_one, offset_one, gain_two, offset_two,
):
    row = lax.axis_index("row")
    dp = lax.axis_index("dp")
    outputs[...] = rows_out[...]

    def apply(pos):
        here = pl.ds(pos, 16)
        both = swapped[here, :] / WIDTH
        scale = stats[here, 1:2]
        xhat = (x[here, :].astype(F32) - stats[here, 0:1]) * scale
        ingrad[here, :] = own_branch[here, :].astype(F32) + scale * (
            raw[here, :] * gain[...] - both[:, 0:1] - xhat * both[:, 1:2]
        )

    sweep(256, 16, apply, 4)
    for index in range(12):
        made = []
        for block in (2 * index, 2 * index + 1):
            head, third = block // 3, block % 3
            place_in = third * 4 + head % 4
            made.append((group_of(rqkv.at[head // 4], place_in // 2), place_in % 2))
        (left, left_odd), (right, right_odd) = made
        qkv[:, index * 128 : index * 128 + 128] = merge(
            left, right, left_odd == 1, right_odd == 0
        )
    for index in range(16):
        fc1[:, index * 128 : index * 128 + 128] = merge(
            group_of(rfc1.at[0], index // 2),
            group_of(rfc1.at[1], index // 2),
            index % 2 == 1,
            index % 2 == 0,
        )
    fc2[0:64, :] = rfc2[0].astype(F32)
    fc2[64:128, :] = rfc2[1].astype(F32)
    dense[...] = rdense[0].astype(F32) + rdense[1].astype(F32)
    for index in range(4):
        cols = slice(index * 256, index * 256 + 256)
        products = first_sums[pl.ds(row * 4 + index, 1), :]
        plain = first_sums[pl.ds(row * 4 + index + 8, 1), :]
        gain_one[:, cols] = (products - offset[:, cols] * plain) / gain[:, cols]
        offset_one[:, cols] = plain
    half = pl.ds(pl.multiple_of(row * HALF, HALF), HALF)
    gain_two[...] = vector[2:3, half]
    offset_two[...] = vector[3:4, half]
    odd = lax.rem(dp, 2)
    start = lax.div(dp, 2) * 128

    def swap_if(values, swap):
        return jnp.where(swap == 1, pltpu.roll(values, 64, 1), values)

    def eight(line, lane):
        return vector[line : line + 1, pl.ds(pl.multiple_of(lane, 128), 128)] + jnp.zeros(
            (8, 128), F32
        )

    dense_add[...] = swap_if(eight(4, row * HALF + start), odd)[0:1, 0:64]
    output_add[...] = swap_if(eight(5, row * HALF + start), odd)[0:1, 0:64]
    own, other = eight(6, start), eight(7, start)
    first = jnp.where(row == 0, own, other)
    second = jnp.where(row == 0, other, own)
    lanes = lax.broadcasted_iota(jnp.int32, (8, 128), 1)
    hidden_add[...] = jnp.where(
        lanes < 64, swap_if(first, odd), swap_if(second, 1 - odd)
    )[0:1, :]
    theirs = lax.div(dp, 8) == row
    inside = lax.rem(dp, 8)
    quarter = lax.rem(inside, 4)
    upper = lax.div(inside, 4) == 1
    for target, base in ((query, 16), (value, 17)):
        lines = [
            first_sums[at : at + 1, lanes_from : lanes_from + 128]
            + jnp.zeros((8, 128), F32)
            for at in (base, base + 2)
            for lanes_from in (0, 128)
        ]
        mine = jnp.where(upper, lines[1], lines[0])
        other = jnp.where(upper, lines[3], lines[2])
        chosen = jnp.where(theirs, mine, other)
        moved = chosen
        for step in range(1, 4):
            moved = jnp.where(quarter == step, pltpu.roll(chosen, 128 - 32 * step, 1), moved)
        target[...] = moved[0:1, 0:32]


def finish(*args):
    full = lambda *shape: jax.ShapeDtypeStruct(shape, F32)
    whole = lambda shape: pl.BlockSpec(shape, lambda index: (0,) * len(shape))
    shapes = (
            jax.ShapeDtypeStruct((256, HALF), BF16),
            full(256, HALF),
            full(64, 1536),
            full(1, 32),
            full(1, 32),
            full(32, 1024),
            full(1, 64),
            full(64, 2048),
            full(1, 128),
            full(128, HALF),
            full(1, 64),
            full(1, HALF),
            full(1, HALF),
            full(1, HALF),
            full(1, HALF),
        )
    return pl.pallas_call(
        finish_kernel,
        out_shape=shapes,
        grid=(1,),
        in_specs=[whole(value.shape) for value in args],
        out_specs=tuple(whole(value.shape) for value in shapes),
        compiler_params=pltpu.CompilerParams(vmem_limit_bytes=62 << 20),
        name="finish",
    )(*args)


def local(
    inputs,
    cotangent,
    lengths,
    attention_norm_gain,
    attention_norm_bias,
    qkv_weight,
    query_bias,
    value_bias,
    dense_weight,
    dense_bias,
    feedforward_norm_gain,
    feedforward_norm_bias,
    fc1_weight,
    fc1_bias,
    fc2_weight,
    fc2_bias,
):
    zeros = jnp.zeros((64,), BF16)
    small = jnp.concatenate(
        [fc1_bias, query_bias, value_bias, dense_bias, fc2_bias, zeros]
    ).astype(F32)
    (
        rows_cot, qkv_full, dense_full, fc1_full, fc2_full, rows_one, rows_two, heads,
        logs, residual, stats, vectors, grad_act,
    ) = forward(
        lengths,
        inputs,
        cotangent,
        qkv_weight,
        dense_weight,
        fc1_weight,
        fc2_weight.reshape(2, 64, 1024),
        small.reshape(1, 384),
        attention_norm_gain.reshape(1, HALF),
        attention_norm_bias.reshape(1, HALF),
        feedforward_norm_gain.reshape(1, HALF),
        feedforward_norm_bias.reshape(1, HALF),
    )
    rows_branch, part_out, grad_fc1, mid_fc2, sums_two = turn(
        rows_two, fc1_full, fc2_full, rows_cot, grad_act, residual, vectors
    )
    (
        raw, rows_out, red_qkv, red_dense, red_fc1, red_fc2, vector, first_sums, swapped,
        own_branch,
    ) = last(
        lengths, inputs, stats, rows_branch, dense_full, qkv_full, heads, logs, rows_one,
        part_out, grad_fc1, mid_fc2, attention_norm_gain.reshape(1, HALF), residual, vectors,
        sums_two,
    )
    results = finish(
        raw, rows_out, red_qkv, red_dense, red_fc1, red_fc2, vector, first_sums, swapped, own_branch,
        inputs, stats, attention_norm_gain.reshape(1, HALF),
        attention_norm_bias.reshape(1, HALF),
    )
    return tuple(
        value.reshape(value.shape[1]) if value.shape[0] == 1 else value
        for value in results
    )


def solution(mesh):
    return jax.shard_map(
        local,
        mesh=mesh,
        in_specs=(
            P(("dp", "col"), "row"),
            P(("dp", "col"), "row"),
            P("dp"),
            P("row"),
            P("row"),
            P(("row", "dp"), "col"),
            P(("col", "dp")),
            P(("col", "dp")),
            P(("col", "dp"), "row"),
            P(("row", "dp")),
            P("row"),
            P("row"),
            P(("row", "dp"), "col"),
            P(("col", "dp")),
            P(("col", "dp"), "row"),
            P(("row", "dp")),
        ),
        out_specs=(
            P(("dp", "col"), "row"),
            P(("dp", "col"), "row"),
            P(("row", "dp"), "col"),
            P(("col", "dp")),
            P(("col", "dp")),
            P(("col", "dp"), "row"),
            P(("row", "dp")),
            P(("row", "dp"), "col"),
            P(("col", "dp")),
            P(("col", "dp"), "row"),
            P(("row", "dp")),
            P("row"),
            P("row"),
            P("row"),
            P("row"),
        ),
        check_vma=False,
    )
```

```python
import jax
import jax.numpy as jnp
from jax import lax
from jax.experimental import pallas as pl
from jax.experimental.pallas import tpu as pltpu
from jax.sharding import PartitionSpec as P

HEADS = 32
HEAD_DIM = 64
BLOCK = 256
SEQ = 1024
WIDTH = 2048
HALF = WIDTH // 2
LOCAL = 256
EPSILON = 1e-05
FAR = 1e30
MESH = pl.DeviceIdType.MESH
F32 = jnp.float32
BF16 = jnp.bfloat16


def wrap(position):
    return lax.rem(position + 4, 4)


class Place:
    def __init__(self):
        self.row = lax.axis_index("row")
        self.col = lax.axis_index("col")
        self.dp = lax.axis_index("dp")
        self.chip = self.row * 2 + lax.div(self.col, 2)
        self.core = lax.rem(self.col, 2)
        self.z = lax.div(self.dp, 4)
        self.y = lax.rem(self.dp, 4)

    def on_x(self, step):
        return self.x_at(wrap(self.chip + step), self.core)

    def x_at(self, chip, core):
        return {"row": lax.div(chip, 2), "col": lax.rem(chip, 2) * 2 + core}

    def on_y(self, step):
        return {"dp": self.z * 4 + wrap(self.y + step)}

    def on_z(self, step):
        return {"dp": wrap(self.z + step) * 4 + self.y}

    def partner(self):
        return {"row": 1 - self.row}

    def mate(self):
        return {"col": lax.div(self.col, 2) * 2 + 1 - self.core}


class Net:
    def __init__(self, send, recv):
        self.send, self.recv, self.used = send, recv, 0

    def copy(self, source, target, device):
        slot = self.used
        self.used += 1
        return pltpu.make_async_remote_copy(
            src_ref=source,
            dst_ref=target,
            send_sem=self.send.at[slot],
            recv_sem=self.recv.at[slot],
            device_id=device,
            device_id_type=MESH,
        )


class Near:
    def __init__(self, sems):
        self.sems, self.used = sems, 0

    def copy(self, source, target):
        slot = self.used
        self.used += 1
        return pltpu.make_async_copy(source, target, self.sems.at[slot])


def announce(devices):
    barrier = pltpu.get_barrier_semaphore()
    for device in devices:
        pl.semaphore_signal(barrier, inc=1, device_id=device, device_id_type=MESH)


def meet(devices):
    pl.semaphore_wait(pltpu.get_barrier_semaphore(), len(devices))


class RingGather:
    def __init__(self, net, block, me, right, left, own=None):
        before, after = wrap(me - 1), wrap(me + 1)
        own = own or (lambda half: block(me, half))
        self.first = [
            net.copy(own(0), block(me, 0), right),
            net.copy(own(1), block(me, 1), left),
        ]
        self.second = [
            net.copy(own(1), block(me, 1), right),
            net.copy(own(0), block(me, 0), left),
        ]
        self.passed = [
            net.copy(block(before, 0), block(before, 0), right),
            net.copy(block(after, 1), block(after, 1), left),
        ]

    def start(self):
        for copy in self.first + self.second:
            copy.start()

    def forward(self):
        for came, on in zip(self.first, self.passed):
            came.wait_recv()
            on.start()

    def near_done(self):
        for copy in self.second:
            copy.wait_recv()

    def far_done(self):
        for copy in self.passed:
            copy.wait_recv()

    def drain(self):
        for copy in self.first + self.second + self.passed:
            copy.wait_send()


class DirectGather:
    def __init__(self, net, own, target, devices):
        self.sends = [net.copy(own, target, device) for device in devices]

    def start(self):
        for copy in self.sends:
            copy.start()

    def forward(self):
        pass

    def near_done(self):
        for copy in self.sends:
            copy.wait_recv()

    def far_done(self):
        pass

    def drain(self):
        for copy in self.sends:
            copy.wait_send()


class GroupGather:
    def __init__(self, net, place, block, own):
        core, chip = place.core, place.chip
        self.ring = RingGather(
            net,
            lambda position, half: block(position, core, half),
            chip,
            place.on_x(1),
            place.on_x(-1),
            own,
        )
        whole = [
            own(None),
            block(wrap(chip - 1), core, None),
            block(wrap(chip + 1), core, None),
            block(wrap(chip + 2), core, None),
        ]
        target = [block(chip, core, None)] + whole[1:]
        self.mates = [
            net.copy(source, there, place.mate()) for source, there in zip(whole, target)
        ]

    def start(self):
        self.ring.start()
        self.mates[0].start()

    def forward(self):
        self.ring.forward()

    def share(self):
        self.ring.near_done()
        self.mates[1].start()
        self.mates[2].start()

    def near_finish(self):
        for copy in self.mates[1:3]:
            copy.wait_recv()

    def finish(self):
        self.ring.far_done()
        self.mates[3].start()
        for copy in (self.mates[0], self.mates[3]):
            copy.wait_recv()
        self.ring.drain()
        for copy in self.mates:
            copy.wait_send()


def sweep(rows, step, body, unroll=2):
    def one(index, carry):
        body(pl.multiple_of(index * step, step))
        return carry

    lax.fori_loop(0, rows // step, one, 0, unroll=unroll)


class GroupScatter:
    def __init__(self, net, place, part, slices, shape, total, ring_in):
        self.part, self.slices, self.place = part, slices, place
        self.rows, self.cols = shape
        self.total, self.ring_in = total, ring_in
        chip = place.chip
        half = self.rows // 2
        self.half = half
        self.order = [wrap(chip + 2), wrap(chip + 1), wrap(chip - 1), chip]
        mate = place.mate()
        self.mates = []
        for index, there in enumerate(self.order):
            rows, cols = slices(there, 1 - place.core)
            self.mates.append(
                net.copy(
                    part.at[pl.ds(rows, self.rows), pl.ds(cols, self.cols)],
                    total.at[index],
                    mate,
                )
            )
        right, left = place.on_x(1), place.on_x(-1)
        top, low = pl.ds(0, half), pl.ds(half, half)
        self.sends = [
            net.copy(total.at[0, top], ring_in.at[0], right),
            net.copy(total.at[0, low], ring_in.at[1], left),
            net.copy(total.at[1, low], ring_in.at[2], right),
            net.copy(total.at[2, top], ring_in.at[3], left),
            net.copy(ring_in.at[0], ring_in.at[4], right),
            net.copy(ring_in.at[1], ring_in.at[5], left),
        ]

    def start(self):
        for copy in self.mates:
            copy.start()

    def mine(self, index, row, step):
        rows, cols = self.slices(self.order[index], self.place.core)
        return self.part[
            pl.ds(pl.multiple_of(rows + row, 16), step), pl.ds(cols, self.cols)
        ].astype(F32)

    def first(self, *indices):
        for index in indices:
            self.mates[index].wait_recv()

            def add(row, index=index):
                here = pl.ds(row, 16)
                self.total[index, here, :] = (
                    self.mine(index, row, 16) + self.total[index, here, :].astype(F32)
                ).astype(BF16)

            sweep(self.rows, 16, add)
            if index == 0:
                self.sends[0].start()
                self.sends[1].start()
            else:
                self.sends[index + 1].start()

    def second(self):
        for side in range(2):
            self.sends[side].wait_recv()

            def add(row, side=side):
                here = pl.ds(row, 16)
                there = pl.ds(pl.multiple_of(row + side * self.half, 16), 16)
                self.ring_in[side, here, :] = (
                    self.total[1 + side, there, :].astype(F32)
                    + self.ring_in[side, here, :].astype(F32)
                ).astype(BF16)

            sweep(self.half, 16, add)
            self.sends[4 + side].start()

    def arrive(self):
        self.mates[3].wait_recv()
        for index in range(2, 6):
            self.sends[index].wait_recv()

    def result(self, side, row):
        here = pl.ds(row, 16)
        there = pl.multiple_of(row + side * self.half, 16)
        one, two = ((4, 3), (2, 5))[side]
        return (
            self.mine(3, there, 16)
            + self.total[3, pl.ds(there, 16), :].astype(F32)
            + self.ring_in[one, here, :].astype(F32)
            + self.ring_in[two, here, :].astype(F32)
        )

    def drain(self):
        for copy in self.mates + self.sends:
            copy.wait_send()


class PairSum:
    def __init__(self, net, place, part, total):
        self.part, self.place, self.total = part, place, total
        chip = place.chip
        self.order = [wrap(chip + 2), wrap(chip + 1), wrap(chip - 1), chip]
        self.mates = [
            net.copy(
                part.at[pl.ds(rows_of(there, 1 - place.core), 128), :],
                total.at[index],
                place.mate(),
            )
            for index, there in enumerate(self.order)
        ]

    def start(self):
        for copy in self.mates:
            copy.start()

    def finish(self):
        for index, there in enumerate(self.order):
            self.mates[index].wait_recv()
            start = rows_of(there, self.place.core)

            def add(row, index=index, start=start):
                here = pl.ds(row, 16)
                there = pl.ds(pl.multiple_of(start + row, 16), 16)
                self.total[index, here, :] = (
                    self.part[there, :].astype(F32)
                    + self.total[index, here, :].astype(F32)
                ).astype(BF16)

            sweep(128, 16, add)

    def drain(self):
        for copy in self.mates:
            copy.wait_send()


class RingSum:
    def __init__(self, net, place, pairs, near, ring_in):
        self.near, self.ring_in = near, ring_in
        right, left = place.on_x(1), place.on_x(-1)
        top, low = pl.ds(0, 64), pl.ds(64, 64)
        self.sends = [
            net.copy(pairs.at[0, top], ring_in.at[0], right),
            net.copy(pairs.at[0, low], ring_in.at[1], left),
            net.copy(pairs.at[1, low], ring_in.at[2], right),
            net.copy(pairs.at[2, top], ring_in.at[3], left),
            net.copy(ring_in.at[0], ring_in.at[4], right),
            net.copy(ring_in.at[1], ring_in.at[5], left),
        ]

    def start(self):
        for copy in self.sends[:4]:
            copy.start()

    def second(self):
        for side in range(2):
            self.sends[side].wait_recv()

            def add(row, side=side):
                here = pl.ds(row, 16)
                there = pl.ds(pl.multiple_of(row + side * 64, 16), 16)
                self.ring_in[side, here, :] = (
                    self.near[side, there, :].astype(F32)
                    + self.ring_in[side, here, :].astype(F32)
                ).astype(BF16)

            sweep(64, 16, add)
            self.sends[4 + side].start()

    def arrive(self):
        for copy in self.sends[2:]:
            copy.wait_recv()

    def result(self, side, row):
        here = pl.ds(row, 16)
        there = pl.ds(pl.multiple_of(row + side * 64, 16), 16)
        one, two = ((4, 3), (2, 5))[side]
        return (
            self.near[2, there, :].astype(F32)
            + self.ring_in[one, here, :].astype(F32)
            + self.ring_in[two, here, :].astype(F32)
        )

    def drain(self):
        for copy in self.sends:
            copy.wait_send()


def scatter_scratch(rows, cols):
    return [
        pltpu.VMEM((4, rows, cols), BF16),
        pltpu.VMEM((6, rows // 2, cols), BF16),
    ]


def add_rows(target, sources):
    shape = target.shape
    if len(shape) == 3:
        for index in range(shape[0]):
            add_rows(target.at[index], [source.at[index] for source in sources])
        return

    def one(row):
        here = pl.ds(row, 16)
        total = sources[0][here, :].astype(F32)
        for source in sources[1:]:
            total = total + source[here, :].astype(F32)
        target[here, :] = total.astype(BF16)

    sweep(shape[0], 16, one)


class RingScatter:
    def __init__(self, net, part, me, right, left, ring_in, target, read=None):
        before, after, across = wrap(me - 1), wrap(me + 1), wrap(me + 2)
        self.read = read or [part(after, 0), part(before, 1), part(me, 0), part(me, 1)]
        self.ring_in, self.target = ring_in, target
        self.sends = [
            net.copy(part(across, 0), ring_in.at[0], right),
            net.copy(part(across, 1), ring_in.at[1], left),
            net.copy(part(after, 1), ring_in.at[2], right),
            net.copy(part(before, 0), ring_in.at[3], left),
            net.copy(ring_in.at[0], ring_in.at[4], right),
            net.copy(ring_in.at[1], ring_in.at[5], left),
        ]

    def start(self):
        for copy in self.sends[:4]:
            copy.start()

    def middle(self):
        for side in range(2):
            self.sends[side].wait_recv()
            add_rows(
                self.ring_in.at[side], [self.read[side], self.ring_in.at[side]]
            )
            self.sends[4 + side].start()

    def finish(self):
        for index in range(2, 6):
            self.sends[index].wait_recv()
        for side, (one, two) in enumerate(((4, 3), (2, 5))):
            add_rows(
                self.target(side),
                [self.read[2 + side], self.ring_in.at[one], self.ring_in.at[two]],
            )

    def drain(self):
        for copy in self.sends:
            copy.wait_send()


def stacked_rows(ref, first):
    def at(part, z, y, rows):
        return ref.at[part, z, y, pl.ds(first + rows.start, rows.size), :]

    return at


class DirectScatter:
    def __init__(self, net, part, me, devices, arrived, target, mine=None):
        self.arrived, self.target = arrived, target
        self.mine = part(me) if mine is None else mine
        self.sends = [
            net.copy(part(wrap(me + step)), arrived.at[index], device)
            for index, (step, device) in enumerate(zip((1, 3, 2), devices))
        ]

    def start(self):
        for copy in self.sends:
            copy.start()

    def finish(self):
        for copy in self.sends:
            copy.wait_recv()
        add_rows(
            self.target, [self.mine] + [self.arrived.at[index] for index in range(3)]
        )

    def drain(self):
        for copy in self.sends:
            copy.wait_send()


class OuterScatter:
    def __init__(self, net, place, at, size, rings, mids, reads=None):
        z, y = place.z, place.y
        self.rings = []
        for h in range(2):

            def along_z(pos, half, h=h):
                return at(h, pos, pl.ds(2 * half, 2), pl.ds(0, size))

            def along_y(pos, half, h=h):
                return at(h, pl.ds(2 * half, 2), pos, pl.ds(0, size))

            def mid_half(half, h=h):
                return mids[h].at[pl.ds(2 * half, 2)]

            outer = (
                (along_z, z, place.on_z(1), place.on_z(-1))
                if h == 0
                else (along_y, y, place.on_y(1), place.on_y(-1))
            )
            read = reads[h] if reads else None
            self.rings.append(RingScatter(net, *outer, rings[h], mid_half, read))

    def start(self):
        for ring in self.rings:
            ring.start()

    def middle(self):
        for ring in self.rings:
            ring.middle()

    def finish(self):
        for ring in self.rings:
            ring.finish()

    def drain(self):
        for ring in self.rings:
            ring.drain()


class InnerScatter:
    def __init__(self, net, near, place, mids, mine, arrived, done, final):
        row, z, y = place.row, place.z, place.y
        over_y = [place.on_y(step) for step in (1, 3, 2)]
        over_z = [place.on_z(step) for step in (1, 3, 2)]
        self.stages = []
        for h in range(2):
            me, devices = (y, over_y) if h == 0 else (z, over_z)
            self.stages.append(
                DirectScatter(
                    net,
                    lambda pos, mid=mids[h]: mid.at[pos],
                    me,
                    devices,
                    arrived[h],
                    done.at[h],
                    mine[h] if mine else None,
                )
            )
        self.swap = net.copy(done.at[1 - row], final.at[row], place.partner())
        self.keep = near.copy(done.at[row], final.at[row])

    def start(self):
        for stage in self.stages:
            stage.start()

    def finish(self):
        for stage in self.stages:
            stage.finish()
        self.swap.start()
        self.keep.start()

    def close(self):
        self.swap.wait_recv()
        self.keep.wait()
        self.swap.wait_send()
        for stage in self.stages:
            stage.drain()


def outer_scratch(size, cols):
    return [pltpu.VMEM((6, 2, size, cols), BF16)] * 2


def mid_scratch(size, cols):
    return [pltpu.VMEM((4, size, cols), BF16)] * 2


def inner_scratch(size, cols):
    return [pltpu.VMEM((3, size, cols), BF16)] * 2 + [pltpu.VMEM((2, size, cols), BF16)]


def any_specs(count):
    return [pl.BlockSpec(memory_space=pl.ANY)] * count


def vmem_specs(count):
    return [pl.BlockSpec(memory_space=pltpu.VMEM)] * count


def sem_arrays(remote, near=0):
    arrays = [pltpu.SemaphoreType.DMA((remote,)), pltpu.SemaphoreType.DMA((remote,))]
    if near:
        arrays.append(pltpu.SemaphoreType.DMA((near,)))
    return arrays


def comm_params(identity, megabytes=60):
    return pltpu.CompilerParams(
        collective_id=identity, has_side_effects=True, vmem_limit_bytes=megabytes << 20
    )


def quarter_block(ref):
    def block(chip, core, half):
        rows = (lax.rem(chip, 2) * 2 + core) * 256
        cols = lax.div(chip, 2) * HALF
        if half is None:
            return ref.at[pl.ds(rows, 256), pl.ds(cols, HALF)]
        return ref.at[pl.ds(rows + 128 * half, 128), pl.ds(cols, HALF)]

    return block


def rows_of(chip, core):
    return (lax.rem(chip, 2) * 2 + core) * 256 + lax.div(chip, 2) * 128


def row_block(ref):
    def block(chip, core, half):
        rows = rows_of(chip, core)
        if half is None:
            return ref.at[pl.ds(rows, 128), :]
        return ref.at[pl.ds(rows + 64 * half, 64), :]

    return block


def row_slices(chip, core):
    return rows_of(chip, core), 0


def quarter_slices(chip, core):
    return (lax.rem(chip, 2) * 2 + core) * 256, lax.div(chip, 2) * HALF


def stacked(ref, size):
    def at(part, z, y, rows):
        return ref.at[part, z, y, rows, :]

    return at, size


def beside(ref, size):
    def at(part, z, y, rows):
        return ref.at[z, y, rows, pl.ds(part * HALF, HALF)]

    return at, size


def head_mask(values, head):
    lane = lax.broadcasted_iota(jnp.int32, values.shape, 1)
    return jnp.where(lax.div(lane, HEAD_DIM) == head, values, jnp.zeros_like(values))


def key_places(length, places):
    key = lax.broadcasted_iota(jnp.int32, places.shape, 0)
    places[...] = jnp.where(key < length, key.astype(F32), FAR)


def penalties(places, rows, start, slope):
    here = places[rows, :]
    query = (lax.broadcasted_iota(jnp.int32, (1, BLOCK), 1) + start).astype(F32)
    return slope * jnp.abs(query - jnp.concatenate([here, here], 1))


def fold(values, combine):
    return combine(values.reshape(16, 8, BLOCK), 0)


def slope_of(head):
    base = lax.axis_index("col") * 8 + lax.axis_index("row") * 4
    number = (base + head + 1).astype(F32)
    return jnp.exp2(jnp.full((1, BLOCK), -8.0 / HEADS, F32) * number)


def nt(left, right):
    return lax.dot_general(left, right, (((1,), (1,)), ((), ())), preferred_element_type=F32)


def nn(left, right):
    return jnp.dot(left, right, preferred_element_type=F32)


def attend_back_block(
    block, q, k, v, attended, grad, logs, places, kt, dk, dv, dqt, probs, dscores, deltas
):
    start, keys = block * BLOCK, (block + 1) * BLOCK
    here = pl.ds(start, BLOCK)
    inner = (grad[here, :].astype(F32) * attended[here, :].astype(F32)).T
    for head in range(4):
        lines = slice(head * HEAD_DIM, (head + 1) * HEAD_DIM)
        deltas[head] = jnp.sum(inner[lines, :], 0, keepdims=True)

    def pair(index, carry):
        heads = (2 * index, 2 * index + 1)
        for side, head in enumerate(heads):
            cols = slice(side * BLOCK, (side + 1) * BLOCK)
            slope, log, delta = slope_of(head), logs[head, :, here], deltas[head]
            for chunk in range(keys // 128):
                rows = slice(chunk * 128, (chunk + 1) * 128)
                scores = nt(head_mask(k[rows, :], head), q[here, :])
                prob = jnp.exp(scores - penalties(places, rows, start, slope) - log)
                dprob = nt(head_mask(v[rows, :], head), grad[here, :])
                probs[rows, cols] = prob.astype(BF16)
                dscores[rows, cols] = (prob * (dprob - delta)).astype(BF16)
            lines = pl.ds(pl.multiple_of(head * HEAD_DIM, HEAD_DIM), HEAD_DIM)
            dqt[lines, here] = nn(kt[lines, 0:keys], dscores[0:keys, cols]).astype(BF16)
        both = [
            jnp.concatenate([head_mask(ref[here, :], head) for head in heads], 0)
            for ref in (grad, q)
        ]
        dv[0:keys, :] += nn(probs[0:keys, :], both[0])
        dk[0:keys, :] += nn(dscores[0:keys, :], both[1])
        return carry

    lax.fori_loop(0, 2, pair, 0)


def normalize(values):
    mean = jnp.mean(values, 1, keepdims=True)
    centered = values - mean
    scale = lax.rsqrt(jnp.mean(centered * centered, 1, keepdims=True) + EPSILON)
    return centered * scale, scale


def x_devices(place):
    return [place.on_x(1), place.on_x(-1), place.mate()]


def merge(left, right, swap_left, swap_right):
    left, right = left.astype(F32), right.astype(F32)
    left = pltpu.roll(left, 64, 1) if swap_left else left
    right = pltpu.roll(right, 64, 1) if swap_right else right
    lane = lax.broadcasted_iota(jnp.int32, left.shape, 1)
    return jnp.where(lane < 64, left, right)


def group_of(ref, index):
    return ref[:, index * 128 : (index + 1) * 128]


def spread(small, line, base, per, first, width):
    entry = lax.broadcasted_iota(jnp.int32, (128, width), 1)
    piece = lax.broadcasted_iota(jnp.int32, (128, width), 0)
    wanted = (lax.div(entry, per) + first) * 8 + line
    chosen = jnp.where(piece == wanted, 1.0, 0.0).astype(BF16)
    spread_out = lax.dot_general(
        small, chosen, (((0,), (0,)), ((), ())), preferred_element_type=F32
    )
    lane = lax.broadcasted_iota(jnp.int32, (128, width), 0)
    entry = lax.broadcasted_iota(jnp.int32, (128, width), 1)
    return jnp.sum(
        jnp.where(lane == base + lax.rem(entry, per), spread_out, 0.0), 0, keepdims=True
    )


def attend_block(block, q, k, vt, out_t, logs, places, raws, probs):
    start, keys = block * BLOCK, (block + 1) * BLOCK
    here = pl.ds(start, BLOCK)

    def one(head, carry):
        slope = slope_of(head)
        peak = jnp.full((8, BLOCK), -3e38, F32)
        for chunk in range(keys // 128):
            rows = slice(chunk * 128, (chunk + 1) * 128)
            scores = nt(head_mask(k[rows, :], head), q[here, :])
            scores = scores - penalties(places, rows, start, slope)
            raws[rows, :] = scores
            peak = jnp.maximum(peak, fold(scores, jnp.max))
        peak = jnp.max(peak, 0, keepdims=True)
        total = jnp.zeros((8, BLOCK), F32)
        for chunk in range(keys // 128):
            rows = slice(chunk * 128, (chunk + 1) * 128)
            exponent = jnp.exp(raws[rows, :] - peak)
            total = total + fold(exponent, jnp.sum)
            probs[rows, :] = exponent.astype(BF16)
        total = jnp.sum(total, 0, keepdims=True)
        lines = pl.ds(pl.multiple_of(head * HEAD_DIM, HEAD_DIM), HEAD_DIM)
        out_t[lines, here] = nn(vt[lines, 0:keys], probs[0:keys, :]) / total
        logs[head, :, here] = peak + jnp.log(total)
        return carry

    lax.fori_loop(0, 4, one, 0)


def forward_kernel(
    length, x, cot, qkv_own, dense, fc1_own, fc2, small_own, norm_a, norm_b, norm_c, norm_d,
    gcot, gqkv, gdense, gfc1, gfc2, rows_one, rows_two, heads, logs, residual, stats,
    vectors, grad_act,
    vx, vcot, vqkv, vdense, vfc2, vsmall, vnorm, n1, vheads, vt, out_t, part, own, tile,
    vlogs, qkv, fc1, small, norms, places, raws, probs, total, ring_in,
    send, recv, near_sems,
):
    place = Place()
    net, near = Net(send, recv), Near(near_sems)
    row, z, y = place.row, place.z, place.y
    partner = place.partner()
    y_ring = [place.on_y(step) for step in (1, 3, 2)]
    z_ring = [place.on_z(step) for step in (1, 3, 2)]
    peers = [partner, place.on_x(1), place.on_x(-1), place.mate()] + y_ring + z_ring
    announce(peers)
    for part_of in range(2):
        for third in range(3):
            for pair in range(2):
                left = (4 * part_of + 2 * pair) * 3 + third
                right = left + 3
                made = merge(
                    group_of(qkv_own, left // 2),
                    group_of(qkv_own, right // 2),
                    left % 2 == 1,
                    right % 2 == 0,
                )
                start = (third * 2 + pair) * 128
                qkv[part_of, :, start : start + 128] = made.astype(BF16)
    for pair in range(8):
        left, right = group_of(fc1_own, 2 * pair), group_of(fc1_own, 2 * pair + 1)
        for part_of in range(2):
            made = merge(left, right, part_of == 1, part_of == 0)
            fc1[part_of, :, pair * 128 : pair * 128 + 128] = made.astype(BF16)
    small[...] = jnp.zeros_like(small)
    for line in range(3):
        small[line : line + 1, :] = group_of(small_own, line)
    for line, source in enumerate((norm_a, norm_b, norm_c, norm_d)):
        norms[line : line + 1, :] = source[...]
        norms[line + 4 : line + 5, :] = source[...]
    weights = [
        (stacked(vqkv, 64), qkv.at[row], qkv.at[1 - row]),
        (stacked(vsmall, 8), small, small),
        (beside(vdense, 32), dense, dense),
        (stacked(gfc1, 64), fc1.at[row], fc1.at[1 - row]),
        (beside(vfc2, 64), fc2.at[row], fc2.at[1 - row]),
    ]
    swaps, copies = [], []
    for (at, size), own_cut, other in weights:
        there = at(row, z, y, pl.ds(0, size))
        swaps.append(net.copy(other, there, partner))
        copies.append(near.copy(own_cut, there))
    swap_norms = net.copy(norms, vnorm.at[row], partner)
    groups = []
    for source, target in ((x, vx), (cot, vcot)):
        block = quarter_block(target)

        def own_part(half, source=source):
            if half is None:
                return source
            return source.at[pl.ds(128 * half, 128), :]

        groups.append(GroupGather(net, place, block, own_part))
        copies.append(near.copy(source, block(place.chip, place.core, None)))
    copies.append(near.copy(norms, vnorm.at[row]))
    for copy in copies:
        copy.start()
    meet(peers)
    ones, twos = [], []
    for (at, size), own_cut, other in weights:
        half_rows = size // 2
        rows = pl.ds(0, size)

        def along_y(position, half, at=at, half_rows=half_rows):
            return at(row, z, position, pl.ds(half * half_rows, half_rows))

        def along_z(position, half, at=at, half_rows=half_rows):
            return at(1 - row, position, y, pl.ds(half * half_rows, half_rows))

        def mine(half, own_cut=own_cut, half_rows=half_rows):
            return own_cut.at[pl.ds(half * half_rows, half_rows), :]

        def planes_z(position, half, at=at, rows=rows):
            return at(row, position, pl.ds(2 * half, 2), rows)

        def planes_y(position, half, at=at, rows=rows):
            return at(1 - row, pl.ds(2 * half, 2), position, rows)

        over_y = (y, place.on_y(1), place.on_y(-1))
        over_z = (z, place.on_z(1), place.on_z(-1))
        if len(ones) < 2:
            there = at(1 - row, z, y, rows)
            ones.append(
                (
                    DirectGather(net, own_cut, at(row, z, y, rows), y_ring),
                    DirectGather(net, there, there, z_ring),
                )
            )
        else:
            ones.append(
                (
                    RingGather(net, along_y, *over_y, mine),
                    RingGather(net, along_z, *over_z),
                )
            )
        twos.append((RingGather(net, planes_z, *over_z), RingGather(net, planes_y, *over_y)))

    def begin(index):
        ones[index][0].start()
        swaps[index].wait_recv()
        ones[index][1].start()

    def pass_one(index):
        for ring in ones[index]:
            ring.forward()

    def turn_over(index):
        for ring, then in zip(ones[index], twos[index]):
            ring.near_done()
            ring.far_done()
            then.start()

    def pass_two(index):
        for ring in twos[index]:
            ring.forward()

    def complete(index):
        for ring in twos[index]:
            ring.near_done()
            ring.far_done()

    group_x, group_cot = groups
    swaps[0].start()
    ones[0][0].start()
    swap_norms.start()
    swaps[1].start()
    ones[1][0].start()
    group_x.start()
    for swap in swaps[2:]:
        swap.start()
    swaps[0].wait_recv()
    ones[0][1].start()
    swaps[1].wait_recv()
    ones[1][1].start()
    for copy in copies:
        copy.wait()
    turn_over(0)
    group_x.forward()
    turn_over(1)
    pass_two(0)
    pass_two(1)
    begin(2)
    begin(3)
    begin(4)
    group_x.share()
    swap_norms.wait_recv()

    def first_norm(pos):
        here = pl.ds(pos, 16)
        left, right = vx[here, 0:HALF].astype(F32), vx[here, HALF:WIDTH].astype(F32)
        mean = (
            jnp.sum(left, 1, keepdims=True) + jnp.sum(right, 1, keepdims=True)
        ) / WIDTH
        left, right = left - mean, right - mean
        scale = lax.rsqrt(
            (
                jnp.sum(left * left, 1, keepdims=True)
                + jnp.sum(right * right, 1, keepdims=True)
            )
            / WIDTH
            + EPSILON
        )
        lane = lax.broadcasted_iota(jnp.int32, (16, 128), 1)
        vlogs[here, :] = jnp.where(lane == 0, mean, scale)
        n1[here, 0:HALF] = (left * scale * vnorm[0, 0:1, :] + vnorm[0, 1:2, :]).astype(BF16)
        n1[here, HALF:WIDTH] = (
            right * scale * vnorm[1, 0:1, :] + vnorm[1, 1:2, :]
        ).astype(BF16)

    def norm_rows(start):
        sweep(512, 16, lambda pos: first_norm(pl.multiple_of(start + pos, 16)), 4)

    group_x.near_finish()
    norm_rows(512 - 512 * lax.rem(place.chip, 2))
    group_x.finish()
    group_cot.start()
    norm_rows(512 * lax.rem(place.chip, 2))
    for index in (2, 3, 4):
        pass_one(index)
    key_places(length[0], places)
    keep_n1 = near.copy(n1, rows_one)
    keep_n1.start()
    complete(1)
    smalls = [vsmall[index].reshape(128, 128).astype(BF16) for index in range(2)]
    query_add = spread(smalls[0], 1, 0, 32, 8 * row, LOCAL)
    value_add = spread(smalls[0], 1, 32, 32, 8 * row, LOCAL)
    complete(0)
    keep_qkv = near.copy(vqkv, gqkv)
    keep_qkv.start()

    def project(index, carry):
        here = pl.ds(pl.multiple_of(index * 256, 256), 256)
        for third, add in enumerate((query_add, None, value_add)):
            cols = slice(third * 256, (third + 1) * 256)
            made = nn(n1[here, :], vqkv[:, :, :, :, cols].reshape(WIDTH, 256))
            if add is not None:
                made = made + add
            made = made.astype(BF16)
            if third == 0:
                made = made * BF16(HEAD_DIM**-0.5)
            vheads[third, here, :] = made
        return carry

    turn_over(2)
    lax.fori_loop(0, 4, project, 0)
    group_cot.forward()
    vt[...] = vheads[2].T
    args = (vheads.at[0], vheads.at[1], vt, out_t, logs, places, raws, probs)
    attend_block(0, *args)
    pass_two(2)
    turn_over(3)
    turn_over(4)
    attend_block(1, *args)
    attend_block(2, *args)
    group_cot.share()
    group_cot.near_finish()
    attend_block(3, *args)
    vheads[3] = out_t[...].T.astype(BF16)
    complete(2)
    keep_heads = near.copy(vheads, heads)
    keep_heads.start()
    keep_dense = near.copy(vdense, gdense)
    keep_dense.start()

    scatter = GroupScatter(
        net, place, part, row_slices, (128, WIDTH), total, ring_in
    )
    weight = vdense[pl.ds(2 * row, 2)].reshape(LOCAL, WIDTH)
    for index, chip in enumerate(scatter.order):
        starts = [pl.multiple_of(rows_of(chip, core), 128) for core in range(2)]
        both = jnp.concatenate([vheads[3, pl.ds(start, 128), :] for start in starts], 0)
        made = nn(both, weight).astype(BF16)
        part[pl.ds(starts[0], 128), :] = made[0:128]
        part[pl.ds(starts[1], 128), :] = made[128:256]
        scatter.mates[index].start()
    scatter.first(0, 1, 2)
    group_cot.finish()
    keep_cot = near.copy(vcot, gcot)
    keep_cot.start()
    for side in range(2):
        half = pl.ds(side * HALF, HALF)
        vectors[0:1, half] = spread(smalls[side], 1, 64, 64, 0, HALF)
        vectors[1:2, half] = spread(smalls[side], 2, 0, 64, 0, HALF)
        vectors[3:4, half] = vnorm[side, 2:3, :]
        vectors[4:5, half] = vnorm[side, 3:4, :]
    vectors[2:3, 0:HALF] = jnp.where(
        row == 0,
        spread(smalls[0], 0, 0, 64, 0, HALF),
        spread(smalls[0], 0, 64, 64, 0, HALF),
    )
    scatter.second()
    pass_two(3)
    pass_two(4)
    scatter.arrive()
    group_two = GroupGather(
        net,
        place,
        row_block(rows_two),
        lambda half: own if half is None else own.at[pl.ds(64 * half, 64), :],
    )
    keep_own = near.copy(own, row_block(rows_two)(place.chip, place.core, None))
    first_row = rows_of(place.chip, place.core)
    for side in range(2):

        def one(pos, side=side):
            here = pl.ds(pl.multiple_of(pos + 64 * side, 16), 16)
            there = pl.ds(pl.multiple_of(first_row + pos + 64 * side, 16), 16)
            values = (
                vx[there, :].astype(F32) + scatter.result(side, pos) + vectors[0:1, :]
            )
            residual[here, :] = values
            own[here, :] = (
                normalize(values)[0] * vectors[3:4, :] + vectors[4:5, :]
            ).astype(BF16)

        sweep(64, 16, one)
    group_two.start()
    keep_own.start()
    complete(3)
    stats[...] = vlogs[pl.ds(pl.multiple_of(place.col * 256, 256), 256), :]
    complete(4)
    keep_fc2 = near.copy(vfc2, gfc2)
    keep_fc2.start()
    keeps = []
    for index in range(4):
        here = pl.ds(index * 256, 256)
        for piece in range(4):
            lines = vfc2[piece].reshape(256, WIDTH)
            tile[index, :, pl.ds(piece * 256, 256)] = nt(vcot[here, :], lines)
        keep = near.copy(tile.at[index], grad_act.at[here, :])
        keep.start()
        keeps.append(keep)
        if index == 1:
            group_two.forward()
        if index == 3:
            group_two.share()
    group_two.near_finish()
    group_two.finish()
    keeps += [keep_n1, keep_qkv, keep_heads, keep_dense, keep_cot, keep_own, keep_fc2]
    for keep in keeps:
        keep.wait()
    swap_norms.wait_send()
    for swap in swaps:
        swap.wait_send()
    for pair in ones + twos:
        for ring in pair:
            ring.drain()
    scatter.drain()


def forward(*args):
    remote = 6 + 3 * 10 + 10 + 5 * 4 * 6
    bf, full = (lambda *shape: jax.ShapeDtypeStruct(shape, BF16)), (
        lambda *shape: jax.ShapeDtypeStruct(shape, F32)
    )
    return pl.pallas_call(
        forward_kernel,
        out_shape=(
            bf(SEQ, WIDTH),
            bf(2, 4, 4, 64, 768),
            bf(4, 4, 32, 2048),
            bf(2, 4, 4, 64, 1024),
            bf(4, 4, 64, 2048),
            bf(SEQ, WIDTH),
            bf(SEQ, WIDTH),
            bf(4, SEQ, LOCAL),
            full(4, 1, SEQ),
            full(128, WIDTH),
            full(256, 128),
            full(8, WIDTH),
            full(SEQ, 1024),
        ),
        in_specs=[pl.BlockSpec(memory_space=pltpu.SMEM)]
        + any_specs(2)
        + vmem_specs(1)
        + any_specs(1)
        + vmem_specs(1)
        + any_specs(1)
        + vmem_specs(5),
        out_specs=tuple(any_specs(8) + vmem_specs(4) + any_specs(1)),
        scratch_shapes=[
            pltpu.VMEM((SEQ, WIDTH), BF16),
            pltpu.VMEM((SEQ, WIDTH), BF16),
            pltpu.VMEM((2, 4, 4, 64, 768), BF16),
            pltpu.VMEM((4, 4, 32, 2048), BF16),
            pltpu.VMEM((4, 4, 64, 2048), BF16),
            pltpu.VMEM((2, 4, 4, 8, 128), F32),
            pltpu.VMEM((2, 8, HALF), F32),
            pltpu.VMEM((SEQ, WIDTH), BF16),
            pltpu.VMEM((4, SEQ, LOCAL), BF16),
            pltpu.VMEM((LOCAL, SEQ), BF16),
            pltpu.VMEM((LOCAL, SEQ), F32),
            pltpu.VMEM((SEQ, WIDTH), BF16),
            pltpu.VMEM((128, WIDTH), BF16),
            pltpu.VMEM((4, 256, 1024), F32),
            pltpu.VMEM((SEQ, 128), F32),
            pltpu.VMEM((2, 64, 768), BF16),
            pltpu.VMEM((2, 64, 1024), BF16),
            pltpu.VMEM((8, 128), F32),
            pltpu.VMEM((8, HALF), F32),
            pltpu.VMEM((SEQ, 128), F32),
            pltpu.VMEM((SEQ, BLOCK), F32),
            pltpu.VMEM((SEQ, BLOCK), BF16),
        ]
        + scatter_scratch(128, WIDTH)
        + sem_arrays(remote, 20),
        compiler_params=comm_params(0),
        name="forward",
    )(*args)


def tn(left, right):
    return lax.dot_general(left, right, (((0,), (0,)), ((), ())), preferred_element_type=F32)


def turn_kernel(
    rows_two, fc1, fc2, cot, grad_act, residual, vectors,
    gathered, pairs_out, grad_fc1, mid_fc2, mid_fc1, sums,
    n2, w1, w2, vcot, gact, act, gh, part, own, pout, g1, g2, many, total_out, total, ring_in, *rest,
):
    *rings, send, recv, near_sems = rest
    place = Place()
    net, near = Net(send, recv), Near(near_sems)
    peers = (
        x_devices(place)
        + [place.on_y(1), place.on_y(-1), place.on_z(1), place.on_z(-1)]
    )
    announce(peers)
    load_n2, load_w1 = near.copy(rows_two, n2), near.copy(fc1, w1)
    load_n2.start()
    load_w1.start()
    scatter = GroupScatter(
        net, place, part, row_slices, (128, WIDTH), total, ring_in
    )
    tiles = [
        [pl.multiple_of(rows_of(chip, core), 128) for core in range(2)]
        for chip in scatter.order
    ]
    load_act = []
    for index, starts in enumerate(tiles):
        load_act.append(
            [
                near.copy(
                    grad_act.at[pl.ds(start, 128), :],
                    gact.at[index % 2, pl.ds(128 * core, 128), :],
                )
                for core, start in enumerate(starts)
            ]
        )
    for index in range(2):
        for copy in load_act[index]:
            copy.start()
    load_w2, load_cot = near.copy(fc2, w2), near.copy(cot, vcot)
    sums[...] = jnp.zeros_like(sums)
    load_n2.wait()
    load_w1.wait()
    for index, starts in enumerate(tiles):
        for copy in load_act[index]:
            copy.wait()
        rows = [pl.ds(start, 128) for start in starts]
        both = jnp.concatenate([n2[here, :] for here in rows], 0)
        for piece in range(4):
            cols = slice(piece * 256, (piece + 1) * 256)
            hidden = (
                nn(both, w1[:, :, :, :, cols].reshape(WIDTH, 256)) + vectors[2:3, cols]
            )
            below = 0.5 + 0.5 * lax.erf(hidden * 0.5**0.5)
            density = jnp.exp(-0.5 * hidden * hidden) * 0.3989422804014327
            made = (hidden * below).astype(BF16)
            back = (
                gact[index % 2, :, cols] * (below + hidden * density)
            ).astype(BF16)
            for core, here in enumerate(rows):
                act[here, cols] = made[128 * core : 128 * core + 128]
                gh[here, cols] = back[128 * core : 128 * core + 128]
            sums[3:4, cols] += jnp.sum(back.astype(F32), 0, keepdims=True)
        if index < 2:
            for copy in load_act[index + 2]:
                copy.start()
        back = jnp.concatenate([gh[here, :] for here in rows], 0)
        if index > 0:
            scatter.first(index - 1)
        for side in range(2):
            for piece in range(4):
                cols = slice(side * HALF + piece * 256, side * HALF + piece * 256 + 256)
                made = nt(back, w1[side, piece].reshape(256, 1024)).astype(BF16)
                for core, here in enumerate(rows):
                    part[here, cols] = made[128 * core : 128 * core + 128]
        if index == 0:
            load_w2.start()
            load_cot.start()
            meet(peers)
        scatter.mates[index].start()
    load_w2.wait()
    load_cot.wait()

    def one_g2(index, carry):
        cols = pl.ds(pl.multiple_of(index * 256, 256), 256)
        for side in range(2):
            half = slice(side * HALF, (side + 1) * HALF)
            made = tn(act[:, cols], vcot[:, half]).astype(BF16)
            g2[index, :, :, half] = made.reshape(4, 64, HALF)
        return carry

    lax.fori_loop(0, 2, one_g2, 0)
    scatter.second()
    lax.fori_loop(2, 4, one_g2, 0)
    mids = [mid_fc2.at[index] for index in range(2)]
    over = OuterScatter(net, place, beside(g2, 64)[0], 64, rings[0:2], mids)
    over.start()

    def one_g1(index, carry):
        side, piece = lax.div(index, 4), lax.rem(index, 4)
        cols = pl.ds(pl.multiple_of(index * 256, 256), 256)
        g1[side, piece] = tn(n2[:, cols], gh[...]).astype(BF16).reshape(4, 64, 1024)
        return carry

    def one_out(index, carry):
        here = pl.ds(pl.multiple_of(index * 256, 256), 256)
        for side in range(2):
            half = slice(side * HALF, (side + 1) * HALF)
            made = nn(act[here, :], w2[:, :, :, half].reshape(1024, HALF))
            pout[here, half] = made.astype(BF16)
        return carry

    lax.fori_loop(0, 8, one_g1, 0)
    keep_g1 = near.copy(g1, grad_fc1)
    keep_g1.start()
    mids = [mid_fc1.at[index] for index in range(2)]
    over_fc1 = OuterScatter(net, place, stacked_rows(g1, 0), 32, rings[2:4], mids)
    over_fc1.start()
    many[...] = jnp.zeros_like(many)
    scatter.arrive()
    group = GroupGather(
        net,
        place,
        row_block(gathered),
        lambda half: own if half is None else own.at[pl.ds(64 * half, 64), :],
    )
    first_row = rows_of(place.chip, place.core)
    for side in range(2):

        def one(pos, side=side):
            here = pl.ds(pl.multiple_of(pos + 64 * side, 16), 16)
            there = pl.ds(pl.multiple_of(first_row + pos + 64 * side, 16), 16)
            arrived = scatter.result(side, pos)
            xhat, scale = normalize(residual[here, :])
            scaled = arrived * vectors[3:4, :]
            flat = jnp.mean(scaled, 1, keepdims=True)
            cross = jnp.mean(scaled * xhat, 1, keepdims=True)
            given = vcot[there, :].astype(F32)
            branch = (given + scale * (scaled - flat - xhat * cross)).astype(BF16)
            own[here, :] = branch
            many[0] += arrived * xhat
            many[1] += arrived
            many[2] += given
            many[3] += branch.astype(F32)

        sweep(64, 16, one)
    group.start()
    keep_own = near.copy(own, row_block(gathered)(place.chip, place.core, None))
    keep_own.start()
    for index, line in enumerate((0, 1, 2, 4)):
        sums[line : line + 1, :] = jnp.sum(many[index], 0, keepdims=True)
    over.middle()
    lax.fori_loop(0, 2, one_out, 0)
    group.forward()
    lax.fori_loop(2, 4, one_out, 0)
    pair = PairSum(net, place, pout, total_out)
    pair.start()
    over_fc1.middle()

    group.share()
    pair.finish()
    keep_out = near.copy(total_out, pairs_out)
    keep_out.start()
    over.finish()
    over_fc1.finish()

    group.near_finish()
    group.finish()
    for keep in (keep_own, keep_out, keep_g1):
        keep.wait()
    pair.drain()
    over.drain()
    over_fc1.drain()
    scatter.drain()


def turn(rows_two, fc1, fc2, cot, grad_act, residual, vectors):
    bf = lambda *shape: jax.ShapeDtypeStruct(shape, BF16)
    return pl.pallas_call(
        turn_kernel,
        out_shape=(
            bf(SEQ, WIDTH),
            bf(4, 128, WIDTH),
            bf(2, 4, 4, 64, 1024),
            bf(2, 4, 64, 1024),
            bf(2, 4, 32, 1024),
            jax.ShapeDtypeStruct((8, WIDTH), F32),
        ),
        in_specs=any_specs(5) + vmem_specs(2),
        out_specs=tuple(any_specs(3) + vmem_specs(3)),
        scratch_shapes=[
            pltpu.VMEM((SEQ, WIDTH), BF16),
            pltpu.VMEM((2, 4, 4, 64, 1024), BF16),
            pltpu.VMEM((4, 4, 64, 2048), BF16),
            pltpu.VMEM((SEQ, WIDTH), BF16),
            pltpu.VMEM((2, 256, 1024), F32),
            pltpu.VMEM((SEQ, 1024), BF16),
            pltpu.VMEM((SEQ, 1024), BF16),
            pltpu.VMEM((SEQ, WIDTH), BF16),
            pltpu.VMEM((128, WIDTH), BF16),
            pltpu.VMEM((SEQ, WIDTH), BF16),
            pltpu.VMEM((2, 4, 4, 64, 1024), BF16),
            pltpu.VMEM((4, 4, 64, 2048), BF16),
            pltpu.VMEM((4, 16, WIDTH), F32),
            pltpu.VMEM((4, 128, WIDTH), BF16),
        ]
        + scatter_scratch(128, WIDTH)
        + outer_scratch(64, 1024)
        + outer_scratch(32, 1024)
        + sem_arrays(20 + 24 + 4, 20),
        compiler_params=comm_params(2),
        name="turn",
    )(rows_two, fc1, fc2, cot, grad_act, residual, vectors)


def last_kernel(
    length, x, stats, branch, dense, qkv, heads, logs, rows_one, pairs_out, grad_fc1,
    mid_fc2, mid_fc1, gain, residual, vectors, sums_two,
    raw, out, rqkv, rdense, rfc1, rfc1_b, rfc2, vector, first_sums, swapped, own_branch,
    rows, wd, wq, vheads, datt, kt, dk, dv, dqt, gproj, part, pout, g1, mine_fc2, mine_fc1, gd, gq,
    result, stats_rows, stats_out, stats_in, mate_in, chips_in, y_in, z_in, vec_a, vec_b,
    stacks, late, late_two, late_group, late_y, late_z, places, probs, dscores, deltas,
    total, ring_in, ring_out, *rest,
):
    *rest, send, recv, near_sems = rest
    rest = list(rest)

    def take(count):
        taken = rest[:count]
        del rest[:count]
        return taken

    place = Place()
    row, z, y = place.row, place.z, place.y
    net, near = Net(send, recv), Near(near_sems)
    load_rows = near.copy(branch, rows)
    load_wd = near.copy(dense.at[pl.ds(2 * row, 2)], wd)
    load_heads = near.copy(heads, vheads)
    load_g1 = []
    reads = []
    for h, me in enumerate((z, y)):
        views = []
        for index, (pos, half) in enumerate(
            ((wrap(me + 1), 0), (wrap(me - 1), 1), (me, 0), (me, 1))
        ):
            pair = pl.ds(2 * half, 2)
            low = pl.ds(32, 32)
            source = (
                grad_fc1.at[0, pos, pair, low] if h == 0 else grad_fc1.at[1, pair, pos, low]
            )
            load_g1.append(near.copy(source, g1.at[h, index]))
            views.append(g1.at[h, index])
        reads.append(views)
    load_mid = [
        near.copy(mid.at[h, me], mine.at[h])
        for mid, mine in ((mid_fc2, mine_fc2), (mid_fc1, mine_fc1))
        for h, me in enumerate((y, z))
    ]
    load_out = near.copy(pairs_out.at[pl.ds(1, 3)], pout)
    load_wq = near.copy(qkv, wq)
    quarter = quarter_slices(place.chip, place.core)
    load_own = near.copy(
        branch.at[pl.ds(quarter[0], 256), pl.ds(quarter[1], HALF)], own_branch
    )
    load_own.start()
    load_rows.start()
    load_wd.start()
    load_heads.start()
    x_group = [
        place.x_at(wrap(place.chip + step), core)
        for step in range(4)
        for core in (place.core, 1 - place.core)
    ][1:]
    y_ring = [place.on_y(step) for step in (1, 2, 3)]
    z_ring = [place.on_z(step) for step in (1, 2, 3)]
    peers = x_group + y_ring + z_ring
    announce(peers)
    scatter = GroupScatter(net, place, part, quarter_slices, (256, HALF), total, ring_in)
    scatter_out = RingSum(net, place, pairs_out, pout, ring_out)
    rings_fc1, rings_dense, rings_qkv = take(2), take(2), take(2)
    mids_fc1, mids_dense, mids_qkv = take(2), take(2), take(2)
    out_fc1 = OuterScatter(
        net, place, stacked_rows(grad_fc1, 32), 32, rings_fc1, mids_fc1, reads
    )
    out_dense = OuterScatter(net, place, beside(gd, 32)[0], 32, rings_dense, mids_dense)
    out_qkv = OuterScatter(net, place, stacked(gq, 64)[0], 64, rings_qkv, mids_qkv)
    inner = []
    for mids, mine, final in (
        ([mid_fc2.at[h] for h in range(2)], [mine_fc2.at[h] for h in range(2)], rfc2),
        ([mid_fc1.at[h] for h in range(2)], [mine_fc1.at[h] for h in range(2)], rfc1),
        (mids_fc1, None, rfc1_b),
        (mids_dense, None, rdense),
        (mids_qkv, None, rqkv),
    ):
        arrived, done = take(2), take(1)[0]
        inner.append(InnerScatter(net, near, place, mids, mine, arrived, done, final))
    in_fc2, in_fc1_a, in_fc1, in_dense, in_qkv = inner
    vec_a[...] = jnp.zeros_like(vec_a)
    vec_a[2:4, :] = sums_two[0:2, :]
    vec_a[4:5, :] = sums_two[4:5, :]
    vec_a[5:6, :] = sums_two[2:3, :]
    vec_a[6:7, 0:HALF] = sums_two[3:4, 0:HALF]
    load_rows.wait()
    load_wd.wait()
    load_heads.wait()
    for load in load_g1 + load_mid:
        load.start()
    load_out.start()
    load_wq.start()

    def back_attended(index, carry):
        here = pl.ds(pl.multiple_of(index * 256, 256), 256)
        datt[here, :] = nt(rows[here, :], wd[...].reshape(LOCAL, WIDTH)).astype(BF16)
        return carry

    lax.fori_loop(0, 4, back_attended, 0)
    meet(peers)
    scatter_out.start()
    in_fc2.start()
    in_fc1_a.start()
    out_fc1.start()
    mate_send = net.copy(vec_a, mate_in, place.mate())
    mate_send.start()
    for side in range(2):
        half = slice(side * HALF, (side + 1) * HALF)
        made = tn(vheads[3], rows[:, half]).astype(BF16).reshape(2, 4, 32, HALF)
        gd[pl.ds(2 * row, 2), :, :, half] = made
        gd[pl.ds(2 - 2 * row, 2), :, :, half] = jnp.zeros_like(made)
    out_dense.start()
    for load in load_g1 + load_mid:
        load.wait()
    load_one = near.copy(rows_one, rows)
    load_one.start()
    kt[...] = vheads[1].T
    dk[...] = jnp.zeros_like(dk)
    dv[...] = jnp.zeros_like(dv)
    key_places(length[0], places)
    args = [vheads.at[index] for index in range(4)]
    args += [datt, logs, places, kt, dk, dv, dqt, probs, dscores, deltas]
    attend_back_block(0, *args)
    mate_send.wait_recv()
    vec_b[...] = vec_a[...]
    vec_b[2:6, :] += mate_in[2:6, :]
    chip_sends = [
        net.copy(vec_b, chips_in.at[step - 1], place.on_x(step)) for step in (1, 2, 3)
    ]
    for copy in chip_sends:
        copy.start()
    attend_back_block(1, *args)
    load_out.wait()
    scatter_out.second()
    attend_back_block(2, *args)
    mate_send.wait_send()
    for copy in chip_sends:
        copy.wait_recv()
    vec_a[...] = vec_b[...]
    for index in range(3):
        vec_a[2:6, :] += chips_in[index, 2:6, :]
    vec_a[7:8, :] = chips_in[1, 6:7, :]
    y_sends = [net.copy(vec_a, y_in.at[i], device) for i, device in enumerate(y_ring)]
    for copy in y_sends:
        copy.start()
    attend_back_block(3, *args)
    gproj[:, 0:256] = dqt[...].T * BF16(HEAD_DIM**-0.5)
    gproj[:, 256:512] = dk[...].astype(BF16)
    gproj[:, 512:768] = dv[...].astype(BF16)
    load_wq.wait()
    load_one.wait()
    columns = jnp.concatenate(
        [
            jnp.sum(gproj[:, third * 256 : third * 256 + 256].astype(F32), 0, keepdims=True)
            for third in range(3)
        ],
        1,
    )
    def one_gq(index, carry):
        side, piece = lax.div(index, 4), lax.rem(index, 4)
        cols = pl.ds(pl.multiple_of(index * 256, 256), 256)
        made = tn(rows[:, cols], gproj[...])
        gq[side, piece] = made.astype(BF16).reshape(4, 64, 768)
        return carry

    lax.fori_loop(0, 4, one_gq, 0)
    out_qkv.rings[0].start()
    lax.fori_loop(4, 8, one_gq, 0)
    out_qkv.rings[1].start()
    scatter_out.arrive()
    for side in range(2):

        def finish_rows(pos, side=side):
            here = pl.ds(pl.multiple_of(pos + 64 * side, 16), 16)
            result[here, :] = (
                residual[here, :] + scatter_out.result(side, pos) + vectors[1:2, :]
            ).astype(BF16)

        sweep(64, 16, finish_rows)
    there = pl.ds(row * 128, 128)
    out_swap = net.copy(
        result.at[:, pl.ds((1 - row) * HALF, HALF)], out.at[there, :], place.partner()
    )
    out_keep = near.copy(result.at[:, pl.ds(row * HALF, HALF)], out.at[there, :])
    out_swap.start()
    out_keep.start()
    for index, chip in enumerate(scatter.order):
        here = pl.ds(pl.multiple_of(lax.rem(chip, 2) * 512, 512), 512)
        cols = pl.ds(pl.multiple_of(lax.div(chip, 2) * HALF, HALF), HALF)
        weight = wq[lax.div(chip, 2)].reshape(HALF, 768)
        part[here, cols] = nt(gproj[here, :], weight).astype(BF16)
        scatter.mates[index].start()
        if index > 0:
            scatter.first(index - 1)
    out_fc1.middle()
    out_dense.middle()
    lane = lax.broadcasted_iota(jnp.int32, (256, 128), 1)
    stacks[...] = jnp.zeros_like(stacks)

    def one_stack(index, carry):
        side, piece = lax.div(index, 4), lax.rem(index, 4)
        weight = wq[side, piece].reshape(256, 768).astype(F32)
        made = gq[side, piece].reshape(256, 768).astype(F32)
        stacks[...] += jnp.where(
            lane == index, jnp.sum(weight * made, 1, keepdims=True), 0.0
        ) + jnp.where(lane == index + 8, jnp.sum(weight * columns, 1, keepdims=True), 0.0)
        return carry

    lax.fori_loop(0, 8, one_stack, 0)
    late[...] = jnp.zeros_like(late)
    late[0:16, :] = stacks[...].T[0:16, :]
    late[16:17, :] = columns[:, 0:256]
    late[17:18, :] = columns[:, 512:768]
    late_x_sends = [
        net.copy(late, late_group.at[index], device) for index, device in enumerate(x_group)
    ]
    for copy in late_x_sends:
        copy.start()
    out_qkv.middle()
    scatter.second()
    out_fc1.finish()
    in_fc1.start()
    out_dense.finish()
    in_dense.start()
    for copy in y_sends:
        copy.wait_recv()
    for copy in chip_sends:
        copy.wait_send()
    vec_b[...] = vec_a[...]
    for index in range(3):
        vec_b[...] += y_in[index]
    z_sends = [net.copy(vec_b, z_in.at[i], device) for i, device in enumerate(z_ring)]
    for copy in z_sends:
        copy.start()
    out_qkv.finish()
    in_qkv.start()
    for copy in late_x_sends:
        copy.wait_recv()
    late_two[...] = late[...]
    for index in range(7):
        late_two[0:16, :] += late_group[index, 0:16, :]
    late_two[18:20, :] = late_group[3, 16:18, :]
    late_y_sends = [
        net.copy(late_two, late_y.at[i], device) for i, device in enumerate(y_ring)
    ]
    for copy in late_y_sends:
        copy.start()
    in_fc2.finish()
    in_fc1_a.finish()
    scatter.arrive()

    lane = lax.broadcasted_iota(jnp.int32, (16, 128), 1)
    for side in range(2):

        def sums(pos, side=side):
            here = pl.ds(pl.multiple_of(pos + 128 * side, 16), 16)
            arrived = scatter.result(side, pos)
            scaled = arrived * gain[...]
            xhat = (x[here, :].astype(F32) - stats[here, 0:1]) * stats[here, 1:2]
            flat = jnp.sum(scaled, 1, keepdims=True)
            cross = jnp.sum(scaled * xhat, 1, keepdims=True)
            stats_rows[here, :] = jnp.where(lane == 0, flat, cross)
            raw[here, :] = arrived

        sweep(128, 16, sums, 4)
    stats_out[...] = stats_rows[...].T[0:8, :]
    swap_stats = net.copy(stats_out, stats_in, place.partner())
    swap_stats.start()
    in_qkv.finish()
    for copy in late_y_sends:
        copy.wait_recv()
    for copy in late_x_sends:
        copy.wait_send()
    late[...] = late_two[...]
    for index in range(3):
        late[...] += late_y[index]
    late_z_sends = [net.copy(late, late_z.at[i], device) for i, device in enumerate(z_ring)]
    for copy in late_z_sends:
        copy.start()
    in_fc1.finish()
    in_dense.finish()
    swap_stats.wait_recv()
    swapped[...] = stats_out[...] + stats_in[...]
    for copy in z_sends + late_z_sends:
        copy.wait_recv()
    vector[...] = vec_b[...]
    first_sums[...] = late[...]
    for index in range(3):
        vector[...] += z_in[index]
        first_sums[...] += late_z[index]
    load_own.wait()
    out_swap.wait_recv()
    for stage in (out_fc1, out_dense, out_qkv):
        stage.drain()
    for stage in inner:
        stage.close()
    out_keep.wait()
    out_swap.wait_send()
    swap_stats.wait_send()
    for copy in y_sends + late_y_sends + z_sends + late_z_sends:
        copy.wait_send()
    scatter.drain()
    scatter_out.drain()


def last(*args):
    bf = lambda *shape: jax.ShapeDtypeStruct(shape, BF16)
    full = lambda *shape: jax.ShapeDtypeStruct(shape, F32)
    anywhere, inside = any_specs(1)[0], vmem_specs(1)[0]
    where = (
        [pl.BlockSpec(memory_space=pltpu.SMEM), inside, inside]
        + [anywhere] * 4
        + [inside]
        + [anywhere] * 5
        + [inside] * 4
    )
    return pl.pallas_call(
        last_kernel,
        out_shape=(
            full(256, HALF),
            bf(256, HALF),
            bf(2, 64, 768),
            bf(2, 32, 1024),
            bf(2, 32, 1024),
            bf(2, 32, 1024),
            bf(2, 64, 1024),
            full(8, WIDTH),
            full(24, 256),
            full(8, 256),
            bf(256, HALF),
        ),
        in_specs=where,
        out_specs=tuple(vmem_specs(10) + any_specs(1)),
        scratch_shapes=[
            pltpu.VMEM((SEQ, WIDTH), BF16),
            pltpu.VMEM((2, 4, 32, WIDTH), BF16),
            pltpu.VMEM((2, 4, 4, 64, 768), BF16),
            pltpu.VMEM((4, SEQ, LOCAL), BF16),
            pltpu.VMEM((SEQ, LOCAL), BF16),
            pltpu.VMEM((LOCAL, SEQ), BF16),
            pltpu.VMEM((SEQ, LOCAL), F32),
            pltpu.VMEM((SEQ, LOCAL), F32),
            pltpu.VMEM((LOCAL, SEQ), BF16),
            pltpu.VMEM((SEQ, 768), BF16),
            pltpu.VMEM((SEQ, WIDTH), BF16),
            pltpu.VMEM((3, 128, WIDTH), BF16),
            pltpu.VMEM((2, 4, 2, 32, 1024), BF16),
            pltpu.VMEM((2, 64, 1024), BF16),
            pltpu.VMEM((2, 32, 1024), BF16),
            pltpu.VMEM((4, 4, 32, 2048), BF16),
            pltpu.VMEM((2, 4, 4, 64, 768), BF16),
            pltpu.VMEM((128, WIDTH), BF16),
            pltpu.VMEM((256, 128), F32),
            pltpu.VMEM((8, 256), F32),
            pltpu.VMEM((8, 256), F32),
            pltpu.VMEM((8, WIDTH), F32),
            pltpu.VMEM((3, 8, WIDTH), F32),
            pltpu.VMEM((3, 8, WIDTH), F32),
            pltpu.VMEM((3, 8, WIDTH), F32),
            pltpu.VMEM((8, WIDTH), F32),
            pltpu.VMEM((8, WIDTH), F32),
            pltpu.VMEM((256, 128), F32),
            pltpu.VMEM((24, 256), F32),
            pltpu.VMEM((24, 256), F32),
            pltpu.VMEM((7, 24, 256), F32),
            pltpu.VMEM((3, 24, 256), F32),
            pltpu.VMEM((3, 24, 256), F32),
            pltpu.VMEM((SEQ, 128), F32),
            pltpu.VMEM((SEQ, 2 * BLOCK), BF16),
            pltpu.VMEM((SEQ, 2 * BLOCK), BF16),
            pltpu.VMEM((4, 1, BLOCK), F32),
        ]
        + scatter_scratch(256, HALF)
        + [pltpu.VMEM((6, 64, WIDTH), BF16)]
        + outer_scratch(32, 1024)
        + outer_scratch(32, 1024)
        + outer_scratch(64, 768)
        + mid_scratch(32, 1024)
        + mid_scratch(32, 1024)
        + mid_scratch(64, 768)
        + inner_scratch(64, 1024)
        + inner_scratch(32, 1024)
        + inner_scratch(32, 1024)
        + inner_scratch(32, 1024)
        + inner_scratch(64, 768)
        + sem_arrays(20 + 3 * 12 + 5 * 7 + 30, 32),
        compiler_params=comm_params(3, 62),
        name="last",
    )(*args)


def finish_kernel(
    raw, rows_out, rqkv, rdense, rfc1, rfc1_b, rfc2, vector, first_sums, swapped, own_branch,
    x, stats, gain, offset,
    outputs, ingrad, qkv, query, value, dense, dense_add, fc1, hidden_add, fc2, output_add,
    gain_one, offset_one, gain_two, offset_two, turned,
):
    row = lax.axis_index("row")
    dp = lax.axis_index("dp")
    outputs[...] = rows_out[...]
    turned[...] = jnp.concatenate([swapped[...], jnp.zeros((120, 256), F32)], 0).T

    def apply(pos):
        here = pl.ds(pos, 16)
        both = turned[here, :] / WIDTH
        scale = stats[here, 1:2]
        xhat = (x[here, :].astype(F32) - stats[here, 0:1]) * scale
        ingrad[here, :] = own_branch[here, :].astype(F32) + scale * (
            raw[here, :] * gain[...] - both[:, 0:1] - xhat * both[:, 1:2]
        )

    sweep(256, 16, apply, 4)
    for index in range(12):
        made = []
        for block in (2 * index, 2 * index + 1):
            head, third = block // 3, block % 3
            place_in = third * 4 + head % 4
            made.append((group_of(rqkv.at[head // 4], place_in // 2), place_in % 2))
        (left, left_odd), (right, right_odd) = made
        qkv[:, index * 128 : index * 128 + 128] = merge(
            left, right, left_odd == 1, right_odd == 0
        )
    for index in range(16):
        for side, source in enumerate((rfc1, rfc1_b)):
            fc1[side * 32 : side * 32 + 32, index * 128 : index * 128 + 128] = merge(
                group_of(source.at[0], index // 2),
                group_of(source.at[1], index // 2),
                index % 2 == 1,
                index % 2 == 0,
            )
    fc2[0:64, :] = rfc2[0].astype(F32)
    fc2[64:128, :] = rfc2[1].astype(F32)
    dense[...] = rdense[0].astype(F32) + rdense[1].astype(F32)
    for index in range(4):
        cols = slice(index * 256, index * 256 + 256)
        products = first_sums[pl.ds(row * 4 + index, 1), :]
        plain = first_sums[pl.ds(row * 4 + index + 8, 1), :]
        gain_one[:, cols] = (products - offset[:, cols] * plain) / gain[:, cols]
        offset_one[:, cols] = plain
    half = pl.ds(pl.multiple_of(row * HALF, HALF), HALF)
    gain_two[...] = vector[2:3, half]
    offset_two[...] = vector[3:4, half]
    odd = lax.rem(dp, 2)
    start = lax.div(dp, 2) * 128

    def swap_if(values, swap):
        return jnp.where(swap == 1, pltpu.roll(values, 64, 1), values)

    def eight(line, lane):
        return vector[line : line + 1, pl.ds(pl.multiple_of(lane, 128), 128)] + jnp.zeros(
            (8, 128), F32
        )

    dense_add[...] = swap_if(eight(4, row * HALF + start), odd)[0:1, 0:64]
    output_add[...] = swap_if(eight(5, row * HALF + start), odd)[0:1, 0:64]
    own, other = eight(6, start), eight(7, start)
    first = jnp.where(row == 0, own, other)
    second = jnp.where(row == 0, other, own)
    lanes = lax.broadcasted_iota(jnp.int32, (8, 128), 1)
    hidden_add[...] = jnp.where(
        lanes < 64, swap_if(first, odd), swap_if(second, 1 - odd)
    )[0:1, :]
    theirs = lax.div(dp, 8) == row
    inside = lax.rem(dp, 8)
    quarter = lax.rem(inside, 4)
    upper = lax.div(inside, 4) == 1
    for target, base in ((query, 16), (value, 17)):
        lines = [
            first_sums[at : at + 1, lanes_from : lanes_from + 128]
            + jnp.zeros((8, 128), F32)
            for at in (base, base + 2)
            for lanes_from in (0, 128)
        ]
        mine = jnp.where(upper, lines[1], lines[0])
        other = jnp.where(upper, lines[3], lines[2])
        chosen = jnp.where(theirs, mine, other)
        moved = chosen
        for step in range(1, 4):
            moved = jnp.where(quarter == step, pltpu.roll(chosen, 128 - 32 * step, 1), moved)
        target[...] = moved[0:1, 0:32]


def finish(*args):
    full = lambda *shape: jax.ShapeDtypeStruct(shape, F32)
    whole = lambda shape: pl.BlockSpec(shape, lambda index: (0,) * len(shape))
    shapes = (
            jax.ShapeDtypeStruct((256, HALF), BF16),
            full(256, HALF),
            full(64, 1536),
            full(1, 32),
            full(1, 32),
            full(32, 1024),
            full(1, 64),
            full(64, 2048),
            full(1, 128),
            full(128, HALF),
            full(1, 64),
            full(1, HALF),
            full(1, HALF),
            full(1, HALF),
            full(1, HALF),
        )
    return pl.pallas_call(
        finish_kernel,
        out_shape=shapes,
        grid=(1,),
        in_specs=[whole(value.shape) for value in args],
        out_specs=tuple(whole(value.shape) for value in shapes),
        scratch_shapes=[pltpu.VMEM((256, 128), F32)],
        compiler_params=pltpu.CompilerParams(vmem_limit_bytes=62 << 20),
        name="finish",
    )(*args)


def local(
    inputs,
    cotangent,
    lengths,
    attention_norm_gain,
    attention_norm_bias,
    qkv_weight,
    query_bias,
    value_bias,
    dense_weight,
    dense_bias,
    feedforward_norm_gain,
    feedforward_norm_bias,
    fc1_weight,
    fc1_bias,
    fc2_weight,
    fc2_bias,
):
    zeros = jnp.zeros((64,), BF16)
    small = jnp.concatenate(
        [fc1_bias, query_bias, value_bias, dense_bias, fc2_bias, zeros]
    ).astype(F32)
    (
        rows_cot, qkv_full, dense_full, fc1_full, fc2_full, rows_one, rows_two, heads,
        logs, residual, stats, vectors, grad_act,
    ) = forward(
        lengths,
        inputs,
        cotangent,
        qkv_weight,
        dense_weight,
        fc1_weight,
        fc2_weight.reshape(2, 64, 1024),
        small.reshape(1, 384),
        attention_norm_gain.reshape(1, HALF),
        attention_norm_bias.reshape(1, HALF),
        feedforward_norm_gain.reshape(1, HALF),
        feedforward_norm_bias.reshape(1, HALF),
    )
    rows_branch, pairs_out, grad_fc1, mid_fc2, mid_fc1, sums_two = turn(
        rows_two, fc1_full, fc2_full, rows_cot, grad_act, residual, vectors
    )
    (
        raw, rows_out, red_qkv, red_dense, red_fc1, red_fc1_b, red_fc2, vector,
        first_sums, swapped, own_branch,
    ) = last(
        lengths, inputs, stats, rows_branch, dense_full, qkv_full, heads, logs, rows_one,
        pairs_out, grad_fc1, mid_fc2, mid_fc1, attention_norm_gain.reshape(1, HALF), residual, vectors,
        sums_two,
    )
    results = finish(
        raw, rows_out, red_qkv, red_dense, red_fc1, red_fc1_b, red_fc2, vector,
        first_sums, swapped, own_branch,
        inputs, stats, attention_norm_gain.reshape(1, HALF),
        attention_norm_bias.reshape(1, HALF),
    )
    return tuple(
        value.reshape(value.shape[1]) if value.shape[0] == 1 else value
        for value in results
    )


def solution(mesh):
    return jax.shard_map(
        local,
        mesh=mesh,
        in_specs=(
            P(("dp", "col"), "row"),
            P(("dp", "col"), "row"),
            P("dp"),
            P("row"),
            P("row"),
            P(("row", "dp"), "col"),
            P(("col", "dp")),
            P(("col", "dp")),
            P(("col", "dp"), "row"),
            P(("row", "dp")),
            P("row"),
            P("row"),
            P(("row", "dp"), "col"),
            P(("col", "dp")),
            P(("col", "dp"), "row"),
            P(("row", "dp")),
        ),
        out_specs=(
            P(("dp", "col"), "row"),
            P(("dp", "col"), "row"),
            P(("row", "dp"), "col"),
            P(("col", "dp")),
            P(("col", "dp")),
            P(("col", "dp"), "row"),
            P(("row", "dp")),
            P(("row", "dp"), "col"),
            P(("col", "dp")),
            P(("col", "dp"), "row"),
            P(("row", "dp")),
            P("row"),
            P("row"),
            P("row"),
            P("row"),
        ),
        check_vma=False,
    )
```

```python
import jax
import jax.numpy as jnp
from jax import lax
from jax.experimental import pallas as pl
from jax.experimental.pallas import tpu as pltpu
from jax.sharding import PartitionSpec as P

HEADS = 32
HEAD_DIM = 64
BLOCK = 256
SEQ = 1024
WIDTH = 2048
HALF = WIDTH // 2
LOCAL = 256
EPSILON = 1e-05
FAR = 1e30
MESH = pl.DeviceIdType.MESH
F32 = jnp.float32
BF16 = jnp.bfloat16


def wrap(position):
    return lax.rem(position + 4, 4)


class Place:
    def __init__(self):
        self.row = lax.axis_index("row")
        self.col = lax.axis_index("col")
        self.dp = lax.axis_index("dp")
        self.chip = self.row * 2 + lax.div(self.col, 2)
        self.core = lax.rem(self.col, 2)
        self.z = lax.div(self.dp, 4)
        self.y = lax.rem(self.dp, 4)

    def on_x(self, step):
        return self.x_at(wrap(self.chip + step), self.core)

    def x_at(self, chip, core):
        return {"row": lax.div(chip, 2), "col": lax.rem(chip, 2) * 2 + core}

    def on_y(self, step):
        return {"dp": self.z * 4 + wrap(self.y + step)}

    def on_z(self, step):
        return {"dp": wrap(self.z + step) * 4 + self.y}

    def partner(self):
        return {"row": 1 - self.row}

    def mate(self):
        return {"col": lax.div(self.col, 2) * 2 + 1 - self.core}


class Net:
    def __init__(self, send, recv):
        self.send, self.recv, self.used = send, recv, 0

    def copy(self, source, target, device):
        slot = self.used
        self.used += 1
        return pltpu.make_async_remote_copy(
            src_ref=source,
            dst_ref=target,
            send_sem=self.send.at[slot],
            recv_sem=self.recv.at[slot],
            device_id=device,
            device_id_type=MESH,
        )


class Near:
    def __init__(self, sems):
        self.sems, self.used = sems, 0

    def copy(self, source, target):
        slot = self.used
        self.used += 1
        return pltpu.make_async_copy(source, target, self.sems.at[slot])


def announce(devices):
    barrier = pltpu.get_barrier_semaphore()
    for device in devices:
        pl.semaphore_signal(barrier, inc=1, device_id=device, device_id_type=MESH)


def meet(devices):
    pl.semaphore_wait(pltpu.get_barrier_semaphore(), len(devices))


class RingGather:
    def __init__(self, net, block, me, right, left, own=None):
        before, after = wrap(me - 1), wrap(me + 1)
        own = own or (lambda half: block(me, half))
        self.first = [
            net.copy(own(0), block(me, 0), right),
            net.copy(own(1), block(me, 1), left),
        ]
        self.second = [
            net.copy(own(1), block(me, 1), right),
            net.copy(own(0), block(me, 0), left),
        ]
        self.passed = [
            net.copy(block(before, 0), block(before, 0), right),
            net.copy(block(after, 1), block(after, 1), left),
        ]

    def start(self):
        for copy in self.first + self.second:
            copy.start()

    def forward(self):
        for came, on in zip(self.first, self.passed):
            came.wait_recv()
            on.start()

    def near_done(self):
        for copy in self.second:
            copy.wait_recv()

    def far_done(self):
        for copy in self.passed:
            copy.wait_recv()

    def drain(self):
        for copy in self.first + self.second + self.passed:
            copy.wait_send()


class DirectGather:
    def __init__(self, net, own, target, devices):
        self.sends = [net.copy(own, target, device) for device in devices]

    def start(self):
        for copy in self.sends:
            copy.start()

    def forward(self):
        pass

    def near_done(self):
        for copy in self.sends:
            copy.wait_recv()

    def far_done(self):
        pass

    def drain(self):
        for copy in self.sends:
            copy.wait_send()


class GroupGather:
    def __init__(self, net, place, block, own):
        core, chip = place.core, place.chip
        self.ring = RingGather(
            net,
            lambda position, half: block(position, core, half),
            chip,
            place.on_x(1),
            place.on_x(-1),
            own,
        )
        whole = [
            own(None),
            block(wrap(chip - 1), core, None),
            block(wrap(chip + 1), core, None),
            block(wrap(chip + 2), core, None),
        ]
        target = [block(chip, core, None)] + whole[1:]
        self.mates = [
            net.copy(source, there, place.mate()) for source, there in zip(whole, target)
        ]

    def start(self):
        self.ring.start()
        self.mates[0].start()

    def forward(self):
        self.ring.forward()

    def share(self):
        self.ring.near_done()
        self.mates[1].start()
        self.mates[2].start()

    def near_finish(self):
        for copy in self.mates[1:3]:
            copy.wait_recv()

    def finish(self):
        self.ring.far_done()
        self.mates[3].start()
        for copy in (self.mates[0], self.mates[3]):
            copy.wait_recv()
        self.ring.drain()
        for copy in self.mates:
            copy.wait_send()


def sweep(rows, step, body, unroll=2):
    def one(index, carry):
        body(pl.multiple_of(index * step, step))
        return carry

    lax.fori_loop(0, rows // step, one, 0, unroll=unroll)


class GroupScatter:
    def __init__(self, net, place, part, slices, shape, total, ring_in):
        self.part, self.slices, self.place = part, slices, place
        self.rows, self.cols = shape
        self.total, self.ring_in = total, ring_in
        chip = place.chip
        half = self.rows // 2
        self.half = half
        self.order = [wrap(chip + 2), wrap(chip + 1), wrap(chip - 1), chip]
        mate = place.mate()
        self.mates = []
        for index, there in enumerate(self.order):
            rows, cols = slices(there, 1 - place.core)
            self.mates.append(
                net.copy(
                    part.at[pl.ds(rows, self.rows), pl.ds(cols, self.cols)],
                    total.at[index],
                    mate,
                )
            )
        right, left = place.on_x(1), place.on_x(-1)
        top, low = pl.ds(0, half), pl.ds(half, half)
        self.sends = [
            net.copy(total.at[0, top], ring_in.at[0], right),
            net.copy(total.at[0, low], ring_in.at[1], left),
            net.copy(total.at[1, low], ring_in.at[2], right),
            net.copy(total.at[2, top], ring_in.at[3], left),
            net.copy(ring_in.at[0], ring_in.at[4], right),
            net.copy(ring_in.at[1], ring_in.at[5], left),
        ]

    def start(self):
        for copy in self.mates:
            copy.start()

    def mine(self, index, row, step):
        rows, cols = self.slices(self.order[index], self.place.core)
        return self.part[
            pl.ds(pl.multiple_of(rows + row, 16), step), pl.ds(cols, self.cols)
        ].astype(F32)

    def first(self, *indices):
        for index in indices:
            self.mates[index].wait_recv()

            def add(row, index=index):
                here = pl.ds(row, 16)
                self.total[index, here, :] = (
                    self.mine(index, row, 16) + self.total[index, here, :].astype(F32)
                ).astype(BF16)

            sweep(self.rows, 16, add)
            if index == 0:
                self.sends[0].start()
                self.sends[1].start()
            else:
                self.sends[index + 1].start()

    def second(self):
        for side in range(2):
            self.sends[side].wait_recv()

            def add(row, side=side):
                here = pl.ds(row, 16)
                there = pl.ds(pl.multiple_of(row + side * self.half, 16), 16)
                self.ring_in[side, here, :] = (
                    self.total[1 + side, there, :].astype(F32)
                    + self.ring_in[side, here, :].astype(F32)
                ).astype(BF16)

            sweep(self.half, 16, add)
            self.sends[4 + side].start()

    def arrive(self):
        self.mates[3].wait_recv()
        for index in range(2, 6):
            self.sends[index].wait_recv()

    def result(self, side, row):
        here = pl.ds(row, 16)
        there = pl.multiple_of(row + side * self.half, 16)
        one, two = ((4, 3), (2, 5))[side]
        return (
            self.mine(3, there, 16)
            + self.total[3, pl.ds(there, 16), :].astype(F32)
            + self.ring_in[one, here, :].astype(F32)
            + self.ring_in[two, here, :].astype(F32)
        )

    def drain(self):
        for copy in self.mates + self.sends:
            copy.wait_send()


class PairSum:
    def __init__(self, net, place, part, total):
        self.part, self.place, self.total = part, place, total
        chip = place.chip
        self.order = [wrap(chip + 2), wrap(chip + 1), wrap(chip - 1), chip]
        self.mates = [
            net.copy(
                part.at[pl.ds(rows_of(there, 1 - place.core), 128), :],
                total.at[index],
                place.mate(),
            )
            for index, there in enumerate(self.order)
        ]

    def start(self):
        for copy in self.mates:
            copy.start()

    def finish(self):
        for index, there in enumerate(self.order):
            self.mates[index].wait_recv()
            start = rows_of(there, self.place.core)

            def add(row, index=index, start=start):
                here = pl.ds(row, 16)
                there = pl.ds(pl.multiple_of(start + row, 16), 16)
                self.total[index, here, :] = (
                    self.part[there, :].astype(F32)
                    + self.total[index, here, :].astype(F32)
                ).astype(BF16)

            sweep(128, 16, add)

    def drain(self):
        for copy in self.mates:
            copy.wait_send()


class RingSum:
    def __init__(self, net, place, pairs, near, ring_in):
        self.near, self.ring_in = near, ring_in
        right, left = place.on_x(1), place.on_x(-1)
        top, low = pl.ds(0, 64), pl.ds(64, 64)
        self.sends = [
            net.copy(pairs.at[0, top], ring_in.at[0], right),
            net.copy(pairs.at[0, low], ring_in.at[1], left),
            net.copy(pairs.at[1, low], ring_in.at[2], right),
            net.copy(pairs.at[2, top], ring_in.at[3], left),
            net.copy(ring_in.at[0], ring_in.at[4], right),
            net.copy(ring_in.at[1], ring_in.at[5], left),
        ]

    def start(self):
        for copy in self.sends[:4]:
            copy.start()

    def second(self):
        for side in range(2):
            self.sends[side].wait_recv()

            def add(row, side=side):
                here = pl.ds(row, 16)
                there = pl.ds(pl.multiple_of(row + side * 64, 16), 16)
                self.ring_in[side, here, :] = (
                    self.near[side, there, :].astype(F32)
                    + self.ring_in[side, here, :].astype(F32)
                ).astype(BF16)

            sweep(64, 16, add)
            self.sends[4 + side].start()

    def arrive(self):
        for copy in self.sends[2:]:
            copy.wait_recv()

    def result(self, side, row):
        here = pl.ds(row, 16)
        there = pl.ds(pl.multiple_of(row + side * 64, 16), 16)
        one, two = ((4, 3), (2, 5))[side]
        return (
            self.near[2, there, :].astype(F32)
            + self.ring_in[one, here, :].astype(F32)
            + self.ring_in[two, here, :].astype(F32)
        )

    def drain(self):
        for copy in self.sends:
            copy.wait_send()


def scatter_scratch(rows, cols):
    return [
        pltpu.VMEM((4, rows, cols), BF16),
        pltpu.VMEM((6, rows // 2, cols), BF16),
    ]


def add_rows(target, sources):
    shape = target.shape
    if len(shape) == 3:
        for index in range(shape[0]):
            add_rows(target.at[index], [source.at[index] for source in sources])
        return

    def one(row):
        here = pl.ds(row, 16)
        total = sources[0][here, :].astype(F32)
        for source in sources[1:]:
            total = total + source[here, :].astype(F32)
        target[here, :] = total.astype(BF16)

    sweep(shape[0], 16, one)


class RingScatter:
    def __init__(self, net, part, me, right, left, ring_in, target, read=None):
        before, after, across = wrap(me - 1), wrap(me + 1), wrap(me + 2)
        self.read = read or [part(after, 0), part(before, 1), part(me, 0), part(me, 1)]
        self.ring_in, self.target = ring_in, target
        self.sends = [
            net.copy(part(across, 0), ring_in.at[0], right),
            net.copy(part(across, 1), ring_in.at[1], left),
            net.copy(part(after, 1), ring_in.at[2], right),
            net.copy(part(before, 0), ring_in.at[3], left),
            net.copy(ring_in.at[0], ring_in.at[4], right),
            net.copy(ring_in.at[1], ring_in.at[5], left),
        ]

    def start(self):
        for copy in self.sends[:4]:
            copy.start()

    def middle(self):
        for side in range(2):
            self.sends[side].wait_recv()
            add_rows(
                self.ring_in.at[side], [self.read[side], self.ring_in.at[side]]
            )
            self.sends[4 + side].start()

    def finish(self):
        for index in range(2, 6):
            self.sends[index].wait_recv()
        for side, (one, two) in enumerate(((4, 3), (2, 5))):
            add_rows(
                self.target(side),
                [self.read[2 + side], self.ring_in.at[one], self.ring_in.at[two]],
            )

    def drain(self):
        for copy in self.sends:
            copy.wait_send()


def stacked_rows(ref, first):
    def at(part, z, y, rows):
        return ref.at[part, z, y, pl.ds(first + rows.start, rows.size), :]

    return at


class DirectScatter:
    def __init__(self, net, part, me, devices, arrived, target, mine=None):
        self.arrived, self.target = arrived, target
        self.mine = part(me) if mine is None else mine
        self.sends = [
            net.copy(part(wrap(me + step)), arrived.at[index], device)
            for index, (step, device) in enumerate(zip((1, 3, 2), devices))
        ]

    def start(self):
        for copy in self.sends:
            copy.start()

    def finish(self):
        for copy in self.sends:
            copy.wait_recv()
        add_rows(
            self.target, [self.mine] + [self.arrived.at[index] for index in range(3)]
        )

    def drain(self):
        for copy in self.sends:
            copy.wait_send()


class OuterScatter:
    def __init__(self, net, place, at, size, rings, mids, reads=None):
        z, y = place.z, place.y
        self.rings = []
        for h in range(2):

            def along_z(pos, half, h=h):
                return at(h, pos, pl.ds(2 * half, 2), pl.ds(0, size))

            def along_y(pos, half, h=h):
                return at(h, pl.ds(2 * half, 2), pos, pl.ds(0, size))

            def mid_half(half, h=h):
                return mids[h].at[pl.ds(2 * half, 2)]

            outer = (
                (along_z, z, place.on_z(1), place.on_z(-1))
                if h == 0
                else (along_y, y, place.on_y(1), place.on_y(-1))
            )
            read = reads[h] if reads else None
            self.rings.append(RingScatter(net, *outer, rings[h], mid_half, read))

    def start(self):
        for ring in self.rings:
            ring.start()

    def middle(self):
        for ring in self.rings:
            ring.middle()

    def finish(self):
        for ring in self.rings:
            ring.finish()

    def drain(self):
        for ring in self.rings:
            ring.drain()


class InnerScatter:
    def __init__(self, net, near, place, mids, mine, arrived, done, final):
        row, z, y = place.row, place.z, place.y
        over_y = [place.on_y(step) for step in (1, 3, 2)]
        over_z = [place.on_z(step) for step in (1, 3, 2)]
        self.stages = []
        for h in range(2):
            me, devices = (y, over_y) if h == 0 else (z, over_z)
            self.stages.append(
                DirectScatter(
                    net,
                    lambda pos, mid=mids[h]: mid.at[pos],
                    me,
                    devices,
                    arrived[h],
                    done.at[h],
                    mine[h] if mine else None,
                )
            )
        self.swap = net.copy(done.at[1 - row], final.at[row], place.partner())
        self.keep = near.copy(done.at[row], final.at[row])

    def start(self):
        for stage in self.stages:
            stage.start()

    def finish(self):
        for stage in self.stages:
            stage.finish()
        self.swap.start()
        self.keep.start()

    def close(self):
        self.swap.wait_recv()
        self.keep.wait()
        self.swap.wait_send()
        for stage in self.stages:
            stage.drain()


def outer_scratch(size, cols):
    return [pltpu.VMEM((6, 2, size, cols), BF16)] * 2


def mid_scratch(size, cols):
    return [pltpu.VMEM((4, size, cols), BF16)] * 2


def inner_scratch(size, cols):
    return [pltpu.VMEM((3, size, cols), BF16)] * 2 + [pltpu.VMEM((2, size, cols), BF16)]


def any_specs(count):
    return [pl.BlockSpec(memory_space=pl.ANY)] * count


def vmem_specs(count):
    return [pl.BlockSpec(memory_space=pltpu.VMEM)] * count


def sem_arrays(remote, near=0):
    arrays = [pltpu.SemaphoreType.DMA((remote,)), pltpu.SemaphoreType.DMA((remote,))]
    if near:
        arrays.append(pltpu.SemaphoreType.DMA((near,)))
    return arrays


def comm_params(identity, megabytes=60):
    return pltpu.CompilerParams(
        collective_id=identity, has_side_effects=True, vmem_limit_bytes=megabytes << 20
    )


def quarter_block(ref):
    def block(chip, core, half):
        rows = (lax.rem(chip, 2) * 2 + core) * 256
        cols = lax.div(chip, 2) * HALF
        if half is None:
            return ref.at[pl.ds(rows, 256), pl.ds(cols, HALF)]
        return ref.at[pl.ds(rows + 128 * half, 128), pl.ds(cols, HALF)]

    return block


def rows_of(chip, core):
    return (lax.rem(chip, 2) * 2 + core) * 256 + lax.div(chip, 2) * 128


def row_block(ref):
    def block(chip, core, half):
        rows = rows_of(chip, core)
        if half is None:
            return ref.at[pl.ds(rows, 128), :]
        return ref.at[pl.ds(rows + 64 * half, 64), :]

    return block


def row_slices(chip, core):
    return rows_of(chip, core), 0


def quarter_slices(chip, core):
    return (lax.rem(chip, 2) * 2 + core) * 256, lax.div(chip, 2) * HALF


def stacked(ref, size):
    def at(part, z, y, rows):
        return ref.at[part, z, y, rows, :]

    return at, size


def beside(ref, size):
    def at(part, z, y, rows):
        return ref.at[z, y, rows, pl.ds(part * HALF, HALF)]

    return at, size


def head_mask(values, head):
    lane = lax.broadcasted_iota(jnp.int32, values.shape, 1)
    return jnp.where(lax.div(lane, HEAD_DIM) == head, values, jnp.zeros_like(values))


def key_places(length, places):
    key = lax.broadcasted_iota(jnp.int32, places.shape, 0)
    places[...] = jnp.where(key < length, key.astype(F32), FAR)


def penalties(places, rows, start, slope):
    here = places[rows, :]
    query = (lax.broadcasted_iota(jnp.int32, (1, BLOCK), 1) + start).astype(F32)
    return slope * jnp.abs(query - jnp.concatenate([here, here], 1))


def fold(values, combine):
    return combine(values.reshape(16, 8, BLOCK), 0)


def slope_of(head):
    base = lax.axis_index("col") * 8 + lax.axis_index("row") * 4
    number = (base + head + 1).astype(F32)
    return jnp.exp2(jnp.full((1, BLOCK), -8.0 / HEADS, F32) * number)


def nt(left, right):
    return lax.dot_general(left, right, (((1,), (1,)), ((), ())), preferred_element_type=F32)


def nn(left, right):
    return jnp.dot(left, right, preferred_element_type=F32)


def attend_back_block(
    block, q, k, v, attended, grad, logs, places, kt, dk, dv, dqt, probs, dscores, deltas
):
    start, keys = block * BLOCK, (block + 1) * BLOCK
    here = pl.ds(start, BLOCK)
    inner = (grad[here, :].astype(F32) * attended[here, :].astype(F32)).T
    for head in range(4):
        lines = slice(head * HEAD_DIM, (head + 1) * HEAD_DIM)
        deltas[head] = jnp.sum(inner[lines, :], 0, keepdims=True)

    def pair(index, carry):
        heads = (2 * index, 2 * index + 1)
        for side, head in enumerate(heads):
            cols = slice(side * BLOCK, (side + 1) * BLOCK)
            slope, log, delta = slope_of(head), logs[head, :, here], deltas[head]
            for chunk in range(keys // 128):
                rows = slice(chunk * 128, (chunk + 1) * 128)
                scores = nt(head_mask(k[rows, :], head), q[here, :])
                prob = jnp.exp(scores - penalties(places, rows, start, slope) - log)
                dprob = nt(head_mask(v[rows, :], head), grad[here, :])
                probs[rows, cols] = prob.astype(BF16)
                dscores[rows, cols] = (prob * (dprob - delta)).astype(BF16)
            lines = pl.ds(pl.multiple_of(head * HEAD_DIM, HEAD_DIM), HEAD_DIM)
            dqt[lines, here] = nn(kt[lines, 0:keys], dscores[0:keys, cols]).astype(BF16)
        both = [
            jnp.concatenate([head_mask(ref[here, :], head) for head in heads], 0)
            for ref in (grad, q)
        ]
        dv[0:keys, :] += nn(probs[0:keys, :], both[0])
        dk[0:keys, :] += nn(dscores[0:keys, :], both[1])
        return carry

    lax.fori_loop(0, 2, pair, 0)


def normalize(values):
    mean = jnp.mean(values, 1, keepdims=True)
    centered = values - mean
    scale = lax.rsqrt(jnp.mean(centered * centered, 1, keepdims=True) + EPSILON)
    return centered * scale, scale


def x_devices(place):
    return [place.on_x(1), place.on_x(-1), place.mate()]


def merge(left, right, swap_left, swap_right):
    left, right = left.astype(F32), right.astype(F32)
    left = pltpu.roll(left, 64, 1) if swap_left else left
    right = pltpu.roll(right, 64, 1) if swap_right else right
    lane = lax.broadcasted_iota(jnp.int32, left.shape, 1)
    return jnp.where(lane < 64, left, right)


def group_of(ref, index):
    return ref[:, index * 128 : (index + 1) * 128]


def spread(small, line, base, per, first, width):
    entry = lax.broadcasted_iota(jnp.int32, (128, width), 1)
    piece = lax.broadcasted_iota(jnp.int32, (128, width), 0)
    wanted = (lax.div(entry, per) + first) * 8 + line
    chosen = jnp.where(piece == wanted, 1.0, 0.0).astype(BF16)
    spread_out = lax.dot_general(
        small, chosen, (((0,), (0,)), ((), ())), preferred_element_type=F32
    )
    lane = lax.broadcasted_iota(jnp.int32, (128, width), 0)
    entry = lax.broadcasted_iota(jnp.int32, (128, width), 1)
    return jnp.sum(
        jnp.where(lane == base + lax.rem(entry, per), spread_out, 0.0), 0, keepdims=True
    )


def attend_block(block, q, k, vt, out_t, logs, places, raws, probs):
    start, keys = block * BLOCK, (block + 1) * BLOCK
    here = pl.ds(start, BLOCK)

    def one(head, carry):
        slope = slope_of(head)
        peak = jnp.full((8, BLOCK), -3e38, F32)
        for chunk in range(keys // 128):
            rows = slice(chunk * 128, (chunk + 1) * 128)
            scores = nt(head_mask(k[rows, :], head), q[here, :])
            scores = scores - penalties(places, rows, start, slope)
            raws[rows, :] = scores
            peak = jnp.maximum(peak, fold(scores, jnp.max))
        peak = jnp.max(peak, 0, keepdims=True)
        total = jnp.zeros((8, BLOCK), F32)
        for chunk in range(keys // 128):
            rows = slice(chunk * 128, (chunk + 1) * 128)
            exponent = jnp.exp(raws[rows, :] - peak)
            total = total + fold(exponent, jnp.sum)
            probs[rows, :] = exponent.astype(BF16)
        total = jnp.sum(total, 0, keepdims=True)
        lines = pl.ds(pl.multiple_of(head * HEAD_DIM, HEAD_DIM), HEAD_DIM)
        out_t[lines, here] = nn(vt[lines, 0:keys], probs[0:keys, :]) / total
        logs[head, :, here] = peak + jnp.log(total)
        return carry

    lax.fori_loop(0, 4, one, 0, unroll=2)


def forward_kernel(
    length, x, cot, qkv_own, dense, fc1_own, fc2, small_own, norm_a, norm_b, norm_c, norm_d,
    gcot, gqkv, gdense, gfc1, gfc2, rows_one, rows_two, heads, logs, residual, stats,
    vectors, grad_act,
    vx, vcot, vqkv, vdense, vfc2, vsmall, vnorm, n1, vheads, vt, out_t, part, own, tile,
    vlogs, qkv, fc1, small, norms, places, raws, probs, total, ring_in,
    send, recv, near_sems,
):
    place = Place()
    net, near = Net(send, recv), Near(near_sems)
    row, z, y = place.row, place.z, place.y
    partner = place.partner()
    y_ring = [place.on_y(step) for step in (1, 3, 2)]
    z_ring = [place.on_z(step) for step in (1, 3, 2)]
    peers = [partner, place.on_x(1), place.on_x(-1), place.mate()] + y_ring + z_ring
    announce(peers)
    for part_of in range(2):
        for third in range(3):
            for pair in range(2):
                left = (4 * part_of + 2 * pair) * 3 + third
                right = left + 3
                made = merge(
                    group_of(qkv_own, left // 2),
                    group_of(qkv_own, right // 2),
                    left % 2 == 1,
                    right % 2 == 0,
                )
                start = (third * 2 + pair) * 128
                qkv[part_of, :, start : start + 128] = made.astype(BF16)
    for pair in range(8):
        left, right = group_of(fc1_own, 2 * pair), group_of(fc1_own, 2 * pair + 1)
        for part_of in range(2):
            made = merge(left, right, part_of == 1, part_of == 0)
            fc1[part_of, :, pair * 128 : pair * 128 + 128] = made.astype(BF16)
    small[...] = jnp.zeros_like(small)
    for line in range(3):
        small[line : line + 1, :] = group_of(small_own, line)
    for line, source in enumerate((norm_a, norm_b, norm_c, norm_d)):
        norms[line : line + 1, :] = source[...]
        norms[line + 4 : line + 5, :] = source[...]
    weights = [
        (stacked(vqkv, 64), qkv.at[row], qkv.at[1 - row]),
        (stacked(vsmall, 8), small, small),
        (beside(vdense, 32), dense, dense),
        (stacked(gfc1, 64), fc1.at[row], fc1.at[1 - row]),
        (beside(vfc2, 64), fc2.at[row], fc2.at[1 - row]),
    ]
    swaps, copies = [], []
    for (at, size), own_cut, other in weights:
        there = at(row, z, y, pl.ds(0, size))
        swaps.append(net.copy(other, there, partner))
        copies.append(near.copy(own_cut, there))
    swap_norms = net.copy(norms, vnorm.at[row], partner)
    groups = []
    for source, target in ((x, vx), (cot, vcot)):
        block = quarter_block(target)

        def own_part(half, source=source):
            if half is None:
                return source
            return source.at[pl.ds(128 * half, 128), :]

        groups.append(GroupGather(net, place, block, own_part))
        copies.append(near.copy(source, block(place.chip, place.core, None)))
    copies.append(near.copy(norms, vnorm.at[row]))
    for copy in copies:
        copy.start()
    meet(peers)
    ones, twos = [], []
    for (at, size), own_cut, other in weights:
        half_rows = size // 2
        rows = pl.ds(0, size)

        def along_y(position, half, at=at, half_rows=half_rows):
            return at(row, z, position, pl.ds(half * half_rows, half_rows))

        def along_z(position, half, at=at, half_rows=half_rows):
            return at(1 - row, position, y, pl.ds(half * half_rows, half_rows))

        def mine(half, own_cut=own_cut, half_rows=half_rows):
            return own_cut.at[pl.ds(half * half_rows, half_rows), :]

        def planes_z(position, half, at=at, rows=rows):
            return at(row, position, pl.ds(2 * half, 2), rows)

        def planes_y(position, half, at=at, rows=rows):
            return at(1 - row, pl.ds(2 * half, 2), position, rows)

        over_y = (y, place.on_y(1), place.on_y(-1))
        over_z = (z, place.on_z(1), place.on_z(-1))
        if len(ones) < 2:
            there = at(1 - row, z, y, rows)
            ones.append(
                (
                    DirectGather(net, own_cut, at(row, z, y, rows), y_ring),
                    DirectGather(net, there, there, z_ring),
                )
            )
        else:
            ones.append(
                (
                    RingGather(net, along_y, *over_y, mine),
                    RingGather(net, along_z, *over_z),
                )
            )
        twos.append((RingGather(net, planes_z, *over_z), RingGather(net, planes_y, *over_y)))

    def begin(index):
        ones[index][0].start()
        swaps[index].wait_recv()
        ones[index][1].start()

    def pass_one(index):
        for ring in ones[index]:
            ring.forward()

    def turn_over(index):
        for ring, then in zip(ones[index], twos[index]):
            ring.near_done()
            ring.far_done()
            then.start()

    def pass_two(index):
        for ring in twos[index]:
            ring.forward()

    def complete(index):
        for ring in twos[index]:
            ring.near_done()
            ring.far_done()

    group_x, group_cot = groups
    swaps[0].start()
    ones[0][0].start()
    swap_norms.start()
    swaps[1].start()
    ones[1][0].start()
    group_x.start()
    for swap in swaps[2:]:
        swap.start()
    swaps[0].wait_recv()
    ones[0][1].start()
    swaps[1].wait_recv()
    ones[1][1].start()
    for copy in copies:
        copy.wait()
    turn_over(0)
    group_x.forward()
    turn_over(1)
    pass_two(0)
    pass_two(1)
    begin(2)
    begin(3)
    begin(4)
    group_x.share()
    swap_norms.wait_recv()

    def first_norm(pos):
        here = pl.ds(pos, 16)
        left, right = vx[here, 0:HALF].astype(F32), vx[here, HALF:WIDTH].astype(F32)
        mean = (
            jnp.sum(left, 1, keepdims=True) + jnp.sum(right, 1, keepdims=True)
        ) / WIDTH
        left, right = left - mean, right - mean
        scale = lax.rsqrt(
            (
                jnp.sum(left * left, 1, keepdims=True)
                + jnp.sum(right * right, 1, keepdims=True)
            )
            / WIDTH
            + EPSILON
        )
        lane = lax.broadcasted_iota(jnp.int32, (16, 128), 1)
        vlogs[here, :] = jnp.where(lane == 0, mean, scale)
        n1[here, 0:HALF] = (left * scale * vnorm[0, 0:1, :] + vnorm[0, 1:2, :]).astype(BF16)
        n1[here, HALF:WIDTH] = (
            right * scale * vnorm[1, 0:1, :] + vnorm[1, 1:2, :]
        ).astype(BF16)

    def norm_rows(start):
        sweep(512, 16, lambda pos: first_norm(pl.multiple_of(start + pos, 16)), 4)

    group_x.near_finish()
    norm_rows(512 - 512 * lax.rem(place.chip, 2))
    group_x.finish()
    group_cot.start()
    norm_rows(512 * lax.rem(place.chip, 2))
    for index in (2, 3, 4):
        pass_one(index)
    key_places(length[0], places)
    keep_n1 = near.copy(n1, rows_one)
    keep_n1.start()
    complete(1)
    smalls = [vsmall[index].reshape(128, 128).astype(BF16) for index in range(2)]
    query_add = spread(smalls[0], 1, 0, 32, 8 * row, LOCAL)
    value_add = spread(smalls[0], 1, 32, 32, 8 * row, LOCAL)
    complete(0)
    keep_qkv = near.copy(vqkv, gqkv)
    keep_qkv.start()

    def project(index, carry):
        here = pl.ds(pl.multiple_of(index * 256, 256), 256)
        for third, add in enumerate((query_add, None, value_add)):
            cols = slice(third * 256, (third + 1) * 256)
            made = nn(n1[here, :], vqkv[:, :, :, :, cols].reshape(WIDTH, 256))
            if add is not None:
                made = made + add
            made = made.astype(BF16)
            if third == 0:
                made = made * BF16(HEAD_DIM**-0.5)
            vheads[third, here, :] = made
        return carry

    turn_over(2)
    lax.fori_loop(0, 4, project, 0)
    group_cot.forward()
    vt[...] = vheads[2].T
    args = (vheads.at[0], vheads.at[1], vt, out_t, logs, places, raws, probs)
    attend_block(0, *args)
    pass_two(2)
    turn_over(3)
    turn_over(4)
    attend_block(1, *args)
    attend_block(2, *args)
    attend_block(3, *args)
    vheads[3] = out_t[...].T.astype(BF16)
    complete(2)
    keep_heads = near.copy(vheads, heads)
    keep_heads.start()
    keep_dense = near.copy(vdense, gdense)
    keep_dense.start()

    scatter = GroupScatter(
        net, place, part, row_slices, (128, WIDTH), total, ring_in
    )
    weight = vdense[pl.ds(2 * row, 2)].reshape(LOCAL, WIDTH)
    for index, chip in enumerate(scatter.order):
        starts = [pl.multiple_of(rows_of(chip, core), 128) for core in range(2)]
        both = jnp.concatenate([vheads[3, pl.ds(start, 128), :] for start in starts], 0)
        made = nn(both, weight).astype(BF16)
        part[pl.ds(starts[0], 128), :] = made[0:128]
        part[pl.ds(starts[1], 128), :] = made[128:256]
        scatter.mates[index].start()
    scatter.first(0, 1, 2)
    group_cot.share()
    group_cot.near_finish()
    group_cot.finish()
    keep_cot = near.copy(vcot, gcot)
    keep_cot.start()
    for side in range(2):
        half = pl.ds(side * HALF, HALF)
        vectors[0:1, half] = spread(smalls[side], 1, 64, 64, 0, HALF)
        vectors[1:2, half] = spread(smalls[side], 2, 0, 64, 0, HALF)
        vectors[3:4, half] = vnorm[side, 2:3, :]
        vectors[4:5, half] = vnorm[side, 3:4, :]
    vectors[2:3, 0:HALF] = jnp.where(
        row == 0,
        spread(smalls[0], 0, 0, 64, 0, HALF),
        spread(smalls[0], 0, 64, 64, 0, HALF),
    )
    scatter.second()
    pass_two(3)
    pass_two(4)
    scatter.arrive()
    group_two = GroupGather(
        net,
        place,
        row_block(rows_two),
        lambda half: own if half is None else own.at[pl.ds(64 * half, 64), :],
    )
    keep_own = near.copy(own, row_block(rows_two)(place.chip, place.core, None))
    first_row = rows_of(place.chip, place.core)
    for side in range(2):

        def one(pos, side=side):
            here = pl.ds(pl.multiple_of(pos + 64 * side, 16), 16)
            there = pl.ds(pl.multiple_of(first_row + pos + 64 * side, 16), 16)
            values = (
                vx[there, :].astype(F32) + scatter.result(side, pos) + vectors[0:1, :]
            )
            residual[here, :] = values
            own[here, :] = (
                normalize(values)[0] * vectors[3:4, :] + vectors[4:5, :]
            ).astype(BF16)

        sweep(64, 16, one)
    group_two.start()
    keep_own.start()
    complete(3)
    stats[...] = vlogs[pl.ds(pl.multiple_of(place.col * 256, 256), 256), :]
    complete(4)
    keep_fc2 = near.copy(vfc2, gfc2)
    keep_fc2.start()
    keeps = []
    for index in range(4):
        here = pl.ds(index * 256, 256)
        for piece in range(4):
            lines = vfc2[piece].reshape(256, WIDTH)
            tile[index, :, pl.ds(piece * 256, 256)] = nt(vcot[here, :], lines)
        keep = near.copy(tile.at[index], grad_act.at[here, :])
        keep.start()
        keeps.append(keep)
        if index == 1:
            group_two.forward()
        if index == 3:
            group_two.share()
    group_two.near_finish()
    group_two.finish()
    keeps += [keep_n1, keep_qkv, keep_heads, keep_dense, keep_cot, keep_own, keep_fc2]
    for keep in keeps:
        keep.wait()
    swap_norms.wait_send()
    for swap in swaps:
        swap.wait_send()
    for pair in ones + twos:
        for ring in pair:
            ring.drain()
    scatter.drain()


def forward(*args):
    remote = 6 + 3 * 10 + 10 + 5 * 4 * 6
    bf, full = (lambda *shape: jax.ShapeDtypeStruct(shape, BF16)), (
        lambda *shape: jax.ShapeDtypeStruct(shape, F32)
    )
    return pl.pallas_call(
        forward_kernel,
        out_shape=(
            bf(SEQ, WIDTH),
            bf(2, 4, 4, 64, 768),
            bf(4, 4, 32, 2048),
            bf(2, 4, 4, 64, 1024),
            bf(4, 4, 64, 2048),
            bf(SEQ, WIDTH),
            bf(SEQ, WIDTH),
            bf(4, SEQ, LOCAL),
            full(4, 1, SEQ),
            full(128, WIDTH),
            full(256, 128),
            full(8, WIDTH),
            full(SEQ, 1024),
        ),
        in_specs=[pl.BlockSpec(memory_space=pltpu.SMEM)]
        + any_specs(2)
        + vmem_specs(1)
        + any_specs(1)
        + vmem_specs(1)
        + any_specs(1)
        + vmem_specs(5),
        out_specs=tuple(any_specs(8) + vmem_specs(4) + any_specs(1)),
        scratch_shapes=[
            pltpu.VMEM((SEQ, WIDTH), BF16),
            pltpu.VMEM((SEQ, WIDTH), BF16),
            pltpu.VMEM((2, 4, 4, 64, 768), BF16),
            pltpu.VMEM((4, 4, 32, 2048), BF16),
            pltpu.VMEM((4, 4, 64, 2048), BF16),
            pltpu.VMEM((2, 4, 4, 8, 128), F32),
            pltpu.VMEM((2, 8, HALF), F32),
            pltpu.VMEM((SEQ, WIDTH), BF16),
            pltpu.VMEM((4, SEQ, LOCAL), BF16),
            pltpu.VMEM((LOCAL, SEQ), BF16),
            pltpu.VMEM((LOCAL, SEQ), F32),
            pltpu.VMEM((SEQ, WIDTH), BF16),
            pltpu.VMEM((128, WIDTH), BF16),
            pltpu.VMEM((4, 256, 1024), F32),
            pltpu.VMEM((SEQ, 128), F32),
            pltpu.VMEM((2, 64, 768), BF16),
            pltpu.VMEM((2, 64, 1024), BF16),
            pltpu.VMEM((8, 128), F32),
            pltpu.VMEM((8, HALF), F32),
            pltpu.VMEM((SEQ, 128), F32),
            pltpu.VMEM((SEQ, BLOCK), F32),
            pltpu.VMEM((SEQ, BLOCK), BF16),
        ]
        + scatter_scratch(128, WIDTH)
        + sem_arrays(remote, 20),
        compiler_params=comm_params(0),
        name="forward",
    )(*args)


def tn(left, right):
    return lax.dot_general(left, right, (((0,), (0,)), ((), ())), preferred_element_type=F32)


def turn_kernel(
    rows_two, fc1, fc2, cot, grad_act, residual, vectors,
    gathered, pairs_out, grad_fc1, mid_fc2, mid_fc1, sums,
    n2, w1, w2, vcot, gact, act, gh, part, own, pout, g1, g2, many, total_out, total, ring_in, *rest,
):
    *rings, send, recv, near_sems = rest
    place = Place()
    net, near = Net(send, recv), Near(near_sems)
    peers = (
        x_devices(place)
        + [place.on_y(1), place.on_y(-1), place.on_z(1), place.on_z(-1)]
    )
    announce(peers)
    load_n2, load_w1 = near.copy(rows_two, n2), near.copy(fc1, w1)
    load_n2.start()
    load_w1.start()
    scatter = GroupScatter(
        net, place, part, row_slices, (128, WIDTH), total, ring_in
    )
    tiles = [
        [pl.multiple_of(rows_of(chip, core), 128) for core in range(2)]
        for chip in scatter.order
    ]
    load_act = []
    for index, starts in enumerate(tiles):
        load_act.append(
            [
                near.copy(
                    grad_act.at[pl.ds(start, 128), :],
                    gact.at[index % 2, pl.ds(128 * core, 128), :],
                )
                for core, start in enumerate(starts)
            ]
        )
    for index in range(2):
        for copy in load_act[index]:
            copy.start()
    load_w2, load_cot = near.copy(fc2, w2), near.copy(cot, vcot)
    sums[...] = jnp.zeros_like(sums)
    load_n2.wait()
    load_w1.wait()
    for index, starts in enumerate(tiles):
        for copy in load_act[index]:
            copy.wait()
        rows = [pl.ds(start, 128) for start in starts]
        both = jnp.concatenate([n2[here, :] for here in rows], 0)
        for piece in range(4):
            cols = slice(piece * 256, (piece + 1) * 256)
            hidden = (
                nn(both, w1[:, :, :, :, cols].reshape(WIDTH, 256)) + vectors[2:3, cols]
            )
            below = 0.5 + 0.5 * lax.erf(hidden * 0.5**0.5)
            density = jnp.exp(-0.5 * hidden * hidden) * 0.3989422804014327
            made = (hidden * below).astype(BF16)
            back = (
                gact[index % 2, :, cols] * (below + hidden * density)
            ).astype(BF16)
            for core, here in enumerate(rows):
                act[here, cols] = made[128 * core : 128 * core + 128]
                gh[here, cols] = back[128 * core : 128 * core + 128]
            sums[3:4, cols] += jnp.sum(back.astype(F32), 0, keepdims=True)
        if index < 2:
            for copy in load_act[index + 2]:
                copy.start()
        back = jnp.concatenate([gh[here, :] for here in rows], 0)
        if index > 0:
            scatter.first(index - 1)
        for side in range(2):
            for piece in range(4):
                cols = slice(side * HALF + piece * 256, side * HALF + piece * 256 + 256)
                made = nt(back, w1[side, piece].reshape(256, 1024)).astype(BF16)
                for core, here in enumerate(rows):
                    part[here, cols] = made[128 * core : 128 * core + 128]
        if index == 0:
            load_w2.start()
            load_cot.start()
            meet(peers)
        scatter.mates[index].start()
    load_w2.wait()
    load_cot.wait()

    def one_g2(index, carry):
        cols = pl.ds(pl.multiple_of(index * 256, 256), 256)
        for side in range(2):
            half = slice(side * HALF, (side + 1) * HALF)
            made = tn(act[:, cols], vcot[:, half]).astype(BF16)
            g2[index, :, :, half] = made.reshape(4, 64, HALF)
        return carry

    lax.fori_loop(0, 2, one_g2, 0)
    scatter.second()
    lax.fori_loop(2, 4, one_g2, 0)
    mids = [mid_fc2.at[index] for index in range(2)]
    over = OuterScatter(net, place, beside(g2, 64)[0], 64, rings[0:2], mids)
    over.start()

    def one_g1(index, carry):
        side, piece = lax.div(index, 4), lax.rem(index, 4)
        cols = pl.ds(pl.multiple_of(index * 256, 256), 256)
        g1[side, piece] = tn(n2[:, cols], gh[...]).astype(BF16).reshape(4, 64, 1024)
        return carry

    def one_out(index, carry):
        here = pl.ds(pl.multiple_of(index * 256, 256), 256)
        for side in range(2):
            half = slice(side * HALF, (side + 1) * HALF)
            made = nn(act[here, :], w2[:, :, :, half].reshape(1024, HALF))
            pout[here, half] = made.astype(BF16)
        return carry

    lax.fori_loop(0, 8, one_g1, 0)
    keep_g1 = near.copy(g1, grad_fc1)
    keep_g1.start()
    mids = [mid_fc1.at[index] for index in range(2)]
    over_fc1 = OuterScatter(net, place, stacked_rows(g1, 0), 32, rings[2:4], mids)
    over_fc1.start()
    many[...] = jnp.zeros_like(many)
    scatter.arrive()
    group = GroupGather(
        net,
        place,
        row_block(gathered),
        lambda half: own if half is None else own.at[pl.ds(64 * half, 64), :],
    )
    first_row = rows_of(place.chip, place.core)
    for side in range(2):

        def one(pos, side=side):
            here = pl.ds(pl.multiple_of(pos + 64 * side, 16), 16)
            there = pl.ds(pl.multiple_of(first_row + pos + 64 * side, 16), 16)
            arrived = scatter.result(side, pos)
            xhat, scale = normalize(residual[here, :])
            scaled = arrived * vectors[3:4, :]
            flat = jnp.mean(scaled, 1, keepdims=True)
            cross = jnp.mean(scaled * xhat, 1, keepdims=True)
            given = vcot[there, :].astype(F32)
            branch = (given + scale * (scaled - flat - xhat * cross)).astype(BF16)
            own[here, :] = branch
            many[0] += arrived * xhat
            many[1] += arrived
            many[2] += given
            many[3] += branch.astype(F32)

        sweep(64, 16, one)
    group.start()
    keep_own = near.copy(own, row_block(gathered)(place.chip, place.core, None))
    keep_own.start()
    for index, line in enumerate((0, 1, 2, 4)):
        sums[line : line + 1, :] = jnp.sum(many[index], 0, keepdims=True)
    over.middle()
    lax.fori_loop(0, 2, one_out, 0)
    group.forward()
    lax.fori_loop(2, 4, one_out, 0)
    pair = PairSum(net, place, pout, total_out)
    pair.start()
    over_fc1.middle()

    group.share()
    pair.finish()
    keep_out = near.copy(total_out, pairs_out)
    keep_out.start()
    over.finish()
    over_fc1.finish()

    group.near_finish()
    group.finish()
    for keep in (keep_own, keep_out, keep_g1):
        keep.wait()
    pair.drain()
    over.drain()
    over_fc1.drain()
    scatter.drain()


def turn(rows_two, fc1, fc2, cot, grad_act, residual, vectors):
    bf = lambda *shape: jax.ShapeDtypeStruct(shape, BF16)
    return pl.pallas_call(
        turn_kernel,
        out_shape=(
            bf(SEQ, WIDTH),
            bf(4, 128, WIDTH),
            bf(2, 4, 4, 64, 1024),
            bf(2, 4, 64, 1024),
            bf(2, 4, 32, 1024),
            jax.ShapeDtypeStruct((8, WIDTH), F32),
        ),
        in_specs=any_specs(5) + vmem_specs(2),
        out_specs=tuple(any_specs(3) + vmem_specs(3)),
        scratch_shapes=[
            pltpu.VMEM((SEQ, WIDTH), BF16),
            pltpu.VMEM((2, 4, 4, 64, 1024), BF16),
            pltpu.VMEM((4, 4, 64, 2048), BF16),
            pltpu.VMEM((SEQ, WIDTH), BF16),
            pltpu.VMEM((2, 256, 1024), F32),
            pltpu.VMEM((SEQ, 1024), BF16),
            pltpu.VMEM((SEQ, 1024), BF16),
            pltpu.VMEM((SEQ, WIDTH), BF16),
            pltpu.VMEM((128, WIDTH), BF16),
            pltpu.VMEM((SEQ, WIDTH), BF16),
            pltpu.VMEM((2, 4, 4, 64, 1024), BF16),
            pltpu.VMEM((4, 4, 64, 2048), BF16),
            pltpu.VMEM((4, 16, WIDTH), F32),
            pltpu.VMEM((4, 128, WIDTH), BF16),
        ]
        + scatter_scratch(128, WIDTH)
        + outer_scratch(64, 1024)
        + outer_scratch(32, 1024)
        + sem_arrays(20 + 24 + 4, 20),
        compiler_params=comm_params(2),
        name="turn",
    )(rows_two, fc1, fc2, cot, grad_act, residual, vectors)


def last_kernel(
    length, x, stats, branch, dense, qkv, heads, logs, rows_one, pairs_out, grad_fc1,
    mid_fc2, mid_fc1, gain, residual, vectors, sums_two,
    raw, out, rqkv, rdense, rfc1, rfc1_b, rfc2, vector, first_sums, swapped, own_branch,
    rows, wd, wq, vheads, datt, kt, dk, dv, dqt, gproj, part, pout, g1, mine_fc2, mine_fc1, gd, gq,
    result, stats_rows, stats_out, stats_in, mate_in, chips_in, y_in, z_in, vec_a, vec_b,
    stacks, late, late_two, late_group, late_y, late_z, places, probs, dscores, deltas,
    total, ring_in, ring_out, *rest,
):
    *rest, send, recv, near_sems = rest
    rest = list(rest)

    def take(count):
        taken = rest[:count]
        del rest[:count]
        return taken

    place = Place()
    row, z, y = place.row, place.z, place.y
    net, near = Net(send, recv), Near(near_sems)
    load_rows = near.copy(branch, rows)
    load_wd = near.copy(dense.at[pl.ds(2 * row, 2)], wd)
    load_heads = near.copy(heads, vheads)
    load_g1 = []
    reads = []
    for h, me in enumerate((z, y)):
        views = []
        for index, (pos, half) in enumerate(
            ((wrap(me + 1), 0), (wrap(me - 1), 1), (me, 0), (me, 1))
        ):
            pair = pl.ds(2 * half, 2)
            low = pl.ds(32, 32)
            source = (
                grad_fc1.at[0, pos, pair, low] if h == 0 else grad_fc1.at[1, pair, pos, low]
            )
            load_g1.append(near.copy(source, g1.at[h, index]))
            views.append(g1.at[h, index])
        reads.append(views)
    load_mid = [
        near.copy(mid.at[h, me], mine.at[h])
        for mid, mine in ((mid_fc2, mine_fc2), (mid_fc1, mine_fc1))
        for h, me in enumerate((y, z))
    ]
    load_out = near.copy(pairs_out.at[pl.ds(1, 3)], pout)
    load_wq = near.copy(qkv, wq)
    quarter = quarter_slices(place.chip, place.core)
    load_own = near.copy(
        branch.at[pl.ds(quarter[0], 256), pl.ds(quarter[1], HALF)], own_branch
    )
    load_own.start()
    load_rows.start()
    load_wd.start()
    load_heads.start()
    x_group = [
        place.x_at(wrap(place.chip + step), core)
        for step in range(4)
        for core in (place.core, 1 - place.core)
    ][1:]
    y_ring = [place.on_y(step) for step in (1, 2, 3)]
    z_ring = [place.on_z(step) for step in (1, 2, 3)]
    peers = x_group + y_ring + z_ring
    announce(peers)
    scatter = GroupScatter(net, place, part, quarter_slices, (256, HALF), total, ring_in)
    scatter_out = RingSum(net, place, pairs_out, pout, ring_out)
    rings_fc1, rings_dense, rings_qkv = take(2), take(2), take(2)
    mids_fc1, mids_dense, mids_qkv = take(2), take(2), take(2)
    out_fc1 = OuterScatter(
        net, place, stacked_rows(grad_fc1, 32), 32, rings_fc1, mids_fc1, reads
    )
    out_dense = OuterScatter(net, place, beside(gd, 32)[0], 32, rings_dense, mids_dense)
    out_qkv = OuterScatter(net, place, stacked(gq, 64)[0], 64, rings_qkv, mids_qkv)
    inner = []
    for mids, mine, final in (
        ([mid_fc2.at[h] for h in range(2)], [mine_fc2.at[h] for h in range(2)], rfc2),
        ([mid_fc1.at[h] for h in range(2)], [mine_fc1.at[h] for h in range(2)], rfc1),
        (mids_fc1, None, rfc1_b),
        (mids_dense, None, rdense),
        (mids_qkv, None, rqkv),
    ):
        arrived, done = take(2), take(1)[0]
        inner.append(InnerScatter(net, near, place, mids, mine, arrived, done, final))
    in_fc2, in_fc1_a, in_fc1, in_dense, in_qkv = inner
    vec_a[...] = jnp.zeros_like(vec_a)
    vec_a[2:4, :] = sums_two[0:2, :]
    vec_a[4:5, :] = sums_two[4:5, :]
    vec_a[5:6, :] = sums_two[2:3, :]
    vec_a[6:7, 0:HALF] = sums_two[3:4, 0:HALF]
    load_rows.wait()
    load_wd.wait()
    load_heads.wait()
    for load in load_g1 + load_mid:
        load.start()
    load_out.start()
    load_wq.start()

    def back_attended(index, carry):
        here = pl.ds(pl.multiple_of(index * 256, 256), 256)
        datt[here, :] = nt(rows[here, :], wd[...].reshape(LOCAL, WIDTH)).astype(BF16)
        return carry

    lax.fori_loop(0, 4, back_attended, 0)
    meet(peers)
    scatter_out.start()
    in_fc2.start()
    in_fc1_a.start()
    out_fc1.start()
    mate_send = net.copy(vec_a, mate_in, place.mate())
    mate_send.start()
    for side in range(2):
        half = slice(side * HALF, (side + 1) * HALF)
        made = tn(vheads[3], rows[:, half]).astype(BF16).reshape(2, 4, 32, HALF)
        gd[pl.ds(2 * row, 2), :, :, half] = made
        gd[pl.ds(2 - 2 * row, 2), :, :, half] = jnp.zeros_like(made)
    out_dense.start()
    for load in load_g1 + load_mid:
        load.wait()
    load_one = near.copy(rows_one, rows)
    load_one.start()
    kt[...] = vheads[1].T
    dk[...] = jnp.zeros_like(dk)
    dv[...] = jnp.zeros_like(dv)
    key_places(length[0], places)
    args = [vheads.at[index] for index in range(4)]
    args += [datt, logs, places, kt, dk, dv, dqt, probs, dscores, deltas]
    attend_back_block(0, *args)
    mate_send.wait_recv()
    vec_b[...] = vec_a[...]
    vec_b[2:6, :] += mate_in[2:6, :]
    chip_sends = [
        net.copy(vec_b, chips_in.at[step - 1], place.on_x(step)) for step in (1, 2, 3)
    ]
    for copy in chip_sends:
        copy.start()
    attend_back_block(1, *args)
    load_out.wait()
    scatter_out.second()
    attend_back_block(2, *args)
    mate_send.wait_send()
    for copy in chip_sends:
        copy.wait_recv()
    vec_a[...] = vec_b[...]
    for index in range(3):
        vec_a[2:6, :] += chips_in[index, 2:6, :]
    vec_a[7:8, :] = chips_in[1, 6:7, :]
    y_sends = [net.copy(vec_a, y_in.at[i], device) for i, device in enumerate(y_ring)]
    for copy in y_sends:
        copy.start()
    attend_back_block(3, *args)
    gproj[:, 0:256] = dqt[...].T * BF16(HEAD_DIM**-0.5)
    gproj[:, 256:512] = dk[...].astype(BF16)
    gproj[:, 512:768] = dv[...].astype(BF16)
    load_wq.wait()
    load_one.wait()
    columns = jnp.concatenate(
        [
            jnp.sum(gproj[:, third * 256 : third * 256 + 256].astype(F32), 0, keepdims=True)
            for third in range(3)
        ],
        1,
    )
    def one_gq(index, carry):
        side, piece = lax.div(index, 4), lax.rem(index, 4)
        cols = pl.ds(pl.multiple_of(index * 256, 256), 256)
        made = tn(rows[:, cols], gproj[...])
        gq[side, piece] = made.astype(BF16).reshape(4, 64, 768)
        return carry

    lax.fori_loop(0, 4, one_gq, 0)
    out_qkv.rings[0].start()
    lax.fori_loop(4, 8, one_gq, 0)
    out_qkv.rings[1].start()
    scatter_out.arrive()
    for side in range(2):

        def finish_rows(pos, side=side):
            here = pl.ds(pl.multiple_of(pos + 64 * side, 16), 16)
            result[here, :] = (
                residual[here, :] + scatter_out.result(side, pos) + vectors[1:2, :]
            ).astype(BF16)

        sweep(64, 16, finish_rows)
    there = pl.ds(row * 128, 128)
    out_swap = net.copy(
        result.at[:, pl.ds((1 - row) * HALF, HALF)], out.at[there, :], place.partner()
    )
    out_keep = near.copy(result.at[:, pl.ds(row * HALF, HALF)], out.at[there, :])
    out_swap.start()
    out_keep.start()
    for index, chip in enumerate(scatter.order):
        here = pl.ds(pl.multiple_of(lax.rem(chip, 2) * 512, 512), 512)
        cols = pl.ds(pl.multiple_of(lax.div(chip, 2) * HALF, HALF), HALF)
        weight = wq[lax.div(chip, 2)].reshape(HALF, 768)
        part[here, cols] = nt(gproj[here, :], weight).astype(BF16)
        scatter.mates[index].start()
        if index > 0:
            scatter.first(index - 1)
    out_fc1.middle()
    out_dense.middle()
    lane = lax.broadcasted_iota(jnp.int32, (256, 128), 1)
    stacks[...] = jnp.zeros_like(stacks)

    def one_stack(index, carry):
        side, piece = lax.div(index, 4), lax.rem(index, 4)
        weight = wq[side, piece].reshape(256, 768).astype(F32)
        made = gq[side, piece].reshape(256, 768).astype(F32)
        stacks[...] += jnp.where(
            lane == index, jnp.sum(weight * made, 1, keepdims=True), 0.0
        ) + jnp.where(lane == index + 8, jnp.sum(weight * columns, 1, keepdims=True), 0.0)
        return carry

    lax.fori_loop(0, 8, one_stack, 0)
    late[...] = jnp.zeros_like(late)
    late[0:16, :] = stacks[...].T[0:16, :]
    late[16:17, :] = columns[:, 0:256]
    late[17:18, :] = columns[:, 512:768]
    late_x_sends = [
        net.copy(late, late_group.at[index], device) for index, device in enumerate(x_group)
    ]
    for copy in late_x_sends:
        copy.start()
    out_qkv.middle()
    scatter.second()
    out_fc1.finish()
    in_fc1.start()
    out_dense.finish()
    in_dense.start()
    for copy in y_sends:
        copy.wait_recv()
    for copy in chip_sends:
        copy.wait_send()
    vec_b[...] = vec_a[...]
    for index in range(3):
        vec_b[...] += y_in[index]
    z_sends = [net.copy(vec_b, z_in.at[i], device) for i, device in enumerate(z_ring)]
    for copy in z_sends:
        copy.start()
    out_qkv.finish()
    in_qkv.start()
    for copy in late_x_sends:
        copy.wait_recv()
    late_two[...] = late[...]
    for index in range(7):
        late_two[0:16, :] += late_group[index, 0:16, :]
    late_two[18:20, :] = late_group[3, 16:18, :]
    late_y_sends = [
        net.copy(late_two, late_y.at[i], device) for i, device in enumerate(y_ring)
    ]
    for copy in late_y_sends:
        copy.start()
    in_fc2.finish()
    in_fc1_a.finish()
    scatter.arrive()

    lane = lax.broadcasted_iota(jnp.int32, (16, 128), 1)
    for side in range(2):

        def sums(pos, side=side):
            here = pl.ds(pl.multiple_of(pos + 128 * side, 16), 16)
            arrived = scatter.result(side, pos)
            scaled = arrived * gain[...]
            xhat = (x[here, :].astype(F32) - stats[here, 0:1]) * stats[here, 1:2]
            flat = jnp.sum(scaled, 1, keepdims=True)
            cross = jnp.sum(scaled * xhat, 1, keepdims=True)
            stats_rows[here, :] = jnp.where(lane == 0, flat, cross)
            raw[here, :] = arrived

        sweep(128, 16, sums, 4)
    stats_out[...] = stats_rows[...].T[0:8, :]
    swap_stats = net.copy(stats_out, stats_in, place.partner())
    swap_stats.start()
    in_qkv.finish()
    for copy in late_y_sends:
        copy.wait_recv()
    for copy in late_x_sends:
        copy.wait_send()
    late[...] = late_two[...]
    for index in range(3):
        late[...] += late_y[index]
    late_z_sends = [net.copy(late, late_z.at[i], device) for i, device in enumerate(z_ring)]
    for copy in late_z_sends:
        copy.start()
    in_fc1.finish()
    in_dense.finish()
    swap_stats.wait_recv()
    swapped[...] = stats_out[...] + stats_in[...]
    for copy in z_sends + late_z_sends:
        copy.wait_recv()
    vector[...] = vec_b[...]
    first_sums[...] = late[...]
    for index in range(3):
        vector[...] += z_in[index]
        first_sums[...] += late_z[index]
    load_own.wait()
    out_swap.wait_recv()
    for stage in (out_fc1, out_dense, out_qkv):
        stage.drain()
    for stage in inner:
        stage.close()
    out_keep.wait()
    out_swap.wait_send()
    swap_stats.wait_send()
    for copy in y_sends + late_y_sends + z_sends + late_z_sends:
        copy.wait_send()
    scatter.drain()
    scatter_out.drain()


def last(*args):
    bf = lambda *shape: jax.ShapeDtypeStruct(shape, BF16)
    full = lambda *shape: jax.ShapeDtypeStruct(shape, F32)
    anywhere, inside = any_specs(1)[0], vmem_specs(1)[0]
    where = (
        [pl.BlockSpec(memory_space=pltpu.SMEM), inside, inside]
        + [anywhere] * 4
        + [inside]
        + [anywhere] * 5
        + [inside] * 4
    )
    return pl.pallas_call(
        last_kernel,
        out_shape=(
            full(256, HALF),
            bf(256, HALF),
            bf(2, 64, 768),
            bf(2, 32, 1024),
            bf(2, 32, 1024),
            bf(2, 32, 1024),
            bf(2, 64, 1024),
            full(8, WIDTH),
            full(24, 256),
            full(8, 256),
            bf(256, HALF),
        ),
        in_specs=where,
        out_specs=tuple(vmem_specs(10) + any_specs(1)),
        scratch_shapes=[
            pltpu.VMEM((SEQ, WIDTH), BF16),
            pltpu.VMEM((2, 4, 32, WIDTH), BF16),
            pltpu.VMEM((2, 4, 4, 64, 768), BF16),
            pltpu.VMEM((4, SEQ, LOCAL), BF16),
            pltpu.VMEM((SEQ, LOCAL), BF16),
            pltpu.VMEM((LOCAL, SEQ), BF16),
            pltpu.VMEM((SEQ, LOCAL), F32),
            pltpu.VMEM((SEQ, LOCAL), F32),
            pltpu.VMEM((LOCAL, SEQ), BF16),
            pltpu.VMEM((SEQ, 768), BF16),
            pltpu.VMEM((SEQ, WIDTH), BF16),
            pltpu.VMEM((3, 128, WIDTH), BF16),
            pltpu.VMEM((2, 4, 2, 32, 1024), BF16),
            pltpu.VMEM((2, 64, 1024), BF16),
            pltpu.VMEM((2, 32, 1024), BF16),
            pltpu.VMEM((4, 4, 32, 2048), BF16),
            pltpu.VMEM((2, 4, 4, 64, 768), BF16),
            pltpu.VMEM((128, WIDTH), BF16),
            pltpu.VMEM((256, 128), F32),
            pltpu.VMEM((8, 256), F32),
            pltpu.VMEM((8, 256), F32),
            pltpu.VMEM((8, WIDTH), F32),
            pltpu.VMEM((3, 8, WIDTH), F32),
            pltpu.VMEM((3, 8, WIDTH), F32),
            pltpu.VMEM((3, 8, WIDTH), F32),
            pltpu.VMEM((8, WIDTH), F32),
            pltpu.VMEM((8, WIDTH), F32),
            pltpu.VMEM((256, 128), F32),
            pltpu.VMEM((24, 256), F32),
            pltpu.VMEM((24, 256), F32),
            pltpu.VMEM((7, 24, 256), F32),
            pltpu.VMEM((3, 24, 256), F32),
            pltpu.VMEM((3, 24, 256), F32),
            pltpu.VMEM((SEQ, 128), F32),
            pltpu.VMEM((SEQ, 2 * BLOCK), BF16),
            pltpu.VMEM((SEQ, 2 * BLOCK), BF16),
            pltpu.VMEM((4, 1, BLOCK), F32),
        ]
        + scatter_scratch(256, HALF)
        + [pltpu.VMEM((6, 64, WIDTH), BF16)]
        + outer_scratch(32, 1024)
        + outer_scratch(32, 1024)
        + outer_scratch(64, 768)
        + mid_scratch(32, 1024)
        + mid_scratch(32, 1024)
        + mid_scratch(64, 768)
        + inner_scratch(64, 1024)
        + inner_scratch(32, 1024)
        + inner_scratch(32, 1024)
        + inner_scratch(32, 1024)
        + inner_scratch(64, 768)
        + sem_arrays(20 + 3 * 12 + 5 * 7 + 30, 32),
        compiler_params=comm_params(3, 62),
        name="last",
    )(*args)


def finish_kernel(
    raw, rows_out, rqkv, rdense, rfc1, rfc1_b, rfc2, vector, first_sums, swapped, own_branch,
    x, stats, gain, offset,
    outputs, ingrad, qkv, query, value, dense, dense_add, fc1, hidden_add, fc2, output_add,
    gain_one, offset_one, gain_two, offset_two, turned,
):
    row = lax.axis_index("row")
    dp = lax.axis_index("dp")
    outputs[...] = rows_out[...]
    turned[...] = jnp.concatenate([swapped[...], jnp.zeros((120, 256), F32)], 0).T

    def apply(pos):
        here = pl.ds(pos, 16)
        both = turned[here, :] / WIDTH
        scale = stats[here, 1:2]
        xhat = (x[here, :].astype(F32) - stats[here, 0:1]) * scale
        ingrad[here, :] = own_branch[here, :].astype(F32) + scale * (
            raw[here, :] * gain[...] - both[:, 0:1] - xhat * both[:, 1:2]
        )

    sweep(256, 16, apply, 4)
    for index in range(12):
        made = []
        for block in (2 * index, 2 * index + 1):
            head, third = block // 3, block % 3
            place_in = third * 4 + head % 4
            made.append((group_of(rqkv.at[head // 4], place_in // 2), place_in % 2))
        (left, left_odd), (right, right_odd) = made
        qkv[:, index * 128 : index * 128 + 128] = merge(
            left, right, left_odd == 1, right_odd == 0
        )
    for index in range(16):
        for side, source in enumerate((rfc1, rfc1_b)):
            fc1[side * 32 : side * 32 + 32, index * 128 : index * 128 + 128] = merge(
                group_of(source.at[0], index // 2),
                group_of(source.at[1], index // 2),
                index % 2 == 1,
                index % 2 == 0,
            )
    fc2[0:64, :] = rfc2[0].astype(F32)
    fc2[64:128, :] = rfc2[1].astype(F32)
    dense[...] = rdense[0].astype(F32) + rdense[1].astype(F32)
    for index in range(4):
        cols = slice(index * 256, index * 256 + 256)
        products = first_sums[pl.ds(row * 4 + index, 1), :]
        plain = first_sums[pl.ds(row * 4 + index + 8, 1), :]
        gain_one[:, cols] = (products - offset[:, cols] * plain) / gain[:, cols]
        offset_one[:, cols] = plain
    half = pl.ds(pl.multiple_of(row * HALF, HALF), HALF)
    gain_two[...] = vector[2:3, half]
    offset_two[...] = vector[3:4, half]
    odd = lax.rem(dp, 2)
    start = lax.div(dp, 2) * 128

    def swap_if(values, swap):
        return jnp.where(swap == 1, pltpu.roll(values, 64, 1), values)

    def eight(line, lane):
        return vector[line : line + 1, pl.ds(pl.multiple_of(lane, 128), 128)] + jnp.zeros(
            (8, 128), F32
        )

    dense_add[...] = swap_if(eight(4, row * HALF + start), odd)[0:1, 0:64]
    output_add[...] = swap_if(eight(5, row * HALF + start), odd)[0:1, 0:64]
    own, other = eight(6, start), eight(7, start)
    first = jnp.where(row == 0, own, other)
    second = jnp.where(row == 0, other, own)
    lanes = lax.broadcasted_iota(jnp.int32, (8, 128), 1)
    hidden_add[...] = jnp.where(
        lanes < 64, swap_if(first, odd), swap_if(second, 1 - odd)
    )[0:1, :]
    theirs = lax.div(dp, 8) == row
    inside = lax.rem(dp, 8)
    quarter = lax.rem(inside, 4)
    upper = lax.div(inside, 4) == 1
    for target, base in ((query, 16), (value, 17)):
        lines = [
            first_sums[at : at + 1, lanes_from : lanes_from + 128]
            + jnp.zeros((8, 128), F32)
            for at in (base, base + 2)
            for lanes_from in (0, 128)
        ]
        mine = jnp.where(upper, lines[1], lines[0])
        other = jnp.where(upper, lines[3], lines[2])
        chosen = jnp.where(theirs, mine, other)
        moved = chosen
        for step in range(1, 4):
            moved = jnp.where(quarter == step, pltpu.roll(chosen, 128 - 32 * step, 1), moved)
        target[...] = moved[0:1, 0:32]


def finish(*args):
    full = lambda *shape: jax.ShapeDtypeStruct(shape, F32)
    whole = lambda shape: pl.BlockSpec(shape, lambda index: (0,) * len(shape))
    shapes = (
            jax.ShapeDtypeStruct((256, HALF), BF16),
            full(256, HALF),
            full(64, 1536),
            full(1, 32),
            full(1, 32),
            full(32, 1024),
            full(1, 64),
            full(64, 2048),
            full(1, 128),
            full(128, HALF),
            full(1, 64),
            full(1, HALF),
            full(1, HALF),
            full(1, HALF),
            full(1, HALF),
        )
    return pl.pallas_call(
        finish_kernel,
        out_shape=shapes,
        grid=(1,),
        in_specs=[whole(value.shape) for value in args],
        out_specs=tuple(whole(value.shape) for value in shapes),
        scratch_shapes=[pltpu.VMEM((256, 128), F32)],
        compiler_params=pltpu.CompilerParams(vmem_limit_bytes=62 << 20),
        name="finish",
    )(*args)


def local(
    inputs,
    cotangent,
    lengths,
    attention_norm_gain,
    attention_norm_bias,
    qkv_weight,
    query_bias,
    value_bias,
    dense_weight,
    dense_bias,
    feedforward_norm_gain,
    feedforward_norm_bias,
    fc1_weight,
    fc1_bias,
    fc2_weight,
    fc2_bias,
):
    zeros = jnp.zeros((64,), BF16)
    small = jnp.concatenate(
        [fc1_bias, query_bias, value_bias, dense_bias, fc2_bias, zeros]
    ).astype(F32)
    (
        rows_cot, qkv_full, dense_full, fc1_full, fc2_full, rows_one, rows_two, heads,
        logs, residual, stats, vectors, grad_act,
    ) = forward(
        lengths,
        inputs,
        cotangent,
        qkv_weight,
        dense_weight,
        fc1_weight,
        fc2_weight.reshape(2, 64, 1024),
        small.reshape(1, 384),
        attention_norm_gain.reshape(1, HALF),
        attention_norm_bias.reshape(1, HALF),
        feedforward_norm_gain.reshape(1, HALF),
        feedforward_norm_bias.reshape(1, HALF),
    )
    rows_branch, pairs_out, grad_fc1, mid_fc2, mid_fc1, sums_two = turn(
        rows_two, fc1_full, fc2_full, rows_cot, grad_act, residual, vectors
    )
    (
        raw, rows_out, red_qkv, red_dense, red_fc1, red_fc1_b, red_fc2, vector,
        first_sums, swapped, own_branch,
    ) = last(
        lengths, inputs, stats, rows_branch, dense_full, qkv_full, heads, logs, rows_one,
        pairs_out, grad_fc1, mid_fc2, mid_fc1, attention_norm_gain.reshape(1, HALF), residual, vectors,
        sums_two,
    )
    results = finish(
        raw, rows_out, red_qkv, red_dense, red_fc1, red_fc1_b, red_fc2, vector,
        first_sums, swapped, own_branch,
        inputs, stats, attention_norm_gain.reshape(1, HALF),
        attention_norm_bias.reshape(1, HALF),
    )
    return tuple(
        value.reshape(value.shape[1]) if value.shape[0] == 1 else value
        for value in results
    )


def solution(mesh):
    return jax.shard_map(
        local,
        mesh=mesh,
        in_specs=(
            P(("dp", "col"), "row"),
            P(("dp", "col"), "row"),
            P("dp"),
            P("row"),
            P("row"),
            P(("row", "dp"), "col"),
            P(("col", "dp")),
            P(("col", "dp")),
            P(("col", "dp"), "row"),
            P(("row", "dp")),
            P("row"),
            P("row"),
            P(("row", "dp"), "col"),
            P(("col", "dp")),
            P(("col", "dp"), "row"),
            P(("row", "dp")),
        ),
        out_specs=(
            P(("dp", "col"), "row"),
            P(("dp", "col"), "row"),
            P(("row", "dp"), "col"),
            P(("col", "dp")),
            P(("col", "dp")),
            P(("col", "dp"), "row"),
            P(("row", "dp")),
            P(("row", "dp"), "col"),
            P(("col", "dp")),
            P(("col", "dp"), "row"),
            P(("row", "dp")),
            P("row"),
            P("row"),
            P("row"),
            P("row"),
        ),
        check_vma=False,
    )
```

```python
import jax
import jax.numpy as jnp
from jax import lax
from jax.experimental import pallas as pl
from jax.experimental.pallas import tpu as pltpu
from jax.sharding import PartitionSpec as P

HEADS = 32
HEAD_DIM = 64
BLOCK = 256
SEQ = 1024
WIDTH = 2048
HALF = WIDTH // 2
LOCAL = 256
EPSILON = 1e-05
FAR = 1e30
MESH = pl.DeviceIdType.MESH
F32 = jnp.float32
BF16 = jnp.bfloat16


def wrap(position):
    return lax.rem(position + 4, 4)


class Place:
    def __init__(self):
        self.row = lax.axis_index("row")
        self.col = lax.axis_index("col")
        self.dp = lax.axis_index("dp")
        self.chip = self.row * 2 + lax.div(self.col, 2)
        self.core = lax.rem(self.col, 2)
        self.z = lax.div(self.dp, 4)
        self.y = lax.rem(self.dp, 4)

    def on_x(self, step):
        return self.x_at(wrap(self.chip + step), self.core)

    def x_at(self, chip, core):
        return {"row": lax.div(chip, 2), "col": lax.rem(chip, 2) * 2 + core}

    def on_y(self, step):
        return {"dp": self.z * 4 + wrap(self.y + step)}

    def on_z(self, step):
        return {"dp": wrap(self.z + step) * 4 + self.y}

    def partner(self):
        return {"row": 1 - self.row}

    def mate(self):
        return {"col": lax.div(self.col, 2) * 2 + 1 - self.core}


class Net:
    def __init__(self, send, recv):
        self.send, self.recv, self.used = send, recv, 0

    def copy(self, source, target, device):
        slot = self.used
        self.used += 1
        return pltpu.make_async_remote_copy(
            src_ref=source,
            dst_ref=target,
            send_sem=self.send.at[slot],
            recv_sem=self.recv.at[slot],
            device_id=device,
            device_id_type=MESH,
        )


class Near:
    def __init__(self, sems):
        self.sems, self.used = sems, 0

    def copy(self, source, target):
        slot = self.used
        self.used += 1
        return pltpu.make_async_copy(source, target, self.sems.at[slot])


def announce(devices):
    barrier = pltpu.get_barrier_semaphore()
    for device in devices:
        pl.semaphore_signal(barrier, inc=1, device_id=device, device_id_type=MESH)


def meet(devices):
    pl.semaphore_wait(pltpu.get_barrier_semaphore(), len(devices))


class RingGather:
    def __init__(self, net, block, me, right, left, own=None):
        before, after = wrap(me - 1), wrap(me + 1)
        own = own or (lambda half: block(me, half))
        self.first = [
            net.copy(own(0), block(me, 0), right),
            net.copy(own(1), block(me, 1), left),
        ]
        self.second = [
            net.copy(own(1), block(me, 1), right),
            net.copy(own(0), block(me, 0), left),
        ]
        self.passed = [
            net.copy(block(before, 0), block(before, 0), right),
            net.copy(block(after, 1), block(after, 1), left),
        ]

    def start(self):
        for copy in self.first + self.second:
            copy.start()

    def forward(self):
        for came, on in zip(self.first, self.passed):
            came.wait_recv()
            on.start()

    def near_done(self):
        for copy in self.second:
            copy.wait_recv()

    def far_done(self):
        for copy in self.passed:
            copy.wait_recv()

    def drain(self):
        for copy in self.first + self.second + self.passed:
            copy.wait_send()


class DirectGather:
    def __init__(self, net, own, target, devices):
        self.sends = [net.copy(own, target, device) for device in devices]

    def start(self):
        for copy in self.sends:
            copy.start()

    def forward(self):
        pass

    def near_done(self):
        for copy in self.sends:
            copy.wait_recv()

    def far_done(self):
        pass

    def drain(self):
        for copy in self.sends:
            copy.wait_send()


class GroupGather:
    def __init__(self, net, place, block, own):
        core, chip = place.core, place.chip
        self.ring = RingGather(
            net,
            lambda position, half: block(position, core, half),
            chip,
            place.on_x(1),
            place.on_x(-1),
            own,
        )
        whole = [
            own(None),
            block(wrap(chip - 1), core, None),
            block(wrap(chip + 1), core, None),
            block(wrap(chip + 2), core, None),
        ]
        target = [block(chip, core, None)] + whole[1:]
        self.mates = [
            net.copy(source, there, place.mate()) for source, there in zip(whole, target)
        ]

    def start(self):
        self.ring.start()
        self.mates[0].start()

    def forward(self):
        self.ring.forward()

    def share(self):
        self.ring.near_done()
        self.mates[1].start()
        self.mates[2].start()

    def near_finish(self):
        for copy in self.mates[1:3]:
            copy.wait_recv()

    def finish(self):
        self.ring.far_done()
        self.mates[3].start()
        for copy in (self.mates[0], self.mates[3]):
            copy.wait_recv()
        self.ring.drain()
        for copy in self.mates:
            copy.wait_send()


def sweep(rows, step, body, unroll=2):
    def one(index, carry):
        body(pl.multiple_of(index * step, step))
        return carry

    lax.fori_loop(0, rows // step, one, 0, unroll=unroll)


class GroupScatter:
    def __init__(self, net, place, part, slices, shape, total, ring_in):
        self.part, self.slices, self.place = part, slices, place
        self.rows, self.cols = shape
        self.total, self.ring_in = total, ring_in
        chip = place.chip
        half = self.rows // 2
        self.half = half
        self.order = [wrap(chip + 2), wrap(chip + 1), wrap(chip - 1), chip]
        mate = place.mate()
        self.mates = []
        for index, there in enumerate(self.order):
            rows, cols = slices(there, 1 - place.core)
            self.mates.append(
                net.copy(
                    part.at[pl.ds(rows, self.rows), pl.ds(cols, self.cols)],
                    total.at[index],
                    mate,
                )
            )
        right, left = place.on_x(1), place.on_x(-1)
        top, low = pl.ds(0, half), pl.ds(half, half)
        self.sends = [
            net.copy(total.at[0, top], ring_in.at[0], right),
            net.copy(total.at[0, low], ring_in.at[1], left),
            net.copy(total.at[1, low], ring_in.at[2], right),
            net.copy(total.at[2, top], ring_in.at[3], left),
            net.copy(ring_in.at[0], ring_in.at[4], right),
            net.copy(ring_in.at[1], ring_in.at[5], left),
        ]

    def start(self):
        for copy in self.mates:
            copy.start()

    def mine(self, index, row, step):
        rows, cols = self.slices(self.order[index], self.place.core)
        return self.part[
            pl.ds(pl.multiple_of(rows + row, 16), step), pl.ds(cols, self.cols)
        ].astype(F32)

    def first(self, *indices):
        for index in indices:
            self.mates[index].wait_recv()

            def add(row, index=index):
                here = pl.ds(row, 16)
                self.total[index, here, :] = (
                    self.mine(index, row, 16) + self.total[index, here, :].astype(F32)
                ).astype(BF16)

            sweep(self.rows, 16, add)
            if index == 0:
                self.sends[0].start()
                self.sends[1].start()
            else:
                self.sends[index + 1].start()

    def second(self):
        for side in range(2):
            self.sends[side].wait_recv()

            def add(row, side=side):
                here = pl.ds(row, 16)
                there = pl.ds(pl.multiple_of(row + side * self.half, 16), 16)
                self.ring_in[side, here, :] = (
                    self.total[1 + side, there, :].astype(F32)
                    + self.ring_in[side, here, :].astype(F32)
                ).astype(BF16)

            sweep(self.half, 16, add)
            self.sends[4 + side].start()

    def arrive(self):
        self.mates[3].wait_recv()
        for index in range(2, 6):
            self.sends[index].wait_recv()

    def result(self, side, row):
        here = pl.ds(row, 16)
        there = pl.multiple_of(row + side * self.half, 16)
        one, two = ((4, 3), (2, 5))[side]
        return (
            self.mine(3, there, 16)
            + self.total[3, pl.ds(there, 16), :].astype(F32)
            + self.ring_in[one, here, :].astype(F32)
            + self.ring_in[two, here, :].astype(F32)
        )

    def drain(self):
        for copy in self.mates + self.sends:
            copy.wait_send()


class PairSum:
    def __init__(self, net, place, part, total):
        self.part, self.place, self.total = part, place, total
        chip = place.chip
        self.order = [wrap(chip + 2), wrap(chip + 1), wrap(chip - 1), chip]
        self.mates = [
            net.copy(
                part.at[pl.ds(rows_of(there, 1 - place.core), 128), :],
                total.at[index],
                place.mate(),
            )
            for index, there in enumerate(self.order)
        ]

    def start(self):
        for copy in self.mates:
            copy.start()

    def finish(self):
        for index, there in enumerate(self.order):
            self.mates[index].wait_recv()
            start = rows_of(there, self.place.core)

            def add(row, index=index, start=start):
                here = pl.ds(row, 16)
                there = pl.ds(pl.multiple_of(start + row, 16), 16)
                self.total[index, here, :] = (
                    self.part[there, :].astype(F32)
                    + self.total[index, here, :].astype(F32)
                ).astype(BF16)

            sweep(128, 16, add)

    def drain(self):
        for copy in self.mates:
            copy.wait_send()


class RingSum:
    def __init__(self, net, place, pairs, near, ring_in):
        self.near, self.ring_in = near, ring_in
        right, left = place.on_x(1), place.on_x(-1)
        top, low = pl.ds(0, 64), pl.ds(64, 64)
        self.sends = [
            net.copy(pairs.at[0, top], ring_in.at[0], right),
            net.copy(pairs.at[0, low], ring_in.at[1], left),
            net.copy(pairs.at[1, low], ring_in.at[2], right),
            net.copy(pairs.at[2, top], ring_in.at[3], left),
            net.copy(ring_in.at[0], ring_in.at[4], right),
            net.copy(ring_in.at[1], ring_in.at[5], left),
        ]

    def start(self):
        for copy in self.sends[:4]:
            copy.start()

    def second(self):
        for side in range(2):
            self.sends[side].wait_recv()

            def add(row, side=side):
                here = pl.ds(row, 16)
                there = pl.ds(pl.multiple_of(row + side * 64, 16), 16)
                self.ring_in[side, here, :] = (
                    self.near[side, there, :].astype(F32)
                    + self.ring_in[side, here, :].astype(F32)
                ).astype(BF16)

            sweep(64, 16, add)
            self.sends[4 + side].start()

    def arrive(self):
        for copy in self.sends[2:]:
            copy.wait_recv()

    def result(self, side, row):
        here = pl.ds(row, 16)
        there = pl.ds(pl.multiple_of(row + side * 64, 16), 16)
        one, two = ((4, 3), (2, 5))[side]
        return (
            self.near[2, there, :].astype(F32)
            + self.ring_in[one, here, :].astype(F32)
            + self.ring_in[two, here, :].astype(F32)
        )

    def drain(self):
        for copy in self.sends:
            copy.wait_send()


def scatter_scratch(rows, cols):
    return [
        pltpu.VMEM((4, rows, cols), BF16),
        pltpu.VMEM((6, rows // 2, cols), BF16),
    ]


def add_rows(target, sources):
    shape = target.shape
    if len(shape) == 3:
        for index in range(shape[0]):
            add_rows(target.at[index], [source.at[index] for source in sources])
        return

    def one(row):
        here = pl.ds(row, 16)
        total = sources[0][here, :].astype(F32)
        for source in sources[1:]:
            total = total + source[here, :].astype(F32)
        target[here, :] = total.astype(BF16)

    sweep(shape[0], 16, one)


class RingScatter:
    def __init__(self, net, part, me, right, left, ring_in, target, read=None):
        before, after, across = wrap(me - 1), wrap(me + 1), wrap(me + 2)
        self.read = read or [part(after, 0), part(before, 1), part(me, 0), part(me, 1)]
        self.ring_in, self.target = ring_in, target
        self.sends = [
            net.copy(part(across, 0), ring_in.at[0], right),
            net.copy(part(across, 1), ring_in.at[1], left),
            net.copy(part(after, 1), ring_in.at[2], right),
            net.copy(part(before, 0), ring_in.at[3], left),
            net.copy(ring_in.at[0], ring_in.at[4], right),
            net.copy(ring_in.at[1], ring_in.at[5], left),
        ]

    def start(self):
        for copy in self.sends[:4]:
            copy.start()

    def middle(self):
        for side in range(2):
            self.sends[side].wait_recv()
            add_rows(
                self.ring_in.at[side], [self.read[side], self.ring_in.at[side]]
            )
            self.sends[4 + side].start()

    def finish(self):
        for index in range(2, 6):
            self.sends[index].wait_recv()
        for side, (one, two) in enumerate(((4, 3), (2, 5))):
            add_rows(
                self.target(side),
                [self.read[2 + side], self.ring_in.at[one], self.ring_in.at[two]],
            )

    def drain(self):
        for copy in self.sends:
            copy.wait_send()


def stacked_rows(ref, first):
    def at(part, z, y, rows):
        return ref.at[part, z, y, pl.ds(first + rows.start, rows.size), :]

    return at


class DirectScatter:
    def __init__(self, net, part, me, devices, arrived, target, mine=None):
        self.arrived, self.target = arrived, target
        self.mine = part(me) if mine is None else mine
        self.sends = [
            net.copy(part(wrap(me + step)), arrived.at[index], device)
            for index, (step, device) in enumerate(zip((1, 3, 2), devices))
        ]

    def start(self):
        for copy in self.sends:
            copy.start()

    def finish(self):
        for copy in self.sends:
            copy.wait_recv()
        add_rows(
            self.target, [self.mine] + [self.arrived.at[index] for index in range(3)]
        )

    def drain(self):
        for copy in self.sends:
            copy.wait_send()


class OuterScatter:
    def __init__(self, net, place, at, size, rings, mids, reads=None):
        z, y = place.z, place.y
        self.rings = []
        for h in range(2):

            def along_z(pos, half, h=h):
                return at(h, pos, pl.ds(2 * half, 2), pl.ds(0, size))

            def along_y(pos, half, h=h):
                return at(h, pl.ds(2 * half, 2), pos, pl.ds(0, size))

            def mid_half(half, h=h):
                return mids[h].at[pl.ds(2 * half, 2)]

            outer = (
                (along_z, z, place.on_z(1), place.on_z(-1))
                if h == 0
                else (along_y, y, place.on_y(1), place.on_y(-1))
            )
            read = reads[h] if reads else None
            self.rings.append(RingScatter(net, *outer, rings[h], mid_half, read))

    def start(self):
        for ring in self.rings:
            ring.start()

    def middle(self):
        for ring in self.rings:
            ring.middle()

    def finish(self):
        for ring in self.rings:
            ring.finish()

    def drain(self):
        for ring in self.rings:
            ring.drain()


class InnerScatter:
    def __init__(self, net, near, place, mids, mine, arrived, done, final):
        row, z, y = place.row, place.z, place.y
        over_y = [place.on_y(step) for step in (1, 3, 2)]
        over_z = [place.on_z(step) for step in (1, 3, 2)]
        self.stages = []
        for h in range(2):
            me, devices = (y, over_y) if h == 0 else (z, over_z)
            self.stages.append(
                DirectScatter(
                    net,
                    lambda pos, mid=mids[h]: mid.at[pos],
                    me,
                    devices,
                    arrived[h],
                    done.at[h],
                    mine[h] if mine else None,
                )
            )
        self.swap = net.copy(done.at[1 - row], final.at[row], place.partner())
        self.keep = near.copy(done.at[row], final.at[row])

    def start(self):
        for stage in self.stages:
            stage.start()

    def finish(self):
        for stage in self.stages:
            stage.finish()
        self.swap.start()
        self.keep.start()

    def close(self):
        self.swap.wait_recv()
        self.keep.wait()
        self.swap.wait_send()
        for stage in self.stages:
            stage.drain()


def outer_scratch(size, cols):
    return [pltpu.VMEM((6, 2, size, cols), BF16)] * 2


def mid_scratch(size, cols):
    return [pltpu.VMEM((4, size, cols), BF16)] * 2


def inner_scratch(size, cols):
    return [pltpu.VMEM((3, size, cols), BF16)] * 2 + [pltpu.VMEM((2, size, cols), BF16)]


def any_specs(count):
    return [pl.BlockSpec(memory_space=pl.ANY)] * count


def vmem_specs(count):
    return [pl.BlockSpec(memory_space=pltpu.VMEM)] * count


def sem_arrays(remote, near=0):
    arrays = [pltpu.SemaphoreType.DMA((remote,)), pltpu.SemaphoreType.DMA((remote,))]
    if near:
        arrays.append(pltpu.SemaphoreType.DMA((near,)))
    return arrays


def comm_params(identity, megabytes=60):
    return pltpu.CompilerParams(
        collective_id=identity, has_side_effects=True, vmem_limit_bytes=megabytes << 20
    )


def quarter_block(ref):
    def block(chip, core, half):
        rows = (lax.rem(chip, 2) * 2 + core) * 256
        cols = lax.div(chip, 2) * HALF
        if half is None:
            return ref.at[pl.ds(rows, 256), pl.ds(cols, HALF)]
        return ref.at[pl.ds(rows + 128 * half, 128), pl.ds(cols, HALF)]

    return block


def rows_of(chip, core):
    return (lax.rem(chip, 2) * 2 + core) * 256 + lax.div(chip, 2) * 128


def row_block(ref):
    def block(chip, core, half):
        rows = rows_of(chip, core)
        if half is None:
            return ref.at[pl.ds(rows, 128), :]
        return ref.at[pl.ds(rows + 64 * half, 64), :]

    return block


def row_slices(chip, core):
    return rows_of(chip, core), 0


def quarter_slices(chip, core):
    return (lax.rem(chip, 2) * 2 + core) * 256, lax.div(chip, 2) * HALF


def stacked(ref, size):
    def at(part, z, y, rows):
        return ref.at[part, z, y, rows, :]

    return at, size


def beside(ref, size):
    def at(part, z, y, rows):
        return ref.at[z, y, rows, pl.ds(part * HALF, HALF)]

    return at, size


def head_mask(values, head):
    lane = lax.broadcasted_iota(jnp.int32, values.shape, 1)
    return jnp.where(lax.div(lane, HEAD_DIM) == head, values, jnp.zeros_like(values))


def key_places(length, places):
    key = lax.broadcasted_iota(jnp.int32, places.shape, 0)
    places[...] = jnp.where(key < length, key.astype(F32), FAR)


def penalties(places, rows, start, slope):
    here = places[rows, :]
    query = (lax.broadcasted_iota(jnp.int32, (1, BLOCK), 1) + start).astype(F32)
    return slope * jnp.abs(query - jnp.concatenate([here, here], 1))


def fold(values, combine):
    return combine(values.reshape(16, 8, BLOCK), 0)


def slope_of(head):
    base = lax.axis_index("col") * 8 + lax.axis_index("row") * 4
    number = (base + head + 1).astype(F32)
    return jnp.exp2(jnp.full((1, BLOCK), -8.0 / HEADS, F32) * number)


def nt(left, right):
    return lax.dot_general(left, right, (((1,), (1,)), ((), ())), preferred_element_type=F32)


def nn(left, right):
    return jnp.dot(left, right, preferred_element_type=F32)


def attend_back_block(
    block, q, k, v, attended, grad, logs, places, kt, dk, dv, dqt, probs, dscores, deltas
):
    start, keys = block * BLOCK, (block + 1) * BLOCK
    here = pl.ds(start, BLOCK)
    inner = (grad[here, :].astype(F32) * attended[here, :].astype(F32)).T
    for head in range(4):
        lines = slice(head * HEAD_DIM, (head + 1) * HEAD_DIM)
        deltas[head] = jnp.sum(inner[lines, :], 0, keepdims=True)

    def pair(index, carry):
        heads = (2 * index, 2 * index + 1)
        for side, head in enumerate(heads):
            cols = slice(side * BLOCK, (side + 1) * BLOCK)
            slope, log, delta = slope_of(head), logs[head, :, here], deltas[head]
            for chunk in range(keys // 128):
                rows = slice(chunk * 128, (chunk + 1) * 128)
                scores = nt(head_mask(k[rows, :], head), q[here, :])
                prob = jnp.exp(scores - penalties(places, rows, start, slope) - log)
                dprob = nt(head_mask(v[rows, :], head), grad[here, :])
                probs[rows, cols] = prob.astype(BF16)
                dscores[rows, cols] = (prob * (dprob - delta)).astype(BF16)
            lines = pl.ds(pl.multiple_of(head * HEAD_DIM, HEAD_DIM), HEAD_DIM)
            dqt[lines, here] = nn(kt[lines, 0:keys], dscores[0:keys, cols]).astype(BF16)
        both = [
            jnp.concatenate([head_mask(ref[here, :], head) for head in heads], 0)
            for ref in (grad, q)
        ]
        dv[0:keys, :] += nn(probs[0:keys, :], both[0])
        dk[0:keys, :] += nn(dscores[0:keys, :], both[1])
        return carry

    lax.fori_loop(0, 2, pair, 0)


def normalize(values):
    mean = jnp.mean(values, 1, keepdims=True)
    centered = values - mean
    scale = lax.rsqrt(jnp.mean(centered * centered, 1, keepdims=True) + EPSILON)
    return centered * scale, scale


def x_devices(place):
    return [place.on_x(1), place.on_x(-1), place.mate()]


def merge(left, right, swap_left, swap_right):
    left, right = left.astype(F32), right.astype(F32)
    left = pltpu.roll(left, 64, 1) if swap_left else left
    right = pltpu.roll(right, 64, 1) if swap_right else right
    lane = lax.broadcasted_iota(jnp.int32, left.shape, 1)
    return jnp.where(lane < 64, left, right)


def group_of(ref, index):
    return ref[:, index * 128 : (index + 1) * 128]


def spread(small, line, base, per, first, width):
    entry = lax.broadcasted_iota(jnp.int32, (128, width), 1)
    piece = lax.broadcasted_iota(jnp.int32, (128, width), 0)
    wanted = (lax.div(entry, per) + first) * 8 + line
    chosen = jnp.where(piece == wanted, 1.0, 0.0).astype(BF16)
    spread_out = lax.dot_general(
        small, chosen, (((0,), (0,)), ((), ())), preferred_element_type=F32
    )
    lane = lax.broadcasted_iota(jnp.int32, (128, width), 0)
    entry = lax.broadcasted_iota(jnp.int32, (128, width), 1)
    return jnp.sum(
        jnp.where(lane == base + lax.rem(entry, per), spread_out, 0.0), 0, keepdims=True
    )


def attend_block(block, q, k, vt, out_t, logs, places, raws, probs):
    start, keys = block * BLOCK, (block + 1) * BLOCK
    here = pl.ds(start, BLOCK)

    def one(head, carry):
        slope = slope_of(head)
        peak = jnp.full((8, BLOCK), -3e38, F32)
        for chunk in range(keys // 128):
            rows = slice(chunk * 128, (chunk + 1) * 128)
            scores = nt(head_mask(k[rows, :], head), q[here, :])
            scores = scores - penalties(places, rows, start, slope)
            raws[rows, :] = scores
            peak = jnp.maximum(peak, fold(scores, jnp.max))
        peak = jnp.max(peak, 0, keepdims=True)
        total = jnp.zeros((8, BLOCK), F32)
        for chunk in range(keys // 128):
            rows = slice(chunk * 128, (chunk + 1) * 128)
            exponent = jnp.exp(raws[rows, :] - peak)
            total = total + fold(exponent, jnp.sum)
            probs[rows, :] = exponent.astype(BF16)
        total = jnp.sum(total, 0, keepdims=True)
        lines = pl.ds(pl.multiple_of(head * HEAD_DIM, HEAD_DIM), HEAD_DIM)
        out_t[lines, here] = nn(vt[lines, 0:keys], probs[0:keys, :]) / total
        logs[head, :, here] = peak + jnp.log(total)
        return carry

    lax.fori_loop(0, 4, one, 0, unroll=2)


def forward_kernel(
    length, x, cot, qkv_own, dense, fc1_own, fc2, small_own, norm_a, norm_b, norm_c, norm_d,
    gcot, gqkv, gdense, gfc1, gfc2, rows_one, rows_two, heads, logs, residual, stats,
    vectors, grad_act,
    vx, vcot, vqkv, vdense, vfc2, vsmall, vnorm, n1, vheads, vt, out_t, part, own, tile,
    vlogs, qkv, fc1, small, norms, places, raws, probs, total, ring_in,
    send, recv, near_sems,
):
    place = Place()
    net, near = Net(send, recv), Near(near_sems)
    row, z, y = place.row, place.z, place.y
    partner = place.partner()
    y_ring = [place.on_y(step) for step in (1, 3, 2)]
    z_ring = [place.on_z(step) for step in (1, 3, 2)]
    peers = [partner, place.on_x(1), place.on_x(-1), place.mate()] + y_ring + z_ring
    announce(peers)
    for part_of in range(2):
        for third in range(3):
            for pair in range(2):
                left = (4 * part_of + 2 * pair) * 3 + third
                right = left + 3
                made = merge(
                    group_of(qkv_own, left // 2),
                    group_of(qkv_own, right // 2),
                    left % 2 == 1,
                    right % 2 == 0,
                )
                start = (third * 2 + pair) * 128
                qkv[part_of, :, start : start + 128] = made.astype(BF16)
    for pair in range(8):
        left, right = group_of(fc1_own, 2 * pair), group_of(fc1_own, 2 * pair + 1)
        for part_of in range(2):
            made = merge(left, right, part_of == 1, part_of == 0)
            fc1[part_of, :, pair * 128 : pair * 128 + 128] = made.astype(BF16)
    small[...] = jnp.zeros_like(small)
    for line in range(3):
        small[line : line + 1, :] = group_of(small_own, line)
    for line, source in enumerate((norm_a, norm_b, norm_c, norm_d)):
        norms[line : line + 1, :] = source[...]
        norms[line + 4 : line + 5, :] = source[...]
    weights = [
        (stacked(vqkv, 64), qkv.at[row], qkv.at[1 - row]),
        (stacked(vsmall, 8), small, small),
        (beside(vdense, 32), dense, dense),
        (stacked(gfc1, 64), fc1.at[row], fc1.at[1 - row]),
        (beside(vfc2, 64), fc2.at[row], fc2.at[1 - row]),
    ]
    swaps, copies = [], []
    for (at, size), own_cut, other in weights:
        there = at(row, z, y, pl.ds(0, size))
        swaps.append(net.copy(other, there, partner))
        copies.append(near.copy(own_cut, there))
    swap_norms = net.copy(norms, vnorm.at[row], partner)
    groups = []
    for source, target in ((x, vx), (cot, vcot)):
        block = quarter_block(target)

        def own_part(half, source=source):
            if half is None:
                return source
            return source.at[pl.ds(128 * half, 128), :]

        groups.append(GroupGather(net, place, block, own_part))
        copies.append(near.copy(source, block(place.chip, place.core, None)))
    copies.append(near.copy(norms, vnorm.at[row]))
    for copy in copies:
        copy.start()
    meet(peers)
    ones, twos = [], []
    for (at, size), own_cut, other in weights:
        half_rows = size // 2
        rows = pl.ds(0, size)

        def along_y(position, half, at=at, half_rows=half_rows):
            return at(row, z, position, pl.ds(half * half_rows, half_rows))

        def along_z(position, half, at=at, half_rows=half_rows):
            return at(1 - row, position, y, pl.ds(half * half_rows, half_rows))

        def mine(half, own_cut=own_cut, half_rows=half_rows):
            return own_cut.at[pl.ds(half * half_rows, half_rows), :]

        def planes_z(position, half, at=at, rows=rows):
            return at(row, position, pl.ds(2 * half, 2), rows)

        def planes_y(position, half, at=at, rows=rows):
            return at(1 - row, pl.ds(2 * half, 2), position, rows)

        over_y = (y, place.on_y(1), place.on_y(-1))
        over_z = (z, place.on_z(1), place.on_z(-1))
        if len(ones) < 2:
            there = at(1 - row, z, y, rows)
            ones.append(
                (
                    DirectGather(net, own_cut, at(row, z, y, rows), y_ring),
                    DirectGather(net, there, there, z_ring),
                )
            )
        else:
            ones.append(
                (
                    RingGather(net, along_y, *over_y, mine),
                    RingGather(net, along_z, *over_z),
                )
            )
        twos.append((RingGather(net, planes_z, *over_z), RingGather(net, planes_y, *over_y)))

    def begin(index):
        ones[index][0].start()
        swaps[index].wait_recv()
        ones[index][1].start()

    def pass_one(index):
        for ring in ones[index]:
            ring.forward()

    def turn_over(index):
        for ring, then in zip(ones[index], twos[index]):
            ring.near_done()
            ring.far_done()
            then.start()

    def pass_two(index):
        for ring in twos[index]:
            ring.forward()

    def complete(index):
        for ring in twos[index]:
            ring.near_done()
            ring.far_done()

    group_x, group_cot = groups
    swaps[0].start()
    ones[0][0].start()
    swap_norms.start()
    swaps[1].start()
    ones[1][0].start()
    group_x.start()
    for swap in swaps[2:]:
        swap.start()
    swaps[0].wait_recv()
    ones[0][1].start()
    swaps[1].wait_recv()
    ones[1][1].start()
    for copy in copies:
        copy.wait()
    turn_over(0)
    group_x.forward()
    turn_over(1)
    pass_two(0)
    pass_two(1)
    begin(2)
    begin(3)
    begin(4)
    group_x.share()
    swap_norms.wait_recv()

    def first_norm(pos):
        here = pl.ds(pos, 16)
        left, right = vx[here, 0:HALF].astype(F32), vx[here, HALF:WIDTH].astype(F32)
        mean = (
            jnp.sum(left, 1, keepdims=True) + jnp.sum(right, 1, keepdims=True)
        ) / WIDTH
        left, right = left - mean, right - mean
        scale = lax.rsqrt(
            (
                jnp.sum(left * left, 1, keepdims=True)
                + jnp.sum(right * right, 1, keepdims=True)
            )
            / WIDTH
            + EPSILON
        )
        lane = lax.broadcasted_iota(jnp.int32, (16, 128), 1)
        vlogs[here, :] = jnp.where(lane == 0, mean, scale)
        n1[here, 0:HALF] = (left * scale * vnorm[0, 0:1, :] + vnorm[0, 1:2, :]).astype(BF16)
        n1[here, HALF:WIDTH] = (
            right * scale * vnorm[1, 0:1, :] + vnorm[1, 1:2, :]
        ).astype(BF16)

    def norm_rows(start):
        sweep(512, 16, lambda pos: first_norm(pl.multiple_of(start + pos, 16)), 4)

    group_x.near_finish()
    norm_rows(512 - 512 * lax.rem(place.chip, 2))
    group_x.finish()
    group_cot.start()
    norm_rows(512 * lax.rem(place.chip, 2))
    for index in (2, 3, 4):
        pass_one(index)
    key_places(length[0], places)
    keep_n1 = near.copy(n1, rows_one)
    keep_n1.start()
    complete(1)
    smalls = [vsmall[index].reshape(128, 128).astype(BF16) for index in range(2)]
    query_add = spread(smalls[0], 1, 0, 32, 8 * row, LOCAL)
    value_add = spread(smalls[0], 1, 32, 32, 8 * row, LOCAL)
    complete(0)
    keep_qkv = near.copy(vqkv, gqkv)
    keep_qkv.start()

    def project(index, carry):
        here = pl.ds(pl.multiple_of(index * 256, 256), 256)
        for third, add in enumerate((query_add, None, value_add)):
            cols = slice(third * 256, (third + 1) * 256)
            made = nn(n1[here, :], vqkv[:, :, :, :, cols].reshape(WIDTH, 256))
            if add is not None:
                made = made + add
            made = made.astype(BF16)
            if third == 0:
                made = made * BF16(HEAD_DIM**-0.5)
            vheads[third, here, :] = made
        return carry

    turn_over(2)
    lax.fori_loop(0, 4, project, 0)
    group_cot.forward()
    vt[...] = vheads[2].T
    args = (vheads.at[0], vheads.at[1], vt, out_t, logs, places, raws, probs)
    attend_block(0, *args)
    pass_two(2)
    turn_over(3)
    turn_over(4)
    attend_block(1, *args)
    attend_block(2, *args)
    attend_block(3, *args)
    vheads[3] = out_t[...].T.astype(BF16)
    complete(2)
    keep_heads = near.copy(vheads, heads)
    keep_heads.start()
    keep_dense = near.copy(vdense, gdense)
    keep_dense.start()

    scatter = GroupScatter(
        net, place, part, row_slices, (128, WIDTH), total, ring_in
    )
    weight = vdense[pl.ds(2 * row, 2)].reshape(LOCAL, WIDTH)
    for index, chip in enumerate(scatter.order):
        starts = [pl.multiple_of(rows_of(chip, core), 128) for core in range(2)]
        both = jnp.concatenate([vheads[3, pl.ds(start, 128), :] for start in starts], 0)
        made = nn(both, weight).astype(BF16)
        part[pl.ds(starts[0], 128), :] = made[0:128]
        part[pl.ds(starts[1], 128), :] = made[128:256]
        scatter.mates[index].start()
    scatter.first(0, 1, 2)
    group_cot.share()
    group_cot.near_finish()
    group_cot.finish()
    keep_cot = near.copy(vcot, gcot)
    keep_cot.start()
    for side in range(2):
        half = pl.ds(side * HALF, HALF)
        vectors[0:1, half] = spread(smalls[side], 1, 64, 64, 0, HALF)
        vectors[1:2, half] = spread(smalls[side], 2, 0, 64, 0, HALF)
        vectors[3:4, half] = vnorm[side, 2:3, :]
        vectors[4:5, half] = vnorm[side, 3:4, :]
    vectors[2:3, 0:HALF] = jnp.where(
        row == 0,
        spread(smalls[0], 0, 0, 64, 0, HALF),
        spread(smalls[0], 0, 64, 64, 0, HALF),
    )
    scatter.second()
    pass_two(3)
    pass_two(4)
    scatter.arrive()
    group_two = GroupGather(
        net,
        place,
        row_block(rows_two),
        lambda half: own if half is None else own.at[pl.ds(64 * half, 64), :],
    )
    keep_own = near.copy(own, row_block(rows_two)(place.chip, place.core, None))
    first_row = rows_of(place.chip, place.core)
    for side in range(2):

        def one(pos, side=side):
            here = pl.ds(pl.multiple_of(pos + 64 * side, 16), 16)
            there = pl.ds(pl.multiple_of(first_row + pos + 64 * side, 16), 16)
            values = (
                vx[there, :].astype(F32) + scatter.result(side, pos) + vectors[0:1, :]
            )
            residual[here, :] = values
            own[here, :] = (
                normalize(values)[0] * vectors[3:4, :] + vectors[4:5, :]
            ).astype(BF16)

        sweep(64, 16, one)
    group_two.start()
    keep_own.start()
    complete(3)
    stats[...] = vlogs[pl.ds(pl.multiple_of(place.col * 256, 256), 256), :]
    complete(4)
    keep_fc2 = near.copy(vfc2, gfc2)
    keep_fc2.start()
    keeps = []
    for index in range(4):
        here = pl.ds(index * 256, 256)
        for piece in range(4):
            lines = vfc2[piece].reshape(256, WIDTH)
            tile[index, :, pl.ds(piece * 256, 256)] = nt(vcot[here, :], lines)
        keep = near.copy(tile.at[index], grad_act.at[here, :])
        keep.start()
        keeps.append(keep)
        if index == 1:
            group_two.forward()
        if index == 3:
            group_two.share()
    group_two.near_finish()
    group_two.finish()
    keeps += [keep_n1, keep_qkv, keep_heads, keep_dense, keep_cot, keep_own, keep_fc2]
    for keep in keeps:
        keep.wait()
    swap_norms.wait_send()
    for swap in swaps:
        swap.wait_send()
    for pair in ones + twos:
        for ring in pair:
            ring.drain()
    scatter.drain()


def forward(*args):
    remote = 6 + 3 * 10 + 10 + 5 * 4 * 6
    bf, full = (lambda *shape: jax.ShapeDtypeStruct(shape, BF16)), (
        lambda *shape: jax.ShapeDtypeStruct(shape, F32)
    )
    return pl.pallas_call(
        forward_kernel,
        out_shape=(
            bf(SEQ, WIDTH),
            bf(2, 4, 4, 64, 768),
            bf(4, 4, 32, 2048),
            bf(2, 4, 4, 64, 1024),
            bf(4, 4, 64, 2048),
            bf(SEQ, WIDTH),
            bf(SEQ, WIDTH),
            bf(4, SEQ, LOCAL),
            full(4, 1, SEQ),
            full(128, WIDTH),
            full(256, 128),
            full(8, WIDTH),
            full(SEQ, 1024),
        ),
        in_specs=[pl.BlockSpec(memory_space=pltpu.SMEM)]
        + any_specs(2)
        + vmem_specs(1)
        + any_specs(1)
        + vmem_specs(1)
        + any_specs(1)
        + vmem_specs(5),
        out_specs=tuple(any_specs(8) + vmem_specs(4) + any_specs(1)),
        scratch_shapes=[
            pltpu.VMEM((SEQ, WIDTH), BF16),
            pltpu.VMEM((SEQ, WIDTH), BF16),
            pltpu.VMEM((2, 4, 4, 64, 768), BF16),
            pltpu.VMEM((4, 4, 32, 2048), BF16),
            pltpu.VMEM((4, 4, 64, 2048), BF16),
            pltpu.VMEM((2, 4, 4, 8, 128), F32),
            pltpu.VMEM((2, 8, HALF), F32),
            pltpu.VMEM((SEQ, WIDTH), BF16),
            pltpu.VMEM((4, SEQ, LOCAL), BF16),
            pltpu.VMEM((LOCAL, SEQ), BF16),
            pltpu.VMEM((LOCAL, SEQ), F32),
            pltpu.VMEM((SEQ, WIDTH), BF16),
            pltpu.VMEM((128, WIDTH), BF16),
            pltpu.VMEM((4, 256, 1024), F32),
            pltpu.VMEM((SEQ, 128), F32),
            pltpu.VMEM((2, 64, 768), BF16),
            pltpu.VMEM((2, 64, 1024), BF16),
            pltpu.VMEM((8, 128), F32),
            pltpu.VMEM((8, HALF), F32),
            pltpu.VMEM((SEQ, 128), F32),
            pltpu.VMEM((SEQ, BLOCK), F32),
            pltpu.VMEM((SEQ, BLOCK), BF16),
        ]
        + scatter_scratch(128, WIDTH)
        + sem_arrays(remote, 20),
        compiler_params=comm_params(0),
        name="forward",
    )(*args)


def tn(left, right):
    return lax.dot_general(left, right, (((0,), (0,)), ((), ())), preferred_element_type=F32)


def turn_kernel(
    rows_two, fc1, fc2, cot, grad_act, residual, vectors,
    gathered, pairs_out, grad_fc1, mid_fc2, mid_fc1, sums,
    n2, w1, w2, vcot, gact, act, gh, part, own, pout, g1, g2, many, total_out, total, ring_in, *rest,
):
    *rings, send, recv, near_sems = rest
    place = Place()
    net, near = Net(send, recv), Near(near_sems)
    peers = (
        x_devices(place)
        + [place.on_y(1), place.on_y(-1), place.on_z(1), place.on_z(-1)]
    )
    announce(peers)
    load_n2, load_w1 = near.copy(rows_two, n2), near.copy(fc1, w1)
    load_n2.start()
    load_w1.start()
    scatter = GroupScatter(
        net, place, part, row_slices, (128, WIDTH), total, ring_in
    )
    tiles = [
        [pl.multiple_of(rows_of(chip, core), 128) for core in range(2)]
        for chip in scatter.order
    ]
    load_act = []
    for index, starts in enumerate(tiles):
        load_act.append(
            [
                near.copy(
                    grad_act.at[pl.ds(start, 128), :],
                    gact.at[index % 2, pl.ds(128 * core, 128), :],
                )
                for core, start in enumerate(starts)
            ]
        )
    for index in range(2):
        for copy in load_act[index]:
            copy.start()
    load_w2, load_cot = near.copy(fc2, w2), near.copy(cot, vcot)
    sums[...] = jnp.zeros_like(sums)
    load_n2.wait()
    load_w1.wait()
    for index, starts in enumerate(tiles):
        for copy in load_act[index]:
            copy.wait()
        rows = [pl.ds(start, 128) for start in starts]
        both = jnp.concatenate([n2[here, :] for here in rows], 0)
        for piece in range(4):
            cols = slice(piece * 256, (piece + 1) * 256)
            hidden = (
                nn(both, w1[:, :, :, :, cols].reshape(WIDTH, 256)) + vectors[2:3, cols]
            )
            below = 0.5 + 0.5 * lax.erf(hidden * 0.5**0.5)
            density = jnp.exp(-0.5 * hidden * hidden) * 0.3989422804014327
            made = (hidden * below).astype(BF16)
            back = (
                gact[index % 2, :, cols] * (below + hidden * density)
            ).astype(BF16)
            for core, here in enumerate(rows):
                act[here, cols] = made[128 * core : 128 * core + 128]
                gh[here, cols] = back[128 * core : 128 * core + 128]
            sums[3:4, cols] += jnp.sum(back.astype(F32), 0, keepdims=True)
        if index < 2:
            for copy in load_act[index + 2]:
                copy.start()
        back = jnp.concatenate([gh[here, :] for here in rows], 0)
        if index > 0:
            scatter.first(index - 1)
        for side in range(2):
            for piece in range(4):
                cols = slice(side * HALF + piece * 256, side * HALF + piece * 256 + 256)
                made = nt(back, w1[side, piece].reshape(256, 1024)).astype(BF16)
                for core, here in enumerate(rows):
                    part[here, cols] = made[128 * core : 128 * core + 128]
        if index == 0:
            load_w2.start()
            load_cot.start()
            meet(peers)
        scatter.mates[index].start()
    load_w2.wait()
    load_cot.wait()

    def one_g2(index, carry):
        cols = pl.ds(pl.multiple_of(index * 256, 256), 256)
        for side in range(2):
            half = slice(side * HALF, (side + 1) * HALF)
            made = tn(act[:, cols], vcot[:, half]).astype(BF16)
            g2[index, :, :, half] = made.reshape(4, 64, HALF)
        return carry

    lax.fori_loop(0, 2, one_g2, 0)
    scatter.second()
    lax.fori_loop(2, 4, one_g2, 0)
    mids = [mid_fc2.at[index] for index in range(2)]
    over = OuterScatter(net, place, beside(g2, 64)[0], 64, rings[0:2], mids)
    over.start()

    def one_g1(index, carry):
        side, piece = lax.div(index, 4), lax.rem(index, 4)
        cols = pl.ds(pl.multiple_of(index * 256, 256), 256)
        g1[side, piece] = tn(n2[:, cols], gh[...]).astype(BF16).reshape(4, 64, 1024)
        return carry

    def one_out(index, carry):
        here = pl.ds(pl.multiple_of(index * 256, 256), 256)
        for side in range(2):
            half = slice(side * HALF, (side + 1) * HALF)
            made = nn(act[here, :], w2[:, :, :, half].reshape(1024, HALF))
            pout[here, half] = made.astype(BF16)
        return carry

    lax.fori_loop(0, 8, one_g1, 0)
    keep_g1 = near.copy(g1, grad_fc1)
    keep_g1.start()
    mids = [mid_fc1.at[index] for index in range(2)]
    over_fc1 = OuterScatter(net, place, stacked_rows(g1, 0), 32, rings[2:4], mids)
    over_fc1.start()
    many[...] = jnp.zeros_like(many)
    scatter.arrive()
    group = GroupGather(
        net,
        place,
        row_block(gathered),
        lambda half: own if half is None else own.at[pl.ds(64 * half, 64), :],
    )
    first_row = rows_of(place.chip, place.core)
    for side in range(2):

        def one(pos, side=side):
            here = pl.ds(pl.multiple_of(pos + 64 * side, 16), 16)
            there = pl.ds(pl.multiple_of(first_row + pos + 64 * side, 16), 16)
            arrived = scatter.result(side, pos)
            xhat, scale = normalize(residual[here, :])
            scaled = arrived * vectors[3:4, :]
            flat = jnp.mean(scaled, 1, keepdims=True)
            cross = jnp.mean(scaled * xhat, 1, keepdims=True)
            given = vcot[there, :].astype(F32)
            branch = (given + scale * (scaled - flat - xhat * cross)).astype(BF16)
            own[here, :] = branch
            many[0] += arrived * xhat
            many[1] += arrived
            many[2] += given
            many[3] += branch.astype(F32)

        sweep(64, 16, one)
    group.start()
    keep_own = near.copy(own, row_block(gathered)(place.chip, place.core, None))
    keep_own.start()
    for index, line in enumerate((0, 1, 2, 4)):
        sums[line : line + 1, :] = jnp.sum(many[index], 0, keepdims=True)
    over.middle()
    lax.fori_loop(0, 2, one_out, 0)
    group.forward()
    lax.fori_loop(2, 4, one_out, 0)
    pair = PairSum(net, place, pout, total_out)
    pair.start()
    over_fc1.middle()

    group.share()
    pair.finish()
    keep_out = near.copy(total_out, pairs_out)
    keep_out.start()
    over.finish()
    over_fc1.finish()

    group.near_finish()
    group.finish()
    for keep in (keep_own, keep_out, keep_g1):
        keep.wait()
    pair.drain()
    over.drain()
    over_fc1.drain()
    scatter.drain()


def turn(rows_two, fc1, fc2, cot, grad_act, residual, vectors):
    bf = lambda *shape: jax.ShapeDtypeStruct(shape, BF16)
    return pl.pallas_call(
        turn_kernel,
        out_shape=(
            bf(SEQ, WIDTH),
            bf(4, 128, WIDTH),
            bf(2, 4, 4, 64, 1024),
            bf(2, 4, 64, 1024),
            bf(2, 4, 32, 1024),
            jax.ShapeDtypeStruct((8, WIDTH), F32),
        ),
        in_specs=any_specs(5) + vmem_specs(2),
        out_specs=tuple(any_specs(3) + vmem_specs(3)),
        scratch_shapes=[
            pltpu.VMEM((SEQ, WIDTH), BF16),
            pltpu.VMEM((2, 4, 4, 64, 1024), BF16),
            pltpu.VMEM((4, 4, 64, 2048), BF16),
            pltpu.VMEM((SEQ, WIDTH), BF16),
            pltpu.VMEM((2, 256, 1024), F32),
            pltpu.VMEM((SEQ, 1024), BF16),
            pltpu.VMEM((SEQ, 1024), BF16),
            pltpu.VMEM((SEQ, WIDTH), BF16),
            pltpu.VMEM((128, WIDTH), BF16),
            pltpu.VMEM((SEQ, WIDTH), BF16),
            pltpu.VMEM((2, 4, 4, 64, 1024), BF16),
            pltpu.VMEM((4, 4, 64, 2048), BF16),
            pltpu.VMEM((4, 16, WIDTH), F32),
            pltpu.VMEM((4, 128, WIDTH), BF16),
        ]
        + scatter_scratch(128, WIDTH)
        + outer_scratch(64, 1024)
        + outer_scratch(32, 1024)
        + sem_arrays(20 + 24 + 4, 20),
        compiler_params=comm_params(2),
        name="turn",
    )(rows_two, fc1, fc2, cot, grad_act, residual, vectors)


def last_kernel(
    length, x, stats, branch, dense, qkv, heads, logs, rows_one, pairs_out, grad_fc1,
    mid_fc2, mid_fc1, gain, residual, vectors, sums_two,
    raw, out, rqkv, rdense, rfc1, rfc1_b, rfc2, vector, first_sums, swapped, own_branch,
    rows, wd, wq, vheads, datt, kt, dk, dv, dqt, gproj, part, pout, g1, mine_fc2, mine_fc1, gd, gq,
    result, stats_rows, stats_out, stats_in, mate_in, chips_in, y_in, z_in, vec_a, vec_b,
    stacks, late, late_two, late_group, late_y, late_z, places, probs, dscores, deltas,
    total, ring_in, ring_out, *rest,
):
    *rest, send, recv, near_sems = rest
    rest = list(rest)

    def take(count):
        taken = rest[:count]
        del rest[:count]
        return taken

    place = Place()
    row, z, y = place.row, place.z, place.y
    net, near = Net(send, recv), Near(near_sems)
    load_rows = near.copy(branch, rows)
    load_wd = near.copy(dense.at[pl.ds(2 * row, 2)], wd)
    load_heads = near.copy(heads, vheads)
    load_g1 = []
    reads = []
    for h, me in enumerate((z, y)):
        views = []
        for index, (pos, half) in enumerate(
            ((wrap(me + 1), 0), (wrap(me - 1), 1), (me, 0), (me, 1))
        ):
            pair = pl.ds(2 * half, 2)
            low = pl.ds(32, 32)
            source = (
                grad_fc1.at[0, pos, pair, low] if h == 0 else grad_fc1.at[1, pair, pos, low]
            )
            load_g1.append(near.copy(source, g1.at[h, index]))
            views.append(g1.at[h, index])
        reads.append(views)
    load_mid = [
        near.copy(mid.at[h, me], mine.at[h])
        for mid, mine in ((mid_fc2, mine_fc2), (mid_fc1, mine_fc1))
        for h, me in enumerate((y, z))
    ]
    load_out = near.copy(pairs_out.at[pl.ds(1, 3)], pout)
    load_wq = near.copy(qkv, wq)
    quarter = quarter_slices(place.chip, place.core)
    load_own = near.copy(
        branch.at[pl.ds(quarter[0], 256), pl.ds(quarter[1], HALF)], own_branch
    )
    load_own.start()
    load_rows.start()
    load_wd.start()
    load_heads.start()
    x_group = [
        place.x_at(wrap(place.chip + step), core)
        for step in range(4)
        for core in (place.core, 1 - place.core)
    ][1:]
    y_ring = [place.on_y(step) for step in (1, 2, 3)]
    z_ring = [place.on_z(step) for step in (1, 2, 3)]
    peers = x_group + y_ring + z_ring
    announce(peers)
    scatter = GroupScatter(net, place, part, quarter_slices, (256, HALF), total, ring_in)
    scatter_out = RingSum(net, place, pairs_out, pout, ring_out)
    rings_fc1, rings_dense, rings_qkv = take(2), take(2), take(2)
    mids_fc1, mids_dense, mids_qkv = take(2), take(2), take(2)
    out_fc1 = OuterScatter(
        net, place, stacked_rows(grad_fc1, 32), 32, rings_fc1, mids_fc1, reads
    )
    out_dense = OuterScatter(net, place, beside(gd, 32)[0], 32, rings_dense, mids_dense)
    out_qkv = OuterScatter(net, place, stacked(gq, 64)[0], 64, rings_qkv, mids_qkv)
    inner = []
    for mids, mine, final in (
        ([mid_fc2.at[h] for h in range(2)], [mine_fc2.at[h] for h in range(2)], rfc2),
        ([mid_fc1.at[h] for h in range(2)], [mine_fc1.at[h] for h in range(2)], rfc1),
        (mids_fc1, None, rfc1_b),
        (mids_dense, None, rdense),
        (mids_qkv, None, rqkv),
    ):
        arrived, done = take(2), take(1)[0]
        inner.append(InnerScatter(net, near, place, mids, mine, arrived, done, final))
    in_fc2, in_fc1_a, in_fc1, in_dense, in_qkv = inner
    vec_a[...] = jnp.zeros_like(vec_a)
    vec_a[2:4, :] = sums_two[0:2, :]
    vec_a[4:5, :] = sums_two[4:5, :]
    vec_a[5:6, :] = sums_two[2:3, :]
    vec_a[6:7, 0:HALF] = sums_two[3:4, 0:HALF]
    load_rows.wait()
    load_wd.wait()
    load_heads.wait()
    for load in load_g1 + load_mid:
        load.start()
    load_out.start()
    load_wq.start()

    def back_attended(index, carry):
        here = pl.ds(pl.multiple_of(index * 256, 256), 256)
        datt[here, :] = nt(rows[here, :], wd[...].reshape(LOCAL, WIDTH)).astype(BF16)
        return carry

    lax.fori_loop(0, 4, back_attended, 0)
    meet(peers)
    scatter_out.start()
    in_fc2.start()
    in_fc1_a.start()
    out_fc1.start()
    mate_send = net.copy(vec_a, mate_in, place.mate())
    mate_send.start()
    for side in range(2):
        half = slice(side * HALF, (side + 1) * HALF)
        made = tn(vheads[3], rows[:, half]).astype(BF16).reshape(2, 4, 32, HALF)
        gd[pl.ds(2 * row, 2), :, :, half] = made
        gd[pl.ds(2 - 2 * row, 2), :, :, half] = jnp.zeros_like(made)
    out_dense.start()
    for load in load_g1 + load_mid:
        load.wait()
    load_one = near.copy(rows_one, rows)
    load_one.start()
    kt[...] = vheads[1].T
    dk[...] = jnp.zeros_like(dk)
    dv[...] = jnp.zeros_like(dv)
    key_places(length[0], places)
    args = [vheads.at[index] for index in range(4)]
    args += [datt, logs, places, kt, dk, dv, dqt, probs, dscores, deltas]
    attend_back_block(0, *args)
    mate_send.wait_recv()
    vec_b[...] = vec_a[...]
    vec_b[2:6, :] += mate_in[2:6, :]
    chip_sends = [
        net.copy(vec_b, chips_in.at[step - 1], place.on_x(step)) for step in (1, 2, 3)
    ]
    for copy in chip_sends:
        copy.start()
    attend_back_block(1, *args)
    load_out.wait()
    scatter_out.second()
    attend_back_block(2, *args)
    mate_send.wait_send()
    for copy in chip_sends:
        copy.wait_recv()
    vec_a[...] = vec_b[...]
    for index in range(3):
        vec_a[2:6, :] += chips_in[index, 2:6, :]
    vec_a[7:8, :] = chips_in[1, 6:7, :]
    y_sends = [net.copy(vec_a, y_in.at[i], device) for i, device in enumerate(y_ring)]
    for copy in y_sends:
        copy.start()
    attend_back_block(3, *args)
    gproj[:, 0:256] = dqt[...].T * BF16(HEAD_DIM**-0.5)
    gproj[:, 256:512] = dk[...].astype(BF16)
    gproj[:, 512:768] = dv[...].astype(BF16)
    load_wq.wait()
    load_one.wait()
    columns = jnp.concatenate(
        [
            jnp.sum(gproj[:, third * 256 : third * 256 + 256].astype(F32), 0, keepdims=True)
            for third in range(3)
        ],
        1,
    )
    def one_gq(index, carry):
        side, piece = lax.div(index, 4), lax.rem(index, 4)
        cols = pl.ds(pl.multiple_of(index * 256, 256), 256)
        made = tn(rows[:, cols], gproj[...])
        gq[side, piece] = made.astype(BF16).reshape(4, 64, 768)
        return carry

    scatter_out.arrive()
    for side in range(2):

        def finish_rows(pos, side=side):
            here = pl.ds(pl.multiple_of(pos + 64 * side, 16), 16)
            result[here, :] = (
                residual[here, :] + scatter_out.result(side, pos) + vectors[1:2, :]
            ).astype(BF16)

        sweep(64, 16, finish_rows)
    there = pl.ds(row * 128, 128)
    out_swap = net.copy(
        result.at[:, pl.ds((1 - row) * HALF, HALF)], out.at[there, :], place.partner()
    )
    out_keep = near.copy(result.at[:, pl.ds(row * HALF, HALF)], out.at[there, :])
    out_swap.start()
    out_keep.start()
    lax.fori_loop(0, 4, one_gq, 0)
    out_qkv.rings[0].start()
    lax.fori_loop(4, 8, one_gq, 0)
    out_qkv.rings[1].start()
    for index, chip in enumerate(scatter.order):
        here = pl.ds(pl.multiple_of(lax.rem(chip, 2) * 512, 512), 512)
        cols = pl.ds(pl.multiple_of(lax.div(chip, 2) * HALF, HALF), HALF)
        weight = wq[lax.div(chip, 2)].reshape(HALF, 768)
        part[here, cols] = nt(gproj[here, :], weight).astype(BF16)
        scatter.mates[index].start()
        if index > 0:
            scatter.first(index - 1)
    out_fc1.middle()
    out_dense.middle()
    lane = lax.broadcasted_iota(jnp.int32, (256, 128), 1)
    stacks[...] = jnp.zeros_like(stacks)

    def one_stack(index, carry):
        side, piece = lax.div(index, 4), lax.rem(index, 4)
        weight = wq[side, piece].reshape(256, 768).astype(F32)
        made = gq[side, piece].reshape(256, 768).astype(F32)
        stacks[...] += jnp.where(
            lane == index, jnp.sum(weight * made, 1, keepdims=True), 0.0
        ) + jnp.where(lane == index + 8, jnp.sum(weight * columns, 1, keepdims=True), 0.0)
        return carry

    lax.fori_loop(0, 8, one_stack, 0)
    late[...] = jnp.zeros_like(late)
    late[0:16, :] = stacks[...].T[0:16, :]
    late[16:17, :] = columns[:, 0:256]
    late[17:18, :] = columns[:, 512:768]
    late_x_sends = [
        net.copy(late, late_group.at[index], device) for index, device in enumerate(x_group)
    ]
    for copy in late_x_sends:
        copy.start()
    out_qkv.middle()
    scatter.second()
    out_fc1.finish()
    in_fc1.start()
    out_dense.finish()
    in_dense.start()
    for copy in y_sends:
        copy.wait_recv()
    for copy in chip_sends:
        copy.wait_send()
    vec_b[...] = vec_a[...]
    for index in range(3):
        vec_b[...] += y_in[index]
    z_sends = [net.copy(vec_b, z_in.at[i], device) for i, device in enumerate(z_ring)]
    for copy in z_sends:
        copy.start()
    out_qkv.finish()
    in_qkv.start()
    for copy in late_x_sends:
        copy.wait_recv()
    late_two[...] = late[...]
    for index in range(7):
        late_two[0:16, :] += late_group[index, 0:16, :]
    late_two[18:20, :] = late_group[3, 16:18, :]
    late_y_sends = [
        net.copy(late_two, late_y.at[i], device) for i, device in enumerate(y_ring)
    ]
    for copy in late_y_sends:
        copy.start()
    in_fc2.finish()
    in_fc1_a.finish()
    scatter.arrive()

    lane = lax.broadcasted_iota(jnp.int32, (16, 128), 1)
    for side in range(2):

        def sums(pos, side=side):
            here = pl.ds(pl.multiple_of(pos + 128 * side, 16), 16)
            arrived = scatter.result(side, pos)
            scaled = arrived * gain[...]
            xhat = (x[here, :].astype(F32) - stats[here, 0:1]) * stats[here, 1:2]
            flat = jnp.sum(scaled, 1, keepdims=True)
            cross = jnp.sum(scaled * xhat, 1, keepdims=True)
            stats_rows[here, :] = jnp.where(lane == 0, flat, cross)
            raw[here, :] = arrived

        sweep(128, 16, sums, 4)
    stats_out[...] = stats_rows[...].T[0:8, :]
    swap_stats = net.copy(stats_out, stats_in, place.partner())
    swap_stats.start()
    in_qkv.finish()
    for copy in late_y_sends:
        copy.wait_recv()
    for copy in late_x_sends:
        copy.wait_send()
    late[...] = late_two[...]
    for index in range(3):
        late[...] += late_y[index]
    late_z_sends = [net.copy(late, late_z.at[i], device) for i, device in enumerate(z_ring)]
    for copy in late_z_sends:
        copy.start()
    in_fc1.finish()
    in_dense.finish()
    swap_stats.wait_recv()
    swapped[...] = stats_out[...] + stats_in[...]
    for copy in z_sends + late_z_sends:
        copy.wait_recv()
    vector[...] = vec_b[...]
    first_sums[...] = late[...]
    for index in range(3):
        vector[...] += z_in[index]
        first_sums[...] += late_z[index]
    load_own.wait()
    out_swap.wait_recv()
    for stage in (out_fc1, out_dense, out_qkv):
        stage.drain()
    for stage in inner:
        stage.close()
    out_keep.wait()
    out_swap.wait_send()
    swap_stats.wait_send()
    for copy in y_sends + late_y_sends + z_sends + late_z_sends:
        copy.wait_send()
    scatter.drain()
    scatter_out.drain()


def last(*args):
    bf = lambda *shape: jax.ShapeDtypeStruct(shape, BF16)
    full = lambda *shape: jax.ShapeDtypeStruct(shape, F32)
    anywhere, inside = any_specs(1)[0], vmem_specs(1)[0]
    where = (
        [pl.BlockSpec(memory_space=pltpu.SMEM), inside, inside]
        + [anywhere] * 4
        + [inside]
        + [anywhere] * 5
        + [inside] * 4
    )
    return pl.pallas_call(
        last_kernel,
        out_shape=(
            full(256, HALF),
            bf(256, HALF),
            bf(2, 64, 768),
            bf(2, 32, 1024),
            bf(2, 32, 1024),
            bf(2, 32, 1024),
            bf(2, 64, 1024),
            full(8, WIDTH),
            full(24, 256),
            full(8, 256),
            bf(256, HALF),
        ),
        in_specs=where,
        out_specs=tuple(vmem_specs(10) + any_specs(1)),
        scratch_shapes=[
            pltpu.VMEM((SEQ, WIDTH), BF16),
            pltpu.VMEM((2, 4, 32, WIDTH), BF16),
            pltpu.VMEM((2, 4, 4, 64, 768), BF16),
            pltpu.VMEM((4, SEQ, LOCAL), BF16),
            pltpu.VMEM((SEQ, LOCAL), BF16),
            pltpu.VMEM((LOCAL, SEQ), BF16),
            pltpu.VMEM((SEQ, LOCAL), F32),
            pltpu.VMEM((SEQ, LOCAL), F32),
            pltpu.VMEM((LOCAL, SEQ), BF16),
            pltpu.VMEM((SEQ, 768), BF16),
            pltpu.VMEM((SEQ, WIDTH), BF16),
            pltpu.VMEM((3, 128, WIDTH), BF16),
            pltpu.VMEM((2, 4, 2, 32, 1024), BF16),
            pltpu.VMEM((2, 64, 1024), BF16),
            pltpu.VMEM((2, 32, 1024), BF16),
            pltpu.VMEM((4, 4, 32, 2048), BF16),
            pltpu.VMEM((2, 4, 4, 64, 768), BF16),
            pltpu.VMEM((128, WIDTH), BF16),
            pltpu.VMEM((256, 128), F32),
            pltpu.VMEM((8, 256), F32),
            pltpu.VMEM((8, 256), F32),
            pltpu.VMEM((8, WIDTH), F32),
            pltpu.VMEM((3, 8, WIDTH), F32),
            pltpu.VMEM((3, 8, WIDTH), F32),
            pltpu.VMEM((3, 8, WIDTH), F32),
            pltpu.VMEM((8, WIDTH), F32),
            pltpu.VMEM((8, WIDTH), F32),
            pltpu.VMEM((256, 128), F32),
            pltpu.VMEM((24, 256), F32),
            pltpu.VMEM((24, 256), F32),
            pltpu.VMEM((7, 24, 256), F32),
            pltpu.VMEM((3, 24, 256), F32),
            pltpu.VMEM((3, 24, 256), F32),
            pltpu.VMEM((SEQ, 128), F32),
            pltpu.VMEM((SEQ, 2 * BLOCK), BF16),
            pltpu.VMEM((SEQ, 2 * BLOCK), BF16),
            pltpu.VMEM((4, 1, BLOCK), F32),
        ]
        + scatter_scratch(256, HALF)
        + [pltpu.VMEM((6, 64, WIDTH), BF16)]
        + outer_scratch(32, 1024)
        + outer_scratch(32, 1024)
        + outer_scratch(64, 768)
        + mid_scratch(32, 1024)
        + mid_scratch(32, 1024)
        + mid_scratch(64, 768)
        + inner_scratch(64, 1024)
        + inner_scratch(32, 1024)
        + inner_scratch(32, 1024)
        + inner_scratch(32, 1024)
        + inner_scratch(64, 768)
        + sem_arrays(20 + 3 * 12 + 5 * 7 + 30, 32),
        compiler_params=comm_params(3, 62),
        name="last",
    )(*args)


def finish_kernel(
    raw, rows_out, rqkv, rdense, rfc1, rfc1_b, rfc2, vector, first_sums, swapped, own_branch,
    x, stats, gain, offset,
    outputs, ingrad, qkv, query, value, dense, dense_add, fc1, hidden_add, fc2, output_add,
    gain_one, offset_one, gain_two, offset_two, turned,
):
    row = lax.axis_index("row")
    dp = lax.axis_index("dp")
    outputs[...] = rows_out[...]
    turned[...] = jnp.concatenate([swapped[...], jnp.zeros((120, 256), F32)], 0).T

    def apply(pos):
        here = pl.ds(pos, 16)
        both = turned[here, :] / WIDTH
        scale = stats[here, 1:2]
        xhat = (x[here, :].astype(F32) - stats[here, 0:1]) * scale
        ingrad[here, :] = own_branch[here, :].astype(F32) + scale * (
            raw[here, :] * gain[...] - both[:, 0:1] - xhat * both[:, 1:2]
        )

    sweep(256, 16, apply, 4)
    for index in range(12):
        made = []
        for block in (2 * index, 2 * index + 1):
            head, third = block // 3, block % 3
            place_in = third * 4 + head % 4
            made.append((group_of(rqkv.at[head // 4], place_in // 2), place_in % 2))
        (left, left_odd), (right, right_odd) = made
        qkv[:, index * 128 : index * 128 + 128] = merge(
            left, right, left_odd == 1, right_odd == 0
        )
    for index in range(16):
        for side, source in enumerate((rfc1, rfc1_b)):
            fc1[side * 32 : side * 32 + 32, index * 128 : index * 128 + 128] = merge(
                group_of(source.at[0], index // 2),
                group_of(source.at[1], index // 2),
                index % 2 == 1,
                index % 2 == 0,
            )
    fc2[0:64, :] = rfc2[0].astype(F32)
    fc2[64:128, :] = rfc2[1].astype(F32)
    dense[...] = rdense[0].astype(F32) + rdense[1].astype(F32)
    for index in range(4):
        cols = slice(index * 256, index * 256 + 256)
        products = first_sums[pl.ds(row * 4 + index, 1), :]
        plain = first_sums[pl.ds(row * 4 + index + 8, 1), :]
        gain_one[:, cols] = (products - offset[:, cols] * plain) / gain[:, cols]
        offset_one[:, cols] = plain
    half = pl.ds(pl.multiple_of(row * HALF, HALF), HALF)
    gain_two[...] = vector[2:3, half]
    offset_two[...] = vector[3:4, half]
    odd = lax.rem(dp, 2)
    start = lax.div(dp, 2) * 128

    def swap_if(values, swap):
        return jnp.where(swap == 1, pltpu.roll(values, 64, 1), values)

    def eight(line, lane):
        return vector[line : line + 1, pl.ds(pl.multiple_of(lane, 128), 128)] + jnp.zeros(
            (8, 128), F32
        )

    dense_add[...] = swap_if(eight(4, row * HALF + start), odd)[0:1, 0:64]
    output_add[...] = swap_if(eight(5, row * HALF + start), odd)[0:1, 0:64]
    own, other = eight(6, start), eight(7, start)
    first = jnp.where(row == 0, own, other)
    second = jnp.where(row == 0, other, own)
    lanes = lax.broadcasted_iota(jnp.int32, (8, 128), 1)
    hidden_add[...] = jnp.where(
        lanes < 64, swap_if(first, odd), swap_if(second, 1 - odd)
    )[0:1, :]
    theirs = lax.div(dp, 8) == row
    inside = lax.rem(dp, 8)
    quarter = lax.rem(inside, 4)
    upper = lax.div(inside, 4) == 1
    for target, base in ((query, 16), (value, 17)):
        lines = [
            first_sums[at : at + 1, lanes_from : lanes_from + 128]
            + jnp.zeros((8, 128), F32)
            for at in (base, base + 2)
            for lanes_from in (0, 128)
        ]
        mine = jnp.where(upper, lines[1], lines[0])
        other = jnp.where(upper, lines[3], lines[2])
        chosen = jnp.where(theirs, mine, other)
        moved = chosen
        for step in range(1, 4):
            moved = jnp.where(quarter == step, pltpu.roll(chosen, 128 - 32 * step, 1), moved)
        target[...] = moved[0:1, 0:32]


def finish(*args):
    full = lambda *shape: jax.ShapeDtypeStruct(shape, F32)
    whole = lambda shape: pl.BlockSpec(shape, lambda index: (0,) * len(shape))
    shapes = (
            jax.ShapeDtypeStruct((256, HALF), BF16),
            full(256, HALF),
            full(64, 1536),
            full(1, 32),
            full(1, 32),
            full(32, 1024),
            full(1, 64),
            full(64, 2048),
            full(1, 128),
            full(128, HALF),
            full(1, 64),
            full(1, HALF),
            full(1, HALF),
            full(1, HALF),
            full(1, HALF),
        )
    return pl.pallas_call(
        finish_kernel,
        out_shape=shapes,
        grid=(1,),
        in_specs=[whole(value.shape) for value in args],
        out_specs=tuple(whole(value.shape) for value in shapes),
        scratch_shapes=[pltpu.VMEM((256, 128), F32)],
        compiler_params=pltpu.CompilerParams(vmem_limit_bytes=62 << 20),
        name="finish",
    )(*args)


def local(
    inputs,
    cotangent,
    lengths,
    attention_norm_gain,
    attention_norm_bias,
    qkv_weight,
    query_bias,
    value_bias,
    dense_weight,
    dense_bias,
    feedforward_norm_gain,
    feedforward_norm_bias,
    fc1_weight,
    fc1_bias,
    fc2_weight,
    fc2_bias,
):
    zeros = jnp.zeros((64,), BF16)
    small = jnp.concatenate(
        [fc1_bias, query_bias, value_bias, dense_bias, fc2_bias, zeros]
    ).astype(F32)
    (
        rows_cot, qkv_full, dense_full, fc1_full, fc2_full, rows_one, rows_two, heads,
        logs, residual, stats, vectors, grad_act,
    ) = forward(
        lengths,
        inputs,
        cotangent,
        qkv_weight,
        dense_weight,
        fc1_weight,
        fc2_weight.reshape(2, 64, 1024),
        small.reshape(1, 384),
        attention_norm_gain.reshape(1, HALF),
        attention_norm_bias.reshape(1, HALF),
        feedforward_norm_gain.reshape(1, HALF),
        feedforward_norm_bias.reshape(1, HALF),
    )
    rows_branch, pairs_out, grad_fc1, mid_fc2, mid_fc1, sums_two = turn(
        rows_two, fc1_full, fc2_full, rows_cot, grad_act, residual, vectors
    )
    (
        raw, rows_out, red_qkv, red_dense, red_fc1, red_fc1_b, red_fc2, vector,
        first_sums, swapped, own_branch,
    ) = last(
        lengths, inputs, stats, rows_branch, dense_full, qkv_full, heads, logs, rows_one,
        pairs_out, grad_fc1, mid_fc2, mid_fc1, attention_norm_gain.reshape(1, HALF), residual, vectors,
        sums_two,
    )
    results = finish(
        raw, rows_out, red_qkv, red_dense, red_fc1, red_fc1_b, red_fc2, vector,
        first_sums, swapped, own_branch,
        inputs, stats, attention_norm_gain.reshape(1, HALF),
        attention_norm_bias.reshape(1, HALF),
    )
    return tuple(
        value.reshape(value.shape[1]) if value.shape[0] == 1 else value
        for value in results
    )


def solution(mesh):
    return jax.shard_map(
        local,
        mesh=mesh,
        in_specs=(
            P(("dp", "col"), "row"),
            P(("dp", "col"), "row"),
            P("dp"),
            P("row"),
            P("row"),
            P(("row", "dp"), "col"),
            P(("col", "dp")),
            P(("col", "dp")),
            P(("col", "dp"), "row"),
            P(("row", "dp")),
            P("row"),
            P("row"),
            P(("row", "dp"), "col"),
            P(("col", "dp")),
            P(("col", "dp"), "row"),
            P(("row", "dp")),
        ),
        out_specs=(
            P(("dp", "col"), "row"),
            P(("dp", "col"), "row"),
            P(("row", "dp"), "col"),
            P(("col", "dp")),
            P(("col", "dp")),
            P(("col", "dp"), "row"),
            P(("row", "dp")),
            P(("row", "dp"), "col"),
            P(("col", "dp")),
            P(("col", "dp"), "row"),
            P(("row", "dp")),
            P("row"),
            P("row"),
            P("row"),
            P("row"),
        ),
        check_vma=False,
    )
```
